32 devices in a mesh: rep: 8 (over z, core), shard: 4 (over y, x).
Axes of the slice: x: 2, y: 2, z: 4, core: 2. Of those that a mesh axis runs over, the one named last changes fastest.
Arguments:
- tokens: float32 [64, 1024, 768], P(('rep', 'shard')), may hold values from -6 to 6
- segments: int32 [64, 1024], P(('rep', 'shard')), may hold values from 0 to 3, never falling along the last dimension, each value on 1 to 800 neighbouring positions
- time_steps: int32 [64], P(('rep', 'shard')), may hold values from 0 to 1999
- time_table: bfloat16 [2000, 768], P('shard'), may hold values from -4 to 4
- ln1_gain: bfloat16 [768], P('shard'), may hold values from 0.5 to 1.5
- ln1_bias: bfloat16 [768], P('shard'), may hold values from -1 to 1
- q_weight: bfloat16 [768, 768], P('shard'), may hold values from -0.21875 to 0.21875
- q_bias: bfloat16 [768], P('shard'), may hold values from -1 to 1
- k_weight: bfloat16 [768, 768], P('shard'), may hold values from -0.21875 to 0.21875
- v_weight: bfloat16 [768, 768], P('shard'), may hold values from -0.21875 to 0.21875
- v_bias: bfloat16 [768], P('shard'), may hold values from -1 to 1
- o_weight: bfloat16 [768, 768], P('shard'), may hold values from -0.875 to 0.875
- o_bias: bfloat16 [768], P('shard'), may hold values from -1 to 1
- ln2_gain: bfloat16 [768], P('shard'), may hold values from 0.5 to 1.5
- ln2_bias: bfloat16 [768], P('shard'), may hold values from -1 to 1
- up_weight: bfloat16 [768, 3072], P('shard'), may hold values from -0.21875 to 0.21875
- up_bias: bfloat16 [3072], P('shard'), may hold values from -1 to 1
- down_weight: bfloat16 [3072, 768], P('shard'), may hold values from -0.109375 to 0.109375
- down_bias: bfloat16 [768], P('shard'), may hold values from -1 to 1
- cotangent: float32 [64, 1024, 768], P(('rep', 'shard')), may hold values from -6 to 6
Outputs:
- result: float32 [64, 1024, 768], P(('rep', 'shard'))
- grad_tokens: float32 [64, 1024, 768], P(('rep', 'shard'))
- grad_time_table: float32 [2000, 768], P('shard')
- grad_ln1_gain: float32 [768], P('shard')
- grad_ln1_bias: float32 [768], P('shard')
- grad_q_weight: float32 [768, 768], P('shard')
- grad_q_bias: float32 [768], P('shard')
- grad_k_weight: float32 [768, 768], P('shard')
- grad_v_weight: float32 [768, 768], P('shard')
- grad_v_bias: float32 [768], P('shard')
- grad_o_weight: float32 [768, 768], P('shard')
- grad_o_bias: float32 [768], P('shard')
- grad_ln2_gain: float32 [768], P('shard')
- grad_ln2_bias: float32 [768], P('shard')
- grad_up_weight: float32 [768, 3072], P('shard')
- grad_up_bias: float32 [3072], P('shard')
- grad_down_weight: float32 [3072, 768], P('shard')
- grad_down_bias: float32 [768], P('shard')
The draws below stay inside these ranges and needn't reach their ends.
Inputs may be any that keep to these rules, and one draw needn't show every extreme that they name: `segments`: within a sequence segment numbers never fall; each document holds 1 to 800 tokens and one holds exactly 800.
All inputs are finite; a program needn't handle non-finite values.
Results may differ from the reference program's by a relative error of at most 0.022.
Values may be sent and summed in bfloat16 or wider, within the bound.
No kernel may reach another device: no remote copies, remote signals or barrier semaphores. Data moves between devices by JAX's collectives and lax.ppermute only.
A program may use at most 320 MiB of HBM per device.

```python
import math
import jax
import jax.numpy as jnp
import numpy as np
from jax import lax

D = 768
HEADS = 12
FF = 3072
TSTEPS = 2000
LEN = 1024
SEGS = 4
DOC_MOST = 800
SEQS = 64


def set_ends(array, key, smallest, high):
    shape = array.shape
    place = [jax.random.randint(jax.random.fold_in(key, axis), (), 0, shape[axis]) for axis in range(len(shape))]
    array = array.at[tuple(place)].set(smallest)
    longest = shape.index(max(shape))
    place[longest] = (place[longest] + 1) % shape[longest]
    return array.at[tuple(place)].set(high)


def levels(rng, shape, shards, least, top_value):
    factor_of, own = 1.0, jax.random.fold_in(rng, 6)
    for position, blocks in shards:
        steps = jnp.exp(jax.random.uniform(jax.random.fold_in(own, position), (blocks,), jnp.float32, least / len(shards), top_value / len(shards)))
        factor_of = factor_of * jnp.repeat(steps, shape[position] // blocks).reshape([-1 if axis == position else 1 for axis in range(len(shape))])
    return factor_of


def length_profile(number_of, total, limit, lean):
    loads = [(1 << 20) // math.isqrt(grade ** lean) + 1 for grade in range(2, number_of + 1)]
    spare, holding = total - limit - (number_of - 1), [1] * (number_of - 1)
    while spare > 0:
        free = [i for i in range(number_of - 1) if holding[i] < limit]
        pool, remaining = sum([loads[i] for i in free]), spare
        for i in free:
            addition = min(limit - holding[i], max(1, remaining * loads[i] // pool), spare)
            holding[i] = holding[i] + addition
            spare = spare - addition
    return np.array([limit] + holding)


def ragged_sizes(key, number_of, total, most, slope):
    if number_of == 2:
        one = jax.random.randint(key, (), max(1, total - most), min(most, total - 1) + 1)
        return jnp.stack([one, total - one])
    lengths = jnp.asarray(length_profile(number_of, total, most, slope), jnp.int32)
    twos = (number_of - 1) // 2
    donor, taker = lengths[1:1 + 2 * twos:2], lengths[2:2 + 2 * twos:2]
    room = jnp.minimum(donor - 1, most - taker)
    passed = jax.random.randint(jax.random.fold_in(key, 1), (twos,), 0, 1 << 20) % (room + 1)
    lengths = lengths.at[1:1 + 2 * twos:2].set(donor - passed).at[2:2 + 2 * twos:2].set(taker + passed)
    return lengths[jax.random.permutation(jax.random.fold_in(key, 2), number_of)]


def scatter_about(stream_key, extent, scale, limit, pieces=(), dtype=jnp.bfloat16):
    drawn = scale * jax.random.normal(stream_key, extent, jnp.float32)
    if pieces:
        drawn = drawn * levels(stream_key, extent, pieces, -0.22, 0.18)
    return jnp.clip(drawn, -limit, limit).astype(dtype)


def setup_inputs(seed: int = 0) -> dict:
    key_of = jax.random.split(jax.random.key(seed), 21)
    return {
        "tokens": scatter_about(key_of[0], (SEQS, LEN, D), 1.0, 6.0, ((0, 32),), jnp.float32),
        "segments": jax.vmap(lambda own: jnp.searchsorted(jnp.cumsum(ragged_sizes(own, SEGS, LEN, DOC_MOST, 1)), jnp.arange(LEN), side="right"))(jax.random.split(key_of[1], SEQS)).reshape((SEQS, LEN)).astype(jnp.int32),
        "time_steps": set_ends(jax.random.randint(key_of[2], (SEQS,), 0, TSTEPS), jax.random.fold_in(key_of[2], 1), 0, TSTEPS - 1).astype(jnp.int32),
        "time_table": scatter_about(key_of[3], (TSTEPS, D), 0.5, 4.0, ((0, 4),)),
        "ln1_gain": jnp.clip(1.0 + 0.1 * jax.random.normal(key_of[4], (D,), jnp.float32), 0.5, 1.5).astype(jnp.bfloat16),
        "ln1_bias": scatter_about(key_of[5], (D,), 0.2, 1.0, ((0, 4),)),
        "q_weight": scatter_about(key_of[6], (D, D), D ** -0.5, 0.21875, ((0, 4),)),
        "q_bias": scatter_about(key_of[7], (D,), 0.2, 1.0, ((0, 4),)),
        "k_weight": scatter_about(key_of[8], (D, D), D ** -0.5, 0.21875, ((0, 4),)),
        "v_weight": scatter_about(key_of[9], (D, D), D ** -0.5, 0.21875, ((0, 4),)),
        "v_bias": scatter_about(key_of[10], (D,), 0.2, 1.0, ((0, 4),)),
        "o_weight": scatter_about(key_of[11], (D, D), (D // 16) ** -0.5, 0.875, ((0, 4),)),
        "o_bias": scatter_about(key_of[12], (D,), 0.2, 1.0, ((0, 4),)),
        "ln2_gain": jnp.clip(1.0 + 0.1 * jax.random.normal(key_of[13], (D,), jnp.float32), 0.5, 1.5).astype(jnp.bfloat16),
        "ln2_bias": scatter_about(key_of[14], (D,), 0.2, 1.0, ((0, 4),)),
        "up_weight": scatter_about(key_of[15], (D, FF), D ** -0.5, 0.21875, ((0, 4),)),
        "up_bias": scatter_about(key_of[16], (FF,), 0.2, 1.0, ((0, 4),)),
        "down_weight": scatter_about(key_of[17], (FF, D), FF ** -0.5, 0.109375, ((0, 4),)),
        "down_bias": scatter_about(key_of[18], (D,), 0.2, 1.0, ((0, 4),)),
        "cotangent": scatter_about(key_of[19], (SEQS, LEN, D), 1.0, 6.0, ((0, 32),), jnp.float32),
    }


@jax.custom_vjp
def low(v):
    return lax.optimization_barrier(v.astype(jnp.bfloat16)).astype(jnp.float32)

@jax.custom_vjp
def low_back(v):
    return v

def low_keep(v):
    return (low(v), None)

def low_pass(kept, grad):
    return (grad,)

def back_keep(v):
    return (v, None)

def back_low(kept, grad):
    return (low(grad),)
low.defvjp(low_keep, low_pass)
low_back.defvjp(back_keep, back_low)
EPS = 1e-05
NEG = -1e+30
HIGH = lax.Precision.HIGHEST

def layer_norm(values, gain, shift):
    centre = lax.optimization_barrier(jnp.mean(values, axis=-1, keepdims=True))
    offsets = values - centre
    spread = lax.optimization_barrier(jnp.mean(offsets * offsets, axis=-1, keepdims=True))
    return offsets * lax.rsqrt(spread + EPS) * gain + shift

def project(left, right):
    return jnp.dot(left, right, preferred_element_type=jnp.float32, precision=HIGH)

def sequence_forward(weights, rows, segment_ids, step_index):
    table, gain_one, shift_one, w_query, b_query, w_key, w_value, b_value, w_out, b_out, gain_two, shift_two, w_up, b_up, w_down, b_down = weights
    length = rows.shape[0]
    width = rows.shape[1]
    size = width // HEADS
    embedded = rows + lax.dynamic_slice_in_dim(table, step_index.astype(jnp.int32), 1, 0)
    normed1 = low(layer_norm(embedded, gain_one, shift_one))
    queries = low(low_back(project(normed1, w_query) + b_query)).reshape(length, HEADS, size)
    keys = low(low_back(project(normed1, w_key))).reshape(length, HEADS, size)
    values = low(low_back(project(normed1, w_value) + b_value)).reshape(length, HEADS, size)
    scores = low_back(jnp.einsum('qhd,khd->hqk', queries, keys, precision=HIGH) * 0.125)
    same = segment_ids[:, None] == segment_ids[None, :]
    attn_probs = jax.nn.softmax(jnp.where(same[None], scores, NEG), axis=-1)
    mixed = jnp.einsum('hqk,khd->qhd', low(attn_probs), values, precision=HIGH)
    attended = low(low_back(mixed.reshape(length, width)))
    mixed1 = embedded + low_back(project(attended, w_out) + b_out)
    normed2 = low(layer_norm(mixed1, gain_two, shift_two))
    pre_act = low_back(project(normed2, w_up) + b_up)
    activated = low(jax.nn.gelu(pre_act, approximate=False))
    return mixed1 + low_back(project(activated, w_down) + b_down)

def reference(tokens, segments, time_steps, time_table, ln1_gain, ln1_bias, q_weight, q_bias, k_weight, v_weight, v_bias, o_weight, o_bias, ln2_gain, ln2_bias, up_weight, up_bias, down_weight, down_bias, cotangent):
    weights = (time_table, ln1_gain, ln1_bias, q_weight, q_bias, k_weight, v_weight, v_bias, o_weight, o_bias, ln2_gain, ln2_bias, up_weight, up_bias, down_weight, down_bias)
    weights = tuple((item.astype(jnp.float32) for item in weights))
    checked = jax.checkpoint(sequence_forward)

    def whole(rows, params):

        def step(carry, item):
            rows_one, seg_one, step_one = item
            return (carry, checked(params, rows_one, seg_one, step_one))
        _, output = lax.scan(step, jnp.zeros((), jnp.float32), (rows, segments, time_steps))
        return output
    output, pullback = jax.vjp(whole, tokens.astype(jnp.float32), weights)
    grad_in, grads = pullback(cotangent.astype(jnp.float32))
    return (output, grad_in, grads[0], grads[1], grads[2], grads[3], grads[4], grads[5], grads[6], grads[7], grads[8], grads[9], grads[10], grads[11], grads[12], grads[13], grads[14], grads[15])
```

```python
import functools
import math

import jax
import jax.numpy as jnp
from jax import lax
from jax.experimental import pallas as pl
from jax.experimental.pallas import tpu as pltpu
from jax.sharding import PartitionSpec as P

NEG=-1e30
L=1024; QB=256
BF=jnp.bfloat16; F32=jnp.float32
LOG2E=math.log2(math.e); LN2=math.log(2.0)
def nt(a,b): return lax.dot_general(a,b,(((1,),(1,)),((),())),preferred_element_type=F32)
def nn(a,b): return lax.dot_general(a,b,(((1,),(0,)),((),())),preferred_element_type=F32)
def tn(a,b): return lax.dot_general(a,b,(((0,),(0,)),((),())),preferred_element_type=F32)

def seg_features(seg):
    lane=jnp.arange(128)%64
    hit=(seg[:,None]==lane[None,:])
    fq=jnp.where((lane<4)[None]&hit,1.0,0.0).astype(BF)
    fk=jnp.where((lane<4)[None],jnp.where(hit,0.0,NEG),jnp.where(((lane>=4)&(lane<7))[None],1.0,0.0)).astype(BF)
    return fq,fk

def fwd_kernel(q_ref,k_ref,v_ref,fq_ref,fk_ref,o_ref,fx_ref,*,qb):
    lane=lax.broadcasted_iota(jnp.int32,(1,128),1)
    lo=lane<64
    ks=[];vs=[]
    k=k_ref[...];v=v_ref[...];fk=fk_ref[...]
    for h in (0,1):
        own=lo if h==0 else ~lo
        ks.append(jnp.where(own,k,fk))
        vs.append(jnp.where(own,v,jnp.where((lane&63)==0,1.0,0.0).astype(BF)))
    for b in range(L//qb):
        rows=pl.ds(b*qb,qb)
        q=q_ref[rows,:];fq=fq_ref[rows,:]
        accs=[];ls=[]
        for h in (0,1):
            own=lo if h==0 else ~lo
            s=nt(jnp.where(own,q,fq),ks[h])
            m=jnp.max(s,axis=1,keepdims=True)
            p=jnp.exp2(s-m).astype(BF)
            acc=nn(p,vs[h])
            l=acc[:,64:65] if h==0 else acc[:,0:1]
            accs.append(acc*(1.0/l))
            ls.append(-(m+jnp.log2(l)))
        o_ref[rows,:]=jnp.where(lo,accs[0],accs[1]).astype(BF)
        nl=jnp.where(lo,ls[1],ls[0])
        hi=nl.astype(BF).astype(F32)
        r1=nl-hi
        mid=r1.astype(BF).astype(F32)
        r2=r1-mid
        l6=lane&63
        fx_ref[rows,:]=jnp.where(l6==4,hi,jnp.where(l6==5,mid,jnp.where(l6==6,r2,fq.astype(F32)))).astype(BF)

def attn_fwd(q,k,v,fq,fk,nseq,npair,qb=256):
    T=nseq*L
    blk=pl.BlockSpec((L,128),lambda s,p:(s,p))
    fb=pl.BlockSpec((L,128),lambda s,p:(s,0))
    return pl.pallas_call(functools.partial(fwd_kernel,qb=qb),grid=(nseq,npair),
        in_specs=[blk,blk,blk,fb,fb],out_specs=[blk,blk],
        out_shape=[jax.ShapeDtypeStruct((T,npair*128),BF)]*2,
        compiler_params=pltpu.CompilerParams(dimension_semantics=("arbitrary","arbitrary")),
        name="attn_fwd")(q,k,v,fq,fk)

def bwd_kernel(q_ref,k_ref,v_ref,fx_ref,fk_ref,o_ref,do_ref,dq_ref,dk_ref,dv_ref,dqa,*,qb,mode,kb):
    lane=lax.broadcasted_iota(jnp.int32,(1,128),1)
    lo=lane<64; l6=lane&63
    zero=jnp.zeros((),BF)
    ones2=jnp.where(l6<2,1.0,0.0).astype(BF)
    k=k_ref[...];v=v_ref[...];fk=fk_ref[...]
    kx=[];vx=[];km=[]
    for h in (0,1):
        own=lo if h==0 else ~lo
        kx.append(jnp.where(own,k,fk)); vx.append(jnp.where(own,v,ones2)); km.append(jnp.where(own,k,zero))
    dv=jnp.zeros((L,128),F32); dk=jnp.zeros((L,128),F32)
    for b in range(L//qb):
        rows=pl.ds(b*qb,qb)
        q=q_ref[rows,:];fx=fx_ref[rows,:];do=do_ref[rows,:]
        prod=do.astype(F32)*o_ref[rows,:].astype(F32)
        d0=-jnp.sum(jnp.where(lo,prod,0.0),axis=1,keepdims=True)
        d1=-jnp.sum(jnp.where(lo,0.0,prod),axis=1,keepdims=True)
        nd=jnp.where(lo,d1,d0)
        hi=nd.astype(BF).astype(F32)
        fd=jnp.where(l6==0,hi,jnp.where(l6==1,nd-hi,0.0)).astype(BF)
        dq=jnp.zeros((qb,128),F32)
        for h in (0,1):
            own=lo if h==0 else ~lo
            qx=jnp.where(own,q,fx); dx=jnp.where(own,do,fd)
            qm=jnp.where(own,q,zero); dm=jnp.where(own,do,zero)
            st=nt(kx[h],qx)
            p=jnp.exp2(st)
            dpt=nt(vx[h],dx)
            pb=p.astype(BF)
            ds=(p*dpt).astype(BF)
            dv=dv+nn(pb,dm)
            dk=dk+nn(ds,qm)
            dq=dq+tn(ds,km[h])
        dq_ref[rows,:]=(dq*0.125).astype(BF)
    dv_ref[...]=dv.astype(BF)
    dk_ref[...]=(dk*LN2).astype(BF)

def attn_bwd(q,k,v,fx,fk,o,do,nseq,npair,qb=256,mode=0,kb=256):
    T=nseq*L
    blk=pl.BlockSpec((L,128),lambda s,p:(s,p))
    fb=pl.BlockSpec((L,128),lambda s,p:(s,0))
    return pl.pallas_call(functools.partial(bwd_kernel,qb=qb,mode=mode,kb=kb),grid=(nseq,npair),
        in_specs=[blk,blk,blk,blk,fb,blk,blk],out_specs=[blk]*3,
        out_shape=[jax.ShapeDtypeStruct((T,npair*128),BF)]*3,
        scratch_shapes=[pltpu.VMEM((L,128),F32)],
        compiler_params=pltpu.CompilerParams(dimension_semantics=("arbitrary","arbitrary")),
        name="attn_bwd")(q,k,v,fx,fk,o,do)

EPS=1e-5
D=768;FF=3072

def mid_kernel(tok_ref,row_ref,att_ref,cot_ref,ow_ref,up_ref,dn_ref,vec_ref,ub_ref,
               res_ref,gm_ref,ga_ref,dup_ref,ddn_ref,dow_ref,sv_ref,sub_ref,
               aup,adn,aow,*,tb,fc,erfmode):
    i=pl.program_id(0)
    n=pl.num_programs(0)
    @pl.when(i==0)
    def _():
        aup[...]=jnp.zeros_like(aup);adn[...]=jnp.zeros_like(adn);aow[...]=jnp.zeros_like(aow)
        sv_ref[...]=jnp.zeros_like(sv_ref);sub_ref[...]=jnp.zeros_like(sub_ref)
    ob=vec_ref[0:1,:];g2=vec_ref[1:2,:];b2=vec_ref[2:3,:];db=vec_ref[3:4,:]
    att=att_ref[...]
    mixed=tok_ref[...]+row_ref[0]+nn(att,ow_ref[...])+ob
    mean=jnp.mean(mixed,axis=1,keepdims=True)
    off=mixed-mean
    var=jnp.mean(off*off,axis=1,keepdims=True)
    r=lax.rsqrt(var+EPS)
    xhat=off*r
    n2=(xhat*g2+b2).astype(BF)
    n2t=n2.T
    cot=cot_ref[...]
    g=cot.astype(BF)
    gt=g.T
    res=mixed+db
    gn2=jnp.zeros((tb,D),F32)
    for j in range(FF//fc):
        cs=slice(j*fc,(j+1)*fc)
        pre=nn(n2,up_ref[:,cs])+ub_ref[:,cs]
        gact=nt(g,dn_ref[cs,:])
        if erfmode==0:
            phi=0.5+0.5*lax.erf(pre*(2**-0.5))
            pdf=jnp.exp2(pre*pre*(-0.5*LOG2E))*(1.0/math.sqrt(2*math.pi))
        else:
            z=jnp.abs(pre)
            e=jnp.exp2(pre*pre*(-0.5*LOG2E))
            t=1.0/(1.0+(0.3275911*2**-0.5)*z)
            poly=t*(0.5*0.254829592+t*(-0.5*0.284496736+t*(0.5*1.421413741+t*(-0.5*1.453152027+t*(0.5*1.061405429)))))
            tail=poly*e
            phi=jnp.where(pre>=0,1.0-tail,tail)
            pdf=e*(1.0/math.sqrt(2*math.pi))
        act=(pre*phi).astype(BF)
        gp=gact*(phi+pre*pdf)
        gpre=gp.astype(BF)
        sub_ref[:,cs]+=jnp.sum(gp.reshape(tb//8,8,fc),axis=0)
        res=res+nn(act,dn_ref[cs,:])
        gn2=gn2+nt(gpre,up_ref[:,cs])
        adn[:,cs]+=nn(gt,act)
        aup[:,cs]+=nn(n2t,gpre)
    res_ref[...]=res
    e=gn2*g2
    c1=jnp.mean(e,axis=1,keepdims=True)
    c2=jnp.mean(e*xhat,axis=1,keepdims=True)
    gm=cot+r*(e-c1-xhat*c2)
    gml=gm.astype(BF)
    gm_ref[...]=gml
    ga_ref[...]=nt(gml,ow_ref[...]).astype(BF)
    aow[...]+=tn(att,gml)
    def s8(x): return jnp.sum(x.reshape(tb//8,8,D),axis=0)
    sv_ref[0:8,:]+=s8(gm)
    sv_ref[8:16,:]+=s8(gn2*xhat)
    sv_ref[16:24,:]+=s8(gn2)
    sv_ref[24:32,:]+=s8(cot)
    @pl.when(i==n-1)
    def _():
        dow_ref[...]=aow[...].astype(BF)
        dup_ref[...]=aup[...].astype(BF)
        eye=(lax.broadcasted_iota(jnp.int32,(256,256),0)==lax.broadcasted_iota(jnp.int32,(256,256),1)).astype(BF)
        for c in range(FF//256):
            ddn_ref[c*256:(c+1)*256,:]=nt(eye,adn[:,c*256:(c+1)*256].astype(BF)).astype(BF)

def mid(tok,row,att,cot,ow,up,dn,vec,ub,tb=512,fc=512,erfmode=0):
    T=tok.shape[0]
    per=1024//tb
    blk=pl.BlockSpec((tb,D),lambda i:(i,0))
    def full(*s): return pl.BlockSpec(s,lambda i:(0,)*len(s),pipeline_mode=pl.Buffered(1))
    return pl.pallas_call(functools.partial(mid_kernel,tb=tb,fc=fc,erfmode=erfmode),grid=(T//tb,),
        in_specs=[blk,pl.BlockSpec((1,1,D),lambda i:(i//per,0,0)),blk,blk,full(D,D),full(D,FF),full(FF,D),full(8,D),full(1,FF)],
        out_specs=[blk,blk,blk,full(D,FF),full(FF,D),full(D,D),full(32,D),full(8,FF)],
        out_shape=[jax.ShapeDtypeStruct((T,D),F32),jax.ShapeDtypeStruct((T,D),BF),jax.ShapeDtypeStruct((T,D),BF),
            jax.ShapeDtypeStruct((D,FF),BF),jax.ShapeDtypeStruct((FF,D),BF),jax.ShapeDtypeStruct((D,D),BF),
            jax.ShapeDtypeStruct((32,D),F32),jax.ShapeDtypeStruct((8,FF),F32)],
        scratch_shapes=[pltpu.VMEM((D,FF),F32),pltpu.VMEM((D,FF),F32),pltpu.VMEM((D,D),F32)],
        compiler_params=pltpu.CompilerParams(dimension_semantics=("arbitrary",),vmem_limit_bytes=66*1024*1024-2**21),
        name="mid")(tok,row,att,cot,ow,up,dn,vec,ub)

EPS=1e-5
D=768
QS=0.125*LOG2E
def full(*s): return pl.BlockSpec(s,lambda i:(0,)*len(s),pipeline_mode=pl.Buffered(1))
def norm(x):
    mean=jnp.mean(x,axis=1,keepdims=True)
    off=x-mean
    var=jnp.mean(off*off,axis=1,keepdims=True)
    r=lax.rsqrt(var+EPS)
    return off*r,r
def qkv_kernel(tok_ref,row_ref,wq_ref,wk_ref,wv_ref,vec_ref,q_ref,k_ref,v_ref):
    xhat,_=norm(tok_ref[...]+row_ref[0])
    n1=(xhat*vec_ref[0:1,:]+vec_ref[1:2,:]).astype(BF)
    q_ref[...]=((nn(n1,wq_ref[...])+vec_ref[2:3,:])*QS).astype(BF)
    k_ref[...]=nn(n1,wk_ref[...]).astype(BF)
    v_ref[...]=(nn(n1,wv_ref[...])+vec_ref[3:4,:]).astype(BF)
def qkv(tok,row,wq,wk,wv,vec,tb=512):
    T=tok.shape[0];per=1024//tb
    blk=pl.BlockSpec((tb,D),lambda i:(i,0))
    return pl.pallas_call(qkv_kernel,grid=(T//tb,),
      in_specs=[blk,pl.BlockSpec((1,1,D),lambda i:(i//per,0,0)),full(D,D),full(D,D),full(D,D),full(8,D)],
      out_specs=[blk]*3,out_shape=[jax.ShapeDtypeStruct((T,D),BF)]*3,
      compiler_params=pltpu.CompilerParams(dimension_semantics=("arbitrary",)),name="qkv")(tok,row,wq,wk,wv,vec)

def last_kernel(tok_ref,row_ref,dq_ref,dk_ref,dv_ref,gm_ref,wq_ref,wk_ref,wv_ref,vec_ref,
                gt_ref,dwq_ref,dwk_ref,dwv_ref,sv_ref,ts_ref,aq,ak,av,*,tb,per):
    i=pl.program_id(0);n=pl.num_programs(0)
    @pl.when(i==0)
    def _():
        aq[...]=jnp.zeros_like(aq);ak[...]=jnp.zeros_like(ak);av[...]=jnp.zeros_like(av)
        sv_ref[...]=jnp.zeros_like(sv_ref)
    @pl.when(i%per==0)
    def _(): ts_ref[...]=jnp.zeros_like(ts_ref)
    g1=vec_ref[0:1,:]
    xhat,r=norm(tok_ref[...]+row_ref[0])
    n1t=(xhat*g1+vec_ref[1:2,:]).astype(BF).T
    dq=dq_ref[...];dk=dk_ref[...];dv=dv_ref[...]
    gn=nt(dq,wq_ref[...])+nt(dk,wk_ref[...])+nt(dv,wv_ref[...])
    aq[...]+=nn(n1t,dq);ak[...]+=nn(n1t,dk);av[...]+=nn(n1t,dv)
    e=gn*g1
    c1=jnp.mean(e,axis=1,keepdims=True)
    c2=jnp.mean(e*xhat,axis=1,keepdims=True)
    gt=gm_ref[...].astype(F32)+r*(e-c1-xhat*c2)
    gt_ref[...]=gt
    def s8(x): return jnp.sum(x.reshape(tb//8,8,D),axis=0)
    sv_ref[0:8,:]+=s8(gn*xhat)
    sv_ref[8:16,:]+=s8(gn)
    sv_ref[16:24,:]+=s8(dq.astype(F32))
    sv_ref[24:32,:]+=s8(dv.astype(F32))
    ts_ref[0]+=s8(gt)
    @pl.when(i==n-1)
    def _():
        dwq_ref[...]=aq[...].astype(BF);dwk_ref[...]=ak[...].astype(BF);dwv_ref[...]=av[...].astype(BF)
def last(tok,row,dq,dk,dv,gm,wq,wk,wv,vec,tb=256):
    T=tok.shape[0];per=1024//tb
    blk=pl.BlockSpec((tb,D),lambda i:(i,0))
    S=jax.ShapeDtypeStruct
    return pl.pallas_call(functools.partial(last_kernel,tb=tb,per=per),grid=(T//tb,),
      in_specs=[blk,pl.BlockSpec((1,1,D),lambda i:(i//per,0,0)),blk,blk,blk,blk,full(D,D),full(D,D),full(D,D),full(8,D)],
      out_specs=[blk,full(D,D),full(D,D),full(D,D),full(32,D),pl.BlockSpec((1,8,D),lambda i:(i//per,0,0))],
      out_shape=[S((T,D),F32),S((D,D),BF),S((D,D),BF),S((D,D),BF),S((32,D),F32),S((T//1024,8,D),F32)],
      scratch_shapes=[pltpu.VMEM((D,D),F32)]*3,
      compiler_params=pltpu.CompilerParams(dimension_semantics=("arbitrary",)),name="last")(tok,row,dq,dk,dv,gm,wq,wk,wv,vec)

def local(tokens,segments,time_steps,time_table,ln1_gain,ln1_bias,q_weight,q_bias,k_weight,v_weight,v_bias,o_weight,o_bias,ln2_gain,ln2_bias,up_weight,up_bias,down_weight,down_bias,cotangent):
    nseq=tokens.shape[0]
    T=nseq*L
    S=lax.axis_size("shard")
    me=lax.axis_index("shard")
    ag=lambda x: lax.all_gather(x,"shard",axis=0,tiled=True)
    small=jnp.concatenate([ln1_gain,ln1_bias,q_bias,v_bias,o_bias,ln2_gain,ln2_bias,down_bias,up_bias])
    w=ln1_gain.shape[0]
    steps=lax.all_gather(time_steps,"shard",axis=0,tiled=True)
    own=time_table.shape[0]
    idx=steps-me*own
    mine=(idx>=0)&(idx<own)
    rows=jnp.where(mine[:,None],time_table[jnp.clip(idx,0,own-1)],jnp.zeros((),BF))
    rows=lax.psum_scatter(rows,"shard",scatter_dimension=0,tiled=True).astype(F32).reshape(nseq,1,D)
    sm=lax.all_gather(small,"shard",axis=0,tiled=False)
    vecs=[sm[:,i*w:(i+1)*w].reshape(-1).astype(F32) for i in range(8)]
    ub=sm[:,8*w:].reshape(1,-1).astype(F32)
    g1,b1,qb,vb,ob,g2,b2,db=vecs
    z=jnp.zeros_like(g1)
    wq,wk,wv=ag(q_weight),ag(k_weight),ag(v_weight)
    ow,up,dn=ag(o_weight),ag(up_weight),ag(down_weight)
    tok=tokens.reshape(T,D)
    vec1=jnp.stack([g1,b1,qb,vb,z,z,z,z])
    vec2=jnp.stack([ob,g2,b2,db,z,z,z,z])
    fq,fk=seg_features(segments.reshape(T))
    q,k,v=qkv(tok,rows,wq,wk,wv,vec1)
    att,fx=attn_fwd(q,k,v,fq,fk,nseq,6,512)
    res,gm,ga,dup,ddn,dow,sv2,sub=mid(tok,rows,att,cotangent.reshape(T,D),ow,up,dn,vec2,ub,256,512)
    dq,dk,dv=attn_bwd(q,k,v,fx,fk,att,ga,nseq,6,256)
    gt,dwq,dwk,dwv,sv1,ts=last(tok,rows,dq,dk,dv,gm,wq,wk,wv,vec1)
    def red(x): return lax.psum(lax.psum_scatter(x,"shard",scatter_dimension=0,tiled=True),"rep").astype(F32)
    s2=sv2.reshape(4,8,D).sum(1);s1=sv1.reshape(4,8,D).sum(1)
    allv=jnp.concatenate([s1,s2]).reshape(-1,S,w).transpose(1,0,2).astype(BF)
    sums=lax.psum(lax.psum_scatter(allv,"shard",scatter_dimension=0,tiled=True),"rep").astype(F32).reshape(-1,w)
    subs=lax.psum(lax.psum_scatter(sub.sum(0).astype(BF),"shard",scatter_dimension=0,tiled=True),"rep").astype(F32)
    tt=lax.all_gather(ts.sum(1).astype(BF),("rep","shard"),axis=0,tiled=True)
    st=lax.all_gather(time_steps,("rep","shard"),axis=0,tiled=True)
    ids=me*own+jnp.arange(own)
    gtab=jnp.dot((ids[:,None]==st[None,:]).astype(BF),tt,preferred_element_type=F32)
    return (res.reshape(tokens.shape),gt.reshape(tokens.shape),gtab,sums[0],sums[1],red(dwq),sums[2],red(dwk),red(dwv),sums[3],red(dow),sums[4],sums[5],sums[6],red(dup),subs,red(ddn),sums[7])


def solution(mesh):
    b=("rep","shard")
    s=P("shard"); m=P("shard",None); t=P(b,None,None)
    return jax.shard_map(local,mesh=mesh,
        in_specs=(t,P(b,None),P(b),m,s,s,m,s,m,m,s,m,s,s,s,m,s,m,s,t),
        out_specs=(t,t,m,s,s,m,s,m,m,s,m,s,s,s,m,s,m,s),check_vma=False)
```

```python
import functools
import math

import jax
import jax.numpy as jnp
from jax import lax
from jax.experimental import pallas as pl
from jax.experimental.pallas import tpu as pltpu
from jax.sharding import PartitionSpec as P

NEG=-1e30
EPS=1e-5
L=1024
D=768
FF=3072
HC=D//2
BF=jnp.bfloat16
F32=jnp.float32
LOG2E=math.log2(math.e)
LN2=math.log(2.0)
QS=0.125*LOG2E
ANY=pl.BlockSpec(memory_space=pl.ANY)
S_=jax.ShapeDtypeStruct


def nt(a,b):
    return lax.dot_general(a,b,(((1,),(1,)),((),())),preferred_element_type=F32)


def nn(a,b):
    return lax.dot_general(a,b,(((1,),(0,)),((),())),preferred_element_type=F32)


def tn(a,b):
    return lax.dot_general(a,b,(((0,),(0,)),((),())),preferred_element_type=F32)


def full(*s):
    return pl.BlockSpec(s,lambda i,*_:(0,)*len(s),pipeline_mode=pl.Buffered(1))


def norm(x):
    mean=jnp.mean(x,axis=1,keepdims=True)
    off=x-mean
    var=jnp.mean(off*off,axis=1,keepdims=True)
    r=lax.rsqrt(var+EPS)
    return off*r,r


def sum8(x):
    return jnp.sum(x.reshape(x.shape[0]//8,8,x.shape[1]),axis=0)


def cost(flops,nbytes,trans=0):
    return pl.CostEstimate(flops=int(flops),bytes_accessed=int(nbytes),transcendentals=int(trans))


def seg_features(seg):
    lane=jnp.arange(128)%64
    hit=seg[:,None]==lane[None,:]
    first=(lane<4)[None]
    fq=jnp.where(first&hit,1.0,0.0).astype(BF)
    fk=jnp.where(first,jnp.where(hit,0.0,NEG),jnp.where((lane<7)[None],1.0,0.0)).astype(BF)
    return fq,fk


def qkv_kernel(idx_ref,*refs,ns,wr):
    tok_ref,row_ref,vec_ref=refs[:3]
    own=refs[3:6]
    mine=refs[6:5+ns]
    other=refs[5+ns:4+2*ns]
    hi=4+2*ns
    mine=refs[6:6+ns-1]
    other=refs[6+ns-1:6+2*(ns-1)]
    hi=6+2*(ns-1)
    q_ref,k_ref,v_ref,w_ref,sem=refs[hi:hi+5]
    @pl.when(pl.program_id(0)==0)
    def _():
        c=idx_ref[0]
        cps=[]
        def put(src,w,sh,c0,nc):
            dst=w_ref.at[w,pl.ds(pl.multiple_of(sh*wr,16),wr),pl.ds(c0,nc)]
            cp=pltpu.make_async_copy(src,dst,sem.at[len(cps)])
            cp.start()
            cps.append(cp)
        for w in range(3):
            put(own[w],w,idx_ref[1],0,D)
        for j in range(1,ns):
            for w in range(3):
                put(mine[j-1].at[pl.ds(w*wr,wr)],w,idx_ref[1+j],pl.multiple_of(c*HC,128),HC)
                put(other[j-1].at[pl.ds(w*wr,wr)],w,idx_ref[1+ns+j],pl.multiple_of((1-c)*HC,128),HC)
        for cp in cps:
            cp.wait()
    xhat,_=norm(tok_ref[...]+row_ref[0])
    n1=(xhat*vec_ref[0:1,:]+vec_ref[1:2,:]).astype(BF)
    q_ref[...]=((nn(n1,w_ref[0])+vec_ref[2:3,:])*QS).astype(BF)
    k_ref[...]=nn(n1,w_ref[1]).astype(BF)
    v_ref[...]=(nn(n1,w_ref[2])+vec_ref[3:4,:]).astype(BF)


def qkv(idx,tok,row,vec,own,mine,other,tb=512):
    T=tok.shape[0]
    per=L//tb
    ns=len(mine)+1
    wr=own[0].shape[0]
    blk=pl.BlockSpec((tb,D),lambda i,*_:(i,0))
    return pl.pallas_call(
        functools.partial(qkv_kernel,ns=ns,wr=wr),
        grid_spec=pltpu.PrefetchScalarGridSpec(
            num_scalar_prefetch=1,grid=(T//tb,),
            in_specs=[blk,pl.BlockSpec((1,1,D),lambda i,*_:(i//per,0,0)),full(8,D)]+[ANY]*(3+2*(ns-1)),
            out_specs=[blk]*3+[full(3,D,D)],
            scratch_shapes=[pltpu.SemaphoreType.DMA((3+6*(ns-1),))]),
        out_shape=[S_((T,D),BF)]*3+[S_((3,D,D),BF)],
        compiler_params=pltpu.CompilerParams(dimension_semantics=("arbitrary",)),
        cost_estimate=cost(6*T*D*D,T*D*10+9*D*D),
        name="qkv")(idx,tok,row,vec,*own,*mine,*other)


def fwd_kernel(q_ref,k_ref,v_ref,fq_ref,fk_ref,*refs,qb):
    o_ref,fx_ref=refs[-2:]
    lane=lax.broadcasted_iota(jnp.int32,(1,128),1)
    lo=lane<64
    l6=lane&63
    ks=[]
    vs=[]
    k=k_ref[...]
    v=v_ref[...]
    fk=fk_ref[...]
    for h in (0,1):
        own=lo if h==0 else ~lo
        ks.append(jnp.where(own,k,fk))
        vs.append(jnp.where(own,v,jnp.where(l6==0,1.0,0.0).astype(BF)))
    for b in range(L//qb):
        rows=pl.ds(b*qb,qb)
        q=q_ref[rows,:]
        fq=fq_ref[rows,:]
        accs=[]
        ls=[]
        for h in (0,1):
            own=lo if h==0 else ~lo
            s=nt(jnp.where(own,q,fq),ks[h])
            m=jnp.max(s,axis=1,keepdims=True)
            p=jnp.exp2(s-m).astype(BF)
            acc=nn(p,vs[h])
            l=acc[:,64:65] if h==0 else acc[:,0:1]
            accs.append(acc*(1.0/l))
            ls.append(-(m+jnp.log2(l)))
        o_ref[rows,:]=jnp.where(lo,accs[0],accs[1]).astype(BF)
        nl=jnp.where(lo,ls[1],ls[0])
        hi=nl.astype(BF).astype(F32)
        r1=nl-hi
        mid=r1.astype(BF).astype(F32)
        r2=r1-mid
        fx_ref[rows,:]=jnp.where(l6==4,hi,jnp.where(l6==5,mid,jnp.where(l6==6,r2,fq.astype(F32)))).astype(BF)


def attn_fwd(q,k,v,fq,fk,prev,s0,ns,p0,npair,qb=512):
    T=q.shape[0]
    blk=pl.BlockSpec((L,128),lambda s,p:(s0+s,p0+p))
    fb=pl.BlockSpec((L,128),lambda s,p:(s0+s,0))
    n=ns*npair
    prev=list(prev)
    return pl.pallas_call(
        functools.partial(fwd_kernel,qb=qb),grid=(ns,npair),
        in_specs=[blk,blk,blk,fb,fb]+[ANY]*len(prev),out_specs=[blk,blk],
        out_shape=[S_((T,D),BF)]*2,
        input_output_aliases={5+i:i for i in range(len(prev))},
        compiler_params=pltpu.CompilerParams(dimension_semantics=("arbitrary","arbitrary")),
        cost_estimate=cost(n*2*4*L*L*256,n*L*128*14,n*2*L*L),
        name="attn_fwd")(q,k,v,fq,fk,*prev)


def bwd_kernel(q_ref,k_ref,v_ref,fx_ref,fk_ref,o_ref,do_ref,*refs,qb):
    dq_ref,dk_ref,dv_ref=refs[-3:]
    lane=lax.broadcasted_iota(jnp.int32,(1,128),1)
    lo=lane<64
    l6=lane&63
    zero=jnp.zeros((),BF)
    ones2=jnp.where(l6<2,1.0,0.0).astype(BF)
    k=k_ref[...]
    v=v_ref[...]
    fk=fk_ref[...]
    kx=[]
    vx=[]
    km=[]
    for h in (0,1):
        own=lo if h==0 else ~lo
        kx.append(jnp.where(own,k,fk))
        vx.append(jnp.where(own,v,ones2))
        km.append(jnp.where(own,k,zero))
    dv=jnp.zeros((L,128),F32)
    dk=jnp.zeros((L,128),F32)
    for b in range(L//qb):
        rows=pl.ds(b*qb,qb)
        q=q_ref[rows,:]
        fx=fx_ref[rows,:]
        do=do_ref[rows,:]
        prod=do.astype(F32)*o_ref[rows,:].astype(F32)
        d0=-jnp.sum(jnp.where(lo,prod,0.0),axis=1,keepdims=True)
        d1=-jnp.sum(jnp.where(lo,0.0,prod),axis=1,keepdims=True)
        nd=jnp.where(lo,d1,d0)
        hi=nd.astype(BF).astype(F32)
        fd=jnp.where(l6==0,hi,jnp.where(l6==1,nd-hi,0.0)).astype(BF)
        dq=jnp.zeros((qb,128),F32)
        for h in (0,1):
            own=lo if h==0 else ~lo
            qx=jnp.where(own,q,fx)
            dx=jnp.where(own,do,fd)
            qm=jnp.where(own,q,zero)
            dm=jnp.where(own,do,zero)
            p=jnp.exp2(nt(kx[h],qx))
            dpt=nt(vx[h],dx)
            pb=p.astype(BF)
            ds=(p*dpt).astype(BF)
            dv=dv+nn(pb,dm)
            dk=dk+nn(ds,qm)
            dq=dq+tn(ds,km[h])
        dq_ref[rows,:]=(dq*0.125).astype(BF)
    dv_ref[...]=dv.astype(BF)
    dk_ref[...]=(dk*LN2).astype(BF)


def attn_bwd(q,k,v,fx,fk,o,do,prev,s0,ns,p0,npair,qb=256):
    T=q.shape[0]
    blk=pl.BlockSpec((L,128),lambda s,p:(s0+s,p0+p))
    fb=pl.BlockSpec((L,128),lambda s,p:(s0+s,0))
    n=ns*npair
    prev=list(prev)
    return pl.pallas_call(
        functools.partial(bwd_kernel,qb=qb),grid=(ns,npair),
        in_specs=[blk,blk,blk,blk,fb,blk,blk]+[ANY]*len(prev),out_specs=[blk]*3,
        out_shape=[S_((T,D),BF)]*3,
        input_output_aliases={7+i:i for i in range(len(prev))},
        compiler_params=pltpu.CompilerParams(dimension_semantics=("arbitrary","arbitrary")),
        cost_estimate=cost(n*2*10*L*L*256,n*L*128*20,n*2*L*L),
        name="attn_bwd")(q,k,v,fx,fk,o,do,*prev)


def mid_kernel(idx_ref,*refs,tb,fc,ns,wr,fr):
    tok_ref,row_ref,att_ref,cot_ref,vec_ref,ub_ref=refs[:6]
    own=refs[6:9]
    mine=refs[9:9+ns-1]
    other=refs[9+ns-1:9+2*(ns-1)]
    b0=9+2*(ns-1)
    res_ref,gm_ref,ga_ref,keep_ref,send_ref,sv_ref,sub_ref,ow,up,dn,aup,adn,aow,sem=refs[b0:]
    i=pl.program_id(0)
    n=pl.num_programs(0)
    c=idx_ref[0]
    def copies():
        cps=[]
        def put(src,dst):
            cps.append(pltpu.make_async_copy(src,dst,sem.at[len(cps)]))
        r16=lambda sh,m: pl.ds(pl.multiple_of(sh*m,16),m)
        sh=idx_ref[1]
        put(own[0],ow.at[r16(sh,wr)])
        put(own[1],up.at[r16(sh,wr)])
        put(own[2],dn.at[r16(sh,fr)])
        for j in range(1,ns):
            for src,sh,cc in ((mine[j-1],idx_ref[1+j],c),(other[j-1],idx_ref[1+ns+j],1-c)):
                cd=pl.ds(pl.multiple_of(cc*HC,128),HC)
                put(src.at[pl.ds(0,wr)],ow.at[r16(sh,wr),cd])
                for b in range(4):
                    put(src.at[pl.ds(wr+b*wr,wr)],up.at[r16(sh,wr),pl.ds(pl.multiple_of(cc*4*HC+b*HC,128),HC)])
                put(src.at[pl.ds(5*wr,fr)],dn.at[r16(sh,fr),cd])
        return cps
    @pl.when(i==0)
    def _():
        cps=copies()
        for cp in cps:
            cp.start()
        aup[...]=jnp.zeros_like(aup)
        adn[...]=jnp.zeros_like(adn)
        aow[...]=jnp.zeros_like(aow)
        sv_ref[...]=jnp.zeros_like(sv_ref)
        sub_ref[...]=jnp.zeros_like(sub_ref)
        for cp in cps:
            cp.wait()
    ob=vec_ref[0:1,:]
    g2=vec_ref[1:2,:]
    b2=vec_ref[2:3,:]
    db=vec_ref[3:4,:]
    att=att_ref[...]
    mixed=tok_ref[...]+row_ref[0]+nn(att,ow[...])+ob
    xhat,r=norm(mixed)
    n2=(xhat*g2+b2).astype(BF)
    n2t=n2.T
    cot=cot_ref[...]
    g=cot.astype(BF)
    res=mixed+db
    gn2=jnp.zeros((tb,D),F32)
    for j in range(FF//fc):
        cs=slice(j*fc,(j+1)*fc)
        pre=nn(n2,up[:,cs])+ub_ref[:,cs]
        gact=nt(g,dn[cs,:])
        phi=0.5+0.5*lax.erf(pre*(2**-0.5))
        pdf=jnp.exp2(pre*pre*(-0.5*LOG2E))*(1.0/math.sqrt(2*math.pi))
        act=(pre*phi).astype(BF)
        gp=gact*(phi+pre*pdf)
        gpre=gp.astype(BF)
        sub_ref[:,cs]+=sum8(gp)
        res=res+nn(act,dn[cs,:])
        gn2=gn2+nt(gpre,up[:,cs])
        adn[cs,:]+=tn(act,g)
        aup[:,cs]+=nn(n2t,gpre)
    res_ref[...]=res
    e=gn2*g2
    c1=jnp.mean(e,axis=1,keepdims=True)
    c2=jnp.mean(e*xhat,axis=1,keepdims=True)
    gm=cot+r*(e-c1-xhat*c2)
    gml=gm.astype(BF)
    gm_ref[...]=gml
    ga_ref[...]=nt(gml,ow[...]).astype(BF)
    aow[...]+=tn(att,gml)
    sv_ref[0:8,:]+=sum8(gm)
    sv_ref[8:16,:]+=sum8(gn2*xhat)
    sv_ref[16:24,:]+=sum8(gn2)
    sv_ref[24:32,:]+=sum8(cot)
    @pl.when(i==n-1)
    def _():
        for ref,base,odd in ((keep_ref,1,0),(send_ref,1+ns,1)):
            for ch in (0,1):
                @pl.when(c==(ch+odd)%2)
                def _():
                    def body(j,carry):
                        sh=idx_ref[base+j]
                        rw=pl.ds(pl.multiple_of(sh*wr,8),wr)
                        ref[j,0:wr,:]=aow[rw,ch*HC:(ch+1)*HC].astype(BF)
                        for b in range(4):
                            lo=(ch*4+b)*HC
                            ref[j,wr+b*wr:2*wr+b*wr,:]=aup[rw,lo:lo+HC].astype(BF)
                        ref[j,5*wr:5*wr+fr,:]=adn[pl.ds(pl.multiple_of(sh*fr,8),fr),ch*HC:(ch+1)*HC].astype(BF)
                        return carry
                    lax.fori_loop(0,ns,body,0)


def mid(idx,tok,row,att,cot,vec,ub,own,mine,other,tb=256,fc=512):
    T=tok.shape[0]
    per=L//tb
    ns=len(mine)+1
    wr=own[0].shape[0]
    fr=own[2].shape[0]
    rb=5*wr+fr
    blk=pl.BlockSpec((tb,D),lambda i,*_:(i,0))
    return pl.pallas_call(
        functools.partial(mid_kernel,tb=tb,fc=fc,ns=ns,wr=wr,fr=fr),
        grid_spec=pltpu.PrefetchScalarGridSpec(
            num_scalar_prefetch=1,grid=(T//tb,),
            in_specs=[blk,pl.BlockSpec((1,1,D),lambda i,*_:(i//per,0,0)),blk,blk,full(8,D),full(1,FF)]+[ANY]*(3+2*(ns-1)),
            out_specs=[blk,blk,blk,full(ns,rb,HC),full(ns,rb,HC),full(32,D),full(8,FF)],
            scratch_shapes=[pltpu.VMEM((D,D),BF),pltpu.VMEM((D,FF),BF),pltpu.VMEM((FF,D),BF),
                pltpu.VMEM((D,FF),F32),pltpu.VMEM((FF,D),F32),pltpu.VMEM((D,D),F32),
                pltpu.SemaphoreType.DMA((3+12*(ns-1),))]),
        out_shape=[S_((T,D),F32),S_((T,D),BF),S_((T,D),BF),S_((ns,rb,HC),BF),S_((ns,rb,HC),BF),S_((32,D),F32),S_((8,FF),F32)],
        compiler_params=pltpu.CompilerParams(dimension_semantics=("arbitrary",),vmem_limit_bytes=67043328),
        cost_estimate=cost(6*T*D*(D+2*FF),T*D*20+30*D*FF,2*T*FF),
        name="mid")(idx,tok,row,att,cot,vec,ub,*own,*mine,*other)


def dw_kernel(idx_ref,tok_ref,row_ref,dq_ref,dk_ref,dv_ref,vec_ref,keep_ref,send_ref,sv_ref,acc,*,ns,wr):
    i=pl.program_id(0)
    c=idx_ref[0]
    @pl.when(i==0)
    def _():
        acc[...]=jnp.zeros_like(acc)
        sv_ref[...]=jnp.zeros_like(sv_ref)
    xhat,_=norm(tok_ref[...]+row_ref[0])
    n1t=(xhat*vec_ref[0:1,:]+vec_ref[1:2,:]).astype(BF).T
    for w,ref in enumerate((dq_ref,dk_ref,dv_ref)):
        acc[w]+=nn(n1t,ref[...])
    sv_ref[0:8,:]+=sum8(dq_ref[...].astype(F32))
    sv_ref[8:16,:]+=sum8(dv_ref[...].astype(F32))
    @pl.when(i==pl.num_programs(0)-1)
    def _():
        for ref,base,odd in ((keep_ref,1,0),(send_ref,1+ns,1)):
            for ch in (0,1):
                @pl.when(c==(ch+odd)%2)
                def _():
                    def body(j,carry):
                        rw=pl.ds(pl.multiple_of(idx_ref[base+j]*wr,8),wr)
                        for w in range(3):
                            ref[j,w*wr:(w+1)*wr,:]=acc[w,rw,ch*HC:(ch+1)*HC].astype(BF)
                        return carry
                    lax.fori_loop(0,ns,body,0)


def dw(idx,tok,row,dq,dk,dv,vec,ns,tb=512):
    T=tok.shape[0]
    per=L//tb
    wr=D//ns
    blk=pl.BlockSpec((tb,D),lambda i,*_:(i,0))
    return pl.pallas_call(
        functools.partial(dw_kernel,ns=ns,wr=wr),
        grid_spec=pltpu.PrefetchScalarGridSpec(
            num_scalar_prefetch=1,grid=(T//tb,),
            in_specs=[blk,pl.BlockSpec((1,1,D),lambda i,*_:(i//per,0,0)),blk,blk,blk,full(8,D)],
            out_specs=[full(ns,3*wr,HC),full(ns,3*wr,HC),full(16,D)],
            scratch_shapes=[pltpu.VMEM((3,D,D),F32)]),
        out_shape=[S_((ns,3*wr,HC),BF)]*2+[S_((16,D),F32)],
        compiler_params=pltpu.CompilerParams(dimension_semantics=("arbitrary",)),
        cost_estimate=cost(6*T*D*D,T*D*10+12*D*D),
        name="dw")(idx,tok,row,dq,dk,dv,vec)


def dx_kernel(tok_ref,row_ref,dq_ref,dk_ref,dv_ref,gm_ref,w_ref,vec_ref,gt_ref,sv_ref,ts_ref,*,per):
    i=pl.program_id(0)
    @pl.when(i==0)
    def _():
        sv_ref[...]=jnp.zeros_like(sv_ref)
    @pl.when(i%per==0)
    def _():
        ts_ref[...]=jnp.zeros_like(ts_ref)
    gn=nt(dq_ref[...],w_ref[0])+nt(dk_ref[...],w_ref[1])+nt(dv_ref[...],w_ref[2])
    xhat,r=norm(tok_ref[...]+row_ref[0])
    e=gn*vec_ref[0:1,:]
    c1=jnp.mean(e,axis=1,keepdims=True)
    c2=jnp.mean(e*xhat,axis=1,keepdims=True)
    gt=gm_ref[...].astype(F32)+r*(e-c1-xhat*c2)
    gt_ref[...]=gt
    sv_ref[0:8,:]+=sum8(gn*xhat)
    sv_ref[8:16,:]+=sum8(gn)
    ts_ref[0]+=sum8(gt)


def dx(tok,row,dq,dk,dv,gm,w,vec,tb=512):
    T=tok.shape[0]
    per=L//tb
    blk=pl.BlockSpec((tb,D),lambda i:(i,0))
    return pl.pallas_call(
        functools.partial(dx_kernel,per=per),grid=(T//tb,),
        in_specs=[blk,pl.BlockSpec((1,1,D),lambda i:(i//per,0,0)),blk,blk,blk,blk,full(3,D,D),full(8,D)],
        out_specs=[blk,full(16,D),pl.BlockSpec((1,8,D),lambda i:(i//per,0,0))],
        out_shape=[S_((T,D),F32),S_((16,D),F32),S_((T//L,8,D),F32)],
        compiler_params=pltpu.CompilerParams(dimension_semantics=("arbitrary",)),
        cost_estimate=cost(6*T*D*D,T*D*16+6*D*D),
        name="dx")(tok,row,dq,dk,dv,gm,w,vec)


class Ring:
    def __init__(self,rep,shard):
        self.R,self.S=rep,shard
        self.nb=shard.bit_length()-1
        self.Z=rep//2
        r=lax.axis_index("rep")
        self.s=lax.axis_index("shard")
        self.c=r%2
        self.z=r//2

    def move(self,x,to):
        pairs=[]
        for r in range(self.R):
            for s in range(self.S):
                r2,s2=to(r,s)
                pairs.append((r*self.S+s,r2*self.S+s2))
        return lax.ppermute(x,("rep","shard"),pairs)

    def order(self,c,t):
        return (t+c*(self.nb//2))%self.nb

    def mask(self,c,j):
        m=0
        for t in range(self.nb):
            if j>>t&1:
                m|=1<<self.order(c,t)
        return m

    def step(self,x,t):
        return self.move(x,lambda r,s:(r,s^(1<<self.order(r%2,t))))

    def direct(self,x,j):
        return self.move(x,lambda r,s:(r,s^j))

    def core(self,x):
        return self.move(x,lambda r,s:(r^1,s))

    def plane(self,x,j):
        return self.move(x,lambda r,s:(r^(2*j),s))

    def index(self,order_free):
        m=[],[]
        for c in (0,1):
            for j in range(self.S):
                m[c].append(j if order_free else self.mask(c,j))
        t=jnp.array([m[0],m[1]],jnp.int32)
        mine=t[self.c]^self.s
        other=t[1-self.c]^self.s
        return jnp.concatenate([self.c[None],mine,other]).astype(jnp.int32)


def add(a,b):
    return (a.astype(F32)+b.astype(F32)).astype(BF)


def reduce_all(g,keep,send):
    got=g.core(send)
    n=g.S
    x=keep
    for t in reversed(range(g.nb)):
        n//=2
        if got is None:
            up,x=x[n:],x[:n]
        else:
            up,x=add(x[n:],got[n:]),add(x[:n],got[:n])
        got=g.step(up,t)
    x=add(x[0],got[0]).reshape(g.Z,-1,HC)
    mine=lax.dynamic_index_in_dim(x,g.z,0,keepdims=False).astype(F32)
    parts=[g.plane(lax.dynamic_index_in_dim(x,g.z^j,0,keepdims=False),j) for j in range(1,g.Z)]
    for p in parts:
        mine=mine+p.astype(F32)
    mine=mine.astype(BF)
    back=[mine]+[g.plane(mine,j) for j in range(1,g.Z)]
    out=jnp.zeros(x.shape,BF)
    for j in range(g.Z):
        out=lax.dynamic_update_index_in_dim(out,back[j],g.z^j,0)
    out=out.reshape(-1,HC)
    other=g.core(out)
    first=jnp.where(g.c==0,out,other).astype(F32)
    second=jnp.where(g.c==0,other,out).astype(F32)
    return first,second


def local(tokens,segments,time_steps,time_table,ln1_gain,ln1_bias,q_weight,q_bias,k_weight,v_weight,v_bias,o_weight,o_bias,ln2_gain,ln2_bias,up_weight,up_bias,down_weight,down_bias,cotangent):
    nseq=tokens.shape[0]
    T=nseq*L
    g=Ring(lax.axis_size("rep"),lax.axis_size("shard"))
    S=g.S
    w=ln1_gain.shape[0]
    fr=down_weight.shape[0]
    own=time_table.shape[0]
    half=lambda x,b=0: lax.dynamic_slice_in_dim(x,(g.c*(x.shape[1]//D)*HC) + b*HC,HC,1)
    st=jnp.concatenate([time_steps//32,time_steps%32]).astype(BF)
    small=jnp.concatenate([ln1_gain,ln1_bias,q_bias,v_bias,o_bias,ln2_gain,ln2_bias,down_bias,up_bias,st])
    smalls=jnp.stack([small]+[g.direct(small,j) for j in range(1,S)])
    pack_a=jnp.concatenate([half(q_weight),half(k_weight),half(v_weight)])
    mine_a=[g.direct(pack_a,j) for j in range(1,S)]
    steps=smalls[:,-2*nseq:].astype(jnp.int32)
    steps=steps[:,:nseq]*32+steps[:,nseq:]
    idx=steps-g.s*own
    inside=(idx>=0)&(idx<own)
    rows=jnp.where(inside[:,:,None],time_table[jnp.clip(idx,0,own-1)],jnp.zeros((),BF))
    row=rows[0].astype(F32)
    for j in range(1,S):
        row=row+g.direct(rows[j],j).astype(F32)
    row=row.reshape(nseq,1,D)
    sm=jnp.take(smalls[:,:smalls.shape[1]-2*nseq],jnp.arange(S)^g.s,axis=0).astype(F32)
    vecs=[sm[:,i*w:(i+1)*w].reshape(-1) for i in range(8)]
    ub=sm[:,8*w:].reshape(1,-1)
    g1,b1,qb,vb,ob,g2,b2,db=vecs
    z=jnp.zeros_like(g1)
    vec1=jnp.stack([g1,b1,qb,vb,z,z,z,z])
    vec2=jnp.stack([ob,g2,b2,db,z,z,z,z])
    other_a=[g.core(x) for x in mine_a]
    pack_b=jnp.concatenate([half(o_weight)]+[half(up_weight,b) for b in range(4)]+[half(down_weight)])
    pack_b,*mine_a=lax.optimization_barrier((pack_b,*mine_a))
    tok=tokens.reshape(T,D)
    cot=cotangent.reshape(T,D)
    fq,fk=seg_features(segments.reshape(T))
    idx_a=g.index(True)
    idx_b=g.index(False)
    q,k,v,wqkv=qkv(idx_a,tok,row,vec1,(q_weight,k_weight,v_weight),mine_a,other_a)
    mine_b=[pack_b]
    for t in range(g.nb):
        mine_b=mine_b+[g.step(x,t) for x in mine_b]
    other_b=[g.core(x) for x in mine_b[1:]]
    fwd=()
    for s in range(nseq):
        for p in (0,3):
            fwd=attn_fwd(q,k,v,fq,fk,fwd,s,1,p,3)
    att,fx=fwd
    res,gm,ga,keep_b,send_b,sv2,sub=mid(idx_b,tok,row,att,cot,vec2,ub,(o_weight,up_weight,down_weight),mine_b[1:],other_b)
    first_b,second_b=reduce_all(g,keep_b,send_b)
    bwd=()
    for s in range(nseq):
        for p in (0,3):
            bwd=attn_bwd(q,k,v,fx,fk,att,ga,bwd,s,1,p,3)
    dq,dk,dv=bwd
    keep_a,send_a,svq=dw(idx_b,tok,row,dq,dk,dv,vec1,S)
    first_a,second_a=reduce_all(g,keep_a,send_a)
    gt,sv1,ts=dx(tok,row,dq,dk,dv,gm,wqkv,vec1)
    s8=lambda x: x.reshape(-1,8,D).sum(1)
    vs=jnp.concatenate([s8(sv1),s8(svq),s8(sv2)]).reshape(-1,S,w).transpose(1,0,2).reshape(S,-1)
    vs=jnp.concatenate([vs,sub.sum(0).reshape(S,-1)],1).astype(BF)
    tsum=ts.sum(1).astype(BF)
    st=jnp.concatenate([tsum.reshape(-1),st])
    pieces=[lax.dynamic_index_in_dim(vs,g.s,0,keepdims=False)]
    tss=[st]
    for j in range(1,S):
        got=g.direct(jnp.concatenate([lax.dynamic_index_in_dim(vs,g.s^j,0,keepdims=False),st]),j)
        pieces.append(got[:vs.shape[1]])
        tss.append(got[vs.shape[1]:])
    mine_v=sum(x.astype(F32) for x in pieces).astype(BF)
    pay=jnp.concatenate([mine_v]+tss)
    alls=[pay]+[g.move(pay,lambda r,s,j=j:(r^j,s)) for j in range(1,g.R)]
    alls=order_rep(g,alls)
    tot=sum(x[:vs.shape[1]].astype(F32) for x in alls)
    sums=tot[:8*w].reshape(8,w)
    subs=tot[8*w:]
    tt=jnp.stack([x[vs.shape[1]:].reshape(S,-1) for x in alls])
    rows_t=tt[:,:,:nseq*D].reshape(-1,D)
    sids=tt[:,:,nseq*D:].astype(jnp.int32)
    sids=(sids[:,:,:nseq]*32+sids[:,:,nseq:]).reshape(-1)
    ids=g.s*own+jnp.arange(own)
    gtab=jnp.dot((ids[:,None]==sids[None,:]).astype(BF),rows_t,preferred_element_type=F32)
    def unpack(r0,nr):
        return jnp.concatenate([first_a[r0:r0+nr],second_a[r0:r0+nr]],1)
    gq,gk,gv=(unpack(i*w,w) for i in range(3))
    go=jnp.concatenate([first_b[:w],second_b[:w]],1)
    gup=jnp.concatenate([x[w+b*w:w+(b+1)*w] for x in (first_b,second_b) for b in range(4)],1)
    gdn=jnp.concatenate([first_b[5*w:],second_b[5*w:]],1)
    return (res.reshape(tokens.shape),gt.reshape(tokens.shape),gtab,sums[0],sums[1],gq,sums[2],gk,gv,sums[3],go,sums[4],sums[5],sums[6],gup,subs,gdn,sums[7])


def order_rep(g,alls):
    st=jnp.take(jnp.stack(alls),jnp.arange(g.R)^(2*g.z+g.c),axis=0)
    return [st[i] for i in range(g.R)]


def solution(mesh):
    b=("rep","shard")
    s=P("shard")
    m=P("shard",None)
    t=P(b,None,None)
    return jax.shard_map(local,mesh=mesh,
        in_specs=(t,P(b,None),P(b),m,s,s,m,s,m,m,s,m,s,s,s,m,s,m,s,t),
        out_specs=(t,t,m,s,s,m,s,m,m,s,m,s,s,s,m,s,m,s),check_vma=False)
```

```python
import functools
import math

import jax
import jax.numpy as jnp
from jax import lax
from jax.experimental import pallas as pl
from jax.experimental.pallas import tpu as pltpu
from jax.sharding import PartitionSpec as P

NEG=-1e30
EPS=1e-5
L=1024
D=768
FF=3072
HC=D//2
BF=jnp.bfloat16
F32=jnp.float32
LOG2E=math.log2(math.e)
LN2=math.log(2.0)
QS=0.125*LOG2E
VR=14
NV=12
ANY=pl.BlockSpec(memory_space=pl.ANY)
S_=jax.ShapeDtypeStruct


def nt(a,b):
    return lax.dot_general(a,b,(((1,),(1,)),((),())),preferred_element_type=F32)


def nn(a,b):
    return lax.dot_general(a,b,(((1,),(0,)),((),())),preferred_element_type=F32)


def tn(a,b):
    return lax.dot_general(a,b,(((0,),(0,)),((),())),preferred_element_type=F32)


def full(*s):
    return pl.BlockSpec(s,lambda i,*_:(0,)*len(s),pipeline_mode=pl.Buffered(1))


def norm(x):
    mean=jnp.mean(x,axis=1,keepdims=True)
    off=x-mean
    var=jnp.mean(off*off,axis=1,keepdims=True)
    r=lax.rsqrt(var+EPS)
    return off*r,r


def sum8(x):
    return jnp.sum(x.reshape(x.shape[0]//8,8,x.shape[1]),axis=0)


def cost(flops,nbytes,trans=0):
    return pl.CostEstimate(flops=int(flops)//10,bytes_accessed=int(nbytes)//10,transcendentals=int(trans)//10)


def seg_features(seg):
    lane=jnp.arange(128)%64
    hit=seg[:,None]==lane[None,:]
    first=(lane<4)[None]
    fq=jnp.where(first&hit,1.0,0.0).astype(BF)
    fk=jnp.where(first,jnp.where(hit,0.0,NEG),jnp.where((lane<7)[None],1.0,0.0)).astype(BF)
    return fq,fk


def qkv_kernel(idx_ref,*refs,ns,wr):
    tok_ref,row_ref,vec_ref=refs[:3]
    own=refs[3:6]
    mine=refs[6:6+ns-1]
    other=refs[6+ns-1:6+2*(ns-1)]
    hi=6+2*(ns-1)
    q_ref,k_ref,v_ref,nt_ref,w_ref,sem=refs[hi:hi+6]
    @pl.when(pl.program_id(0)==0)
    def _():
        c=idx_ref[0]
        cps=[]
        def put(src,w,sh,c0,nc):
            dst=w_ref.at[w,pl.ds(pl.multiple_of(sh*wr,16),wr),pl.ds(c0,nc)]
            cp=pltpu.make_async_copy(src,dst,sem.at[len(cps)])
            cp.start()
            cps.append(cp)
        for w in range(3):
            put(own[w],w,idx_ref[1],0,D)
        for j in range(1,ns):
            for w in range(3):
                put(mine[j-1].at[pl.ds(w*wr,wr)],w,idx_ref[1+j],pl.multiple_of(c*HC,128),HC)
                put(other[j-1].at[pl.ds(w*wr,wr)],w,idx_ref[1+j],pl.multiple_of((1-c)*HC,128),HC)
        for cp in cps:
            cp.wait()
    xhat,_=norm(tok_ref[...]+row_ref[0])
    n1=(xhat*vec_ref[0:1,:]+vec_ref[1:2,:]).astype(BF)
    q_ref[...]=((nn(n1,w_ref[0])+vec_ref[2:3,:])*QS).astype(BF)
    k_ref[...]=nn(n1,w_ref[1]).astype(BF)
    v_ref[...]=(nn(n1,w_ref[2])+vec_ref[3:4,:]).astype(BF)
    nt_ref[...]=n1.T


def qkv(idx,tok,row,vec,own,mine,other,tb=512):
    T=tok.shape[0]
    per=L//tb
    ns=len(mine)+1
    wr=own[0].shape[0]
    blk=pl.BlockSpec((tb,D),lambda i,*_:(i,0))
    return pl.pallas_call(
        functools.partial(qkv_kernel,ns=ns,wr=wr),
        grid_spec=pltpu.PrefetchScalarGridSpec(
            num_scalar_prefetch=1,grid=(T//tb,),
            in_specs=[blk,pl.BlockSpec((1,1,D),lambda i,*_:(i//per,0,0)),full(VR,D)]+[ANY]*(3+2*(ns-1)),
            out_specs=[blk]*3+[pl.BlockSpec((D,tb),lambda i,*_:(0,i)),full(3,D,D)],
            scratch_shapes=[pltpu.SemaphoreType.DMA((3+6*(ns-1),))]),
        out_shape=[S_((T,D),BF)]*3+[S_((D,T),BF),S_((3,D,D),BF)],
        compiler_params=pltpu.CompilerParams(dimension_semantics=("arbitrary",)),
        cost_estimate=cost(6*T*D*D,T*D*10+9*D*D),
        name="qkv")(idx,tok,row,vec,*own,*mine,*other)


def pack_a_kernel(idx_ref,q_ref,k_ref,v_ref,out_ref):
    wr=q_ref.shape[0]
    for ch in (0,1):
        @pl.when(idx_ref[0]==ch)
        def _():
            for w,ref in enumerate((q_ref,k_ref,v_ref)):
                out_ref[w*wr:(w+1)*wr,:]=ref[:,ch*HC:(ch+1)*HC]


def pack_b_kernel(idx_ref,o_ref,u_ref,d_ref,out_ref):
    wr=o_ref.shape[0]
    for ch in (0,1):
        @pl.when(idx_ref[0]==ch)
        def _():
            out_ref[0:wr,:]=o_ref[:,ch*HC:(ch+1)*HC]
            for b in range(4):
                out_ref[wr+b*wr:2*wr+b*wr,:]=u_ref[:,(ch*4+b)*HC:(ch*4+b+1)*HC]
            out_ref[5*wr:,:]=d_ref[:,ch*HC:(ch+1)*HC]


def pack(kernel,idx,ws,name):
    rows=sum(x.shape[0]*x.shape[1]//D for x in ws)
    vm=pl.BlockSpec(memory_space=pltpu.VMEM)
    return pl.pallas_call(kernel,in_specs=[pl.BlockSpec(memory_space=pltpu.SMEM)]+[vm]*3,out_specs=vm,
        out_shape=S_((rows,HC),BF),cost_estimate=cost(0,4*rows*D),name=name)(idx,*ws)


def fwd_kernel(q_ref,k_ref,v_ref,fq_ref,fk_ref,*refs,qb):
    o_ref,fx_ref=refs[-2:]
    lane=lax.broadcasted_iota(jnp.int32,(1,128),1)
    lo=lane<64
    l6=lane&63
    ks=[]
    vs=[]
    k=k_ref[...]
    v=v_ref[...]
    fk=fk_ref[...]
    for h in (0,1):
        own=lo if h==0 else ~lo
        ks.append(jnp.where(own,k,fk))
        vs.append(jnp.where(own,v,jnp.where(l6==0,1.0,0.0).astype(BF)))
    for b in range(L//qb):
        rows=pl.ds(b*qb,qb)
        q=q_ref[rows,:]
        fq=fq_ref[rows,:]
        accs=[]
        ls=[]
        for h in (0,1):
            own=lo if h==0 else ~lo
            s=nt(jnp.where(own,q,fq),ks[h])
            m=jnp.max(s,axis=1,keepdims=True)
            p=jnp.exp2(s-m).astype(BF)
            acc=nn(p,vs[h])
            l=acc[:,64:65] if h==0 else acc[:,0:1]
            accs.append(acc*(1.0/l))
            ls.append(-(m+jnp.log2(l)))
        o_ref[rows,:]=jnp.where(lo,accs[0],accs[1]).astype(BF)
        nl=jnp.where(lo,ls[1],ls[0])
        hi=nl.astype(BF).astype(F32)
        r1=nl-hi
        mid=r1.astype(BF).astype(F32)
        r2=r1-mid
        fx_ref[rows,:]=jnp.where(l6==4,hi,jnp.where(l6==5,mid,jnp.where(l6==6,r2,fq.astype(F32)))).astype(BF)


def attn_fwd(q,k,v,fq,fk,prev,f0,n,qb=512):
    T=q.shape[0]
    np_=D//128
    blk=pl.BlockSpec((L,128),lambda i:((f0+i)//np_,(f0+i)%np_))
    fb=pl.BlockSpec((L,128),lambda i:((f0+i)//np_,0))
    prev=list(prev)
    return pl.pallas_call(
        functools.partial(fwd_kernel,qb=qb),grid=(n,),
        in_specs=[blk,blk,blk,fb,fb]+[ANY]*len(prev),out_specs=[blk,blk],
        out_shape=[S_((T,D),BF)]*2,
        input_output_aliases={5+i:i for i in range(len(prev))},
        compiler_params=pltpu.CompilerParams(dimension_semantics=("arbitrary",)),
        cost_estimate=cost(n*2*4*L*L*256,n*L*128*14,n*2*L*L),
        name="attn_fwd")(q,k,v,fq,fk,*prev)


def bwd_kernel(q_ref,k_ref,v_ref,fx_ref,fk_ref,o_ref,do_ref,*refs,qb):
    out_ref=refs[-1]
    lane=lax.broadcasted_iota(jnp.int32,(1,128),1)
    lo=lane<64
    l6=lane&63
    zero=jnp.zeros((),BF)
    ones2=jnp.where(l6<2,1.0,0.0).astype(BF)
    k=k_ref[...]
    v=v_ref[...]
    fk=fk_ref[...]
    kx=[]
    vx=[]
    km=[]
    for h in (0,1):
        own=lo if h==0 else ~lo
        kx.append(jnp.where(own,k,fk))
        vx.append(jnp.where(own,v,ones2))
        km.append(jnp.where(own,k,zero))
    dv=jnp.zeros((L,128),F32)
    dk=jnp.zeros((L,128),F32)
    for b in range(L//qb):
        rows=pl.ds(b*qb,qb)
        q=q_ref[rows,:]
        fx=fx_ref[rows,:]
        do=do_ref[rows,:]
        prod=do.astype(F32)*o_ref[rows,:].astype(F32)
        d0=-jnp.sum(jnp.where(lo,prod,0.0),axis=1,keepdims=True)
        d1=-jnp.sum(jnp.where(lo,0.0,prod),axis=1,keepdims=True)
        nd=jnp.where(lo,d1,d0)
        hi=nd.astype(BF).astype(F32)
        fd=jnp.where(l6==0,hi,jnp.where(l6==1,nd-hi,0.0)).astype(BF)
        dq=jnp.zeros((qb,128),F32)
        for h in (0,1):
            own=lo if h==0 else ~lo
            qx=jnp.where(own,q,fx)
            dx=jnp.where(own,do,fd)
            qm=jnp.where(own,q,zero)
            dm=jnp.where(own,do,zero)
            p=jnp.exp2(nt(kx[h],qx))
            dpt=nt(vx[h],dx)
            pb=p.astype(BF)
            ds=(p*dpt).astype(BF)
            dv=dv+nn(pb,dm)
            dk=dk+nn(ds,qm)
            dq=dq+tn(ds,km[h])
        out_ref[0,rows,:]=(dq*0.125).astype(BF)
    out_ref[1]=(dk*LN2).astype(BF)
    out_ref[2]=dv.astype(BF)


def attn_bwd(q,k,v,fx,fk,o,do,prev,f0,n,qb=256):
    T=q.shape[0]
    np_=D//128
    blk=pl.BlockSpec((L,128),lambda i:((f0+i)//np_,(f0+i)%np_))
    fb=pl.BlockSpec((L,128),lambda i:((f0+i)//np_,0))
    prev=list(prev)
    return pl.pallas_call(
        functools.partial(bwd_kernel,qb=qb),grid=(n,),
        in_specs=[blk,blk,blk,blk,fb,blk,blk]+[ANY]*len(prev),out_specs=pl.BlockSpec((3,L,128),lambda i:(0,(f0+i)//np_,(f0+i)%np_)),
        out_shape=S_((3,T,D),BF),
        input_output_aliases={7+i:i for i in range(len(prev))},
        compiler_params=pltpu.CompilerParams(dimension_semantics=("arbitrary",)),
        cost_estimate=cost(n*2*10*L*L*256,n*L*128*20,n*2*L*L),
        name="attn_bwd")(q,k,v,fx,fk,o,do,*prev)


def mid_kernel(idx_ref,*refs,tb,fc,ns,wr,fr):
    tok_ref,row_ref,att_ref,cot_ref,vec_ref=refs[:5]
    own=refs[5:8]
    mine=refs[8:8+ns-1]
    other=refs[8+ns-1:8+2*(ns-1)]
    b0=8+2*(ns-1)
    res_ref,gm_ref,ga_ref,keep_ref,send_ref,sv_ref,sub_ref,ow,up,dn,aup,adn,aow,sem=refs[b0:]
    i=pl.program_id(0)
    n=pl.num_programs(0)
    c=idx_ref[0]
    def copies():
        cps=[]
        def put(src,dst):
            cps.append(pltpu.make_async_copy(src,dst,sem.at[len(cps)]))
        r16=lambda sh,m: pl.ds(pl.multiple_of(sh*m,16),m)
        sh=idx_ref[1+ns]
        put(own[0],ow.at[r16(sh,wr)])
        put(own[1],up.at[r16(sh,wr)])
        put(own[2],dn.at[r16(sh,fr)])
        for j in range(1,ns):
            for src,sh,cc in ((mine[j-1],idx_ref[1+ns+j],c),(other[j-1],idx_ref[1+2*ns+j],1-c)):
                cd=pl.ds(pl.multiple_of(cc*HC,128),HC)
                put(src.at[pl.ds(0,wr)],ow.at[r16(sh,wr),cd])
                for b in range(4):
                    put(src.at[pl.ds(wr+b*wr,wr)],up.at[r16(sh,wr),pl.ds(pl.multiple_of(cc*4*HC+b*HC,128),HC)])
                put(src.at[pl.ds(5*wr,fr)],dn.at[r16(sh,fr),cd])
        return cps
    @pl.when(i==0)
    def _():
        cps=copies()
        for cp in cps:
            cp.start()
        aup[...]=jnp.zeros_like(aup)
        adn[...]=jnp.zeros_like(adn)
        aow[...]=jnp.zeros_like(aow)
        sv_ref[...]=jnp.zeros_like(sv_ref)
        sub_ref[...]=jnp.zeros_like(sub_ref)
        for cp in cps:
            cp.wait()
    ob=vec_ref[4:5,:]
    g2=vec_ref[5:6,:]
    b2=vec_ref[6:7,:]
    db=vec_ref[7:8,:]
    att=att_ref[...]
    mixed=tok_ref[...]+row_ref[0]+nn(att,ow[...])+ob
    xhat,r=norm(mixed)
    n2=(xhat*g2+b2).astype(BF)
    n2t=n2.T
    cot=cot_ref[...]
    g=cot.astype(BF)
    res=mixed+db
    gn2=jnp.zeros((tb,D),F32)
    for j in range(FF//fc):
        cs=slice(j*fc,(j+1)*fc)
        pre=nn(n2,up[:,cs])+vec_ref[8+j:9+j,:]
        gact=nt(g,dn[cs,:])
        phi=0.5+0.5*lax.erf(pre*(2**-0.5))
        pdf=jnp.exp2(pre*pre*(-0.5*LOG2E))*(1.0/math.sqrt(2*math.pi))
        act=(pre*phi).astype(BF)
        gp=gact*(phi+pre*pdf)
        gpre=gp.astype(BF)
        sub_ref[:,cs]+=sum8(gp)
        res=res+nn(act,dn[cs,:])
        gn2=gn2+nt(gpre,up[:,cs])
        adn[cs,:]+=tn(act,g)
        aup[:,cs]+=nn(n2t,gpre)
    res_ref[...]=res
    e=gn2*g2
    c1=jnp.mean(e,axis=1,keepdims=True)
    c2=jnp.mean(e*xhat,axis=1,keepdims=True)
    gm=cot+r*(e-c1-xhat*c2)
    gml=gm.astype(BF)
    gm_ref[...]=gml
    ga_ref[...]=nt(gml,ow[...]).astype(BF)
    aow[...]+=tn(att,gml)
    sv_ref[0:8,:]+=sum8(gm)
    sv_ref[8:16,:]+=sum8(gn2*xhat)
    sv_ref[16:24,:]+=sum8(gn2)
    sv_ref[24:32,:]+=sum8(cot)
    @pl.when(i==n-1)
    def _():
        for ref,base,odd in ((keep_ref,1+ns,0),(send_ref,1+2*ns,1)):
            for ch in (0,1):
                @pl.when(c==(ch+odd)%2)
                def _():
                    def body(j,carry):
                        sh=idx_ref[base+j]
                        rw=pl.ds(pl.multiple_of(sh*wr,8),wr)
                        ref[j,0:wr,:]=aow[rw,ch*HC:(ch+1)*HC].astype(BF)
                        for b in range(4):
                            lo=(ch*4+b)*HC
                            ref[j,wr+b*wr:2*wr+b*wr,:]=aup[rw,lo:lo+HC].astype(BF)
                        ref[j,5*wr:5*wr+fr,:]=adn[pl.ds(pl.multiple_of(sh*fr,8),fr),ch*HC:(ch+1)*HC].astype(BF)
                        return carry
                    lax.fori_loop(0,ns,body,0)


def mid(idx,tok,row,att,cot,vec,own,mine,other,tb=256,fc=D):
    T=tok.shape[0]
    per=L//tb
    ns=len(mine)+1
    wr=own[0].shape[0]
    fr=own[2].shape[0]
    rb=5*wr+fr
    blk=pl.BlockSpec((tb,D),lambda i,*_:(i,0))
    return pl.pallas_call(
        functools.partial(mid_kernel,tb=tb,fc=fc,ns=ns,wr=wr,fr=fr),
        grid_spec=pltpu.PrefetchScalarGridSpec(
            num_scalar_prefetch=1,grid=(T//tb,),
            in_specs=[blk,pl.BlockSpec((1,1,D),lambda i,*_:(i//per,0,0)),blk,blk,full(VR,D)]+[ANY]*(3+2*(ns-1)),
            out_specs=[blk,blk,blk,full(ns,rb,HC),full(ns,rb,HC),full(32,D),full(8,FF)],
            scratch_shapes=[pltpu.VMEM((D,D),BF),pltpu.VMEM((D,FF),BF),pltpu.VMEM((FF,D),BF),
                pltpu.VMEM((D,FF),F32),pltpu.VMEM((FF,D),F32),pltpu.VMEM((D,D),F32),
                pltpu.SemaphoreType.DMA((3+12*(ns-1),))]),
        out_shape=[S_((T,D),F32),S_((T,D),BF),S_((T,D),BF),S_((ns,rb,HC),BF),S_((ns,rb,HC),BF),S_((32,D),F32),S_((8,FF),F32)],
        compiler_params=pltpu.CompilerParams(dimension_semantics=("arbitrary",),vmem_limit_bytes=67043328),
        cost_estimate=cost(6*T*D*(D+2*FF),T*D*20+30*D*FF,2*T*FF),
        name="mid")(idx,tok,row,att,cot,vec,*own,*mine,*other)


def dw_kernel(idx_ref,nt_ref,d_ref,keep_ref,send_ref,sv_ref,acc,*,ns,wr):
    i=pl.program_id(0)
    c=idx_ref[0]
    @pl.when(i==0)
    def _():
        acc[...]=jnp.zeros_like(acc)
        sv_ref[...]=jnp.zeros_like(sv_ref)
    for w in range(3):
        acc[w]+=nn(nt_ref[...],d_ref[w])
    sv_ref[0:8,:]+=sum8(d_ref[0].astype(F32))
    sv_ref[8:16,:]+=sum8(d_ref[2].astype(F32))
    @pl.when(i==pl.num_programs(0)-1)
    def _():
        for ref,base,odd in ((keep_ref,1+ns,0),(send_ref,1+2*ns,1)):
            for ch in (0,1):
                @pl.when(c==(ch+odd)%2)
                def _():
                    def body(j,carry):
                        rw=pl.ds(pl.multiple_of(idx_ref[base+j]*wr,8),wr)
                        for w in range(3):
                            ref[j,w*wr:(w+1)*wr,:]=acc[w,rw,ch*HC:(ch+1)*HC].astype(BF)
                        return carry
                    lax.fori_loop(0,ns,body,0)


def dw(idx,n1t,d,ns,tb=512):
    T=n1t.shape[1]
    wr=D//ns
    return pl.pallas_call(
        functools.partial(dw_kernel,ns=ns,wr=wr),
        grid_spec=pltpu.PrefetchScalarGridSpec(
            num_scalar_prefetch=1,grid=(T//tb,),
            in_specs=[pl.BlockSpec((D,tb),lambda i,*_:(0,i)),pl.BlockSpec((3,tb,D),lambda i,*_:(0,i,0))],
            out_specs=[full(ns,3*wr,HC),full(ns,3*wr,HC),full(16,D)],
            scratch_shapes=[pltpu.VMEM((3,D,D),F32)]),
        out_shape=[S_((ns,3*wr,HC),BF)]*2+[S_((16,D),F32)],
        compiler_params=pltpu.CompilerParams(dimension_semantics=("arbitrary",)),
        cost_estimate=cost(6*T*D*D,T*D*8+12*D*D),
        name="dw")(idx,n1t,d)


def dx_kernel(tok_ref,row_ref,d_ref,gm_ref,w_ref,vec_ref,gt_ref,sv_ref,ts_ref,*,per):
    i=pl.program_id(0)
    @pl.when(i==0)
    def _():
        sv_ref[...]=jnp.zeros_like(sv_ref)
    @pl.when(i%per==0)
    def _():
        ts_ref[...]=jnp.zeros_like(ts_ref)
    gn=nt(d_ref[0],w_ref[0])+nt(d_ref[1],w_ref[1])+nt(d_ref[2],w_ref[2])
    xhat,r=norm(tok_ref[...]+row_ref[0])
    e=gn*vec_ref[0:1,:]
    c1=jnp.mean(e,axis=1,keepdims=True)
    c2=jnp.mean(e*xhat,axis=1,keepdims=True)
    gt=gm_ref[...].astype(F32)+r*(e-c1-xhat*c2)
    gt_ref[...]=gt
    sv_ref[0:8,:]+=sum8(gn*xhat)
    sv_ref[8:16,:]+=sum8(gn)
    ts_ref[0]+=sum8(gt)


def dx(tok,row,d,gm,w,vec,tb=512):
    T=tok.shape[0]
    per=L//tb
    blk=pl.BlockSpec((tb,D),lambda i:(i,0))
    return pl.pallas_call(
        functools.partial(dx_kernel,per=per),grid=(T//tb,),
        in_specs=[blk,pl.BlockSpec((1,1,D),lambda i:(i//per,0,0)),pl.BlockSpec((3,tb,D),lambda i:(0,i,0)),blk,full(3,D,D),full(VR,D)],
        out_specs=[blk,full(16,D),pl.BlockSpec((1,8,D),lambda i:(i//per,0,0))],
        out_shape=[S_((T,D),F32),S_((16,D),F32),S_((T//L,8,D),F32)],
        compiler_params=pltpu.CompilerParams(dimension_semantics=("arbitrary",)),
        cost_estimate=cost(6*T*D*D,T*D*16+6*D*D),
        name="dx")(tok,row,d,gm,w,vec)


def rows8(x):
    return jnp.sum(x,axis=0,keepdims=True)


def sums_kernel(id_ref,sv1_ref,svq_ref,sv2_ref,sub_ref,ts_ref,out_ref):
    src=[sv1_ref[0:8],sv1_ref[8:16],svq_ref[0:8],svq_ref[8:16]]+[sv2_ref[8*i:8*i+8] for i in range(4)]
    src+=[sub_ref[:,i*D:(i+1)*D] for i in range(FF//D)]
    rows=[rows8(x) for x in src]+[id_ref[0:1],id_ref[1:2]]+[rows8(ts_ref[i]) for i in range(ts_ref.shape[0])]
    out_ref[...]=jnp.concatenate(rows,axis=0).astype(BF)


def sums(ids,sv1,svq,sv2,sub,ts):
    vm=pl.BlockSpec(memory_space=pltpu.VMEM)
    return pl.pallas_call(sums_kernel,in_specs=[vm]*6,out_specs=vm,
        out_shape=S_((VR+ts.shape[0],D),BF),cost_estimate=cost(0,10**6),name="sums")(ids,sv1,svq,sv2,sub,ts)


def group_kernel(idx_ref,*refs,ns,nseq):
    out_ref,acc=refs[ns:]
    tot=refs[0][0:VR].astype(F32)
    for j in range(1,ns):
        tot=tot+refs[j][0:VR].astype(F32)
    for j in range(ns):
        acc[idx_ref[1+j]]=refs[j][VR:VR+nseq].astype(F32)
    out_ref[...]=jnp.concatenate([tot]+[acc[j] for j in range(ns)],axis=0).astype(BF)


def group(idx,pays,nseq):
    ns=len(pays)
    vm=pl.BlockSpec(memory_space=pltpu.VMEM)
    return pl.pallas_call(functools.partial(group_kernel,ns=ns,nseq=nseq),
        in_specs=[pl.BlockSpec(memory_space=pltpu.SMEM)]+[vm]*ns,out_specs=vm,
        out_shape=S_((VR+ns*nseq,D),BF),scratch_shapes=[pltpu.VMEM((ns,nseq,D),F32)],
        cost_estimate=cost(0,10**6),name="group")(idx,*pays)


def table_kernel(me_ref,*refs,nr,rows,own):
    sum_ref,tab_ref,acc,allr=refs[nr:]
    r0=me_ref[0]
    for j in range(nr):
        acc[r0^j]=refs[j][...].astype(F32)
    tot=acc[0,0:VR]
    for r in range(1,nr):
        tot=tot+acc[r,0:VR]
    sum_ref[...]=tot
    for r in range(nr):
        allr[r*rows:(r+1)*rows,:]=acc[r,VR:VR+rows]
    n=nr*rows
    ids=tot[NV:NV+1,0:n]*32.0+tot[NV+1:NV+2,0:n]
    line=lax.broadcasted_iota(jnp.int32,(own,n),0)+me_ref[1]*own
    hit=jnp.where(line==ids.astype(jnp.int32),1.0,0.0).astype(BF)
    tab_ref[...]=nn(hit,allr[...].astype(BF))


def table(me,pays,own):
    nr=len(pays)
    rows=pays[0].shape[0]-VR
    vm=pl.BlockSpec(memory_space=pltpu.VMEM)
    return pl.pallas_call(functools.partial(table_kernel,nr=nr,rows=rows,own=own),
        in_specs=[pl.BlockSpec(memory_space=pltpu.SMEM)]+[vm]*nr,out_specs=[vm,vm],
        out_shape=[S_((VR,D),F32),S_((own,D),F32)],
        scratch_shapes=[pltpu.VMEM((nr,VR+rows,D),F32),pltpu.VMEM((nr*rows,D),F32)],
        cost_estimate=cost(0,4*10**6),name="table")(me,*pays)


def unpack_kernel(idx_ref,a_ref,b_ref,*outs,parts):
    for ch in (0,1):
        @pl.when(idx_ref[0]==ch)
        def _():
            for h,ref in enumerate((a_ref,b_ref) if ch==0 else (b_ref,a_ref)):
                r0=0
                for out,(nr,nb) in zip(outs,parts):
                    for b in range(nb):
                        out[:,(h*nb+b)*HC:(h*nb+b+1)*HC]=ref[r0:r0+nr,:].astype(F32)
                        r0+=nr


def unpack(idx,a,b,parts):
    vm=pl.BlockSpec(memory_space=pltpu.VMEM)
    return pl.pallas_call(functools.partial(unpack_kernel,parts=parts),
        in_specs=[pl.BlockSpec(memory_space=pltpu.SMEM),vm,vm],out_specs=[vm]*len(parts),
        out_shape=[S_((nr,2*nb*HC),F32) for nr,nb in parts],
        cost_estimate=cost(0,12*a.shape[0]*HC),name="unpack")(idx,a,b)


def small_kernel(me_ref,x_ref,out_ref,id_ref,*,w,fr,nseq):
    x=x_ref[...].astype(F32)
    def spread(rows,width,at):
        n=rows[0].shape[1]
        y=jnp.concatenate(rows+[jnp.zeros((8-len(rows),n),F32)]*(len(rows)<8),axis=0)
        y=jnp.concatenate([y,jnp.zeros((8,width-n),F32)],axis=1)
        return pltpu.roll(y,at,1)
    v=spread([x[:,i*w:(i+1)*w] for i in range(8)],D,me_ref[1]*w)
    u=spread([x[:,8*w:8*w+fr]],FF,me_ref[1]*fr)
    b=8*w+fr
    st=[x[:,b:b+nseq],x[:,b+nseq:b+2*nseq]]
    g=spread(st,D,me_ref[1]*nseq)
    id_ref[...]=spread(st,D,me_ref[2]*nseq)[0:2]
    out_ref[...]=jnp.concatenate([v]+[u[0:1,i*D:(i+1)*D] for i in range(FF//D)]+[g[0:2]],axis=0).astype(BF)


def small_rows(me,flat,w,fr,nseq):
    vm=pl.BlockSpec(memory_space=pltpu.VMEM)
    return pl.pallas_call(functools.partial(small_kernel,w=w,fr=fr,nseq=nseq),
        in_specs=[pl.BlockSpec(memory_space=pltpu.SMEM),vm],out_specs=[vm,vm],
        out_shape=[S_((VR,D),BF),S_((2,D),F32)],cost_estimate=cost(0,10**6),name="small")(me,flat)


class Ring:
    def __init__(self,rep,shard):
        self.R,self.S=rep,shard
        self.nb=shard.bit_length()-1
        self.Z=rep//2
        r=lax.axis_index("rep")
        self.s=lax.axis_index("shard")
        self.c=r%2
        self.z=r//2

    def move(self,x,to):
        pairs=[]
        for r in range(self.R):
            for s in range(self.S):
                r2,s2=to(r,s)
                pairs.append((r*self.S+s,r2*self.S+s2))
        return lax.ppermute(x,("rep","shard"),pairs)

    def order(self,c,t):
        return (t+c*(self.nb//2))%self.nb

    def mask(self,c,j):
        m=0
        for t in range(self.nb):
            if j>>t&1:
                m|=1<<self.order(c,t)
        return m

    def step(self,x,t):
        return self.move(x,lambda r,s:(r,s^(1<<self.order(r%2,t))))

    def direct(self,x,j):
        return self.move(x,lambda r,s:(r,s^j))

    def core(self,x):
        return self.move(x,lambda r,s:(r^1,s))

    def plane(self,x,j):
        return self.move(x,lambda r,s:(r^(2*j),s))

    def index(self):
        m=[[self.mask(c,j) for j in range(self.S)] for c in (0,1)]
        base=list(range(self.S))
        t=jnp.where(self.c==0,jnp.array([0]+base+m[0]+m[1],jnp.int32),jnp.array([0]+base+m[1]+m[0],jnp.int32))
        head=jnp.arange(1+3*self.S)==0
        return jnp.where(head,self.c,t^self.s).astype(jnp.int32)


def tie(*xs):
    return lax.optimization_barrier(xs)


def add(a,b):
    return (a.astype(F32)+b.astype(F32)).astype(BF)


def fold(x,got,n):
    return add(x[n:],got[n:]),add(x[:n],got[:n])


def plane_rows(g,x):
    x=x.reshape(g.Z,-1,HC)
    return [lax.dynamic_index_in_dim(x,g.z^j,0,keepdims=False) for j in range(1,g.Z)]


def plane_send(g,rows):
    return [g.plane(x,j) for j,x in enumerate(rows,1)]


def plane_sum(g,x,parts):
    mine=lax.dynamic_index_in_dim(x.reshape(g.Z,-1,HC),g.z,0,keepdims=False).astype(F32)
    for p in parts:
        mine=mine+p.astype(F32)
    return mine.astype(BF)


def plane_join(g,mine,parts):
    out=jnp.zeros((g.Z,)+mine.shape,BF)
    for j,p in enumerate([mine]+parts):
        out=lax.dynamic_update_index_in_dim(out,p,g.z^j,0)
    return out.reshape(-1,HC)


def local(tokens,segments,time_steps,time_table,ln1_gain,ln1_bias,q_weight,q_bias,k_weight,v_weight,v_bias,o_weight,o_bias,ln2_gain,ln2_bias,up_weight,up_bias,down_weight,down_bias,cotangent):
    nseq=tokens.shape[0]
    T=nseq*L
    g=Ring(lax.axis_size("rep"),lax.axis_size("shard"))
    S=g.S
    w=ln1_gain.shape[0]
    fr=down_weight.shape[0]
    own=time_table.shape[0]
    idx=g.index()
    pack_a=pack(pack_a_kernel,idx,(q_weight,k_weight,v_weight),"pack_a")
    mine_a=[g.direct(pack_a,j) for j in range(1,S)]
    flat=jnp.concatenate([ln1_gain,ln1_bias,q_bias,v_bias,o_bias,ln2_gain,ln2_bias,down_bias,up_bias,
        (time_steps//32).astype(BF),(time_steps%32).astype(BF)])
    flat,segments,o_weight_,pack_a=tie(flat,segments,o_weight,pack_a)
    r=g.z*2+g.c
    me=jnp.stack([r,g.s,r*S+g.s]).astype(jnp.int32)
    small,ids=small_rows(me,flat[None],w,up_bias.shape[0],nseq)
    vec=small.astype(F32)
    for j in reversed(range(1,S)):
        vec=vec+g.direct(small,j).astype(F32)
    steps=vec[NV,:S*nseq]*32.0+vec[NV+1,:S*nseq]
    hit=steps.astype(jnp.int32)[:,None]==jnp.arange(own)[None,:]+g.s*own
    rows=jnp.dot(hit.astype(BF),time_table,preferred_element_type=F32).astype(BF).reshape(S,nseq,D)
    pick=lambda j: lax.dynamic_index_in_dim(rows,g.s^j,0,keepdims=False)
    picks=[pick(j) for j in range(S)]
    picks[0],*mine_a=tie(picks[0],*mine_a)
    row=picks[0].astype(F32)
    for j in range(1,S):
        row=row+g.direct(picks[j],j).astype(F32)
    row=row.reshape(nseq,1,D)
    pack_b=pack(pack_b_kernel,idx,(o_weight_,up_weight,down_weight),"pack_b")
    tok=tokens.reshape(T,D)
    cot=cotangent.reshape(T,D)
    fq,fk=seg_features(segments.reshape(T))
    fq,fk,pack_b,*mine_a=tie(fq,fk,pack_b,*mine_a)
    other_a=[g.core(x) for x in mine_a]
    mine_b=[pack_b]
    first=[g.step(pack_b,t) for t in range(g.nb)]
    q,k,v,n1t,wqkv=qkv(idx,tok,row,vec,(q_weight,k_weight,v_weight),mine_a,other_a)
    fwd=attn_fwd(q,k,v,fq,fk,(),0,3*nseq//2)
    o1,fx1,*first=tie(*fwd,*first)
    for t in range(g.nb):
        mine_b=mine_b+[first[t]]+[g.step(x,t) for x in mine_b[1:]]
    direct=[1<<t for t in range(g.nb)]
    other_b=[None]+[g.core(x) if j in direct else None for j,x in enumerate(mine_b[1:],1)]
    fwd=attn_fwd(q,k,v,fq,fk,(o1,fx1),3*nseq//2,3*nseq)
    late=[j for j in range(1,S) if j not in direct]
    o1,fx1,*got=tie(*fwd,*[mine_b[j] for j in late])
    for j,x in zip(late,got):
        mine_b[j]=x
        other_b[j]=g.core(x)
    att,fx=attn_fwd(q,k,v,fq,fk,(o1,fx1),9*nseq//2,6*nseq-9*nseq//2)
    res,gm,ga,keep_b,send_b,sv2,sub=mid(idx,tok,row,att,cot,vec,(o_weight,up_weight,down_weight),mine_b[1:],other_b[1:])
    cuts=[0,nseq,nseq+5*nseq//2,5*nseq,6*nseq]
    call=lambda prev,i: attn_bwd(q,k,v,fx,fk,att,ga,prev,cuts[i],cuts[i+1]-cuts[i])
    got=g.core(send_b)
    d=call((),0)
    d,got=tie(d,got)
    n=S
    x=keep_b
    for t in reversed(range(g.nb)):
        n//=2
        up,x=fold(x,got,n)
        d,up,x=tie(d,up,x)
        got=g.step(up,t)
        i=g.nb-t
        if i<=2:
            d=call((d,),i)
            d,got=tie(d,got)
    xb=add(x[0],got[0])
    d,xb,*rows_b=tie(d,xb,*plane_rows(g,xb))
    parts=plane_send(g,rows_b)
    d=call((d,),3)
    keep_a,send_a,svq=dw(idx,n1t,d,S)
    keep_a,send_a,*parts=tie(keep_a,send_a,*parts)
    got=g.core(send_a)
    mine=plane_sum(g,xb,parts)
    back=[g.plane(mine,j) for j in range(1,g.Z)]
    gm,mine_,got=tie(gm,mine,got)
    up,x=fold(keep_a,got,S//2)
    gm,up=tie(gm,up)
    got=g.step(up,g.nb-1)
    gt,sv1,ts=dx(tok,row,d,gm,wqkv,vec)
    ts,got=tie(ts,got)
    n=S//2
    for t in reversed(range(g.nb-1)):
        n//=2
        up,x=fold(x,got,n)
        ts,up=tie(ts,up)
        got=g.step(up,t)
    pay=sums(ids,sv1,svq,sv2,sub,ts)
    pays=[pay]+[g.direct(pay,j) for j in range(1,S)]
    pays[-1],got=tie(pays[-1],got)
    xa=add(x[0],got[0])
    rows_a=plane_rows(g,xa)
    *pays,rows_a[0]=tie(*pays,rows_a[0])
    parts_a=plane_send(g,rows_a)
    pay=group(idx,pays,nseq)
    pay,*parts_a=tie(pay,*parts_a)
    pays=[pay]+[g.move(pay,lambda r,s,j=j:(r^j,s)) for j in range(1,g.R)]
    out_b=plane_join(g,mine_,back)
    out_b,*parts_a=tie(out_b,*parts_a)
    mine=plane_sum(g,xa,parts_a)
    out_b,mine,*pays=tie(out_b,mine,*pays)
    back_a=[g.plane(mine,j) for j in range(1,g.Z)]
    other_b=g.core(out_b)
    vsum,gtab=table(me,pays,own)
    go,gup,gdn=unpack(idx,out_b,other_b,((w,1),(w,4),(fr,1)))
    vsum,gtab,gup,*back_a=tie(vsum,gtab,gup,*back_a)
    out_a=plane_join(g,mine,back_a)
    gq,gk,gv=unpack(idx,out_a,g.core(out_a),((w,1),)*3)
    sums8=lax.dynamic_slice_in_dim(vsum[:8],g.s*w,w,1)
    subs=lax.dynamic_slice_in_dim(vsum[8:NV].reshape(FF),g.s*up_bias.shape[0],up_bias.shape[0],0)
    return (res.reshape(tokens.shape),gt.reshape(tokens.shape),gtab,sums8[0],sums8[1],gq,sums8[2],gk,gv,sums8[3],go,sums8[4],sums8[5],sums8[6],gup,subs,gdn,sums8[7])


def solution(mesh):
    b=("rep","shard")
    s=P("shard")
    m=P("shard",None)
    t=P(b,None,None)
    return jax.shard_map(local,mesh=mesh,
        in_specs=(t,P(b,None),P(b),m,s,s,m,s,m,m,s,m,s,s,s,m,s,m,s,t),
        out_specs=(t,t,m,s,s,m,s,m,m,s,m,s,s,s,m,s,m,s),check_vma=False)
```

```python
import functools
import math

import jax
import jax.numpy as jnp
from jax import lax
from jax.experimental import pallas as pl
from jax.experimental.pallas import tpu as pltpu
from jax.sharding import PartitionSpec as P

NEG=-1e30
EPS=1e-5
L=1024
D=768
FF=3072
HC=D//2
BF=jnp.bfloat16
F32=jnp.float32
LOG2E=math.log2(math.e)
LN2=math.log(2.0)
QS=0.125*LOG2E
VR=14
NV=12
ANY=pl.BlockSpec(memory_space=pl.ANY)
S_=jax.ShapeDtypeStruct


def nt(a,b):
    return lax.dot_general(a,b,(((1,),(1,)),((),())),preferred_element_type=F32)


def nn(a,b):
    return lax.dot_general(a,b,(((1,),(0,)),((),())),preferred_element_type=F32)


def tn(a,b):
    return lax.dot_general(a,b,(((0,),(0,)),((),())),preferred_element_type=F32)


def full(*s):
    return pl.BlockSpec(s,lambda i,*_:(0,)*len(s),pipeline_mode=pl.Buffered(1))


def norm(x):
    mean=jnp.mean(x,axis=1,keepdims=True)
    off=x-mean
    var=jnp.mean(off*off,axis=1,keepdims=True)
    r=lax.rsqrt(var+EPS)
    return off*r,r


def sum8(x):
    return jnp.sum(x.reshape(x.shape[0]//8,8,x.shape[1]),axis=0)


def cost(flops,nbytes,trans=0):
    return pl.CostEstimate(flops=int(flops)//10,bytes_accessed=int(nbytes)//10,transcendentals=int(trans)//10)


def seg_features(seg):
    lane=jnp.arange(128)%64
    hit=seg[:,None]==lane[None,:]
    first=(lane<4)[None]
    fq=jnp.where(first&hit,1.0,0.0).astype(BF)
    fk=jnp.where(first,jnp.where(hit,0.0,NEG),jnp.where((lane<7)[None],1.0,0.0)).astype(BF)
    return fq,fk


def qkv_kernel(idx_ref,*refs,ns,wr):
    tok_ref,row_ref,vec_ref=refs[:3]
    own=refs[3:6]
    mine=refs[6:6+ns-1]
    other=refs[6+ns-1:6+2*(ns-1)]
    hi=6+2*(ns-1)
    q_ref,k_ref,v_ref,nt_ref,w_ref,sem=refs[hi:hi+6]
    @pl.when(pl.program_id(0)==0)
    def _():
        c=idx_ref[0]
        cps=[]
        def put(src,w,sh,c0,nc):
            dst=w_ref.at[w,pl.ds(pl.multiple_of(sh*wr,16),wr),pl.ds(c0,nc)]
            cp=pltpu.make_async_copy(src,dst,sem.at[len(cps)])
            cp.start()
            cps.append(cp)
        for w in range(3):
            put(own[w],w,idx_ref[1],0,D)
        for j in range(1,ns):
            for w in range(3):
                put(mine[j-1].at[pl.ds(w*wr,wr)],w,idx_ref[1+j],pl.multiple_of(c*HC,128),HC)
                put(other[j-1].at[pl.ds(w*wr,wr)],w,idx_ref[1+j],pl.multiple_of((1-c)*HC,128),HC)
        for cp in cps:
            cp.wait()
    xhat,_=norm(tok_ref[...]+row_ref[0])
    n1=(xhat*vec_ref[0:1,:]+vec_ref[1:2,:]).astype(BF)
    q_ref[...]=((nn(n1,w_ref[0])+vec_ref[2:3,:])*QS).astype(BF)
    k_ref[...]=nn(n1,w_ref[1]).astype(BF)
    v_ref[...]=(nn(n1,w_ref[2])+vec_ref[3:4,:]).astype(BF)
    nt_ref[...]=n1.T


def qkv(idx,tok,row,vec,own,mine,other,tb=512):
    T=tok.shape[0]
    per=L//tb
    ns=len(mine)+1
    wr=own[0].shape[0]
    blk=pl.BlockSpec((tb,D),lambda i,*_:(i,0))
    return pl.pallas_call(
        functools.partial(qkv_kernel,ns=ns,wr=wr),
        grid_spec=pltpu.PrefetchScalarGridSpec(
            num_scalar_prefetch=1,grid=(T//tb,),
            in_specs=[blk,pl.BlockSpec((1,1,D),lambda i,*_:(i//per,0,0)),full(VR,D)]+[ANY]*(3+2*(ns-1)),
            out_specs=[blk]*3+[pl.BlockSpec((D,tb),lambda i,*_:(0,i)),full(3,D,D)],
            scratch_shapes=[pltpu.SemaphoreType.DMA((3+6*(ns-1),))]),
        out_shape=[S_((T,D),BF)]*3+[S_((D,T),BF),S_((3,D,D),BF)],
        compiler_params=pltpu.CompilerParams(dimension_semantics=("arbitrary",)),
        cost_estimate=cost(6*T*D*D,T*D*10+9*D*D),
        name="qkv")(idx,tok,row,vec,*own,*mine,*other)


def pack_a_kernel(idx_ref,q_ref,k_ref,v_ref,out_ref):
    wr=q_ref.shape[0]
    for ch in (0,1):
        @pl.when(idx_ref[0]==ch)
        def _():
            for w,ref in enumerate((q_ref,k_ref,v_ref)):
                out_ref[w*wr:(w+1)*wr,:]=ref[:,ch*HC:(ch+1)*HC]


def pack_b_kernel(idx_ref,o_ref,u_ref,d_ref,out_ref):
    wr=o_ref.shape[0]
    for ch in (0,1):
        @pl.when(idx_ref[0]==ch)
        def _():
            out_ref[0:wr,:]=o_ref[:,ch*HC:(ch+1)*HC]
            for b in range(4):
                out_ref[wr+b*wr:2*wr+b*wr,:]=u_ref[:,(ch*4+b)*HC:(ch*4+b+1)*HC]
            out_ref[5*wr:,:]=d_ref[:,ch*HC:(ch+1)*HC]


def pack(kernel,idx,ws,name):
    rows=sum(x.shape[0]*x.shape[1]//D for x in ws)
    vm=pl.BlockSpec(memory_space=pltpu.VMEM)
    return pl.pallas_call(kernel,in_specs=[pl.BlockSpec(memory_space=pltpu.SMEM)]+[vm]*3,out_specs=vm,
        out_shape=S_((rows,HC),BF),cost_estimate=cost(0,4*rows*D),name=name)(idx,*ws)


def fwd_kernel(q_ref,k_ref,v_ref,fq_ref,fk_ref,*refs,qb):
    o_ref,fx_ref=refs[-2:]
    lane=lax.broadcasted_iota(jnp.int32,(1,128),1)
    lo=lane<64
    l6=lane&63
    ks=[]
    vs=[]
    k=k_ref[...]
    v=v_ref[...]
    fk=fk_ref[...]
    for h in (0,1):
        own=lo if h==0 else ~lo
        ks.append(jnp.where(own,k,fk))
        vs.append(jnp.where(own,v,jnp.where(l6==0,1.0,0.0).astype(BF)))
    for b in range(L//qb):
        rows=pl.ds(b*qb,qb)
        q=q_ref[rows,:]
        fq=fq_ref[rows,:]
        accs=[]
        ls=[]
        for h in (0,1):
            own=lo if h==0 else ~lo
            s=nt(jnp.where(own,q,fq),ks[h])
            m=jnp.max(s,axis=1,keepdims=True)
            p=jnp.exp2(s-m).astype(BF)
            acc=nn(p,vs[h])
            l=acc[:,64:65] if h==0 else acc[:,0:1]
            accs.append(acc*(1.0/l))
            ls.append(-(m+jnp.log2(l)))
        o_ref[rows,:]=jnp.where(lo,accs[0],accs[1]).astype(BF)
        nl=jnp.where(lo,ls[1],ls[0])
        hi=nl.astype(BF).astype(F32)
        r1=nl-hi
        mid=r1.astype(BF).astype(F32)
        r2=r1-mid
        fx_ref[rows,:]=jnp.where(l6==4,hi,jnp.where(l6==5,mid,jnp.where(l6==6,r2,fq.astype(F32)))).astype(BF)


def attn_fwd(q,k,v,fq,fk,prev,f0,n,qb=512):
    T=q.shape[0]
    np_=D//128
    blk=pl.BlockSpec((L,128),lambda i:((f0+i)//np_,(f0+i)%np_))
    fb=pl.BlockSpec((L,128),lambda i:((f0+i)//np_,0))
    prev=list(prev)
    return pl.pallas_call(
        functools.partial(fwd_kernel,qb=qb),grid=(n,),
        in_specs=[blk,blk,blk,fb,fb]+[ANY]*len(prev),out_specs=[blk,blk],
        out_shape=[S_((T,D),BF)]*2,
        input_output_aliases={5+i:i for i in range(len(prev))},
        compiler_params=pltpu.CompilerParams(dimension_semantics=("arbitrary",)),
        cost_estimate=cost(n*2*4*L*L*256,n*L*128*14,n*2*L*L),
        name="attn_fwd")(q,k,v,fq,fk,*prev)


def bwd_kernel(q_ref,k_ref,v_ref,fx_ref,fk_ref,o_ref,do_ref,*refs,qb):
    out_ref=refs[-1]
    lane=lax.broadcasted_iota(jnp.int32,(1,128),1)
    lo=lane<64
    l6=lane&63
    zero=jnp.zeros((),BF)
    ones2=jnp.where(l6<2,1.0,0.0).astype(BF)
    k=k_ref[...]
    v=v_ref[...]
    fk=fk_ref[...]
    kx=[]
    vx=[]
    km=[]
    for h in (0,1):
        own=lo if h==0 else ~lo
        kx.append(jnp.where(own,k,fk))
        vx.append(jnp.where(own,v,ones2))
        km.append(jnp.where(own,k,zero))
    dv=jnp.zeros((L,128),F32)
    dk=jnp.zeros((L,128),F32)
    for b in range(L//qb):
        rows=pl.ds(b*qb,qb)
        q=q_ref[rows,:]
        fx=fx_ref[rows,:]
        do=do_ref[rows,:]
        prod=do.astype(F32)*o_ref[rows,:].astype(F32)
        d0=-jnp.sum(jnp.where(lo,prod,0.0),axis=1,keepdims=True)
        d1=-jnp.sum(jnp.where(lo,0.0,prod),axis=1,keepdims=True)
        nd=jnp.where(lo,d1,d0)
        hi=nd.astype(BF).astype(F32)
        fd=jnp.where(l6==0,hi,jnp.where(l6==1,nd-hi,0.0)).astype(BF)
        dq=jnp.zeros((qb,128),F32)
        for h in (0,1):
            own=lo if h==0 else ~lo
            qx=jnp.where(own,q,fx)
            dx=jnp.where(own,do,fd)
            qm=jnp.where(own,q,zero)
            dm=jnp.where(own,do,zero)
            p=jnp.exp2(nt(kx[h],qx))
            dpt=nt(vx[h],dx)
            pb=p.astype(BF)
            ds=(p*dpt).astype(BF)
            dv=dv+nn(pb,dm)
            dk=dk+nn(ds,qm)
            dq=dq+tn(ds,km[h])
        out_ref[0,rows,:]=(dq*0.125).astype(BF)
    out_ref[1]=(dk*LN2).astype(BF)
    out_ref[2]=dv.astype(BF)


def attn_bwd(q,k,v,fx,fk,o,do,prev,f0,n,qb=256):
    T=q.shape[0]
    np_=D//128
    blk=pl.BlockSpec((L,128),lambda i:((f0+i)//np_,(f0+i)%np_))
    fb=pl.BlockSpec((L,128),lambda i:((f0+i)//np_,0))
    prev=list(prev)
    return pl.pallas_call(
        functools.partial(bwd_kernel,qb=qb),grid=(n,),
        in_specs=[blk,blk,blk,blk,fb,blk,blk]+[ANY]*len(prev),out_specs=pl.BlockSpec((3,L,128),lambda i:(0,(f0+i)//np_,(f0+i)%np_)),
        out_shape=S_((3,T,D),BF),
        input_output_aliases={7+i:i for i in range(len(prev))},
        compiler_params=pltpu.CompilerParams(dimension_semantics=("arbitrary",)),
        cost_estimate=cost(n*2*10*L*L*256,n*L*128*20,n*2*L*L),
        name="attn_bwd")(q,k,v,fx,fk,o,do,*prev)


def mid_kernel(idx_ref,*refs,tb,fc,ns,wr,fr):
    tok_ref,row_ref,att_ref,cot_ref,vec_ref=refs[:5]
    own=refs[5:8]
    mine=refs[8:8+ns-1]
    other=refs[8+ns-1:8+2*(ns-1)]
    b0=8+2*(ns-1)
    res_ref,gm_ref,ga_ref,keep_ref,send_ref,sv_ref,sub_ref,ow,up,dn,aup,adn,aow,sem=refs[b0:]
    i=pl.program_id(0)
    n=pl.num_programs(0)
    c=idx_ref[0]
    def copies():
        cps=[]
        def put(src,dst):
            cps.append(pltpu.make_async_copy(src,dst,sem.at[len(cps)]))
        r16=lambda sh,m: pl.ds(pl.multiple_of(sh*m,16),m)
        sh=idx_ref[1+ns]
        put(own[0],ow.at[r16(sh,wr)])
        put(own[1],up.at[r16(sh,wr)])
        put(own[2],dn.at[r16(sh,fr)])
        for j in range(1,ns):
            for src,sh,cc in ((mine[j-1],idx_ref[1+ns+j],c),(other[j-1],idx_ref[1+2*ns+j],1-c)):
                cd=pl.ds(pl.multiple_of(cc*HC,128),HC)
                put(src.at[pl.ds(0,wr)],ow.at[r16(sh,wr),cd])
                for b in range(4):
                    put(src.at[pl.ds(wr+b*wr,wr)],up.at[r16(sh,wr),pl.ds(pl.multiple_of(cc*4*HC+b*HC,128),HC)])
                put(src.at[pl.ds(5*wr,fr)],dn.at[r16(sh,fr),cd])
        return cps
    @pl.when(i==0)
    def _():
        cps=copies()
        for cp in cps:
            cp.start()
        aup[...]=jnp.zeros_like(aup)
        adn[...]=jnp.zeros_like(adn)
        aow[...]=jnp.zeros_like(aow)
        sv_ref[...]=jnp.zeros_like(sv_ref)
        sub_ref[...]=jnp.zeros_like(sub_ref)
        for cp in cps:
            cp.wait()
    ob=vec_ref[4:5,:]
    g2=vec_ref[5:6,:]
    b2=vec_ref[6:7,:]
    db=vec_ref[7:8,:]
    att=att_ref[...]
    mixed=tok_ref[...]+row_ref[0]+nn(att,ow[...])+ob
    xhat,r=norm(mixed)
    n2=(xhat*g2+b2).astype(BF)
    n2t=n2.T
    cot=cot_ref[...]
    g=cot.astype(BF)
    res=mixed+db
    gn2=jnp.zeros((tb,D),F32)
    for j in range(FF//fc):
        cs=slice(j*fc,(j+1)*fc)
        pre=nn(n2,up[:,cs])+vec_ref[8+j:9+j,:]
        gact=nt(g,dn[cs,:])
        phi=0.5+0.5*lax.erf(pre*(2**-0.5))
        pdf=jnp.exp2(pre*pre*(-0.5*LOG2E))*(1.0/math.sqrt(2*math.pi))
        act=(pre*phi).astype(BF)
        gp=gact*(phi+pre*pdf)
        gpre=gp.astype(BF)
        sub_ref[:,cs]+=sum8(gp)
        res=res+nn(act,dn[cs,:])
        gn2=gn2+nt(gpre,up[:,cs])
        adn[cs,:]+=tn(act,g)
        aup[:,cs]+=nn(n2t,gpre)
    res_ref[...]=res
    e=gn2*g2
    c1=jnp.mean(e,axis=1,keepdims=True)
    c2=jnp.mean(e*xhat,axis=1,keepdims=True)
    gm=cot+r*(e-c1-xhat*c2)
    gml=gm.astype(BF)
    gm_ref[...]=gml
    ga_ref[...]=nt(gml,ow[...]).astype(BF)
    aow[...]+=tn(att,gml)
    sv_ref[0:8,:]+=sum8(gm)
    sv_ref[8:16,:]+=sum8(gn2*xhat)
    sv_ref[16:24,:]+=sum8(gn2)
    sv_ref[24:32,:]+=sum8(cot)
    @pl.when(i==n-1)
    def _():
        for ref,base,odd in ((keep_ref,1+ns,0),(send_ref,1+2*ns,1)):
            for ch in (0,1):
                @pl.when(c==(ch+odd)%2)
                def _():
                    def body(j,carry):
                        sh=idx_ref[base+j]
                        rw=pl.ds(pl.multiple_of(sh*wr,8),wr)
                        ref[j,0:wr,:]=aow[rw,ch*HC:(ch+1)*HC].astype(BF)
                        for b in range(4):
                            lo=(ch*4+b)*HC
                            ref[j,wr+b*wr:2*wr+b*wr,:]=aup[rw,lo:lo+HC].astype(BF)
                        ref[j,5*wr:5*wr+fr,:]=adn[pl.ds(pl.multiple_of(sh*fr,8),fr),ch*HC:(ch+1)*HC].astype(BF)
                        return carry
                    lax.fori_loop(0,ns,body,0)


def mid(idx,tok,row,att,cot,vec,own,mine,other,tb=256,fc=D):
    T=tok.shape[0]
    per=L//tb
    ns=len(mine)+1
    wr=own[0].shape[0]
    fr=own[2].shape[0]
    rb=5*wr+fr
    blk=pl.BlockSpec((tb,D),lambda i,*_:(i,0))
    return pl.pallas_call(
        functools.partial(mid_kernel,tb=tb,fc=fc,ns=ns,wr=wr,fr=fr),
        grid_spec=pltpu.PrefetchScalarGridSpec(
            num_scalar_prefetch=1,grid=(T//tb,),
            in_specs=[blk,pl.BlockSpec((1,1,D),lambda i,*_:(i//per,0,0)),blk,blk,full(VR,D)]+[ANY]*(3+2*(ns-1)),
            out_specs=[blk,blk,blk,full(ns,rb,HC),full(ns,rb,HC),full(32,D),full(8,FF)],
            scratch_shapes=[pltpu.VMEM((D,D),BF),pltpu.VMEM((D,FF),BF),pltpu.VMEM((FF,D),BF),
                pltpu.VMEM((D,FF),F32),pltpu.VMEM((FF,D),F32),pltpu.VMEM((D,D),F32),
                pltpu.SemaphoreType.DMA((3+12*(ns-1),))]),
        out_shape=[S_((T,D),F32),S_((T,D),BF),S_((T,D),BF),S_((ns,rb,HC),BF),S_((ns,rb,HC),BF),S_((32,D),F32),S_((8,FF),F32)],
        compiler_params=pltpu.CompilerParams(dimension_semantics=("arbitrary",),vmem_limit_bytes=67043328),
        cost_estimate=cost(6*T*D*(D+2*FF),T*D*20+30*D*FF,2*T*FF),
        name="mid")(idx,tok,row,att,cot,vec,*own,*mine,*other)


def dw_kernel(idx_ref,nt_ref,d_ref,keep_ref,send_ref,sv_ref,acc,*,ns,wr):
    i=pl.program_id(0)
    c=idx_ref[0]
    @pl.when(i==0)
    def _():
        acc[...]=jnp.zeros_like(acc)
        sv_ref[...]=jnp.zeros_like(sv_ref)
    for w in range(3):
        acc[w]+=nn(nt_ref[...],d_ref[w])
    sv_ref[0:8,:]+=sum8(d_ref[0].astype(F32))
    sv_ref[8:16,:]+=sum8(d_ref[2].astype(F32))
    @pl.when(i==pl.num_programs(0)-1)
    def _():
        for ref,base,odd in ((keep_ref,1+ns,0),(send_ref,1+2*ns,1)):
            for ch in (0,1):
                @pl.when(c==(ch+odd)%2)
                def _():
                    def body(j,carry):
                        rw=pl.ds(pl.multiple_of(idx_ref[base+j]*wr,8),wr)
                        for w in range(3):
                            ref[j,w*wr:(w+1)*wr,:]=acc[w,rw,ch*HC:(ch+1)*HC].astype(BF)
                        return carry
                    lax.fori_loop(0,ns,body,0)


def dw(idx,n1t,d,ns,tb=512):
    T=n1t.shape[1]
    wr=D//ns
    return pl.pallas_call(
        functools.partial(dw_kernel,ns=ns,wr=wr),
        grid_spec=pltpu.PrefetchScalarGridSpec(
            num_scalar_prefetch=1,grid=(T//tb,),
            in_specs=[pl.BlockSpec((D,tb),lambda i,*_:(0,i)),pl.BlockSpec((3,tb,D),lambda i,*_:(0,i,0))],
            out_specs=[full(ns,3*wr,HC),full(ns,3*wr,HC),full(16,D)],
            scratch_shapes=[pltpu.VMEM((3,D,D),F32)]),
        out_shape=[S_((ns,3*wr,HC),BF)]*2+[S_((16,D),F32)],
        compiler_params=pltpu.CompilerParams(dimension_semantics=("arbitrary",)),
        cost_estimate=cost(6*T*D*D,T*D*8+12*D*D),
        name="dw")(idx,n1t,d)


def dx_kernel(tok_ref,row_ref,d_ref,gm_ref,w_ref,vec_ref,gt_ref,sv_ref,ts_ref,*,per):
    i=pl.program_id(0)
    @pl.when(i==0)
    def _():
        sv_ref[...]=jnp.zeros_like(sv_ref)
    @pl.when(i%per==0)
    def _():
        ts_ref[...]=jnp.zeros_like(ts_ref)
    gn=nt(d_ref[0],w_ref[0])+nt(d_ref[1],w_ref[1])+nt(d_ref[2],w_ref[2])
    xhat,r=norm(tok_ref[...]+row_ref[0])
    e=gn*vec_ref[0:1,:]
    c1=jnp.mean(e,axis=1,keepdims=True)
    c2=jnp.mean(e*xhat,axis=1,keepdims=True)
    gt=gm_ref[...].astype(F32)+r*(e-c1-xhat*c2)
    gt_ref[...]=gt
    sv_ref[0:8,:]+=sum8(gn*xhat)
    sv_ref[8:16,:]+=sum8(gn)
    ts_ref[0]+=sum8(gt)


def dx(tok,row,d,gm,w,vec,tb=512):
    T=tok.shape[0]
    per=L//tb
    blk=pl.BlockSpec((tb,D),lambda i:(i,0))
    return pl.pallas_call(
        functools.partial(dx_kernel,per=per),grid=(T//tb,),
        in_specs=[blk,pl.BlockSpec((1,1,D),lambda i:(i//per,0,0)),pl.BlockSpec((3,tb,D),lambda i:(0,i,0)),blk,full(3,D,D),full(VR,D)],
        out_specs=[blk,full(16,D),pl.BlockSpec((1,8,D),lambda i:(i//per,0,0))],
        out_shape=[S_((T,D),F32),S_((16,D),F32),S_((T//L,8,D),F32)],
        compiler_params=pltpu.CompilerParams(dimension_semantics=("arbitrary",)),
        cost_estimate=cost(6*T*D*D,T*D*16+6*D*D),
        name="dx")(tok,row,d,gm,w,vec)


def rows8(x):
    return jnp.sum(x,axis=0,keepdims=True)


def sums_kernel(id_ref,sv1_ref,svq_ref,sv2_ref,sub_ref,ts_ref,out_ref):
    src=[sv1_ref[0:8],sv1_ref[8:16],svq_ref[0:8],svq_ref[8:16]]+[sv2_ref[8*i:8*i+8] for i in range(4)]
    src+=[sub_ref[:,i*D:(i+1)*D] for i in range(FF//D)]
    rows=[rows8(x) for x in src]+[id_ref[0:1],id_ref[1:2]]+[rows8(ts_ref[i]) for i in range(ts_ref.shape[0])]
    out_ref[...]=jnp.concatenate(rows,axis=0).astype(BF)


def sums(ids,sv1,svq,sv2,sub,ts):
    vm=pl.BlockSpec(memory_space=pltpu.VMEM)
    return pl.pallas_call(sums_kernel,in_specs=[vm]*6,out_specs=vm,
        out_shape=S_((VR+ts.shape[0],D),BF),cost_estimate=cost(0,10**6),name="sums")(ids,sv1,svq,sv2,sub,ts)


def group_kernel(idx_ref,*refs,ns,nseq):
    out_ref,acc=refs[ns:]
    tot=refs[0][0:VR].astype(F32)
    for j in range(1,ns):
        tot=tot+refs[j][0:VR].astype(F32)
    for j in range(ns):
        acc[idx_ref[1+j]]=refs[j][VR:VR+nseq].astype(F32)
    out_ref[...]=jnp.concatenate([tot]+[acc[j] for j in range(ns)],axis=0).astype(BF)


def group(idx,pays,nseq):
    ns=len(pays)
    vm=pl.BlockSpec(memory_space=pltpu.VMEM)
    return pl.pallas_call(functools.partial(group_kernel,ns=ns,nseq=nseq),
        in_specs=[pl.BlockSpec(memory_space=pltpu.SMEM)]+[vm]*ns,out_specs=vm,
        out_shape=S_((VR+ns*nseq,D),BF),scratch_shapes=[pltpu.VMEM((ns,nseq,D),F32)],
        cost_estimate=cost(0,10**6),name="group")(idx,*pays)


def table_kernel(me_ref,*refs,nr,rows,own):
    sum_ref,tab_ref,acc,allr=refs[nr:]
    r0=me_ref[0]
    for j in range(nr):
        acc[r0^j]=refs[j][...].astype(F32)
    tot=acc[0,0:VR]
    for r in range(1,nr):
        tot=tot+acc[r,0:VR]
    sum_ref[...]=tot
    for r in range(nr):
        allr[r*rows:(r+1)*rows,:]=acc[r,VR:VR+rows]
    n=nr*rows
    ids=tot[NV:NV+1,0:n]*32.0+tot[NV+1:NV+2,0:n]
    line=lax.broadcasted_iota(jnp.int32,(own,n),0)+me_ref[1]*own
    hit=jnp.where(line==ids.astype(jnp.int32),1.0,0.0).astype(BF)
    tab_ref[...]=nn(hit,allr[...].astype(BF))


def table(me,pays,own):
    nr=len(pays)
    rows=pays[0].shape[0]-VR
    vm=pl.BlockSpec(memory_space=pltpu.VMEM)
    return pl.pallas_call(functools.partial(table_kernel,nr=nr,rows=rows,own=own),
        in_specs=[pl.BlockSpec(memory_space=pltpu.SMEM)]+[vm]*nr,out_specs=[vm,vm],
        out_shape=[S_((VR,D),F32),S_((own,D),F32)],
        scratch_shapes=[pltpu.VMEM((nr,VR+rows,D),F32),pltpu.VMEM((nr*rows,D),F32)],
        cost_estimate=cost(0,4*10**6),name="table")(me,*pays)


def unpack_kernel(idx_ref,a_ref,b_ref,*outs,parts):
    for ch in (0,1):
        @pl.when(idx_ref[0]==ch)
        def _():
            for h,ref in enumerate((a_ref,b_ref) if ch==0 else (b_ref,a_ref)):
                r0=0
                for out,(nr,nb) in zip(outs,parts):
                    for b in range(nb):
                        out[:,(h*nb+b)*HC:(h*nb+b+1)*HC]=ref[r0:r0+nr,:].astype(F32)
                        r0+=nr


def unpack(idx,a,b,parts):
    vm=pl.BlockSpec(memory_space=pltpu.VMEM)
    return pl.pallas_call(functools.partial(unpack_kernel,parts=parts),
        in_specs=[pl.BlockSpec(memory_space=pltpu.SMEM),vm,vm],out_specs=[vm]*len(parts),
        out_shape=[S_((nr,2*nb*HC),F32) for nr,nb in parts],
        cost_estimate=cost(0,12*a.shape[0]*HC),name="unpack")(idx,a,b)


def small_kernel(me_ref,ts_ref,*refs,w,fr,nseq):
    vecs=refs[:9]
    out_ref,id_ref=refs[9:]
    def spread(rows,width,at):
        n=rows[0].shape[1]
        y=jnp.concatenate(rows+[jnp.zeros((8-len(rows),n),F32)]*(len(rows)<8),axis=0)
        y=jnp.concatenate([y,jnp.zeros((8,width-n),F32)],axis=1)
        return pltpu.roll(y,at,1)
    row=lambda ref: ref[...].astype(F32).reshape(1,ref.shape[0])
    v=spread([row(r) for r in vecs[:8]],D,me_ref[1]*w)
    u=spread([row(vecs[8])],FF,me_ref[1]*fr)
    lane=lax.broadcasted_iota(jnp.int32,(1,D),1)
    def steps(at,high):
        y=jnp.zeros((1,D),jnp.int32)
        for i in range(nseq):
            t=ts_ref[i]
            y=jnp.where(lane==at*nseq+i,t//32 if high else t%32,y)
        return y.astype(F32)
    id_ref[...]=jnp.concatenate([steps(me_ref[2],True),steps(me_ref[2],False)],axis=0)
    out_ref[...]=jnp.concatenate([v]+[u[0:1,i*D:(i+1)*D] for i in range(FF//D)]+[steps(me_ref[1],True),steps(me_ref[1],False)],axis=0).astype(BF)


def small_rows(me,time_steps,vecs):
    vm=pl.BlockSpec(memory_space=pltpu.VMEM)
    sm=pl.BlockSpec(memory_space=pltpu.SMEM)
    return pl.pallas_call(functools.partial(small_kernel,w=vecs[0].shape[0],fr=vecs[8].shape[0],nseq=time_steps.shape[0]),
        in_specs=[sm,sm]+[vm]*9,out_specs=[vm,vm],
        out_shape=[S_((VR,D),BF),S_((2,D),F32)],cost_estimate=cost(0,10**6),name="small")(me,time_steps,*vecs)


class Ring:
    def __init__(self,rep,shard):
        self.R,self.S=rep,shard
        self.nb=shard.bit_length()-1
        self.Z=rep//2
        r=lax.axis_index("rep")
        self.s=lax.axis_index("shard")
        self.c=r%2
        self.z=r//2

    def move(self,x,to):
        pairs=[]
        for r in range(self.R):
            for s in range(self.S):
                r2,s2=to(r,s)
                pairs.append((r*self.S+s,r2*self.S+s2))
        return lax.ppermute(x,("rep","shard"),pairs)

    def order(self,c,t):
        return (t+c*(self.nb//2))%self.nb

    def mask(self,c,j):
        m=0
        for t in range(self.nb):
            if j>>t&1:
                m|=1<<self.order(c,t)
        return m

    def step(self,x,t):
        return self.move(x,lambda r,s:(r,s^(1<<self.order(r%2,t))))

    def direct(self,x,j):
        return self.move(x,lambda r,s:(r,s^j))

    def core(self,x):
        return self.move(x,lambda r,s:(r^1,s))

    def plane(self,x,j):
        return self.move(x,lambda r,s:(r^(2*j),s))

    def index(self):
        m=[[self.mask(c,j) for j in range(self.S)] for c in (0,1)]
        base=list(range(self.S))
        t=jnp.where(self.c==0,jnp.array([0]+base+m[0]+m[1],jnp.int32),jnp.array([0]+base+m[1]+m[0],jnp.int32))
        head=jnp.arange(1+3*self.S)==0
        return jnp.where(head,self.c,t^self.s).astype(jnp.int32)


def tie(*xs):
    return lax.optimization_barrier(xs)


def add(*terms):
    y=terms[0].astype(F32)
    for x in terms[1:]:
        y=y+x.astype(F32)
    return y.astype(BF)


def upper(terms,n):
    return add(*[x[n:] for x in terms]),[x[:n] for x in terms]


def plane_rows(g,x):
    x=x.reshape(g.Z,-1,HC)
    return [lax.dynamic_index_in_dim(x,g.z^j,0,keepdims=False) for j in range(1,g.Z)]


def plane_send(g,rows):
    return [g.plane(x,j) for j,x in enumerate(rows,1)]


def plane_sum(g,x,parts):
    mine=lax.dynamic_index_in_dim(x.reshape(g.Z,-1,HC),g.z,0,keepdims=False).astype(F32)
    for p in parts:
        mine=mine+p.astype(F32)
    return mine.astype(BF)


def plane_join(g,mine,parts):
    out=jnp.zeros((g.Z,)+mine.shape,BF)
    for j,p in enumerate([mine]+parts):
        out=lax.dynamic_update_index_in_dim(out,p,g.z^j,0)
    return out.reshape(-1,HC)


def local(tokens,segments,time_steps,time_table,ln1_gain,ln1_bias,q_weight,q_bias,k_weight,v_weight,v_bias,o_weight,o_bias,ln2_gain,ln2_bias,up_weight,up_bias,down_weight,down_bias,cotangent):
    nseq=tokens.shape[0]
    T=nseq*L
    g=Ring(lax.axis_size("rep"),lax.axis_size("shard"))
    S=g.S
    w=ln1_gain.shape[0]
    fr=down_weight.shape[0]
    own=time_table.shape[0]
    idx=g.index()
    r=g.z*2+g.c
    me=jnp.stack([r,g.s,r*S+g.s]).astype(jnp.int32)
    small,ids=small_rows(me,time_steps,(ln1_gain,ln1_bias,q_bias,v_bias,o_bias,ln2_gain,ln2_bias,down_bias,up_bias))
    small,segments,o_weight_,q_weight_=tie(small,segments,o_weight,q_weight)
    pack_a=pack(pack_a_kernel,idx,(q_weight_,k_weight,v_weight),"pack_a")
    mine_a=[g.direct(pack_a,j) for j in range(1,S)]
    segments,pack_a=tie(segments,pack_a)
    vec=small.astype(F32)
    for j in reversed(range(1,S)):
        vec=vec+g.direct(small,j).astype(F32)
    steps=vec[NV,:S*nseq]*32.0+vec[NV+1,:S*nseq]
    hit=steps.astype(jnp.int32)[:,None]==jnp.arange(own)[None,:]+g.s*own
    rows=jnp.dot(hit.astype(BF),time_table,preferred_element_type=F32).astype(BF).reshape(S,nseq,D)
    pick=lambda j: lax.dynamic_index_in_dim(rows,g.s^j,0,keepdims=False)
    picks=[pick(j) for j in range(S)]
    picks[0],*mine_a=tie(picks[0],*mine_a)
    row=picks[0].astype(F32)
    for j in range(1,S):
        row=row+g.direct(picks[j],j).astype(F32)
    row=row.reshape(nseq,1,D)
    pack_b=pack(pack_b_kernel,idx,(o_weight_,up_weight,down_weight),"pack_b")
    tok=tokens.reshape(T,D)
    cot=cotangent.reshape(T,D)
    fq,fk=seg_features(segments.reshape(T))
    fq,fk,pack_b,row,*mine_a=tie(fq,fk,pack_b,row,*mine_a)
    other_a=[g.core(x) for x in mine_a]
    mine_b=[pack_b]
    first=[g.step(pack_b,t) for t in range(g.nb)]
    q,k,v,n1t,wqkv=qkv(idx,tok,row,vec,(q_weight,k_weight,v_weight),mine_a,other_a)
    fwd=attn_fwd(q,k,v,fq,fk,(),0,3*nseq//2)
    o1,fx1,*first=tie(*fwd,*first)
    for t in range(g.nb):
        mine_b=mine_b+[first[t]]+[g.step(x,t) for x in mine_b[1:]]
    direct=[1<<t for t in range(g.nb)]
    other_b=[None]+[g.core(x) if j in direct else None for j,x in enumerate(mine_b[1:],1)]
    fwd=attn_fwd(q,k,v,fq,fk,(o1,fx1),3*nseq//2,3*nseq)
    late=[j for j in range(1,S) if j not in direct]
    o1,fx1,*got=tie(*fwd,*[mine_b[j] for j in late])
    for j,x in zip(late,got):
        mine_b[j]=x
        other_b[j]=g.core(x)
    att,fx=attn_fwd(q,k,v,fq,fk,(o1,fx1),9*nseq//2,6*nseq-9*nseq//2)
    res,gm,ga,keep_b,send_b,sv2,sub=mid(idx,tok,row,att,cot,vec,(o_weight,up_weight,down_weight),mine_b[1:],other_b[1:])
    cuts=[0,nseq,nseq+5*nseq//2,5*nseq,6*nseq]
    call=lambda prev,i: attn_bwd(q,k,v,fx,fk,att,ga,prev,cuts[i],cuts[i+1]-cuts[i])
    got=g.core(send_b)
    d=call((),0)
    d,got=tie(d,got)
    n=S
    x=[keep_b]
    for t in reversed(range(g.nb)):
        n//=2
        up,x=upper(x+[got],n)
        d,up=tie(d,up)
        got=g.step(up,t)
        i=g.nb-t
        if i<=2:
            d=call((d,),i)
            d,got=tie(d,got)
    xb=add(*[y[0] for y in x],got[0])
    d,xb,*rows_b=tie(d,xb,*plane_rows(g,xb))
    parts=plane_send(g,rows_b)
    d=call((d,),3)
    keep_a,send_a,svq=dw(idx,n1t,d,S)
    keep_a,send_a,*parts=tie(keep_a,send_a,*parts)
    got=g.core(send_a)
    mine=plane_sum(g,xb,parts)
    back=[g.plane(mine,j) for j in range(1,g.Z)]
    gm,mine_,got=tie(gm,mine,got)
    up,x=upper([keep_a,got],S//2)
    gm,up=tie(gm,up)
    got=g.step(up,g.nb-1)
    gt,sv1,ts=dx(tok,row,d,gm,wqkv,vec)
    ts,got=tie(ts,got)
    n=S//2
    for t in reversed(range(g.nb-1)):
        n//=2
        up,x=upper(x+[got],n)
        ts,up=tie(ts,up)
        got=g.step(up,t)
    pay=sums(ids,sv1,svq,sv2,sub,ts)
    pays=[pay]+[g.direct(pay,j) for j in range(1,S)]
    pays[-1],got=tie(pays[-1],got)
    xa=add(*[y[0] for y in x],got[0])
    rows_a=plane_rows(g,xa)
    *pays,rows_a[0]=tie(*pays,rows_a[0])
    parts_a=plane_send(g,rows_a)
    pay=group(idx,pays,nseq)
    out_b=plane_join(g,mine_,back)
    out_b,pay,*parts_a=tie(out_b,pay,*parts_a)
    other_b=g.core(out_b)
    mine=plane_sum(g,xa,parts_a)
    pay,mine=tie(pay,mine)
    back_a=[g.plane(mine,j) for j in range(1,g.Z)]
    pays=[pay]+[g.move(pay,lambda r,s,j=j:(r^j,s)) for j in range(1,g.R)]
    go,gup,gdn=unpack(idx,out_b,other_b,((w,1),(w,4),(fr,1)))
    gup,*both=tie(gup,*back_a,*pays)
    back_a,pays=both[:g.Z-1],both[g.Z-1:]
    out_a=plane_join(g,mine,back_a)
    other_a=g.core(out_a)
    vsum,gtab=table(me,pays,own)
    vsum,other_a=tie(vsum,other_a)
    gq,gk,gv=unpack(idx,out_a,other_a,((w,1),)*3)
    sums8=lax.dynamic_slice_in_dim(vsum[:8],g.s*w,w,1)
    subs=lax.dynamic_slice_in_dim(vsum[8:NV].reshape(FF),g.s*up_bias.shape[0],up_bias.shape[0],0)
    return (res.reshape(tokens.shape),gt.reshape(tokens.shape),gtab,sums8[0],sums8[1],gq,sums8[2],gk,gv,sums8[3],go,sums8[4],sums8[5],sums8[6],gup,subs,gdn,sums8[7])


def solution(mesh):
    b=("rep","shard")
    s=P("shard")
    m=P("shard",None)
    t=P(b,None,None)
    return jax.shard_map(local,mesh=mesh,
        in_specs=(t,P(b,None),P(b),m,s,s,m,s,m,m,s,m,s,s,s,m,s,m,s,t),
        out_specs=(t,t,m,s,s,m,s,m,m,s,m,s,s,s,m,s,m,s),check_vma=False)
```

```python
import functools
import math

import jax
import jax.numpy as jnp
from jax import lax
from jax.experimental import pallas as pl
from jax.experimental.pallas import tpu as pltpu
from jax.sharding import PartitionSpec as P

NEG=-1e30
EPS=1e-5
L=1024
D=768
FF=3072
HC=D//2
BF=jnp.bfloat16
F32=jnp.float32
LOG2E=math.log2(math.e)
LN2=math.log(2.0)
QS=0.125*LOG2E
VR=14
NV=12
ANY=pl.BlockSpec(memory_space=pl.ANY)
S_=jax.ShapeDtypeStruct


def nt(a,b):
    return lax.dot_general(a,b,(((1,),(1,)),((),())),preferred_element_type=F32)


def nn(a,b):
    return lax.dot_general(a,b,(((1,),(0,)),((),())),preferred_element_type=F32)


def tn(a,b):
    return lax.dot_general(a,b,(((0,),(0,)),((),())),preferred_element_type=F32)


def full(*s):
    return pl.BlockSpec(s,lambda i,*_:(0,)*len(s),pipeline_mode=pl.Buffered(1))


def norm(x):
    mean=jnp.mean(x,axis=1,keepdims=True)
    off=x-mean
    var=jnp.mean(off*off,axis=1,keepdims=True)
    r=lax.rsqrt(var+EPS)
    return off*r,r


def sum8(x):
    return jnp.sum(x.reshape(x.shape[0]//8,8,x.shape[1]),axis=0)


def cost(flops,nbytes,trans=0):
    return pl.CostEstimate(flops=int(flops)//10,bytes_accessed=int(nbytes)//10,transcendentals=int(trans)//10)


def seg_features(seg):
    lane=jnp.arange(128)%64
    hit=seg[:,None]==lane[None,:]
    first=(lane<4)[None]
    fq=jnp.where(first&hit,1.0,0.0).astype(BF)
    fk=jnp.where(first,jnp.where(hit,0.0,NEG),jnp.where((lane<7)[None],1.0,0.0)).astype(BF)
    return fq,fk


def qkv_kernel(idx_ref,*refs,ns,wr):
    tok_ref,row_ref,vec_ref=refs[:3]
    own=refs[3:6]
    mine=refs[6:6+ns-1]
    other=refs[6+ns-1:6+2*(ns-1)]
    hi=6+2*(ns-1)
    q_ref,k_ref,v_ref,nt_ref,w_ref,sem=refs[hi:hi+6]
    @pl.when(pl.program_id(0)==0)
    def _():
        c=idx_ref[0]
        cps=[]
        def put(src,w,sh,c0,nc):
            dst=w_ref.at[w,pl.ds(pl.multiple_of(sh*wr,16),wr),pl.ds(c0,nc)]
            cp=pltpu.make_async_copy(src,dst,sem.at[len(cps)])
            cp.start()
            cps.append(cp)
        for w in range(3):
            put(own[w],w,idx_ref[1],0,D)
        for j in range(1,ns):
            for w in range(3):
                put(mine[j-1].at[pl.ds(w*wr,wr)],w,idx_ref[1+j],pl.multiple_of(c*HC,128),HC)
                put(other[j-1].at[pl.ds(w*wr,wr)],w,idx_ref[1+j],pl.multiple_of((1-c)*HC,128),HC)
        for cp in cps:
            cp.wait()
    xhat,_=norm(tok_ref[...]+row_ref[0])
    n1=(xhat*vec_ref[0:1,:]+vec_ref[1:2,:]).astype(BF)
    q_ref[...]=((nn(n1,w_ref[0])+vec_ref[2:3,:])*QS).astype(BF)
    k_ref[...]=nn(n1,w_ref[1]).astype(BF)
    v_ref[...]=(nn(n1,w_ref[2])+vec_ref[3:4,:]).astype(BF)
    nt_ref[...]=n1.T


def qkv(idx,tok,row,vec,own,mine,other,tb=512):
    T=tok.shape[0]
    per=L//tb
    ns=len(mine)+1
    wr=own[0].shape[0]
    blk=pl.BlockSpec((tb,D),lambda i,*_:(i,0))
    return pl.pallas_call(
        functools.partial(qkv_kernel,ns=ns,wr=wr),
        grid_spec=pltpu.PrefetchScalarGridSpec(
            num_scalar_prefetch=1,grid=(T//tb,),
            in_specs=[blk,pl.BlockSpec((1,1,D),lambda i,*_:(i//per,0,0)),full(VR,D)]+[ANY]*(3+2*(ns-1)),
            out_specs=[blk]*3+[pl.BlockSpec((D,tb),lambda i,*_:(0,i)),full(3,D,D)],
            scratch_shapes=[pltpu.SemaphoreType.DMA((3+6*(ns-1),))]),
        out_shape=[S_((T,D),BF)]*3+[S_((D,T),BF),S_((3,D,D),BF)],
        compiler_params=pltpu.CompilerParams(dimension_semantics=("arbitrary",)),
        cost_estimate=cost(6*T*D*D,T*D*10+9*D*D),
        name="qkv")(idx,tok,row,vec,*own,*mine,*other)


def pack_a_kernel(idx_ref,q_ref,k_ref,v_ref,out_ref):
    wr=q_ref.shape[0]
    for ch in (0,1):
        @pl.when(idx_ref[0]==ch)
        def _():
            for w,ref in enumerate((q_ref,k_ref,v_ref)):
                out_ref[w*wr:(w+1)*wr,:]=ref[:,ch*HC:(ch+1)*HC]


def pack_b_kernel(idx_ref,o_ref,u_ref,d_ref,out_ref):
    wr=o_ref.shape[0]
    for ch in (0,1):
        @pl.when(idx_ref[0]==ch)
        def _():
            out_ref[0:wr,:]=o_ref[:,ch*HC:(ch+1)*HC]
            for b in range(4):
                out_ref[wr+b*wr:2*wr+b*wr,:]=u_ref[:,(ch*4+b)*HC:(ch*4+b+1)*HC]
            out_ref[5*wr:,:]=d_ref[:,ch*HC:(ch+1)*HC]


def pack(kernel,idx,ws,name):
    rows=sum(x.shape[0]*x.shape[1]//D for x in ws)
    vm=pl.BlockSpec(memory_space=pltpu.VMEM)
    return pl.pallas_call(kernel,in_specs=[pl.BlockSpec(memory_space=pltpu.SMEM)]+[vm]*3,out_specs=vm,
        out_shape=S_((rows,HC),BF),cost_estimate=cost(0,4*rows*D),name=name)(idx,*ws)


MAIN=800
ROWS=816
LANES=896
REST=768


def windows(s):
    s16=(s//16)*16
    return pl.multiple_of(jnp.minimum(s16,L-ROWS),16),pl.multiple_of(jnp.minimum(s16,L-LANES),16)


def fwd_kernel(s_ref,q_ref,k_ref,v_ref,fq_ref,fk_ref,*refs):
    o_ref,fx_ref=refs[-2:]
    s0=s_ref[1+(s_ref[0]+pl.program_id(0))//(D//128)]
    wr,wl=windows(s0)
    lane=lax.broadcasted_iota(jnp.int32,(1,128),1)
    lo=lane<64
    l6=lane&63
    rest_row=lax.broadcasted_iota(jnp.int32,(256,1),0)
    ahead=rest_row<s0
    qb=ROWS//3
    rest=lambda ref: jnp.where(ahead,ref[0:256,:],ref[REST:L,:])
    main=lambda ref: ref[pl.ds(wl,LANES),:]
    one=jnp.where(l6==0,1.0,0.0).astype(BF)
    kv=[]
    for take in (rest,main):
        k=take(k_ref)
        v=take(v_ref)
        fk=take(fk_ref)
        kv.append([(jnp.where(own,k,fk),jnp.where(own,v,one)) for own in (lo,~lo)])
    qf=[(rest(q_ref),rest(fq_ref))]
    for b in range(3):
        rows=pl.ds(pl.multiple_of(wr+b*qb,16),qb)
        qf.append((q_ref[rows,:],fq_ref[rows,:]))
    units=[(b,h) for b in range(4) for h in (0,1)]
    def score(b,h):
        return nt(jnp.where(lo if h==0 else ~lo,*qf[b]),kv[min(b,1)][h][0])
    pend=[score(*u) for u in units[:3]]
    accs=[]
    ls=[]
    for i,(b,h) in enumerate(units):
        s=pend.pop(0)
        if i+3<len(units):
            pend.append(score(*units[i+3]))
        m=jnp.max(s,axis=1,keepdims=True)
        p=jnp.exp2(s-m).astype(BF)
        acc=nn(p,kv[min(b,1)][h][1])
        l=acc[:,64:65] if h==0 else acc[:,0:1]
        accs.append(acc*(1.0/l))
        ls.append(-(m+jnp.log2(l)))
        if h==1:
            o=jnp.where(lo,accs[0],accs[1]).astype(BF)
            nl=jnp.where(lo,ls[1],ls[0])
            hi=nl.astype(BF).astype(F32)
            r1=nl-hi
            mid=r1.astype(BF).astype(F32)
            r2=r1-mid
            fx=jnp.where(l6==4,hi,jnp.where(l6==5,mid,jnp.where(l6==6,r2,qf[b][1].astype(F32)))).astype(BF)
            if b==0:
                o_ref[0:256,:]=o
                fx_ref[0:256,:]=fx
                o_ref[REST:L,:]=o
                fx_ref[REST:L,:]=fx
            else:
                at=wr+(b-1)*qb
                rows=pl.ds(pl.multiple_of(at,16),qb)
                pos=lax.broadcasted_iota(jnp.int32,(qb,1),0)+(at-s0)
                inside=(pos>=0)&(pos<MAIN)
                o_ref[rows,:]=jnp.where(inside,o,o_ref[rows,:])
                fx_ref[rows,:]=jnp.where(inside,fx,fx_ref[rows,:])
            accs=[]
            ls=[]


def attn_fwd(starts,q,k,v,fq,fk,prev,f0,n):
    T=q.shape[0]
    np_=D//128
    blk=pl.BlockSpec((L,128),lambda i,s:((s[0]+i)//np_,(s[0]+i)%np_))
    fb=pl.BlockSpec((L,128),lambda i,s:((s[0]+i)//np_,0))
    starts=jnp.concatenate([jnp.array([f0],jnp.int32),starts])
    prev=list(prev)
    return pl.pallas_call(
        fwd_kernel,
        grid_spec=pltpu.PrefetchScalarGridSpec(
            num_scalar_prefetch=1,grid=(n,),
            in_specs=[blk,blk,blk,fb,fb]+[ANY]*len(prev),out_specs=[blk,blk]),
        out_shape=[S_((T,D),BF)]*2,
        input_output_aliases={6+i:i for i in range(len(prev))},
        compiler_params=pltpu.CompilerParams(dimension_semantics=("arbitrary",)),
        cost_estimate=cost(n*2*4*L*L*256,n*L*128*14,n*2*L*L),
        name="attn_fwd")(starts,q,k,v,fq,fk,*prev)


def bwd_kernel(s_ref,q_ref,k_ref,v_ref,fx_ref,fk_ref,o_ref,do_ref,*refs):
    out_ref=refs[-1]
    s0=s_ref[1+(s_ref[0]+pl.program_id(0))//(D//128)]
    wr,wl=windows(s0)
    lane=lax.broadcasted_iota(jnp.int32,(1,128),1)
    lo=lane<64
    l6=lane&63
    zero=jnp.zeros((),BF)
    ones2=jnp.where(l6<2,1.0,0.0).astype(BF)
    rest_row=lax.broadcasted_iota(jnp.int32,(256,1),0)
    ahead=rest_row<s0
    rest=lambda ref: jnp.where(ahead,ref[0:256,:],ref[REST:L,:])
    def block(take_k,nk,takes):
        k=take_k(k_ref)
        v=take_k(v_ref)
        fk=take_k(fk_ref)
        kx=[]
        vx=[]
        km=[]
        for own in (lo,~lo):
            kx.append(jnp.where(own,k,fk))
            vx.append(jnp.where(own,v,ones2))
            km.append(jnp.where(own,k,zero))
        dv=jnp.zeros((nk,128),F32)
        dk=jnp.zeros((nk,128),F32)
        dqs=[]
        for take in takes:
            q=take(q_ref)
            fx=take(fx_ref)
            do=take(do_ref)
            prod=do.astype(F32)*take(o_ref).astype(F32)
            d0=-jnp.sum(jnp.where(lo,prod,0.0),axis=1,keepdims=True)
            d1=-jnp.sum(jnp.where(lo,0.0,prod),axis=1,keepdims=True)
            nd=jnp.where(lo,d1,d0)
            hi=nd.astype(BF).astype(F32)
            fd=jnp.where(l6==0,hi,jnp.where(l6==1,nd-hi,0.0)).astype(BF)
            dq=jnp.zeros(q.shape,F32)
            for h,own in enumerate((lo,~lo)):
                p=jnp.exp2(nt(kx[h],jnp.where(own,q,fx)))
                dpt=nt(vx[h],jnp.where(own,do,fd))
                pb=p.astype(BF)
                ds=(p*dpt).astype(BF)
                dv=dv+nn(pb,jnp.where(own,do,zero))
                dk=dk+nn(ds,jnp.where(own,q,zero))
                dq=dq+tn(ds,km[h])
            dqs.append((dq*0.125).astype(BF))
        return dqs,(dk*LN2).astype(BF),dv.astype(BF)
    dqs,dk,dv=block(rest,256,[rest])
    for w,x in enumerate((dqs[0],dk,dv)):
        out_ref[w,0:256,:]=x
        out_ref[w,REST:L,:]=x
    at=lambda start,n: pl.ds(pl.multiple_of(start,16),n)
    cuts=[(0,256),(256,256),(512,256),(768,128)]
    dqs,dk,dv=block(lambda ref: ref[at(wr,ROWS),:],ROWS,[lambda ref,c=c: ref[at(wl+c[0],c[1]),:] for c in cuts])
    def put(w,start,x):
        n=x.shape[0]
        pos=lax.broadcasted_iota(jnp.int32,(n,1),0)+(start-s0)
        out_ref[w,at(start,n),:]=jnp.where((pos>=0)&(pos<MAIN),x,out_ref[w,at(start,n),:])
    for c,x in zip(cuts,dqs):
        put(0,wl+c[0],x)
    put(1,wr,dk)
    put(2,wr,dv)


def attn_bwd(starts,q,k,v,fx,fk,o,do,prev,f0,n):
    T=q.shape[0]
    np_=D//128
    blk=pl.BlockSpec((L,128),lambda i,s:((s[0]+i)//np_,(s[0]+i)%np_))
    fb=pl.BlockSpec((L,128),lambda i,s:((s[0]+i)//np_,0))
    starts=jnp.concatenate([jnp.array([f0],jnp.int32),starts])
    prev=list(prev)
    return pl.pallas_call(
        bwd_kernel,
        grid_spec=pltpu.PrefetchScalarGridSpec(
            num_scalar_prefetch=1,grid=(n,),
            in_specs=[blk,blk,blk,blk,fb,blk,blk]+[ANY]*len(prev),
            out_specs=pl.BlockSpec((3,L,128),lambda i,s:(0,(s[0]+i)//np_,(s[0]+i)%np_))),
        out_shape=S_((3,T,D),BF),
        input_output_aliases={8+i:i for i in range(len(prev))},
        compiler_params=pltpu.CompilerParams(dimension_semantics=("arbitrary",)),
        cost_estimate=cost(n*2*10*L*L*256,n*L*128*20,n*2*L*L),
        name="attn_bwd")(starts,q,k,v,fx,fk,o,do,*prev)


def mid_kernel(idx_ref,*refs,tb,fc,ns,wr,fr):
    tok_ref,row_ref,att_ref,cot_ref,vec_ref=refs[:5]
    own=refs[5:8]
    mine=refs[8:8+ns-1]
    other=refs[8+ns-1:8+2*(ns-1)]
    b0=8+2*(ns-1)
    res_ref,gm_ref,ga_ref,keep_ref,send_ref,sv_ref,sub_ref,ow,up,dn,aup,adn,aow,sem=refs[b0:]
    i=pl.program_id(0)
    n=pl.num_programs(0)
    c=idx_ref[0]
    def copies():
        cps=[]
        def put(src,dst):
            cps.append(pltpu.make_async_copy(src,dst,sem.at[len(cps)]))
        r16=lambda sh,m: pl.ds(pl.multiple_of(sh*m,16),m)
        sh=idx_ref[1+ns]
        put(own[0],ow.at[r16(sh,wr)])
        put(own[1],up.at[r16(sh,wr)])
        put(own[2],dn.at[r16(sh,fr)])
        for j in range(1,ns):
            for src,sh,cc in ((mine[j-1],idx_ref[1+ns+j],c),(other[j-1],idx_ref[1+2*ns+j],1-c)):
                cd=pl.ds(pl.multiple_of(cc*HC,128),HC)
                put(src.at[pl.ds(0,wr)],ow.at[r16(sh,wr),cd])
                for b in range(4):
                    put(src.at[pl.ds(wr+b*wr,wr)],up.at[r16(sh,wr),pl.ds(pl.multiple_of(cc*4*HC+b*HC,128),HC)])
                put(src.at[pl.ds(5*wr,fr)],dn.at[r16(sh,fr),cd])
        return cps
    @pl.when(i==0)
    def _():
        cps=copies()
        for cp in cps:
            cp.start()
        aup[...]=jnp.zeros_like(aup)
        adn[...]=jnp.zeros_like(adn)
        aow[...]=jnp.zeros_like(aow)
        sv_ref[...]=jnp.zeros_like(sv_ref)
        sub_ref[...]=jnp.zeros_like(sub_ref)
        for cp in cps:
            cp.wait()
    ob=vec_ref[4:5,:]
    g2=vec_ref[5:6,:]
    b2=vec_ref[6:7,:]
    db=vec_ref[7:8,:]
    att=att_ref[...]
    mixed=tok_ref[...]+row_ref[0]+nn(att,ow[...])+ob
    xhat,r=norm(mixed)
    n2=(xhat*g2+b2).astype(BF)
    n2t=n2.T
    cot=cot_ref[...]
    g=cot.astype(BF)
    res=mixed+db
    gn2=jnp.zeros((tb,D),F32)
    for j in range(FF//fc):
        cs=slice(j*fc,(j+1)*fc)
        pre=nn(n2,up[:,cs])+vec_ref[8+j:9+j,:]
        gact=nt(g,dn[cs,:])
        phi=0.5+0.5*lax.erf(pre*(2**-0.5))
        pdf=jnp.exp2(pre*pre*(-0.5*LOG2E))*(1.0/math.sqrt(2*math.pi))
        act=(pre*phi).astype(BF)
        gp=gact*(phi+pre*pdf)
        gpre=gp.astype(BF)
        sub_ref[:,cs]+=sum8(gp)
        res=res+nn(act,dn[cs,:])
        gn2=gn2+nt(gpre,up[:,cs])
        adn[cs,:]+=tn(act,g)
        aup[:,cs]+=nn(n2t,gpre)
    res_ref[...]=res
    e=gn2*g2
    c1=jnp.mean(e,axis=1,keepdims=True)
    c2=jnp.mean(e*xhat,axis=1,keepdims=True)
    gm=cot+r*(e-c1-xhat*c2)
    gml=gm.astype(BF)
    gm_ref[...]=gml
    ga_ref[...]=nt(gml,ow[...]).astype(BF)
    aow[...]+=tn(att,gml)
    sv_ref[0:8,:]+=sum8(gm)
    sv_ref[8:16,:]+=sum8(gn2*xhat)
    sv_ref[16:24,:]+=sum8(gn2)
    sv_ref[24:32,:]+=sum8(cot)
    @pl.when(i==n-1)
    def _():
        for ref,base,odd in ((keep_ref,1+ns,0),(send_ref,1+2*ns,1)):
            for ch in (0,1):
                @pl.when(c==(ch+odd)%2)
                def _():
                    def body(j,carry):
                        sh=idx_ref[base+j]
                        rw=pl.ds(pl.multiple_of(sh*wr,8),wr)
                        ref[j,0:wr,:]=aow[rw,ch*HC:(ch+1)*HC].astype(BF)
                        for b in range(4):
                            lo=(ch*4+b)*HC
                            ref[j,wr+b*wr:2*wr+b*wr,:]=aup[rw,lo:lo+HC].astype(BF)
                        ref[j,5*wr:5*wr+fr,:]=adn[pl.ds(pl.multiple_of(sh*fr,8),fr),ch*HC:(ch+1)*HC].astype(BF)
                        return carry
                    lax.fori_loop(0,ns,body,0)


def mid(idx,tok,row,att,cot,vec,own,mine,other,tb=256,fc=D):
    T=tok.shape[0]
    per=L//tb
    ns=len(mine)+1
    wr=own[0].shape[0]
    fr=own[2].shape[0]
    rb=5*wr+fr
    blk=pl.BlockSpec((tb,D),lambda i,*_:(i,0))
    return pl.pallas_call(
        functools.partial(mid_kernel,tb=tb,fc=fc,ns=ns,wr=wr,fr=fr),
        grid_spec=pltpu.PrefetchScalarGridSpec(
            num_scalar_prefetch=1,grid=(T//tb,),
            in_specs=[blk,pl.BlockSpec((1,1,D),lambda i,*_:(i//per,0,0)),blk,blk,full(VR,D)]+[ANY]*(3+2*(ns-1)),
            out_specs=[blk,blk,blk,full(ns,rb,HC),full(ns,rb,HC),full(32,D),full(8,FF)],
            scratch_shapes=[pltpu.VMEM((D,D),BF),pltpu.VMEM((D,FF),BF),pltpu.VMEM((FF,D),BF),
                pltpu.VMEM((D,FF),F32),pltpu.VMEM((FF,D),F32),pltpu.VMEM((D,D),F32),
                pltpu.SemaphoreType.DMA((3+12*(ns-1),))]),
        out_shape=[S_((T,D),F32),S_((T,D),BF),S_((T,D),BF),S_((ns,rb,HC),BF),S_((ns,rb,HC),BF),S_((32,D),F32),S_((8,FF),F32)],
        compiler_params=pltpu.CompilerParams(dimension_semantics=("arbitrary",),vmem_limit_bytes=67043328),
        cost_estimate=cost(6*T*D*(D+2*FF),T*D*20+30*D*FF,2*T*FF),
        name="mid")(idx,tok,row,att,cot,vec,*own,*mine,*other)


def dw_kernel(idx_ref,nt_ref,d_ref,keep_ref,send_ref,sv_ref,acc,*,ns,wr):
    i=pl.program_id(0)
    c=idx_ref[0]
    @pl.when(i==0)
    def _():
        acc[...]=jnp.zeros_like(acc)
        sv_ref[...]=jnp.zeros_like(sv_ref)
    for w in range(3):
        acc[w]+=nn(nt_ref[...],d_ref[w])
    sv_ref[0:8,:]+=sum8(d_ref[0].astype(F32))
    sv_ref[8:16,:]+=sum8(d_ref[2].astype(F32))
    @pl.when(i==pl.num_programs(0)-1)
    def _():
        for ref,base,odd in ((keep_ref,1+ns,0),(send_ref,1+2*ns,1)):
            for ch in (0,1):
                @pl.when(c==(ch+odd)%2)
                def _():
                    def body(j,carry):
                        rw=pl.ds(pl.multiple_of(idx_ref[base+j]*wr,8),wr)
                        for w in range(3):
                            ref[j,w*wr:(w+1)*wr,:]=acc[w,rw,ch*HC:(ch+1)*HC].astype(BF)
                        return carry
                    lax.fori_loop(0,ns,body,0)


def dw(idx,n1t,d,ns,tb=512):
    T=n1t.shape[1]
    wr=D//ns
    return pl.pallas_call(
        functools.partial(dw_kernel,ns=ns,wr=wr),
        grid_spec=pltpu.PrefetchScalarGridSpec(
            num_scalar_prefetch=1,grid=(T//tb,),
            in_specs=[pl.BlockSpec((D,tb),lambda i,*_:(0,i)),pl.BlockSpec((3,tb,D),lambda i,*_:(0,i,0))],
            out_specs=[full(ns,3*wr,HC),full(ns,3*wr,HC),full(16,D)],
            scratch_shapes=[pltpu.VMEM((3,D,D),F32)]),
        out_shape=[S_((ns,3*wr,HC),BF)]*2+[S_((16,D),F32)],
        compiler_params=pltpu.CompilerParams(dimension_semantics=("arbitrary",)),
        cost_estimate=cost(6*T*D*D,T*D*8+12*D*D),
        name="dw")(idx,n1t,d)


def dx_kernel(tok_ref,row_ref,d_ref,gm_ref,w_ref,vec_ref,gt_ref,sv_ref,ts_ref,*,per):
    i=pl.program_id(0)
    @pl.when(i==0)
    def _():
        sv_ref[...]=jnp.zeros_like(sv_ref)
    @pl.when(i%per==0)
    def _():
        ts_ref[...]=jnp.zeros_like(ts_ref)
    gn=nt(d_ref[0],w_ref[0])+nt(d_ref[1],w_ref[1])+nt(d_ref[2],w_ref[2])
    xhat,r=norm(tok_ref[...]+row_ref[0])
    e=gn*vec_ref[0:1,:]
    c1=jnp.mean(e,axis=1,keepdims=True)
    c2=jnp.mean(e*xhat,axis=1,keepdims=True)
    gt=gm_ref[...].astype(F32)+r*(e-c1-xhat*c2)
    gt_ref[...]=gt
    sv_ref[0:8,:]+=sum8(gn*xhat)
    sv_ref[8:16,:]+=sum8(gn)
    ts_ref[0]+=sum8(gt)


def dx(tok,row,d,gm,w,vec,tb=512):
    T=tok.shape[0]
    per=L//tb
    blk=pl.BlockSpec((tb,D),lambda i:(i,0))
    return pl.pallas_call(
        functools.partial(dx_kernel,per=per),grid=(T//tb,),
        in_specs=[blk,pl.BlockSpec((1,1,D),lambda i:(i//per,0,0)),pl.BlockSpec((3,tb,D),lambda i:(0,i,0)),blk,full(3,D,D),full(VR,D)],
        out_specs=[blk,full(16,D),pl.BlockSpec((1,8,D),lambda i:(i//per,0,0))],
        out_shape=[S_((T,D),F32),S_((16,D),F32),S_((T//L,8,D),F32)],
        compiler_params=pltpu.CompilerParams(dimension_semantics=("arbitrary",)),
        cost_estimate=cost(6*T*D*D,T*D*16+6*D*D),
        name="dx")(tok,row,d,gm,w,vec)


def rows8(x):
    return jnp.sum(x,axis=0,keepdims=True)


def sums_kernel(id_ref,sv1_ref,svq_ref,sv2_ref,sub_ref,ts_ref,out_ref):
    src=[sv1_ref[0:8],sv1_ref[8:16],svq_ref[0:8],svq_ref[8:16]]+[sv2_ref[8*i:8*i+8] for i in range(4)]
    src+=[sub_ref[:,i*D:(i+1)*D] for i in range(FF//D)]
    rows=[rows8(x) for x in src]+[id_ref[0:1],id_ref[1:2]]+[rows8(ts_ref[i]) for i in range(ts_ref.shape[0])]
    out_ref[...]=jnp.concatenate(rows,axis=0).astype(BF)


def sums(ids,sv1,svq,sv2,sub,ts):
    vm=pl.BlockSpec(memory_space=pltpu.VMEM)
    return pl.pallas_call(sums_kernel,in_specs=[vm]*6,out_specs=vm,
        out_shape=S_((VR+ts.shape[0],D),BF),cost_estimate=cost(0,10**6),name="sums")(ids,sv1,svq,sv2,sub,ts)


def group_kernel(idx_ref,*refs,ns,nseq):
    out_ref,acc=refs[ns:]
    tot=refs[0][0:VR].astype(F32)
    for j in range(1,ns):
        tot=tot+refs[j][0:VR].astype(F32)
    for j in range(ns):
        acc[idx_ref[1+j]]=refs[j][VR:VR+nseq].astype(F32)
    out_ref[...]=jnp.concatenate([tot]+[acc[j] for j in range(ns)],axis=0).astype(BF)


def group(idx,pays,nseq):
    ns=len(pays)
    vm=pl.BlockSpec(memory_space=pltpu.VMEM)
    return pl.pallas_call(functools.partial(group_kernel,ns=ns,nseq=nseq),
        in_specs=[pl.BlockSpec(memory_space=pltpu.SMEM)]+[vm]*ns,out_specs=vm,
        out_shape=S_((VR+ns*nseq,D),BF),scratch_shapes=[pltpu.VMEM((ns,nseq,D),F32)],
        cost_estimate=cost(0,10**6),name="group")(idx,*pays)


def table_kernel(me_ref,*refs,nr,rows,own):
    sum_ref,tab_ref,acc,allr=refs[nr:]
    r0=me_ref[0]
    for j in range(nr):
        acc[r0^j]=refs[j][...].astype(F32)
    tot=acc[0,0:VR]
    for r in range(1,nr):
        tot=tot+acc[r,0:VR]
    sum_ref[...]=tot
    for r in range(nr):
        allr[r*rows:(r+1)*rows,:]=acc[r,VR:VR+rows]
    n=nr*rows
    ids=tot[NV:NV+1,0:n]*32.0+tot[NV+1:NV+2,0:n]
    line=lax.broadcasted_iota(jnp.int32,(own,n),0)+me_ref[1]*own
    hit=jnp.where(line==ids.astype(jnp.int32),1.0,0.0).astype(BF)
    tab_ref[...]=nn(hit,allr[...].astype(BF))


def table(me,pays,own):
    nr=len(pays)
    rows=pays[0].shape[0]-VR
    vm=pl.BlockSpec(memory_space=pltpu.VMEM)
    return pl.pallas_call(functools.partial(table_kernel,nr=nr,rows=rows,own=own),
        in_specs=[pl.BlockSpec(memory_space=pltpu.SMEM)]+[vm]*nr,out_specs=[vm,vm],
        out_shape=[S_((VR,D),F32),S_((own,D),F32)],
        scratch_shapes=[pltpu.VMEM((nr,VR+rows,D),F32),pltpu.VMEM((nr*rows,D),F32)],
        cost_estimate=cost(0,4*10**6),name="table")(me,*pays)


def unpack_kernel(idx_ref,a_ref,b_ref,*outs,parts):
    for ch in (0,1):
        @pl.when(idx_ref[0]==ch)
        def _():
            for h,ref in enumerate((a_ref,b_ref) if ch==0 else (b_ref,a_ref)):
                r0=0
                for out,(nr,nb) in zip(outs,parts):
                    for b in range(nb):
                        out[:,(h*nb+b)*HC:(h*nb+b+1)*HC]=ref[r0:r0+nr,:].astype(F32)
                        r0+=nr


def unpack(idx,a,b,parts):
    vm=pl.BlockSpec(memory_space=pltpu.VMEM)
    return pl.pallas_call(functools.partial(unpack_kernel,parts=parts),
        in_specs=[pl.BlockSpec(memory_space=pltpu.SMEM),vm,vm],out_specs=[vm]*len(parts),
        out_shape=[S_((nr,2*nb*HC),F32) for nr,nb in parts],
        cost_estimate=cost(0,12*a.shape[0]*HC),name="unpack")(idx,a,b)


def small_kernel(me_ref,ts_ref,*refs,w,fr,nseq):
    vecs=refs[:9]
    out_ref,id_ref=refs[9:]
    def spread(rows,width,at):
        n=rows[0].shape[1]
        y=jnp.concatenate(rows+[jnp.zeros((8-len(rows),n),F32)]*(len(rows)<8),axis=0)
        y=jnp.concatenate([y,jnp.zeros((8,width-n),F32)],axis=1)
        return pltpu.roll(y,at,1)
    row=lambda ref: ref[...].astype(F32).reshape(1,ref.shape[0])
    v=spread([row(r) for r in vecs[:8]],D,me_ref[1]*w)
    u=spread([row(vecs[8])],FF,me_ref[1]*fr)
    lane=lax.broadcasted_iota(jnp.int32,(1,D),1)
    def steps(at,high):
        y=jnp.zeros((1,D),jnp.int32)
        for i in range(nseq):
            t=ts_ref[i]
            y=jnp.where(lane==at*nseq+i,t//32 if high else t%32,y)
        return y.astype(F32)
    id_ref[...]=jnp.concatenate([steps(me_ref[2],True),steps(me_ref[2],False)],axis=0)
    out_ref[...]=jnp.concatenate([v]+[u[0:1,i*D:(i+1)*D] for i in range(FF//D)]+[steps(me_ref[1],True),steps(me_ref[1],False)],axis=0).astype(BF)


def small_rows(me,time_steps,vecs):
    vm=pl.BlockSpec(memory_space=pltpu.VMEM)
    sm=pl.BlockSpec(memory_space=pltpu.SMEM)
    return pl.pallas_call(functools.partial(small_kernel,w=vecs[0].shape[0],fr=vecs[8].shape[0],nseq=time_steps.shape[0]),
        in_specs=[sm,sm]+[vm]*9,out_specs=[vm,vm],
        out_shape=[S_((VR,D),BF),S_((2,D),F32)],cost_estimate=cost(0,10**6),name="small")(me,time_steps,*vecs)


class Ring:
    def __init__(self,rep,shard):
        self.R,self.S=rep,shard
        self.nb=shard.bit_length()-1
        self.Z=rep//2
        r=lax.axis_index("rep")
        self.s=lax.axis_index("shard")
        self.c=r%2
        self.z=r//2

    def move(self,x,to):
        pairs=[]
        for r in range(self.R):
            for s in range(self.S):
                r2,s2=to(r,s)
                pairs.append((r*self.S+s,r2*self.S+s2))
        return lax.ppermute(x,("rep","shard"),pairs)

    def order(self,c,t):
        return (t+c*(self.nb//2))%self.nb

    def mask(self,c,j):
        m=0
        for t in range(self.nb):
            if j>>t&1:
                m|=1<<self.order(c,t)
        return m

    def step(self,x,t):
        return self.move(x,lambda r,s:(r,s^(1<<self.order(r%2,t))))

    def direct(self,x,j):
        return self.move(x,lambda r,s:(r,s^j))

    def core(self,x):
        return self.move(x,lambda r,s:(r^1,s))

    def plane(self,x,j):
        return self.move(x,lambda r,s:(r^(2*j),s))

    def index(self):
        m=[[self.mask(c,j) for j in range(self.S)] for c in (0,1)]
        base=list(range(self.S))
        t=jnp.where(self.c==0,jnp.array([0]+base+m[0]+m[1],jnp.int32),jnp.array([0]+base+m[1]+m[0],jnp.int32))
        head=jnp.arange(1+3*self.S)==0
        return jnp.where(head,self.c,t^self.s).astype(jnp.int32)


def tie(*xs):
    return lax.optimization_barrier(xs)


def add(*terms):
    y=terms[0].astype(F32)
    for x in terms[1:]:
        y=y+x.astype(F32)
    return y.astype(BF)


def upper(terms,n):
    return add(*[x[n:] for x in terms]),[x[:n] for x in terms]


def plane_rows(g,x):
    x=x.reshape(g.Z,-1,HC)
    return [lax.dynamic_index_in_dim(x,g.z^j,0,keepdims=False) for j in range(1,g.Z)]


def plane_send(g,rows):
    return [g.plane(x,j) for j,x in enumerate(rows,1)]


def plane_sum(g,x,parts):
    mine=lax.dynamic_index_in_dim(x.reshape(g.Z,-1,HC),g.z,0,keepdims=False).astype(F32)
    for p in parts:
        mine=mine+p.astype(F32)
    return mine.astype(BF)


def plane_join(g,mine,parts):
    out=jnp.zeros((g.Z,)+mine.shape,BF)
    for j,p in enumerate([mine]+parts):
        out=lax.dynamic_update_index_in_dim(out,p,g.z^j,0)
    return out.reshape(-1,HC)


def local(tokens,segments,time_steps,time_table,ln1_gain,ln1_bias,q_weight,q_bias,k_weight,v_weight,v_bias,o_weight,o_bias,ln2_gain,ln2_bias,up_weight,up_bias,down_weight,down_bias,cotangent):
    nseq=tokens.shape[0]
    T=nseq*L
    g=Ring(lax.axis_size("rep"),lax.axis_size("shard"))
    S=g.S
    w=ln1_gain.shape[0]
    fr=down_weight.shape[0]
    own=time_table.shape[0]
    idx=g.index()
    r=g.z*2+g.c
    me=jnp.stack([r,g.s,r*S+g.s]).astype(jnp.int32)
    small,ids=small_rows(me,time_steps,(ln1_gain,ln1_bias,q_bias,v_bias,o_bias,ln2_gain,ln2_bias,down_bias,up_bias))
    small,segments,o_weight_,q_weight_=tie(small,segments,o_weight,q_weight)
    pack_a=pack(pack_a_kernel,idx,(q_weight_,k_weight,v_weight),"pack_a")
    mine_a=[g.direct(pack_a,j) for j in range(1,S)]
    segments,pack_a=tie(segments,pack_a)
    vec=small.astype(F32)
    for j in reversed(range(1,S)):
        vec=vec+g.direct(small,j).astype(F32)
    steps=vec[NV,:S*nseq]*32.0+vec[NV+1,:S*nseq]
    hit=steps.astype(jnp.int32)[:,None]==jnp.arange(own)[None,:]+g.s*own
    rows=jnp.dot(hit.astype(BF),time_table,preferred_element_type=F32).astype(BF).reshape(S,nseq,D)
    pick=lambda j: lax.dynamic_index_in_dim(rows,g.s^j,0,keepdims=False)
    picks=[pick(j) for j in range(S)]
    picks[0],*mine_a=tie(picks[0],*mine_a)
    row=picks[0].astype(F32)
    for j in range(1,S):
        row=row+g.direct(picks[j],j).astype(F32)
    row=row.reshape(nseq,1,D)
    pack_b=pack(pack_b_kernel,idx,(o_weight_,up_weight,down_weight),"pack_b")
    tok=tokens.reshape(T,D)
    cot=cotangent.reshape(T,D)
    fq,fk=seg_features(segments.reshape(T))
    counts=jnp.sum(segments[:,:,None]==jnp.arange(4),axis=1)
    before=jnp.cumsum(counts==MAIN,axis=1)==0
    starts=jnp.sum(jnp.where(before,counts,0),axis=1).astype(jnp.int32)
    fq,fk,pack_b,row,*mine_a=tie(fq,fk,pack_b,row,*mine_a)
    other_a=[g.core(x) for x in mine_a]
    mine_b=[pack_b]
    first=[g.step(pack_b,t) for t in range(g.nb)]
    q,k,v,n1t,wqkv=qkv(idx,tok,row,vec,(q_weight,k_weight,v_weight),mine_a,other_a)
    fwd=attn_fwd(starts,q,k,v,fq,fk,(),0,3*nseq//2)
    o1,fx1,*first=tie(*fwd,*first)
    for t in range(g.nb):
        mine_b=mine_b+[first[t]]+[g.step(x,t) for x in mine_b[1:]]
    direct=[1<<t for t in range(g.nb)]
    other_b=[None]+[g.core(x) if j in direct else None for j,x in enumerate(mine_b[1:],1)]
    fwd=attn_fwd(starts,q,k,v,fq,fk,(o1,fx1),3*nseq//2,3*nseq)
    late=[j for j in range(1,S) if j not in direct]
    o1,fx1,*got=tie(*fwd,*[mine_b[j] for j in late])
    for j,x in zip(late,got):
        mine_b[j]=x
        other_b[j]=g.core(x)
    att,fx=attn_fwd(starts,q,k,v,fq,fk,(o1,fx1),9*nseq//2,6*nseq-9*nseq//2)
    res,gm,ga,keep_b,send_b,sv2,sub=mid(idx,tok,row,att,cot,vec,(o_weight,up_weight,down_weight),mine_b[1:],other_b[1:])
    cuts=[0,nseq,nseq+5*nseq//2,5*nseq,6*nseq]
    call=lambda prev,i: attn_bwd(starts,q,k,v,fx,fk,att,ga,prev,cuts[i],cuts[i+1]-cuts[i])
    got=g.core(send_b)
    d=call((),0)
    d,got=tie(d,got)
    n=S
    x=[keep_b]
    for t in reversed(range(g.nb)):
        n//=2
        up,x=upper(x+[got],n)
        d,up=tie(d,up)
        got=g.step(up,t)
        i=g.nb-t
        if i<=2:
            d=call((d,),i)
            d,got=tie(d,got)
    xb=add(*[y[0] for y in x],got[0])
    d,xb,*rows_b=tie(d,xb,*plane_rows(g,xb))
    parts=plane_send(g,rows_b)
    d=call((d,),3)
    keep_a,send_a,svq=dw(idx,n1t,d,S)
    keep_a,send_a,*parts=tie(keep_a,send_a,*parts)
    got=g.core(send_a)
    mine=plane_sum(g,xb,parts)
    back=[g.plane(mine,j) for j in range(1,g.Z)]
    gm,mine_,got=tie(gm,mine,got)
    up,x=upper([keep_a,got],S//2)
    gm,up=tie(gm,up)
    got=g.step(up,g.nb-1)
    gt,sv1,ts=dx(tok,row,d,gm,wqkv,vec)
    ts,got=tie(ts,got)
    n=S//2
    for t in reversed(range(g.nb-1)):
        n//=2
        up,x=upper(x+[got],n)
        ts,up=tie(ts,up)
        got=g.step(up,t)
    pay=sums(ids,sv1,svq,sv2,sub,ts)
    pays=[pay]+[g.direct(pay,j) for j in range(1,S)]
    pays[-1],got=tie(pays[-1],got)
    xa=add(*[y[0] for y in x],got[0])
    rows_a=plane_rows(g,xa)
    *pays,rows_a[0]=tie(*pays,rows_a[0])
    parts_a=plane_send(g,rows_a)
    pay=group(idx,pays,nseq)
    out_b=plane_join(g,mine_,back)
    out_b,pay,*parts_a=tie(out_b,pay,*parts_a)
    other_b=g.core(out_b)
    mine=plane_sum(g,xa,parts_a)
    pay,mine=tie(pay,mine)
    back_a=[g.plane(mine,j) for j in range(1,g.Z)]
    pays=[pay]+[g.move(pay,lambda r,s,j=j:(r^j,s)) for j in range(1,g.R)]
    go,gup,gdn=unpack(idx,out_b,other_b,((w,1),(w,4),(fr,1)))
    gup,*both=tie(gup,*back_a,*pays)
    back_a,pays=both[:g.Z-1],both[g.Z-1:]
    out_a=plane_join(g,mine,back_a)
    other_a=g.core(out_a)
    vsum,gtab=table(me,pays,own)
    vsum,other_a=tie(vsum,other_a)
    gq,gk,gv=unpack(idx,out_a,other_a,((w,1),)*3)
    sums8=lax.dynamic_slice_in_dim(vsum[:8],g.s*w,w,1)
    subs=lax.dynamic_slice_in_dim(vsum[8:NV].reshape(FF),g.s*up_bias.shape[0],up_bias.shape[0],0)
    return (res.reshape(tokens.shape),gt.reshape(tokens.shape),gtab,sums8[0],sums8[1],gq,sums8[2],gk,gv,sums8[3],go,sums8[4],sums8[5],sums8[6],gup,subs,gdn,sums8[7])


def solution(mesh):
    b=("rep","shard")
    s=P("shard")
    m=P("shard",None)
    t=P(b,None,None)
    return jax.shard_map(local,mesh=mesh,
        in_specs=(t,P(b,None),P(b),m,s,s,m,s,m,m,s,m,s,s,s,m,s,m,s,t),
        out_specs=(t,t,m,s,s,m,s,m,m,s,m,s,s,s,m,s,m,s),check_vma=False)
```

```python
import functools
import math

import jax
import jax.numpy as jnp
from jax import lax
from jax.experimental import pallas as pl
from jax.experimental.pallas import tpu as pltpu
from jax.sharding import PartitionSpec as P

NEG=-1e30
EPS=1e-5
L=1024
D=768
FF=3072
HC=D//2
BF=jnp.bfloat16
F32=jnp.float32
LOG2E=math.log2(math.e)
LN2=math.log(2.0)
QS=0.125*LOG2E
VR=14
NV=12
ANY=pl.BlockSpec(memory_space=pl.ANY)
S_=jax.ShapeDtypeStruct


def nt(a,b):
    return lax.dot_general(a,b,(((1,),(1,)),((),())),preferred_element_type=F32)


def nn(a,b):
    return lax.dot_general(a,b,(((1,),(0,)),((),())),preferred_element_type=F32)


def tn(a,b):
    return lax.dot_general(a,b,(((0,),(0,)),((),())),preferred_element_type=F32)


def full(*s):
    return pl.BlockSpec(s,lambda i,*_:(0,)*len(s),pipeline_mode=pl.Buffered(1))


def norm(x):
    mean=jnp.mean(x,axis=1,keepdims=True)
    off=x-mean
    var=jnp.mean(off*off,axis=1,keepdims=True)
    r=lax.rsqrt(var+EPS)
    return off*r,r


def sum8(x):
    return jnp.sum(x.reshape(x.shape[0]//8,8,x.shape[1]),axis=0)


def cost(flops,nbytes,trans=0):
    return pl.CostEstimate(flops=int(flops)//10,bytes_accessed=int(nbytes)//10,transcendentals=int(trans)//10)


def seg_features(seg):
    lane=jnp.arange(128)%64
    hit=seg[:,None]==lane[None,:]
    first=(lane<4)[None]
    fq=jnp.where(first&hit,1.0,0.0).astype(BF)
    fk=jnp.where(first,jnp.where(hit,0.0,NEG),jnp.where((lane<7)[None],1.0,0.0)).astype(BF)
    return fq,fk


def qkv_kernel(idx_ref,*refs,ns,wr):
    tok_ref,row_ref,vec_ref=refs[:3]
    own=refs[3:6]
    mine=refs[6:6+ns-1]
    other=refs[6+ns-1:6+2*(ns-1)]
    hi=6+2*(ns-1)
    q_ref,k_ref,v_ref,nt_ref,w_ref,sem=refs[hi:hi+6]
    @pl.when(pl.program_id(0)==0)
    def _():
        c=idx_ref[0]
        cps=[]
        def put(src,w,sh,c0,nc):
            dst=w_ref.at[w,pl.ds(pl.multiple_of(sh*wr,16),wr),pl.ds(c0,nc)]
            cp=pltpu.make_async_copy(src,dst,sem.at[len(cps)])
            cp.start()
            cps.append(cp)
        for w in range(3):
            put(own[w],w,idx_ref[1],0,D)
        for j in range(1,ns):
            for w in range(3):
                put(mine[j-1].at[pl.ds(w*wr,wr)],w,idx_ref[1+j],pl.multiple_of(c*HC,128),HC)
                put(other[j-1].at[pl.ds(w*wr,wr)],w,idx_ref[1+j],pl.multiple_of((1-c)*HC,128),HC)
        for cp in cps:
            cp.wait()
    xhat,_=norm(tok_ref[...]+row_ref[0])
    n1=(xhat*vec_ref[0:1,:]+vec_ref[1:2,:]).astype(BF)
    q_ref[...]=((nn(n1,w_ref[0])+vec_ref[2:3,:])*QS).astype(BF)
    k_ref[...]=nn(n1,w_ref[1]).astype(BF)
    v_ref[...]=(nn(n1,w_ref[2])+vec_ref[3:4,:]).astype(BF)
    nt_ref[...]=n1.T


def qkv(idx,tok,row,vec,own,mine,other,tb=512):
    T=tok.shape[0]
    per=L//tb
    ns=len(mine)+1
    wr=own[0].shape[0]
    blk=pl.BlockSpec((tb,D),lambda i,*_:(i,0))
    return pl.pallas_call(
        functools.partial(qkv_kernel,ns=ns,wr=wr),
        grid_spec=pltpu.PrefetchScalarGridSpec(
            num_scalar_prefetch=1,grid=(T//tb,),
            in_specs=[blk,pl.BlockSpec((1,1,D),lambda i,*_:(i//per,0,0)),full(VR,D)]+[ANY]*(3+2*(ns-1)),
            out_specs=[blk]*3+[pl.BlockSpec((D,tb),lambda i,*_:(0,i)),full(3,D,D)],
            scratch_shapes=[pltpu.SemaphoreType.DMA((3+6*(ns-1),))]),
        out_shape=[S_((T,D),BF)]*3+[S_((D,T),BF),S_((3,D,D),BF)],
        compiler_params=pltpu.CompilerParams(dimension_semantics=("arbitrary",)),
        cost_estimate=cost(6*T*D*D,T*D*10+9*D*D),
        name="qkv")(idx,tok,row,vec,*own,*mine,*other)


def pack_a_kernel(idx_ref,q_ref,k_ref,v_ref,out_ref):
    wr=q_ref.shape[0]
    for ch in (0,1):
        @pl.when(idx_ref[0]==ch)
        def _():
            for w,ref in enumerate((q_ref,k_ref,v_ref)):
                out_ref[w*wr:(w+1)*wr,:]=ref[:,ch*HC:(ch+1)*HC]


def pack_b_kernel(idx_ref,o_ref,u_ref,d_ref,out_ref):
    wr=o_ref.shape[0]
    for ch in (0,1):
        @pl.when(idx_ref[0]==ch)
        def _():
            out_ref[0:wr,:]=o_ref[:,ch*HC:(ch+1)*HC]
            for b in range(4):
                out_ref[wr+b*wr:2*wr+b*wr,:]=u_ref[:,(ch*4+b)*HC:(ch*4+b+1)*HC]
            out_ref[5*wr:,:]=d_ref[:,ch*HC:(ch+1)*HC]


def pack(kernel,idx,ws,name):
    rows=sum(x.shape[0]*x.shape[1]//D for x in ws)
    vm=pl.BlockSpec(memory_space=pltpu.VMEM)
    return pl.pallas_call(kernel,in_specs=[pl.BlockSpec(memory_space=pltpu.SMEM)]+[vm]*3,out_specs=vm,
        out_shape=S_((rows,HC),BF),cost_estimate=cost(0,4*rows*D),name=name)(idx,*ws)


MAIN=800
ROWS=816
LANES=896
REST=768


def windows(s):
    s16=(s//16)*16
    return pl.multiple_of(jnp.minimum(s16,L-ROWS),16),pl.multiple_of(jnp.minimum(s16,L-LANES),16)


def fwd_kernel(s_ref,q_ref,k_ref,v_ref,fq_ref,fk_ref,*refs,f0,ns):
    o_ref,fx_ref=refs[-2:]
    s0=s_ref[s_ref[ns+f0+pl.program_id(0)]]
    wr,wl=windows(s0)
    lane=lax.broadcasted_iota(jnp.int32,(1,128),1)
    lo=lane<64
    l6=lane&63
    rest_row=lax.broadcasted_iota(jnp.int32,(256,1),0)
    ahead=rest_row<s0
    qb=ROWS//3
    rest=lambda ref: jnp.where(ahead,ref[0:256,:],ref[REST:L,:])
    main=lambda ref: ref[pl.ds(wl,LANES),:]
    one=jnp.where(l6==0,1.0,0.0).astype(BF)
    kv=[]
    for take in (rest,main):
        k=take(k_ref)
        v=take(v_ref)
        fk=take(fk_ref)
        kv.append([(jnp.where(own,k,fk),jnp.where(own,v,one)) for own in (lo,~lo)])
    qf=[(rest(q_ref),rest(fq_ref))]
    for b in range(3):
        rows=pl.ds(pl.multiple_of(wr+b*qb,16),qb)
        qf.append((q_ref[rows,:],fq_ref[rows,:]))
    units=[(b,h) for b in range(4) for h in (0,1)]
    def score(b,h):
        return nt(jnp.where(lo if h==0 else ~lo,*qf[b]),kv[min(b,1)][h][0])
    pend=[score(*u) for u in units[:3]]
    accs=[]
    ls=[]
    for i,(b,h) in enumerate(units):
        s=pend.pop(0)
        if i+3<len(units):
            pend.append(score(*units[i+3]))
        m=jnp.max(s,axis=1,keepdims=True)
        p=jnp.exp2(s-m).astype(BF)
        acc=nn(p,kv[min(b,1)][h][1])
        l=acc[:,64:65] if h==0 else acc[:,0:1]
        accs.append(acc*(1.0/l))
        ls.append(-(m+jnp.log2(l)))
        if h==1:
            o=jnp.where(lo,accs[0],accs[1]).astype(BF)
            nl=jnp.where(lo,ls[1],ls[0])
            hi=nl.astype(BF).astype(F32)
            r1=nl-hi
            mid=r1.astype(BF).astype(F32)
            r2=r1-mid
            fx=jnp.where(l6==4,hi,jnp.where(l6==5,mid,jnp.where(l6==6,r2,qf[b][1].astype(F32)))).astype(BF)
            if b==0:
                o_ref[0:256,:]=o
                fx_ref[0:256,:]=fx
                o_ref[REST:L,:]=o
                fx_ref[REST:L,:]=fx
            else:
                at=wr+(b-1)*qb
                rows=pl.ds(pl.multiple_of(at,16),qb)
                pos=lax.broadcasted_iota(jnp.int32,(qb,1),0)+(at-s0)
                inside=(pos>=0)&(pos<MAIN)
                o_ref[rows,:]=jnp.where(inside,o,o_ref[rows,:])
                fx_ref[rows,:]=jnp.where(inside,fx,fx_ref[rows,:])
            accs=[]
            ls=[]


def attn_fwd(starts,q,k,v,fq,fk,prev,f0,n):
    T=q.shape[0]
    ns=T//L
    nu=ns*(D//128)
    blk=pl.BlockSpec((L,128),lambda i,s:(s[ns+f0+i],s[ns+nu+f0+i]))
    fb=pl.BlockSpec((L,128),lambda i,s:(s[ns+f0+i],0))
    prev=list(prev)
    return pl.pallas_call(
        functools.partial(fwd_kernel,f0=f0,ns=ns),
        grid_spec=pltpu.PrefetchScalarGridSpec(
            num_scalar_prefetch=1,grid=(n,),
            in_specs=[blk,blk,blk,fb,fb]+[ANY]*len(prev),out_specs=[blk,blk]),
        out_shape=[S_((T,D),BF)]*2,
        input_output_aliases={6+i:i for i in range(len(prev))},
        compiler_params=pltpu.CompilerParams(dimension_semantics=("arbitrary",)),
        cost_estimate=cost(n*2*4*L*L*256,n*L*128*14,n*2*L*L),
        name="attn_fwd")(starts,q,k,v,fq,fk,*prev)


def bwd_kernel(s_ref,q_ref,k_ref,v_ref,fx_ref,fk_ref,o_ref,do_ref,*refs,f0,ns):
    out_ref=refs[-1]
    s0=s_ref[s_ref[ns+f0+pl.program_id(0)]]
    wr,wl=windows(s0)
    lane=lax.broadcasted_iota(jnp.int32,(1,128),1)
    lo=lane<64
    l6=lane&63
    zero=jnp.zeros((),BF)
    ones2=jnp.where(l6<2,1.0,0.0).astype(BF)
    rest_row=lax.broadcasted_iota(jnp.int32,(256,1),0)
    ahead=rest_row<s0
    rest=lambda ref: jnp.where(ahead,ref[0:256,:],ref[REST:L,:])
    def block(take_k,nk,takes):
        k=take_k(k_ref)
        v=take_k(v_ref)
        fk=take_k(fk_ref)
        kx=[]
        vx=[]
        km=[]
        for own in (lo,~lo):
            kx.append(jnp.where(own,k,fk))
            vx.append(jnp.where(own,v,ones2))
            km.append(jnp.where(own,k,zero))
        dv=jnp.zeros((nk,128),F32)
        dk=jnp.zeros((nk,128),F32)
        dqs=[]
        for take in takes:
            q=take(q_ref)
            fx=take(fx_ref)
            do=take(do_ref)
            prod=do.astype(F32)*take(o_ref).astype(F32)
            d0=-jnp.sum(jnp.where(lo,prod,0.0),axis=1,keepdims=True)
            d1=-jnp.sum(jnp.where(lo,0.0,prod),axis=1,keepdims=True)
            nd=jnp.where(lo,d1,d0)
            hi=nd.astype(BF).astype(F32)
            fd=jnp.where(l6==0,hi,jnp.where(l6==1,nd-hi,0.0)).astype(BF)
            dq=jnp.zeros(q.shape,F32)
            for h,own in enumerate((lo,~lo)):
                p=jnp.exp2(nt(kx[h],jnp.where(own,q,fx)))
                dpt=nt(vx[h],jnp.where(own,do,fd))
                pb=p.astype(BF)
                ds=(p*dpt).astype(BF)
                dv=dv+nn(pb,jnp.where(own,do,zero))
                dk=dk+nn(ds,jnp.where(own,q,zero))
                dq=dq+tn(ds,km[h])
            dqs.append((dq*0.125).astype(BF))
        return dqs,(dk*LN2).astype(BF),dv.astype(BF)
    dqs,dk,dv=block(rest,256,[rest])
    for w,x in enumerate((dqs[0],dk,dv)):
        out_ref[w,0:256,:]=x
        out_ref[w,REST:L,:]=x
    at=lambda start,n: pl.ds(pl.multiple_of(start,16),n)
    cuts=[(0,256),(256,256),(512,256),(768,128)]
    dqs,dk,dv=block(lambda ref: ref[at(wr,ROWS),:],ROWS,[lambda ref,c=c: ref[at(wl+c[0],c[1]),:] for c in cuts])
    def put(w,start,x):
        n=x.shape[0]
        pos=lax.broadcasted_iota(jnp.int32,(n,1),0)+(start-s0)
        out_ref[w,at(start,n),:]=jnp.where((pos>=0)&(pos<MAIN),x,out_ref[w,at(start,n),:])
    for c,x in zip(cuts,dqs):
        put(0,wl+c[0],x)
    put(1,wr,dk)
    put(2,wr,dv)


def attn_bwd(starts,q,k,v,fx,fk,o,do,prev,f0,n):
    T=q.shape[0]
    ns=T//L
    nu=ns*(D//128)
    blk=pl.BlockSpec((L,128),lambda i,s:(s[ns+f0+i],s[ns+nu+f0+i]))
    fb=pl.BlockSpec((L,128),lambda i,s:(s[ns+f0+i],0))
    prev=list(prev)
    return pl.pallas_call(
        functools.partial(bwd_kernel,f0=f0,ns=ns),
        grid_spec=pltpu.PrefetchScalarGridSpec(
            num_scalar_prefetch=1,grid=(n,),
            in_specs=[blk,blk,blk,blk,fb,blk,blk]+[ANY]*len(prev),
            out_specs=pl.BlockSpec((3,L,128),lambda i,s:(0,s[ns+f0+i],s[ns+nu+f0+i]))),
        out_shape=S_((3,T,D),BF),
        input_output_aliases={8+i:i for i in range(len(prev))},
        compiler_params=pltpu.CompilerParams(dimension_semantics=("arbitrary",)),
        cost_estimate=cost(n*2*10*L*L*256,n*L*128*20,n*2*L*L),
        name="attn_bwd")(starts,q,k,v,fx,fk,o,do,*prev)


def mid_kernel(idx_ref,*refs,tb,fc,ns,wr,fr):
    tok_ref,row_ref,att_ref,cot_ref,vec_ref=refs[:5]
    own=refs[5:8]
    mine=refs[8:8+ns-1]
    other=refs[8+ns-1:8+2*(ns-1)]
    b0=8+2*(ns-1)
    res_ref,gm_ref,ga_ref,keep_ref,send_ref,sv_ref,sub_ref,ow,up,dn,aup,adn,aow,sem=refs[b0:]
    i=pl.program_id(0)
    n=pl.num_programs(0)
    c=idx_ref[0]
    def copies():
        cps=[]
        def put(src,dst):
            cps.append(pltpu.make_async_copy(src,dst,sem.at[len(cps)]))
        r16=lambda sh,m: pl.ds(pl.multiple_of(sh*m,16),m)
        sh=idx_ref[1+ns]
        put(own[0],ow.at[r16(sh,wr)])
        put(own[1],up.at[r16(sh,wr)])
        put(own[2],dn.at[r16(sh,fr)])
        for j in range(1,ns):
            for src,sh,cc in ((mine[j-1],idx_ref[1+ns+j],c),(other[j-1],idx_ref[1+2*ns+j],1-c)):
                cd=pl.ds(pl.multiple_of(cc*HC,128),HC)
                put(src.at[pl.ds(0,wr)],ow.at[r16(sh,wr),cd])
                for b in range(4):
                    put(src.at[pl.ds(wr+b*wr,wr)],up.at[r16(sh,wr),pl.ds(pl.multiple_of(cc*4*HC+b*HC,128),HC)])
                put(src.at[pl.ds(5*wr,fr)],dn.at[r16(sh,fr),cd])
        return cps
    @pl.when(i==0)
    def _():
        cps=copies()
        for cp in cps:
            cp.start()
        aup[...]=jnp.zeros_like(aup)
        adn[...]=jnp.zeros_like(adn)
        aow[...]=jnp.zeros_like(aow)
        sv_ref[...]=jnp.zeros_like(sv_ref)
        sub_ref[...]=jnp.zeros_like(sub_ref)
        for cp in cps:
            cp.wait()
    ob=vec_ref[4:5,:]
    g2=vec_ref[5:6,:]
    b2=vec_ref[6:7,:]
    db=vec_ref[7:8,:]
    att=att_ref[...]
    mixed=tok_ref[...]+row_ref[0]+nn(att,ow[...])+ob
    xhat,r=norm(mixed)
    n2=(xhat*g2+b2).astype(BF)
    n2t=n2.T
    cot=cot_ref[...]
    g=cot.astype(BF)
    res=mixed+db
    gn2=jnp.zeros((tb,D),F32)
    for j in range(FF//fc):
        cs=slice(j*fc,(j+1)*fc)
        pre=nn(n2,up[:,cs])+vec_ref[8+j:9+j,:]
        gact=nt(g,dn[cs,:])
        phi=0.5+0.5*lax.erf(pre*(2**-0.5))
        pdf=jnp.exp2(pre*pre*(-0.5*LOG2E))*(1.0/math.sqrt(2*math.pi))
        act=(pre*phi).astype(BF)
        gp=gact*(phi+pre*pdf)
        gpre=gp.astype(BF)
        sub_ref[:,cs]+=sum8(gp)
        res=res+nn(act,dn[cs,:])
        gn2=gn2+nt(gpre,up[:,cs])
        adn[cs,:]+=tn(act,g)
        aup[:,cs]+=nn(n2t,gpre)
    res_ref[...]=res
    e=gn2*g2
    c1=jnp.mean(e,axis=1,keepdims=True)
    c2=jnp.mean(e*xhat,axis=1,keepdims=True)
    gm=cot+r*(e-c1-xhat*c2)
    gml=gm.astype(BF)
    gm_ref[...]=gml
    ga_ref[...]=nt(gml,ow[...]).astype(BF)
    aow[...]+=tn(att,gml)
    sv_ref[0:8,:]+=sum8(gm)
    sv_ref[8:16,:]+=sum8(gn2*xhat)
    sv_ref[16:24,:]+=sum8(gn2)
    sv_ref[24:32,:]+=sum8(cot)
    @pl.when(i==n-1)
    def _():
        for ref,base,odd in ((keep_ref,1+ns,0),(send_ref,1+2*ns,1)):
            for ch in (0,1):
                @pl.when(c==(ch+odd)%2)
                def _():
                    def body(j,carry):
                        sh=idx_ref[base+j]
                        rw=pl.ds(pl.multiple_of(sh*wr,8),wr)
                        ref[j,0:wr,:]=aow[rw,ch*HC:(ch+1)*HC].astype(BF)
                        for b in range(4):
                            lo=(ch*4+b)*HC
                            ref[j,wr+b*wr:2*wr+b*wr,:]=aup[rw,lo:lo+HC].astype(BF)
                        ref[j,5*wr:5*wr+fr,:]=adn[pl.ds(pl.multiple_of(sh*fr,8),fr),ch*HC:(ch+1)*HC].astype(BF)
                        return carry
                    lax.fori_loop(0,ns,body,0)


def mid(idx,tok,row,att,cot,vec,own,mine,other,tb=256,fc=D):
    T=tok.shape[0]
    per=L//tb
    ns=len(mine)+1
    wr=own[0].shape[0]
    fr=own[2].shape[0]
    rb=5*wr+fr
    blk=pl.BlockSpec((tb,D),lambda i,*_:(i,0))
    return pl.pallas_call(
        functools.partial(mid_kernel,tb=tb,fc=fc,ns=ns,wr=wr,fr=fr),
        grid_spec=pltpu.PrefetchScalarGridSpec(
            num_scalar_prefetch=1,grid=(T//tb,),
            in_specs=[blk,pl.BlockSpec((1,1,D),lambda i,*_:(i//per,0,0)),blk,blk,full(VR,D)]+[ANY]*(3+2*(ns-1)),
            out_specs=[blk,blk,blk,full(ns,rb,HC),full(ns,rb,HC),full(32,D),full(8,FF)],
            scratch_shapes=[pltpu.VMEM((D,D),BF),pltpu.VMEM((D,FF),BF),pltpu.VMEM((FF,D),BF),
                pltpu.VMEM((D,FF),F32),pltpu.VMEM((FF,D),F32),pltpu.VMEM((D,D),F32),
                pltpu.SemaphoreType.DMA((3+12*(ns-1),))]),
        out_shape=[S_((T,D),F32),S_((T,D),BF),S_((T,D),BF),S_((ns,rb,HC),BF),S_((ns,rb,HC),BF),S_((32,D),F32),S_((8,FF),F32)],
        compiler_params=pltpu.CompilerParams(dimension_semantics=("arbitrary",),vmem_limit_bytes=67043328),
        cost_estimate=cost(6*T*D*(D+2*FF),T*D*20+30*D*FF,2*T*FF),
        name="mid")(idx,tok,row,att,cot,vec,*own,*mine,*other)


def dw_kernel(idx_ref,nt_ref,d_ref,keep_ref,send_ref,sv_ref,acc,*,ns,wr):
    i=pl.program_id(0)
    c=idx_ref[0]
    @pl.when(i==0)
    def _():
        acc[...]=jnp.zeros_like(acc)
        sv_ref[...]=jnp.zeros_like(sv_ref)
    for w in range(3):
        acc[w]+=nn(nt_ref[...],d_ref[w])
    sv_ref[0:8,:]+=sum8(d_ref[0].astype(F32))
    sv_ref[8:16,:]+=sum8(d_ref[2].astype(F32))
    @pl.when(i==pl.num_programs(0)-1)
    def _():
        for ref,base,odd in ((keep_ref,1+ns,0),(send_ref,1+2*ns,1)):
            for ch in (0,1):
                @pl.when(c==(ch+odd)%2)
                def _():
                    def body(j,carry):
                        rw=pl.ds(pl.multiple_of(idx_ref[base+j]*wr,8),wr)
                        for w in range(3):
                            ref[j,w*wr:(w+1)*wr,:]=acc[w,rw,ch*HC:(ch+1)*HC].astype(BF)
                        return carry
                    lax.fori_loop(0,ns,body,0)


def dw(idx,n1t,d,ns,tb=512):
    T=n1t.shape[1]
    wr=D//ns
    return pl.pallas_call(
        functools.partial(dw_kernel,ns=ns,wr=wr),
        grid_spec=pltpu.PrefetchScalarGridSpec(
            num_scalar_prefetch=1,grid=(T//tb,),
            in_specs=[pl.BlockSpec((D,tb),lambda i,*_:(0,i)),pl.BlockSpec((3,tb,D),lambda i,*_:(0,i,0))],
            out_specs=[full(ns,3*wr,HC),full(ns,3*wr,HC),full(16,D)],
            scratch_shapes=[pltpu.VMEM((3,D,D),F32)]),
        out_shape=[S_((ns,3*wr,HC),BF)]*2+[S_((16,D),F32)],
        compiler_params=pltpu.CompilerParams(dimension_semantics=("arbitrary",)),
        cost_estimate=cost(6*T*D*D,T*D*8+12*D*D),
        name="dw")(idx,n1t,d)


def dx_kernel(tok_ref,row_ref,d_ref,gm_ref,w_ref,vec_ref,gt_ref,sv_ref,ts_ref,*,per):
    i=pl.program_id(0)
    @pl.when(i==0)
    def _():
        sv_ref[...]=jnp.zeros_like(sv_ref)
    @pl.when(i%per==0)
    def _():
        ts_ref[...]=jnp.zeros_like(ts_ref)
    gn=nt(d_ref[0],w_ref[0])+nt(d_ref[1],w_ref[1])+nt(d_ref[2],w_ref[2])
    xhat,r=norm(tok_ref[...]+row_ref[0])
    e=gn*vec_ref[0:1,:]
    c1=jnp.mean(e,axis=1,keepdims=True)
    c2=jnp.mean(e*xhat,axis=1,keepdims=True)
    gt=gm_ref[...].astype(F32)+r*(e-c1-xhat*c2)
    gt_ref[...]=gt
    sv_ref[0:8,:]+=sum8(gn*xhat)
    sv_ref[8:16,:]+=sum8(gn)
    ts_ref[0]+=sum8(gt)


def dx(tok,row,d,gm,w,vec,tb=512):
    T=tok.shape[0]
    per=L//tb
    blk=pl.BlockSpec((tb,D),lambda i:(i,0))
    return pl.pallas_call(
        functools.partial(dx_kernel,per=per),grid=(T//tb,),
        in_specs=[blk,pl.BlockSpec((1,1,D),lambda i:(i//per,0,0)),pl.BlockSpec((3,tb,D),lambda i:(0,i,0)),blk,full(3,D,D),full(VR,D)],
        out_specs=[blk,full(16,D),pl.BlockSpec((1,8,D),lambda i:(i//per,0,0))],
        out_shape=[S_((T,D),F32),S_((16,D),F32),S_((T//L,8,D),F32)],
        compiler_params=pltpu.CompilerParams(dimension_semantics=("arbitrary",)),
        cost_estimate=cost(6*T*D*D,T*D*16+6*D*D),
        name="dx")(tok,row,d,gm,w,vec)


def rows8(x):
    return jnp.sum(x,axis=0,keepdims=True)


def sums_kernel(id_ref,sv1_ref,svq_ref,sv2_ref,sub_ref,*refs):
    out_ref=refs[-1]
    src=[sv1_ref[0:8],sv1_ref[8:16],svq_ref[0:8],svq_ref[8:16]]+[sv2_ref[8*i:8*i+8] for i in range(4)]
    src+=[sub_ref[:,i*D:(i+1)*D] for i in range(FF//D)]
    rows=[rows8(x) for x in src]+[id_ref[0:1],id_ref[1:2]]+[rows8(refs[0][i]) for i in range(refs[0].shape[0])]
    out_ref[...]=jnp.concatenate(rows,axis=0).astype(BF)


def sums(ids,sv1,svq,sv2,sub,ts):
    vm=pl.BlockSpec(memory_space=pltpu.VMEM)
    return pl.pallas_call(sums_kernel,in_specs=[vm]*6,out_specs=vm,
        out_shape=S_((VR+ts.shape[0],D),BF),cost_estimate=cost(0,10**6),name="sums")(ids,sv1,svq,sv2,sub,ts)


def split_kernel(me_ref,*refs,nz,nt_):
    outs,acc=refs[nt_:-1],refs[-1]
    wz=outs[0].shape[1]
    wr=wz*nz
    y=refs[0][0].astype(F32)
    for ref in refs[1:nt_]:
        y=y+ref[0].astype(F32)
    for z in range(nz):
        for w in range(3):
            acc[z,w]=y[w*wr+z*wz:w*wr+(z+1)*wz,:]
    for j,out in enumerate(outs):
        out[...]=acc[me_ref[3]^j].astype(BF)


def split(me,terms,nz):
    n=terms[0].shape[1]
    wz=n//3//nz
    one=pl.BlockSpec((1,n,HC),lambda i:(0,0,0))
    return pl.pallas_call(functools.partial(split_kernel,nz=nz,nt_=len(terms)),grid=(1,),
        in_specs=[pl.BlockSpec(memory_space=pltpu.SMEM)]+[one]*len(terms),out_specs=[pl.BlockSpec((3,wz,HC),lambda i:(0,0,0))]*nz,
        out_shape=[S_((3,wz,HC),BF)]*nz,scratch_shapes=[pltpu.VMEM((nz,3,wz,HC),F32)],
        cost_estimate=cost(0,8*n*HC),name="split")(me,*terms)


def half_rows(rows):
    return -(-rows//8)*8


def message_kernel(idx_ref,*refs,ns,nz,nseq):
    pays,parts=refs[:ns],refs[ns:ns+nz]
    out_ref,acc=refs[ns+nz:]
    tot=pays[0][0:VR].astype(F32)
    for j in range(1,ns):
        tot=tot+pays[j][0:VR].astype(F32)
    for j in range(ns):
        acc[idx_ref[1+j]]=pays[j][VR:VR+nseq].astype(F32)
    n=VR+ns*nseq
    rows=[tot]+[acc[j] for j in range(ns)]
    if half_rows(n)>n:
        rows.append(jnp.zeros((half_rows(n)-n,D),F32))
    x=jnp.concatenate(rows,axis=0)
    y=parts[0][...].astype(F32)
    for p in parts[1:]:
        y=y+p[...].astype(F32)
    out_ref[...]=jnp.concatenate([x[:,0:HC],x[:,HC:D],y[0],y[1],y[2]],axis=0).astype(BF)


def message(idx,pays,parts,nseq):
    ns,nz=len(pays),len(parts)
    vm=pl.BlockSpec(memory_space=pltpu.VMEM)
    return pl.pallas_call(functools.partial(message_kernel,ns=ns,nz=nz,nseq=nseq),
        in_specs=[pl.BlockSpec(memory_space=pltpu.SMEM)]+[vm]*(ns+nz),out_specs=vm,
        out_shape=S_((2*half_rows(VR+ns*nseq)+3*parts[0].shape[1],HC),BF),scratch_shapes=[pltpu.VMEM((ns,nseq,D),F32)],
        cost_estimate=cost(0,10**6),name="message")(idx,*pays,*parts)


def join_kernel(me_ref,*refs):
    out=refs[-1]
    for j,ref in enumerate(refs[:-1]):
        out[me_ref[3]^j]=ref[...]


def join(me,parts):
    vm=pl.BlockSpec(memory_space=pltpu.VMEM)
    return pl.pallas_call(join_kernel,in_specs=[pl.BlockSpec(memory_space=pltpu.SMEM)]+[vm]*len(parts),out_specs=vm,
        out_shape=S_((len(parts),)+parts[0].shape,BF),cost_estimate=cost(0,4*len(parts)*parts[0].size),name="join")(me,*parts)


def final_kernel(me_ref,a_ref,b_ref,q_ref,k_ref,v_ref,sum_ref,tab_ref,acc,allr,*,nz,rows,own):
    n8=half_rows(VR+rows)
    wz=(a_ref.shape[1]-2*n8)//3
    for ch in (0,1):
        @pl.when(me_ref[4]==ch)
        def _():
            for h,ref in enumerate((a_ref,b_ref) if ch==0 else (b_ref,a_ref)):
                for z in range(nz):
                    x=ref[z].astype(F32)
                    for w,out in enumerate((q_ref,k_ref,v_ref)):
                        out[z*wz:(z+1)*wz,h*HC:(h+1)*HC]=x[2*n8+w*wz:2*n8+(w+1)*wz,:]
                    acc[2*z+h]=jnp.concatenate([x[0:n8],x[n8:2*n8]],axis=1)
    tot=acc[0,0:VR]
    for r in range(1,2*nz):
        tot=tot+acc[r,0:VR]
    sum_ref[...]=tot
    for r in range(2*nz):
        allr[r*rows:(r+1)*rows,:]=acc[r,VR:VR+rows]
    n=2*nz*rows
    ids=tot[NV:NV+1,0:n]*32.0+tot[NV+1:NV+2,0:n]
    line=lax.broadcasted_iota(jnp.int32,(own,n),0)+me_ref[1]*own
    hit=jnp.where(line==ids.astype(jnp.int32),1.0,0.0).astype(BF)
    tab_ref[...]=nn(hit,allr[...].astype(BF))


def final(me,a,b,rows,own):
    nz=a.shape[0]
    n8=half_rows(VR+rows)
    wr=(a.shape[1]-2*n8)//3*nz
    vm=pl.BlockSpec(memory_space=pltpu.VMEM)
    return pl.pallas_call(functools.partial(final_kernel,nz=nz,rows=rows,own=own),
        in_specs=[pl.BlockSpec(memory_space=pltpu.SMEM)]+[vm]*2,out_specs=[vm]*5,
        out_shape=[S_((wr,D),F32)]*3+[S_((VR,D),F32),S_((own,D),F32)],
        scratch_shapes=[pltpu.VMEM((2*nz,n8,D),F32),pltpu.VMEM((2*nz*rows,D),F32)],
        cost_estimate=cost(0,4*10**6),name="final")(me,a,b)


def unpack_kernel(idx_ref,a_ref,b_ref,*outs,parts):
    for ch in (0,1):
        @pl.when(idx_ref[0]==ch)
        def _():
            for h,ref in enumerate((a_ref,b_ref) if ch==0 else (b_ref,a_ref)):
                r0=0
                for out,(nr,nb) in zip(outs,parts):
                    for b in range(nb):
                        out[:,(h*nb+b)*HC:(h*nb+b+1)*HC]=ref[r0:r0+nr,:].astype(F32)
                        r0+=nr


def unpack(idx,a,b,parts):
    vm=pl.BlockSpec(memory_space=pltpu.VMEM)
    return pl.pallas_call(functools.partial(unpack_kernel,parts=parts),
        in_specs=[pl.BlockSpec(memory_space=pltpu.SMEM),vm,vm],out_specs=[vm]*len(parts),
        out_shape=[S_((nr,2*nb*HC),F32) for nr,nb in parts],
        cost_estimate=cost(0,12*a.shape[0]*HC),name="unpack")(idx,a,b)


def small_kernel(me_ref,ts_ref,*refs,w,fr,nseq):
    vecs=refs[:9]
    out_ref,id_ref=refs[9:]
    def spread(rows,width,at):
        n=rows[0].shape[1]
        y=jnp.concatenate(rows+[jnp.zeros((8-len(rows),n),F32)]*(len(rows)<8),axis=0)
        y=jnp.concatenate([y,jnp.zeros((8,width-n),F32)],axis=1)
        return pltpu.roll(y,at,1)
    row=lambda ref: ref[...].astype(F32).reshape(1,ref.shape[0])
    v=spread([row(r) for r in vecs[:8]],D,me_ref[1]*w)
    u=spread([row(vecs[8])],FF,me_ref[1]*fr)
    lane=lax.broadcasted_iota(jnp.int32,(1,D),1)
    def steps(at,high):
        y=jnp.zeros((1,D),jnp.int32)
        for i in range(nseq):
            t=ts_ref[i]
            y=jnp.where(lane==at*nseq+i,t//32 if high else t%32,y)
        return y.astype(F32)
    id_ref[...]=jnp.concatenate([steps(me_ref[2],True),steps(me_ref[2],False)],axis=0)
    out_ref[...]=jnp.concatenate([v]+[u[0:1,i*D:(i+1)*D] for i in range(FF//D)]+[steps(me_ref[1],True),steps(me_ref[1],False)],axis=0).astype(BF)


def small_rows(me,time_steps,vecs):
    vm=pl.BlockSpec(memory_space=pltpu.VMEM)
    sm=pl.BlockSpec(memory_space=pltpu.SMEM)
    return pl.pallas_call(functools.partial(small_kernel,w=vecs[0].shape[0],fr=vecs[8].shape[0],nseq=time_steps.shape[0]),
        in_specs=[sm,sm]+[vm]*9,out_specs=[vm,vm],
        out_shape=[S_((VR,D),BF),S_((2,D),F32)],cost_estimate=cost(0,10**6),name="small")(me,time_steps,*vecs)


class Ring:
    def __init__(self,rep,shard):
        self.R,self.S=rep,shard
        self.nb=shard.bit_length()-1
        self.Z=rep//2
        r=lax.axis_index("rep")
        self.s=lax.axis_index("shard")
        self.c=r%2
        self.z=r//2

    def move(self,x,to):
        pairs=[]
        for r in range(self.R):
            for s in range(self.S):
                r2,s2=to(r,s)
                pairs.append((r*self.S+s,r2*self.S+s2))
        return lax.ppermute(x,("rep","shard"),pairs)

    def order(self,c,t):
        return (t+c*(self.nb//2))%self.nb

    def mask(self,c,j):
        m=0
        for t in range(self.nb):
            if j>>t&1:
                m|=1<<self.order(c,t)
        return m

    def step(self,x,t):
        return self.move(x,lambda r,s:(r,s^(1<<self.order(r%2,t))))

    def direct(self,x,j):
        return self.move(x,lambda r,s:(r,s^j))

    def core(self,x):
        return self.move(x,lambda r,s:(r^1,s))

    def plane(self,x,j):
        return self.move(x,lambda r,s:(r^(2*j),s))

    def index(self):
        m=[[self.mask(c,j) for j in range(self.S)] for c in (0,1)]
        base=list(range(self.S))
        t=jnp.where(self.c==0,jnp.array([0]+base+m[0]+m[1],jnp.int32),jnp.array([0]+base+m[1]+m[0],jnp.int32))
        head=jnp.arange(1+3*self.S)==0
        return jnp.where(head,self.c,t^self.s).astype(jnp.int32)


def tie(*xs):
    return lax.optimization_barrier(xs)


def add(*terms):
    y=terms[0].astype(F32)
    for x in terms[1:]:
        y=y+x.astype(F32)
    return y.astype(BF)


def upper(terms,n):
    return add(*[x[n:2*n] for x in terms])


def plane_rows(g,x):
    x=x.reshape(g.Z,-1,HC)
    return [lax.dynamic_index_in_dim(x,g.z^j,0,keepdims=False) for j in range(1,g.Z)]


def plane_send(g,rows):
    return [g.plane(x,j) for j,x in enumerate(rows,1)]


def plane_sum(g,x,parts):
    mine=lax.dynamic_index_in_dim(x.reshape(g.Z,-1,HC),g.z,0,keepdims=False).astype(F32)
    for p in parts:
        mine=mine+p.astype(F32)
    return mine.astype(BF)


def local(tokens,segments,time_steps,time_table,ln1_gain,ln1_bias,q_weight,q_bias,k_weight,v_weight,v_bias,o_weight,o_bias,ln2_gain,ln2_bias,up_weight,up_bias,down_weight,down_bias,cotangent):
    nseq=tokens.shape[0]
    T=nseq*L
    g=Ring(lax.axis_size("rep"),lax.axis_size("shard"))
    S=g.S
    w=ln1_gain.shape[0]
    fr=down_weight.shape[0]
    own=time_table.shape[0]
    idx=g.index()
    r=g.z*2+g.c
    me=jnp.stack([r,g.s,r*S+g.s,g.z,g.c]).astype(jnp.int32)
    small,ids=small_rows(me,time_steps,(ln1_gain,ln1_bias,q_bias,v_bias,o_bias,ln2_gain,ln2_bias,down_bias,up_bias))
    small,segments,o_weight_,q_weight_=tie(small,segments,o_weight,q_weight)
    pack_a=pack(pack_a_kernel,idx,(q_weight_,k_weight,v_weight),"pack_a")
    mine_a=[g.direct(pack_a,j) for j in range(1,S)]
    segments,pack_a=tie(segments,pack_a)
    vec=small.astype(F32)
    for j in reversed(range(1,S)):
        vec=vec+g.direct(small,j).astype(F32)
    steps=vec[NV,:S*nseq]*32.0+vec[NV+1,:S*nseq]
    hit=steps.astype(jnp.int32)[:,None]==jnp.arange(own)[None,:]+g.s*own
    rows=jnp.dot(hit.astype(BF),time_table,preferred_element_type=F32).astype(BF).reshape(S,nseq,D)
    pick=lambda j: lax.dynamic_index_in_dim(rows,g.s^j,0,keepdims=False)
    picks=[pick(j) for j in range(S)]
    picks[0],*mine_a=tie(picks[0],*mine_a)
    row=picks[0].astype(F32)
    for j in range(1,S):
        row=row+g.direct(picks[j],j).astype(F32)
    row=row.reshape(nseq,1,D)
    pack_b=pack(pack_b_kernel,idx,(o_weight_,up_weight,down_weight),"pack_b")
    tok=tokens.reshape(T,D)
    cot=cotangent.reshape(T,D)
    fq,fk=seg_features(segments.reshape(T))
    counts=jnp.sum(segments[:,:,None]==jnp.arange(4),axis=1)
    before=jnp.cumsum(counts==MAIN,axis=1)==0
    np_=D//128
    starts=jnp.concatenate([jnp.sum(jnp.where(before,counts,0),axis=1).astype(jnp.int32),
        jnp.array([i//np_ for i in range(nseq*np_)]+[i%np_ for i in range(nseq*np_)],jnp.int32)])
    fq,fk,pack_b,row,*mine_a=tie(fq,fk,pack_b,row,*mine_a)
    other_a=[g.core(x) for x in mine_a]
    mine_b=[pack_b]
    first=[g.step(pack_b,t) for t in range(g.nb)]
    q,k,v,n1t,wqkv=qkv(idx,tok,row,vec,(q_weight,k_weight,v_weight),mine_a,other_a)
    fwd=attn_fwd(starts,q,k,v,fq,fk,(),0,3*nseq//2)
    o1,fx1,*first=tie(*fwd,*first)
    for t in range(g.nb):
        mine_b=mine_b+[first[t]]+[g.step(x,t) for x in mine_b[1:]]
    direct=[1<<t for t in range(g.nb)]
    other_b=[None]+[g.core(x) if j in direct else None for j,x in enumerate(mine_b[1:],1)]
    fwd=attn_fwd(starts,q,k,v,fq,fk,(o1,fx1),3*nseq//2,3*nseq)
    late=[j for j in range(1,S) if j not in direct]
    o1,fx1,*got=tie(*fwd,*[mine_b[j] for j in late])
    for j,x in zip(late,got):
        mine_b[j]=x
        other_b[j]=g.core(x)
    att,fx=attn_fwd(starts,q,k,v,fq,fk,(o1,fx1),9*nseq//2,6*nseq-9*nseq//2)
    res,gm,ga,keep_b,send_b,sv2,sub=mid(idx,tok,row,att,cot,vec,(o_weight,up_weight,down_weight),mine_b[1:],other_b[1:])
    cuts=[0,nseq,nseq+5*nseq//2,5*nseq,6*nseq]
    call=lambda prev,i: attn_bwd(starts,q,k,v,fx,fk,att,ga,prev,cuts[i],cuts[i+1]-cuts[i])
    got=g.core(send_b)
    d=call((),0)
    d,got=tie(d,got)
    n=S
    x=[keep_b]
    for t in reversed(range(g.nb)):
        n//=2
        x=x+[got]
        up=upper(x,n)
        d,up=tie(d,up)
        got=g.step(up,t)
        i=g.nb-t
        if i<=2:
            d=call((d,),i)
            d,got=tie(d,got)
    xb=add(*[y[0] for y in x],got[0])
    d,xb,*rows_b=tie(d,xb,*plane_rows(g,xb))
    parts=plane_send(g,rows_b)
    d=call((d,),3)
    keep_a,send_a,svq=dw(idx,n1t,d,S)
    keep_a,send_a,*parts=tie(keep_a,send_a,*parts)
    got=g.core(send_a)
    mine=plane_sum(g,xb,parts)
    back=[g.plane(mine,j) for j in range(1,g.Z)]
    gm,mine_,got=tie(gm,mine,got)
    x=[keep_a,got]
    up=upper(x,S//2)
    gm,up=tie(gm,up)
    got=g.step(up,g.nb-1)
    gt,sv1,ts=dx(tok,row,d,gm,wqkv,vec)
    sv1,*back[:2]=tie(sv1,*back[:2])
    n=S//2
    for t in reversed(range(g.nb-1)):
        n//=2
        sv1,got=tie(sv1,got)
        x=x+[got]
        up=upper(x,n)
        sv1,up=tie(sv1,up)
        got=g.step(up,t)
    pay=sums(ids,sv1,svq,sv2,sub,ts)
    pays=[pay]+[g.direct(pay,j) for j in range(1,S)]
    pays[0],got=tie(pays[0],got)
    own_a,*rows_a=split(me,x+[got],g.Z)
    both=tie(rows_a[0],*pays,*back[2:])
    rows_a[0],pays,back=both[0],both[1:1+S],back[:2]+list(both[1+S:])
    parts_a=plane_send(g,rows_a)
    out_b=join(me,[mine_]+back).reshape(-1,HC)
    out_b,*parts_a=tie(out_b,*parts_a)
    msg=message(idx,pays,[own_a]+parts_a,nseq)
    other_b=g.core(out_b)
    back_a=[g.plane(msg,j) for j in range(1,g.Z)]
    go,gup,gdn=unpack(idx,out_b,other_b,((w,1),(w,4),(fr,1)))
    gup,*back_a=tie(gup,*back_a)
    out_a=join(me,[msg]+back_a)
    gq,gk,gv,vsum,gtab=final(me,out_a,g.core(out_a),S*nseq,own)
    sums8=lax.dynamic_slice_in_dim(vsum[:8],g.s*w,w,1)
    subs=lax.dynamic_slice_in_dim(vsum[8:NV].reshape(FF),g.s*up_bias.shape[0],up_bias.shape[0],0)
    return (res.reshape(tokens.shape),gt.reshape(tokens.shape),gtab,sums8[0],sums8[1],gq,sums8[2],gk,gv,sums8[3],go,sums8[4],sums8[5],sums8[6],gup,subs,gdn,sums8[7])


def solution(mesh):
    b=("rep","shard")
    s=P("shard")
    m=P("shard",None)
    t=P(b,None,None)
    return jax.shard_map(local,mesh=mesh,
        in_specs=(t,P(b,None),P(b),m,s,s,m,s,m,m,s,m,s,s,s,m,s,m,s,t),
        out_specs=(t,t,m,s,s,m,s,m,m,s,m,s,s,s,m,s,m,s),check_vma=False)
```

```python
import functools
import math

import jax
import jax.numpy as jnp
from jax import lax
from jax.experimental import pallas as pl
from jax.experimental.pallas import tpu as pltpu
from jax.sharding import PartitionSpec as P

NEG=-1e30
EPS=1e-5
L=1024
D=768
FF=3072
HC=D//2
BF=jnp.bfloat16
F32=jnp.float32
LOG2E=math.log2(math.e)
LN2=math.log(2.0)
QS=0.125*LOG2E
VR=14
VP=16
NV=12
ANY=pl.BlockSpec(memory_space=pl.ANY)
S_=jax.ShapeDtypeStruct


def nt(a,b):
    return lax.dot_general(a,b,(((1,),(1,)),((),())),preferred_element_type=F32)


def nn(a,b):
    return lax.dot_general(a,b,(((1,),(0,)),((),())),preferred_element_type=F32)


def tn(a,b):
    return lax.dot_general(a,b,(((0,),(0,)),((),())),preferred_element_type=F32)


def full(*s):
    return pl.BlockSpec(s,lambda i,*_:(0,)*len(s),pipeline_mode=pl.Buffered(1))


def norm(x):
    mean=jnp.mean(x,axis=1,keepdims=True)
    off=x-mean
    var=jnp.mean(off*off,axis=1,keepdims=True)
    r=lax.rsqrt(var+EPS)
    return off*r,r


def sum8(x):
    return jnp.sum(x.reshape(x.shape[0]//8,8,x.shape[1]),axis=0)


def cost(flops,nbytes,trans=0):
    return pl.CostEstimate(flops=int(flops)//10,bytes_accessed=int(nbytes)//10,transcendentals=int(trans)//10)


def seg_features(seg):
    lane=jnp.arange(128)%64
    hit=seg[:,None]==lane[None,:]
    first=(lane<4)[None]
    fq=jnp.where(first&hit,1.0,0.0).astype(BF)
    fk=jnp.where(first,jnp.where(hit,0.0,NEG),jnp.where((lane<7)[None],1.0,0.0)).astype(BF)
    return fq,fk


def qkv_kernel(idx_ref,*refs,ns,wr):
    tok_ref,row_ref,vec_ref=refs[:3]
    own=refs[3:6]
    mine=refs[6:6+ns-1]
    other=refs[6+ns-1:6+2*(ns-1)]
    hi=6+2*(ns-1)
    q_ref,k_ref,v_ref,nt_ref,w_ref,sem=refs[hi:hi+6]
    def copies(w):
        c=idx_ref[0]
        cps=[]
        def put(src,sh,cols):
            rows=pl.ds(pl.multiple_of(sh*wr,16),wr)
            dst=w_ref.at[w,rows] if cols is None else w_ref.at[w,rows,pl.ds(pl.multiple_of(cols*HC,128),HC)]
            cps.append(pltpu.make_async_copy(src,dst,sem.at[w,len(cps)]))
        put(own[w],idx_ref[1],None)
        for j in range(1,ns):
            put(mine[j-1].at[pl.ds(w*wr,wr)],idx_ref[1+j],c)
            put(other[j-1].at[pl.ds(w*wr,wr)],idx_ref[1+j],1-c)
        return cps
    first=pl.program_id(0)==0
    @pl.when(first)
    def _():
        for w in range(3):
            for cp in copies(w):
                cp.start()
    def arrived(w):
        @pl.when(first)
        def _():
            for cp in copies(w):
                cp.wait()
    xhat,_=norm(tok_ref[...]+row_ref[0])
    n1=(xhat*vec_ref[0:1,:]+vec_ref[1:2,:]).astype(BF)
    arrived(0)
    q_ref[...]=((nn(n1,w_ref[0])+vec_ref[2:3,:])*QS).astype(BF)
    arrived(1)
    k_ref[...]=nn(n1,w_ref[1]).astype(BF)
    arrived(2)
    v_ref[...]=(nn(n1,w_ref[2])+vec_ref[3:4,:]).astype(BF)
    nt_ref[...]=n1.T


def qkv(idx,tok,row,vec,own,mine,other,tb=512):
    T=tok.shape[0]
    per=L//tb
    ns=len(mine)+1
    wr=own[0].shape[0]
    blk=pl.BlockSpec((tb,D),lambda i,*_:(i,0))
    return pl.pallas_call(
        functools.partial(qkv_kernel,ns=ns,wr=wr),
        grid_spec=pltpu.PrefetchScalarGridSpec(
            num_scalar_prefetch=1,grid=(T//tb,),
            in_specs=[blk,pl.BlockSpec((1,1,D),lambda i,*_:(i//per,0,0)),full(VR,D)]+[ANY]*(3+2*(ns-1)),
            out_specs=[blk]*3+[pl.BlockSpec((D,tb),lambda i,*_:(0,i)),full(3,D,D)],
            scratch_shapes=[pltpu.SemaphoreType.DMA((3,1+2*(ns-1)))]),
        out_shape=[S_((T,D),BF)]*3+[S_((D,T),BF),S_((3,D,D),BF)],
        compiler_params=pltpu.CompilerParams(dimension_semantics=("arbitrary",)),
        cost_estimate=cost(6*T*D*D,T*D*10+9*D*D),
        name="qkv")(idx,tok,row,vec,*own,*mine,*other)


def pack_a_kernel(idx_ref,q_ref,k_ref,v_ref,out_ref):
    wr=q_ref.shape[0]
    for ch in (0,1):
        @pl.when(idx_ref[0]==ch)
        def _():
            for w,ref in enumerate((q_ref,k_ref,v_ref)):
                out_ref[w*wr:(w+1)*wr,:]=ref[:,ch*HC:(ch+1)*HC]


def pack_b_kernel(idx_ref,o_ref,u_ref,d_ref,out_ref):
    wr=o_ref.shape[0]
    for ch in (0,1):
        @pl.when(idx_ref[0]==ch)
        def _():
            out_ref[0:wr,:]=o_ref[:,ch*HC:(ch+1)*HC]
            for b in range(4):
                out_ref[wr+b*wr:2*wr+b*wr,:]=u_ref[:,(ch*4+b)*HC:(ch*4+b+1)*HC]
            out_ref[5*wr:,:]=d_ref[:,ch*HC:(ch+1)*HC]


def pack(kernel,idx,ws,name):
    rows=sum(x.shape[0]*x.shape[1]//D for x in ws)
    vm=pl.BlockSpec(memory_space=pltpu.VMEM)
    return pl.pallas_call(kernel,in_specs=[pl.BlockSpec(memory_space=pltpu.SMEM)]+[vm]*3,out_specs=vm,
        out_shape=S_((rows,HC),BF),cost_estimate=cost(0,4*rows*D),name=name)(idx,*ws)


MAIN=800
ROWS=816
LANES=896
REST=768


def windows(s):
    s16=(s//16)*16
    return pl.multiple_of(jnp.minimum(s16,L-ROWS),16),pl.multiple_of(jnp.minimum(s16,L-LANES),16)


def fwd_kernel(s_ref,q_ref,k_ref,v_ref,fq_ref,fk_ref,*refs,f0,ns):
    o_ref,fx_ref=refs[-2:]
    s0=s_ref[s_ref[ns+f0+pl.program_id(0)]]
    wr,wl=windows(s0)
    lane=lax.broadcasted_iota(jnp.int32,(1,128),1)
    lo=lane<64
    l6=lane&63
    rest_row=lax.broadcasted_iota(jnp.int32,(256,1),0)
    ahead=rest_row<s0
    qb=ROWS//3
    rest=lambda ref: jnp.where(ahead,ref[0:256,:],ref[REST:L,:])
    main=lambda ref: ref[pl.ds(wl,LANES),:]
    one=jnp.where(l6==0,1.0,0.0).astype(BF)
    kv=[]
    for take in (rest,main):
        k=take(k_ref)
        v=take(v_ref)
        fk=take(fk_ref)
        kv.append([(jnp.where(own,k,fk),jnp.where(own,v,one)) for own in (lo,~lo)])
    qf=[(rest(q_ref),rest(fq_ref))]
    for b in range(3):
        rows=pl.ds(pl.multiple_of(wr+b*qb,16),qb)
        qf.append((q_ref[rows,:],fq_ref[rows,:]))
    units=[(b,h) for b in range(4) for h in (0,1)]
    def score(b,h):
        return nt(jnp.where(lo if h==0 else ~lo,*qf[b]),kv[min(b,1)][h][0])
    pend=[score(*u) for u in units[:3]]
    accs=[]
    ls=[]
    for i,(b,h) in enumerate(units):
        s=pend.pop(0)
        if i+3<len(units):
            pend.append(score(*units[i+3]))
        m=jnp.max(s,axis=1,keepdims=True)
        p=jnp.exp2(s-m).astype(BF)
        acc=nn(p,kv[min(b,1)][h][1])
        l=acc[:,64:65] if h==0 else acc[:,0:1]
        accs.append(acc*(1.0/l))
        ls.append(-(m+jnp.log2(l)))
        if h==1:
            o=jnp.where(lo,accs[0],accs[1]).astype(BF)
            nl=jnp.where(lo,ls[1],ls[0])
            hi=nl.astype(BF).astype(F32)
            r1=nl-hi
            mid=r1.astype(BF).astype(F32)
            r2=r1-mid
            fx=jnp.where(l6==4,hi,jnp.where(l6==5,mid,jnp.where(l6==6,r2,qf[b][1].astype(F32)))).astype(BF)
            if b==0:
                o_ref[0:256,:]=o
                fx_ref[0:256,:]=fx
                o_ref[REST:L,:]=o
                fx_ref[REST:L,:]=fx
            else:
                at=wr+(b-1)*qb
                rows=pl.ds(pl.multiple_of(at,16),qb)
                pos=lax.broadcasted_iota(jnp.int32,(qb,1),0)+(at-s0)
                inside=(pos>=0)&(pos<MAIN)
                o_ref[rows,:]=jnp.where(inside,o,o_ref[rows,:])
                fx_ref[rows,:]=jnp.where(inside,fx,fx_ref[rows,:])
            accs=[]
            ls=[]


def attn_fwd(starts,q,k,v,fq,fk,prev,f0,n):
    T=q.shape[0]
    ns=T//L
    nu=ns*(D//128)
    blk=pl.BlockSpec((L,128),lambda i,s:(s[ns+f0+i],s[ns+nu+f0+i]))
    fb=pl.BlockSpec((L,128),lambda i,s:(s[ns+f0+i],0))
    prev=list(prev)
    return pl.pallas_call(
        functools.partial(fwd_kernel,f0=f0,ns=ns),
        grid_spec=pltpu.PrefetchScalarGridSpec(
            num_scalar_prefetch=1,grid=(n,),
            in_specs=[blk,blk,blk,fb,fb]+[ANY]*len(prev),out_specs=[blk,blk]),
        out_shape=[S_((T,D),BF)]*2,
        input_output_aliases={6+i:i for i in range(len(prev))},
        compiler_params=pltpu.CompilerParams(dimension_semantics=("arbitrary",)),
        cost_estimate=cost(n*2*4*L*L*256,n*L*128*14,n*2*L*L),
        name="attn_fwd")(starts,q,k,v,fq,fk,*prev)


def bwd_kernel(s_ref,q_ref,k_ref,v_ref,fx_ref,fk_ref,o_ref,do_ref,*refs,f0,ns):
    out_ref=refs[-1]
    s0=s_ref[s_ref[ns+f0+pl.program_id(0)]]
    wr,wl=windows(s0)
    lane=lax.broadcasted_iota(jnp.int32,(1,128),1)
    lo=lane<64
    l6=lane&63
    zero=jnp.zeros((),BF)
    ones2=jnp.where(l6<2,1.0,0.0).astype(BF)
    rest_row=lax.broadcasted_iota(jnp.int32,(256,1),0)
    ahead=rest_row<s0
    rest=lambda ref: jnp.where(ahead,ref[0:256,:],ref[REST:L,:])
    def block(take_k,nk,takes):
        k=take_k(k_ref)
        v=take_k(v_ref)
        fk=take_k(fk_ref)
        kx=[]
        vx=[]
        km=[]
        for own in (lo,~lo):
            kx.append(jnp.where(own,k,fk))
            vx.append(jnp.where(own,v,ones2))
            km.append(jnp.where(own,k,zero))
        dv=jnp.zeros((nk,128),F32)
        dk=jnp.zeros((nk,128),F32)
        dqs=[]
        for take in takes:
            q=take(q_ref)
            fx=take(fx_ref)
            do=take(do_ref)
            prod=do.astype(F32)*take(o_ref).astype(F32)
            d0=-jnp.sum(jnp.where(lo,prod,0.0),axis=1,keepdims=True)
            d1=-jnp.sum(jnp.where(lo,0.0,prod),axis=1,keepdims=True)
            nd=jnp.where(lo,d1,d0)
            hi=nd.astype(BF).astype(F32)
            fd=jnp.where(l6==0,hi,jnp.where(l6==1,nd-hi,0.0)).astype(BF)
            dq=jnp.zeros(q.shape,F32)
            for h,own in enumerate((lo,~lo)):
                p=jnp.exp2(nt(kx[h],jnp.where(own,q,fx)))
                dpt=nt(vx[h],jnp.where(own,do,fd))
                pb=p.astype(BF)
                ds=(p*dpt).astype(BF)
                dv=dv+nn(pb,jnp.where(own,do,zero))
                dk=dk+nn(ds,jnp.where(own,q,zero))
                dq=dq+tn(ds,km[h])
            dqs.append((dq*0.125).astype(BF))
        return dqs,(dk*LN2).astype(BF),dv.astype(BF)
    dqs,dk,dv=block(rest,256,[rest])
    for w,x in enumerate((dqs[0],dk,dv)):
        out_ref[w,0:256,:]=x
        out_ref[w,REST:L,:]=x
    at=lambda start,n: pl.ds(pl.multiple_of(start,16),n)
    cuts=[(0,256),(256,256),(512,256),(768,128)]
    dqs,dk,dv=block(lambda ref: ref[at(wr,ROWS),:],ROWS,[lambda ref,c=c: ref[at(wl+c[0],c[1]),:] for c in cuts])
    def put(w,start,x):
        n=x.shape[0]
        pos=lax.broadcasted_iota(jnp.int32,(n,1),0)+(start-s0)
        out_ref[w,at(start,n),:]=jnp.where((pos>=0)&(pos<MAIN),x,out_ref[w,at(start,n),:])
    for c,x in zip(cuts,dqs):
        put(0,wl+c[0],x)
    put(1,wr,dk)
    put(2,wr,dv)


def attn_bwd(starts,q,k,v,fx,fk,o,do,prev,f0,n):
    T=q.shape[0]
    ns=T//L
    nu=ns*(D//128)
    blk=pl.BlockSpec((L,128),lambda i,s:(s[ns+f0+i],s[ns+nu+f0+i]))
    fb=pl.BlockSpec((L,128),lambda i,s:(s[ns+f0+i],0))
    prev=list(prev)
    return pl.pallas_call(
        functools.partial(bwd_kernel,f0=f0,ns=ns),
        grid_spec=pltpu.PrefetchScalarGridSpec(
            num_scalar_prefetch=1,grid=(n,),
            in_specs=[blk,blk,blk,blk,fb,blk,blk]+[ANY]*len(prev),
            out_specs=pl.BlockSpec((3,L,128),lambda i,s:(0,s[ns+f0+i],s[ns+nu+f0+i]))),
        out_shape=S_((3,T,D),BF),
        input_output_aliases={8+i:i for i in range(len(prev))},
        compiler_params=pltpu.CompilerParams(dimension_semantics=("arbitrary",)),
        cost_estimate=cost(n*2*10*L*L*256,n*L*128*20,n*2*L*L),
        name="attn_bwd")(starts,q,k,v,fx,fk,o,do,*prev)


def mid_kernel(idx_ref,*refs,tb,fc,ns,wr,fr):
    tok_ref,row_ref,att_ref,cot_ref,vec_ref=refs[:5]
    own=refs[5:8]
    mine=refs[8:8+ns-1]
    other=refs[8+ns-1:8+2*(ns-1)]
    b0=8+2*(ns-1)
    res_ref,gm_ref,ga_ref,keep_ref,send_ref,sv_ref,sub_ref,ow,up,dn,aup,adn,aow,sem=refs[b0:]
    i=pl.program_id(0)
    n=pl.num_programs(0)
    c=idx_ref[0]
    def copies():
        cps=[]
        def put(src,dst):
            cps.append(pltpu.make_async_copy(src,dst,sem.at[len(cps)]))
        r16=lambda sh,m: pl.ds(pl.multiple_of(sh*m,16),m)
        sh=idx_ref[1+ns]
        put(own[0],ow.at[r16(sh,wr)])
        put(own[1],up.at[r16(sh,wr)])
        put(own[2],dn.at[r16(sh,fr)])
        for j in range(1,ns):
            for src,sh,cc in ((mine[j-1],idx_ref[1+ns+j],c),(other[j-1],idx_ref[1+2*ns+j],1-c)):
                cd=pl.ds(pl.multiple_of(cc*HC,128),HC)
                put(src.at[pl.ds(0,wr)],ow.at[r16(sh,wr),cd])
                for b in range(4):
                    put(src.at[pl.ds(wr+b*wr,wr)],up.at[r16(sh,wr),pl.ds(pl.multiple_of(cc*4*HC+b*HC,128),HC)])
                put(src.at[pl.ds(5*wr,fr)],dn.at[r16(sh,fr),cd])
        return cps
    @pl.when(i==0)
    def _():
        cps=copies()
        for cp in cps:
            cp.start()
        aup[...]=jnp.zeros_like(aup)
        adn[...]=jnp.zeros_like(adn)
        aow[...]=jnp.zeros_like(aow)
        sv_ref[...]=jnp.zeros_like(sv_ref)
        sub_ref[...]=jnp.zeros_like(sub_ref)
        for cp in cps:
            cp.wait()
    ob=vec_ref[4:5,:]
    g2=vec_ref[5:6,:]
    b2=vec_ref[6:7,:]
    db=vec_ref[7:8,:]
    att=att_ref[...]
    mixed=tok_ref[...]+row_ref[0]+nn(att,ow[...])+ob
    xhat,r=norm(mixed)
    n2=(xhat*g2+b2).astype(BF)
    n2t=n2.T
    cot=cot_ref[...]
    g=cot.astype(BF)
    res=mixed+db
    gn2=jnp.zeros((tb,D),F32)
    for j in range(FF//fc):
        cs=slice(j*fc,(j+1)*fc)
        pre=nn(n2,up[:,cs])+vec_ref[8+j:9+j,:]
        gact=nt(g,dn[cs,:])
        phi=0.5+0.5*lax.erf(pre*(2**-0.5))
        pdf=jnp.exp2(pre*pre*(-0.5*LOG2E))*(1.0/math.sqrt(2*math.pi))
        act=(pre*phi).astype(BF)
        gp=gact*(phi+pre*pdf)
        gpre=gp.astype(BF)
        sub_ref[:,cs]+=sum8(gp)
        res=res+nn(act,dn[cs,:])
        gn2=gn2+nt(gpre,up[:,cs])
        adn[cs,:]+=tn(act,g)
        aup[:,cs]+=nn(n2t,gpre)
    res_ref[...]=res
    e=gn2*g2
    c1=jnp.mean(e,axis=1,keepdims=True)
    c2=jnp.mean(e*xhat,axis=1,keepdims=True)
    gm=cot+r*(e-c1-xhat*c2)
    gml=gm.astype(BF)
    gm_ref[...]=gml
    ga_ref[...]=nt(gml,ow[...]).astype(BF)
    aow[...]+=tn(att,gml)
    sv_ref[0:8,:]+=sum8(gm)
    sv_ref[8:16,:]+=sum8(gn2*xhat)
    sv_ref[16:24,:]+=sum8(gn2)
    sv_ref[24:32,:]+=sum8(cot)
    @pl.when(i==n-1)
    def _():
        for ref,base,odd in ((keep_ref,1+ns,0),(send_ref,1+2*ns,1)):
            for ch in (0,1):
                @pl.when(c==(ch+odd)%2)
                def _():
                    def body(j,carry):
                        sh=idx_ref[base+j]
                        rw=pl.ds(pl.multiple_of(sh*wr,8),wr)
                        ref[j,0:wr,:]=aow[rw,ch*HC:(ch+1)*HC].astype(BF)
                        for b in range(4):
                            lo=(ch*4+b)*HC
                            ref[j,wr+b*wr:2*wr+b*wr,:]=aup[rw,lo:lo+HC].astype(BF)
                        ref[j,5*wr:5*wr+fr,:]=adn[pl.ds(pl.multiple_of(sh*fr,8),fr),ch*HC:(ch+1)*HC].astype(BF)
                        return carry
                    lax.fori_loop(0,ns,body,0)


def mid(idx,tok,row,att,cot,vec,own,mine,other,tb=256,fc=D):
    T=tok.shape[0]
    per=L//tb
    ns=len(mine)+1
    wr=own[0].shape[0]
    fr=own[2].shape[0]
    rb=5*wr+fr
    blk=pl.BlockSpec((tb,D),lambda i,*_:(i,0))
    return pl.pallas_call(
        functools.partial(mid_kernel,tb=tb,fc=fc,ns=ns,wr=wr,fr=fr),
        grid_spec=pltpu.PrefetchScalarGridSpec(
            num_scalar_prefetch=1,grid=(T//tb,),
            in_specs=[blk,pl.BlockSpec((1,1,D),lambda i,*_:(i//per,0,0)),blk,blk,full(VR,D)]+[ANY]*(3+2*(ns-1)),
            out_specs=[blk,blk,blk,full(ns,rb,HC),full(ns,rb,HC),full(32,D),full(8,FF)],
            scratch_shapes=[pltpu.VMEM((D,D),BF),pltpu.VMEM((D,FF),BF),pltpu.VMEM((FF,D),BF),
                pltpu.VMEM((D,FF),F32),pltpu.VMEM((FF,D),F32),pltpu.VMEM((D,D),F32),
                pltpu.SemaphoreType.DMA((3+12*(ns-1),))]),
        out_shape=[S_((T,D),F32),S_((T,D),BF),S_((T,D),BF),S_((ns,rb,HC),BF),S_((ns,rb,HC),BF),S_((32,D),F32),S_((8,FF),F32)],
        compiler_params=pltpu.CompilerParams(dimension_semantics=("arbitrary",),vmem_limit_bytes=67043328),
        cost_estimate=cost(6*T*D*(D+2*FF),T*D*20+30*D*FF,2*T*FF),
        name="mid")(idx,tok,row,att,cot,vec,*own,*mine,*other)


def dw_kernel(idx_ref,nt_ref,d_ref,keep_ref,send_ref,sv_ref,acc,*,ns,wr):
    i=pl.program_id(0)
    c=idx_ref[0]
    @pl.when(i==0)
    def _():
        acc[...]=jnp.zeros_like(acc)
        sv_ref[...]=jnp.zeros_like(sv_ref)
    for w in range(3):
        acc[w]+=nn(nt_ref[...],d_ref[w])
    sv_ref[0:8,:]+=sum8(d_ref[0].astype(F32))
    sv_ref[8:16,:]+=sum8(d_ref[2].astype(F32))
    @pl.when(i==pl.num_programs(0)-1)
    def _():
        for ref,base,odd in ((keep_ref,1+ns,0),(send_ref,1+2*ns,1)):
            for ch in (0,1):
                @pl.when(c==(ch+odd)%2)
                def _():
                    def body(j,carry):
                        rw=pl.ds(pl.multiple_of(idx_ref[base+j]*wr,8),wr)
                        for w in range(3):
                            ref[j,w*wr:(w+1)*wr,:]=acc[w,rw,ch*HC:(ch+1)*HC].astype(BF)
                        return carry
                    lax.fori_loop(0,ns,body,0)


def dw(idx,n1t,d,ns,tb=512):
    T=n1t.shape[1]
    wr=D//ns
    return pl.pallas_call(
        functools.partial(dw_kernel,ns=ns,wr=wr),
        grid_spec=pltpu.PrefetchScalarGridSpec(
            num_scalar_prefetch=1,grid=(T//tb,),
            in_specs=[pl.BlockSpec((D,tb),lambda i,*_:(0,i)),pl.BlockSpec((3,tb,D),lambda i,*_:(0,i,0))],
            out_specs=[full(ns,3*wr,HC),full(ns,3*wr,HC),full(16,D)],
            scratch_shapes=[pltpu.VMEM((3,D,D),F32)]),
        out_shape=[S_((ns,3*wr,HC),BF)]*2+[S_((16,D),F32)],
        compiler_params=pltpu.CompilerParams(dimension_semantics=("arbitrary",)),
        cost_estimate=cost(6*T*D*D,T*D*8+12*D*D),
        name="dw")(idx,n1t,d)


def dx_kernel(tok_ref,row_ref,d_ref,gm_ref,w_ref,vec_ref,gt_ref,sv_ref,ts_ref,*,per):
    i=pl.program_id(0)
    @pl.when(i==0)
    def _():
        sv_ref[...]=jnp.zeros_like(sv_ref)
    @pl.when(i%per==0)
    def _():
        ts_ref[...]=jnp.zeros_like(ts_ref)
    gn=nt(d_ref[0],w_ref[0])+nt(d_ref[1],w_ref[1])+nt(d_ref[2],w_ref[2])
    xhat,r=norm(tok_ref[...]+row_ref[0])
    e=gn*vec_ref[0:1,:]
    c1=jnp.mean(e,axis=1,keepdims=True)
    c2=jnp.mean(e*xhat,axis=1,keepdims=True)
    gt=gm_ref[...].astype(F32)+r*(e-c1-xhat*c2)
    gt_ref[...]=gt
    sv_ref[0:8,:]+=sum8(gn*xhat)
    sv_ref[8:16,:]+=sum8(gn)
    ts_ref[0]+=sum8(gt)


def dx(tok,row,d,gm,w,vec,tb=512):
    T=tok.shape[0]
    per=L//tb
    blk=pl.BlockSpec((tb,D),lambda i:(i,0))
    return pl.pallas_call(
        functools.partial(dx_kernel,per=per),grid=(T//tb,),
        in_specs=[blk,pl.BlockSpec((1,1,D),lambda i:(i//per,0,0)),pl.BlockSpec((3,tb,D),lambda i:(0,i,0)),blk,full(3,D,D),full(VR,D)],
        out_specs=[blk,full(16,D),pl.BlockSpec((1,8,D),lambda i:(i//per,0,0))],
        out_shape=[S_((T,D),F32),S_((16,D),F32),S_((T//L,8,D),F32)],
        compiler_params=pltpu.CompilerParams(dimension_semantics=("arbitrary",)),
        cost_estimate=cost(6*T*D*D,T*D*16+6*D*D),
        name="dx")(tok,row,d,gm,w,vec)


def rows8(x):
    return jnp.sum(x,axis=0,keepdims=True)


def sums_kernel(me_ref,id_ref,sv1_ref,svq_ref,sv2_ref,sub_ref,ts_ref,out_ref,acc,*,nseq):
    src=[sv1_ref[0:8],sv1_ref[8:16],svq_ref[0:8],svq_ref[8:16]]+[sv2_ref[8*i:8*i+8] for i in range(4)]
    src+=[sub_ref[:,i*D:(i+1)*D] for i in range(FF//D)]
    rows=[rows8(x) for x in src]+[id_ref[0:1],id_ref[1:2]]
    acc[...]=jnp.zeros_like(acc)
    for i in range(nseq):
        acc[me_ref[2]*nseq+i]=jnp.broadcast_to(rows8(ts_ref[i]),(1,D))
    out_ref[0:VP]=jnp.concatenate(rows+[jnp.zeros((VP-VR,D),F32)],axis=0).astype(BF)
    out_ref[VP:]=acc[...].reshape(acc.shape[0],D).astype(BF)


def sums(me,ids,sv1,svq,sv2,sub,ts,n):
    vm=pl.BlockSpec(memory_space=pltpu.VMEM)
    return pl.pallas_call(functools.partial(sums_kernel,nseq=ts.shape[0]),
        in_specs=[pl.BlockSpec(memory_space=pltpu.SMEM)]+[vm]*6,out_specs=vm,
        out_shape=S_((VP+n,D),BF),scratch_shapes=[pltpu.VMEM((n,1,D),F32)],
        cost_estimate=cost(0,10**6),name="sums")(me,ids,sv1,svq,sv2,sub,ts)


def table_kernel(me_ref,pay_ref,sum_ref,tab_ref,*,own):
    n=pay_ref.shape[0]-VP
    tot=pay_ref[0:VP].astype(F32)
    sum_ref[...]=tot
    ids=tot[NV:NV+1,0:n]*32.0+tot[NV+1:NV+2,0:n]
    line=lax.broadcasted_iota(jnp.int32,(own,n),0)+me_ref[1]*own
    hit=jnp.where(line==ids.astype(jnp.int32),1.0,0.0).astype(BF)
    tab_ref[...]=nn(hit,pay_ref[VP:])


def table(me,pay,own):
    vm=pl.BlockSpec(memory_space=pltpu.VMEM)
    return pl.pallas_call(functools.partial(table_kernel,own=own),
        in_specs=[pl.BlockSpec(memory_space=pltpu.SMEM),vm],out_specs=[vm,vm],
        out_shape=[S_((VP,D),F32),S_((own,D),F32)],
        cost_estimate=cost(0,4*10**6),name="table")(me,pay)


def unpack_kernel(idx_ref,a_ref,b_ref,*outs,parts):
    for ch in (0,1):
        @pl.when(idx_ref[0]==ch)
        def _():
            for h,ref in enumerate((a_ref,b_ref) if ch==0 else (b_ref,a_ref)):
                r0=0
                for out,(nr,nb) in zip(outs,parts):
                    for b in range(nb):
                        out[:,(h*nb+b)*HC:(h*nb+b+1)*HC]=ref[r0:r0+nr,:].astype(F32)
                        r0+=nr


def unpack(idx,a,b,parts):
    vm=pl.BlockSpec(memory_space=pltpu.VMEM)
    return pl.pallas_call(functools.partial(unpack_kernel,parts=parts),
        in_specs=[pl.BlockSpec(memory_space=pltpu.SMEM),vm,vm],out_specs=[vm]*len(parts),
        out_shape=[S_((nr,2*nb*HC),F32) for nr,nb in parts],
        cost_estimate=cost(0,12*a.shape[0]*HC),name="unpack")(idx,a,b)


def small_kernel(me_ref,ts_ref,*refs,w,fr,nseq):
    vecs=refs[:9]
    out_ref,id_ref=refs[9:]
    def spread(rows,width,at):
        n=rows[0].shape[1]
        y=jnp.concatenate(rows+[jnp.zeros((8-len(rows),n),F32)]*(len(rows)<8),axis=0)
        y=jnp.concatenate([y,jnp.zeros((8,width-n),F32)],axis=1)
        return pltpu.roll(y,at,1)
    row=lambda ref: ref[...].astype(F32).reshape(1,ref.shape[0])
    v=spread([row(r) for r in vecs[:8]],D,me_ref[1]*w)
    u=spread([row(vecs[8])],FF,me_ref[1]*fr)
    lane=lax.broadcasted_iota(jnp.int32,(1,D),1)
    def steps(at,high):
        y=jnp.zeros((1,D),jnp.int32)
        for i in range(nseq):
            t=ts_ref[i]
            y=jnp.where(lane==at*nseq+i,t//32 if high else t%32,y)
        return y.astype(F32)
    id_ref[...]=jnp.concatenate([steps(me_ref[2],True),steps(me_ref[2],False)],axis=0)
    out_ref[...]=jnp.concatenate([v]+[u[0:1,i*D:(i+1)*D] for i in range(FF//D)]+[steps(me_ref[1],True),steps(me_ref[1],False)],axis=0).astype(BF)


def small_rows(me,time_steps,vecs):
    vm=pl.BlockSpec(memory_space=pltpu.VMEM)
    sm=pl.BlockSpec(memory_space=pltpu.SMEM)
    return pl.pallas_call(functools.partial(small_kernel,w=vecs[0].shape[0],fr=vecs[8].shape[0],nseq=time_steps.shape[0]),
        in_specs=[sm,sm]+[vm]*9,out_specs=[vm,vm],
        out_shape=[S_((VR,D),BF),S_((2,D),F32)],cost_estimate=cost(0,10**6),name="small")(me,time_steps,*vecs)


class Ring:
    def __init__(self,rep,shard):
        self.R,self.S=rep,shard
        self.nb=shard.bit_length()-1
        self.Z=rep//2
        r=lax.axis_index("rep")
        self.s=lax.axis_index("shard")
        self.c=r%2
        self.z=r//2

    def move(self,x,to):
        pairs=[]
        for r in range(self.R):
            for s in range(self.S):
                r2,s2=to(r,s)
                pairs.append((r*self.S+s,r2*self.S+s2))
        return lax.ppermute(x,("rep","shard"),pairs)

    def order(self,c,t):
        return (t+c*(self.nb//2))%self.nb

    def mask(self,c,j):
        m=0
        for t in range(self.nb):
            if j>>t&1:
                m|=1<<self.order(c,t)
        return m

    def step(self,x,t):
        return self.move(x,lambda r,s:(r,s^(1<<self.order(r%2,t))))

    def direct(self,x,j):
        return self.move(x,lambda r,s:(r,s^j))

    def core(self,x):
        return self.move(x,lambda r,s:(r^1,s))

    def plane(self,x,j):
        return self.move(x,lambda r,s:(r^(2*j),s))

    def direct2(self,x,j):
        return self.move(x,lambda r,s:(r,s^self.mask(r%2,j)))

    def index(self):
        m=[[self.mask(c,j) for j in range(self.S)] for c in (0,1)]
        base=list(range(self.S))
        t=jnp.where(self.c==0,jnp.array([0]+base+m[0]+m[1],jnp.int32),jnp.array([0]+base+m[1]+m[0],jnp.int32))
        head=jnp.arange(1+3*self.S)==0
        return jnp.where(head,self.c,t^self.s).astype(jnp.int32)


def tie(*xs):
    return lax.optimization_barrier(xs)


def add(*terms):
    y=terms[0].astype(F32)
    for x in terms[1:]:
        y=y+x.astype(F32)
    return y.astype(BF)


def upper(terms,n):
    return add(*[x[n:2*n] for x in terms])


def plane_rows(g,x):
    x=x.reshape(g.Z,-1,HC)
    return [lax.dynamic_index_in_dim(x,g.z^j,0,keepdims=False) for j in range(1,g.Z)]


def plane_send(g,rows):
    return [g.plane(x,j) for j,x in enumerate(rows,1)]


def plane_sum(g,x,parts):
    mine=lax.dynamic_index_in_dim(x.reshape(g.Z,-1,HC),g.z,0,keepdims=False).astype(F32)
    for p in parts:
        mine=mine+p.astype(F32)
    return mine.astype(BF)


def plane_join(g,mine,parts):
    out=jnp.zeros((g.Z,)+mine.shape,BF)
    for j,p in enumerate([mine]+parts):
        out=lax.dynamic_update_index_in_dim(out,p,g.z^j,0)
    return out.reshape(-1,HC)


def local(tokens,segments,time_steps,time_table,ln1_gain,ln1_bias,q_weight,q_bias,k_weight,v_weight,v_bias,o_weight,o_bias,ln2_gain,ln2_bias,up_weight,up_bias,down_weight,down_bias,cotangent):
    nseq=tokens.shape[0]
    T=nseq*L
    g=Ring(lax.axis_size("rep"),lax.axis_size("shard"))
    S=g.S
    w=ln1_gain.shape[0]
    fr=down_weight.shape[0]
    own=time_table.shape[0]
    idx=g.index()
    r=g.z*2+g.c
    me=jnp.stack([r,g.s,r*S+g.s]).astype(jnp.int32)
    small,ids=small_rows(me,time_steps,(ln1_gain,ln1_bias,q_bias,v_bias,o_bias,ln2_gain,ln2_bias,down_bias,up_bias))
    small,segments,o_weight_,q_weight_=tie(small,segments,o_weight,q_weight)
    pack_a=pack(pack_a_kernel,idx,(q_weight_,k_weight,v_weight),"pack_a")
    mine_a=[g.direct(pack_a,j) for j in range(1,S)]
    segments,pack_a=tie(segments,pack_a)
    vec=small.astype(F32)
    for j in reversed(range(1,S)):
        vec=vec+g.direct(small,j).astype(F32)
    steps=vec[NV,:S*nseq]*32.0+vec[NV+1,:S*nseq]
    hit=steps.astype(jnp.int32)[:,None]==jnp.arange(own)[None,:]+g.s*own
    rows=jnp.dot(hit.astype(BF),time_table,preferred_element_type=F32).astype(BF).reshape(S,nseq,D)
    pick=lambda j: lax.dynamic_index_in_dim(rows,g.s^j,0,keepdims=False)
    picks=[pick(j) for j in range(S)]
    picks[0],*mine_a=tie(picks[0],*mine_a)
    row=picks[0].astype(F32)
    for j in range(1,S):
        row=row+g.direct(picks[j],j).astype(F32)
    row=row.reshape(nseq,1,D)
    pack_b=pack(pack_b_kernel,idx,(o_weight_,up_weight,down_weight),"pack_b")
    tok=tokens.reshape(T,D)
    cot=cotangent.reshape(T,D)
    fq,fk=seg_features(segments.reshape(T))
    counts=jnp.sum(segments[:,:,None]==jnp.arange(4),axis=1)
    before=jnp.cumsum(counts==MAIN,axis=1)==0
    np_=D//128
    starts=jnp.concatenate([jnp.sum(jnp.where(before,counts,0),axis=1).astype(jnp.int32),
        jnp.array([i//np_ for i in range(nseq*np_)]+[i%np_ for i in range(nseq*np_)],jnp.int32)])
    fq,fk,pack_b,row,*mine_a=tie(fq,fk,pack_b,row,*mine_a)
    other_a=[g.core(x) for x in mine_a]
    mine_b=[pack_b]
    first=[g.step(pack_b,t) for t in range(g.nb)]
    q,k,v,n1t,wqkv=qkv(idx,tok,row,vec,(q_weight,k_weight,v_weight),mine_a,other_a)
    fwd=attn_fwd(starts,q,k,v,fq,fk,(),0,3*nseq//2)
    o1,fx1,*first=tie(*fwd,*first)
    for t in range(g.nb):
        mine_b=mine_b+[first[t]]+[g.step(x,t) for x in mine_b[1:]]
    direct=[1<<t for t in range(g.nb)]
    other_b=[None]+[g.core(x) if j in direct else None for j,x in enumerate(mine_b[1:],1)]
    fwd=attn_fwd(starts,q,k,v,fq,fk,(o1,fx1),3*nseq//2,3*nseq)
    late=[j for j in range(1,S) if j not in direct]
    o1,fx1,*got=tie(*fwd,*[mine_b[j] for j in late])
    for j,x in zip(late,got):
        mine_b[j]=x
        other_b[j]=g.core(x)
    att,fx=attn_fwd(starts,q,k,v,fq,fk,(o1,fx1),9*nseq//2,6*nseq-9*nseq//2)
    res,gm,ga,keep_b,send_b,sv2,sub=mid(idx,tok,row,att,cot,vec,(o_weight,up_weight,down_weight),mine_b[1:],other_b[1:])
    cuts=[0,nseq,nseq+5*nseq//2,5*nseq,6*nseq]
    call=lambda prev,i: attn_bwd(starts,q,k,v,fx,fk,att,ga,prev,cuts[i],cuts[i+1]-cuts[i])
    got=g.core(send_b)
    d=call((),0)
    d,got=tie(d,got)
    n=S
    x=[keep_b]
    for t in reversed(range(g.nb)):
        n//=2
        x=x+[got]
        up=upper(x,n)
        d,up=tie(d,up)
        got=g.step(up,t)
        i=g.nb-t
        if i<=2:
            d=call((d,),i)
            d,got=tie(d,got)
    xb=add(*[y[0] for y in x],got[0])
    d,xb,*rows_b=tie(d,xb,*plane_rows(g,xb))
    parts=plane_send(g,rows_b)
    d=call((d,),3)
    keep_a,send_a,svq=dw(idx,n1t,d,S)
    keep_a,send_a,*parts=tie(keep_a,send_a,*parts)
    got=g.core(send_a)
    mine_=plane_sum(g,xb,parts)
    back=[g.plane(mine_,j) for j in range(1,g.Z)]
    gm,mine_,got=tie(gm,mine_,got)
    outs=[add(keep_a[j],got[j]) for j in range(1,S)]
    gm,*outs=tie(gm,*outs)
    gots=[g.direct2(x,j) for j,x in enumerate(outs,1)]
    gt,sv1,ts=dx(tok,row,d,gm,wqkv,vec)
    sv1,back[0],*gots=tie(sv1,back[0],*gots)
    xa=add(keep_a[0],got[0],*gots)
    sv1,*rows_a=tie(sv1,*plane_rows(g,xa))
    parts_a=plane_send(g,rows_a)
    pay=sums(me,ids,sv1,svq,sv2,sub,ts,g.R*S*nseq)
    pay=add(pay,g.core(pay))
    for t in range(g.nb):
        pay=add(pay,g.direct(pay,1<<t))
    out_b=plane_join(g,mine_,back)
    out_b,pay,*parts_a=tie(out_b,pay,*parts_a)
    other_b=g.core(out_b)
    mine=plane_sum(g,xa,parts_a)
    pay,mine=tie(pay,mine)
    back_a=[g.plane(mine,j) for j in range(1,g.Z)]
    j=1
    while j<g.Z:
        pay=add(pay,g.plane(pay,j))
        j*=2
    go,gup,gdn=unpack(idx,out_b,other_b,((w,1),(w,4),(fr,1)))
    gup,pay,*back_a=tie(gup,pay,*back_a)
    out_a=plane_join(g,mine,back_a)
    other_a=g.core(out_a)
    vsum,gtab=table(me,pay,own)
    vsum,other_a=tie(vsum,other_a)
    gq,gk,gv=unpack(idx,out_a,other_a,((w,1),)*3)
    sums8=lax.dynamic_slice_in_dim(vsum[:8],g.s*w,w,1)
    subs=lax.dynamic_slice_in_dim(vsum[8:NV].reshape(FF),g.s*up_bias.shape[0],up_bias.shape[0],0)
    return (res.reshape(tokens.shape),gt.reshape(tokens.shape),gtab,sums8[0],sums8[1],gq,sums8[2],gk,gv,sums8[3],go,sums8[4],sums8[5],sums8[6],gup,subs,gdn,sums8[7])


def solution(mesh):
    b=("rep","shard")
    s=P("shard")
    m=P("shard",None)
    t=P(b,None,None)
    return jax.shard_map(local,mesh=mesh,
        in_specs=(t,P(b,None),P(b),m,s,s,m,s,m,m,s,m,s,s,s,m,s,m,s,t),
        out_specs=(t,t,m,s,s,m,s,m,m,s,m,s,s,s,m,s,m,s),check_vma=False)
```

```python
import functools
import math

import jax
import jax.numpy as jnp
from jax import lax
from jax.experimental import pallas as pl
from jax.experimental.pallas import tpu as pltpu
from jax.sharding import PartitionSpec as P

NEG=-1e30
EPS=1e-5
L=1024
D=768
FF=3072
HC=D//2
BF=jnp.bfloat16
F32=jnp.float32
LOG2E=math.log2(math.e)
LN2=math.log(2.0)
QS=0.125*LOG2E
VR=14
VP=16
NV=12
ANY=pl.BlockSpec(memory_space=pl.ANY)
S_=jax.ShapeDtypeStruct


def nt(a,b):
    return lax.dot_general(a,b,(((1,),(1,)),((),())),preferred_element_type=F32)


def nn(a,b):
    return lax.dot_general(a,b,(((1,),(0,)),((),())),preferred_element_type=F32)


def tn(a,b):
    return lax.dot_general(a,b,(((0,),(0,)),((),())),preferred_element_type=F32)


def full(*s):
    return pl.BlockSpec(s,lambda i,*_:(0,)*len(s),pipeline_mode=pl.Buffered(1))


def norm(x):
    mean=jnp.mean(x,axis=1,keepdims=True)
    off=x-mean
    var=jnp.mean(off*off,axis=1,keepdims=True)
    r=lax.rsqrt(var+EPS)
    return off*r,r


def sum8(x):
    return jnp.sum(x.reshape(x.shape[0]//8,8,x.shape[1]),axis=0)


def cost(flops,nbytes,trans=0):
    return pl.CostEstimate(flops=int(flops)//10,bytes_accessed=int(nbytes)//10,transcendentals=int(trans)//10)


def seg_features(seg):
    lane=jnp.arange(128)%64
    hit=seg[:,None]==lane[None,:]
    first=(lane<4)[None]
    fq=jnp.where(first&hit,1.0,0.0).astype(BF)
    fk=jnp.where(first,jnp.where(hit,0.0,NEG),jnp.where((lane<7)[None],1.0,0.0)).astype(BF)
    return fq,fk


def qkv_kernel(idx_ref,*refs,ns,wr):
    tok_ref,row_ref,vec_ref=refs[:3]
    own=refs[3:6]
    mine=refs[6:6+ns-1]
    other=refs[6+ns-1:6+2*(ns-1)]
    hi=6+2*(ns-1)
    q_ref,k_ref,v_ref,nt_ref,w_ref,sem=refs[hi:hi+6]
    @pl.when(pl.program_id(0)==0)
    def _():
        c=idx_ref[0]
        cps=[]
        def put(src,w,sh,c0,nc):
            dst=w_ref.at[w,pl.ds(pl.multiple_of(sh*wr,16),wr),pl.ds(c0,nc)]
            cp=pltpu.make_async_copy(src,dst,sem.at[len(cps)])
            cp.start()
            cps.append(cp)
        for w in range(3):
            put(own[w],w,idx_ref[1],0,D)
        for j in range(1,ns):
            for w in range(3):
                put(mine[j-1].at[pl.ds(w*wr,wr)],w,idx_ref[1+j],pl.multiple_of(c*HC,128),HC)
                put(other[j-1].at[pl.ds(w*wr,wr)],w,idx_ref[1+j],pl.multiple_of((1-c)*HC,128),HC)
        for cp in cps:
            cp.wait()
    xhat,_=norm(tok_ref[...]+row_ref[0])
    n1=(xhat*vec_ref[0:1,:]+vec_ref[1:2,:]).astype(BF)
    q_ref[...]=((nn(n1,w_ref[0])+vec_ref[2:3,:])*QS).astype(BF)
    k_ref[...]=nn(n1,w_ref[1]).astype(BF)
    v_ref[...]=(nn(n1,w_ref[2])+vec_ref[3:4,:]).astype(BF)
    nt_ref[...]=n1.T


def qkv(idx,tok,row,vec,own,mine,other,tb=512):
    T=tok.shape[0]
    per=L//tb
    ns=len(mine)+1
    wr=own[0].shape[0]
    blk=pl.BlockSpec((tb,D),lambda i,*_:(i,0))
    return pl.pallas_call(
        functools.partial(qkv_kernel,ns=ns,wr=wr),
        grid_spec=pltpu.PrefetchScalarGridSpec(
            num_scalar_prefetch=1,grid=(T//tb,),
            in_specs=[blk,pl.BlockSpec((1,1,D),lambda i,*_:(i//per,0,0)),full(VR,D)]+[ANY]*(3+2*(ns-1)),
            out_specs=[blk]*3+[pl.BlockSpec((D,tb),lambda i,*_:(0,i)),full(3,D,D)],
            scratch_shapes=[pltpu.SemaphoreType.DMA((3+6*(ns-1),))]),
        out_shape=[S_((T,D),BF)]*3+[S_((D,T),BF),S_((3,D,D),BF)],
        compiler_params=pltpu.CompilerParams(dimension_semantics=("arbitrary",)),
        cost_estimate=cost(6*T*D*D,T*D*10+9*D*D),
        name="qkv")(idx,tok,row,vec,*own,*mine,*other)


def pack_a_kernel(idx_ref,q_ref,k_ref,v_ref,out_ref):
    wr=q_ref.shape[0]
    for ch in (0,1):
        @pl.when(idx_ref[0]==ch)
        def _():
            for w,ref in enumerate((q_ref,k_ref,v_ref)):
                out_ref[w*wr:(w+1)*wr,:]=ref[:,ch*HC:(ch+1)*HC]


def pack_b_kernel(idx_ref,o_ref,u_ref,d_ref,out_ref):
    wr=o_ref.shape[0]
    for ch in (0,1):
        @pl.when(idx_ref[0]==ch)
        def _():
            out_ref[0:wr,:]=o_ref[:,ch*HC:(ch+1)*HC]
            for b in range(4):
                out_ref[wr+b*wr:2*wr+b*wr,:]=u_ref[:,(ch*4+b)*HC:(ch*4+b+1)*HC]
            out_ref[5*wr:,:]=d_ref[:,ch*HC:(ch+1)*HC]


def pack(kernel,idx,ws,name):
    rows=sum(x.shape[0]*x.shape[1]//D for x in ws)
    vm=pl.BlockSpec(memory_space=pltpu.VMEM)
    return pl.pallas_call(kernel,in_specs=[pl.BlockSpec(memory_space=pltpu.SMEM)]+[vm]*3,out_specs=vm,
        out_shape=S_((rows,HC),BF),cost_estimate=cost(0,4*rows*D),name=name)(idx,*ws)


MAIN=800
ROWS=816
LANES=896
REST=768


def windows(s):
    s16=(s//16)*16
    return pl.multiple_of(jnp.minimum(s16,L-ROWS),16),pl.multiple_of(jnp.minimum(s16,L-LANES),16)


def fwd_kernel(s_ref,q_ref,k_ref,v_ref,fq_ref,fk_ref,*refs,f0,ns):
    o_ref,fx_ref=refs[-2:]
    s0=s_ref[s_ref[ns+f0+pl.program_id(0)]]
    wr,wl=windows(s0)
    lane=lax.broadcasted_iota(jnp.int32,(1,128),1)
    lo=lane<64
    l6=lane&63
    rest_row=lax.broadcasted_iota(jnp.int32,(256,1),0)
    ahead=rest_row<s0
    qb=ROWS//3
    rest=lambda ref: jnp.where(ahead,ref[0:256,:],ref[REST:L,:])
    main=lambda ref: ref[pl.ds(wl,LANES),:]
    one=jnp.where(l6==0,1.0,0.0).astype(BF)
    kv=[]
    for take in (rest,main):
        k=take(k_ref)
        v=take(v_ref)
        fk=take(fk_ref)
        kv.append([(jnp.where(own,k,fk),jnp.where(own,v,one)) for own in (lo,~lo)])
    qf=[(rest(q_ref),rest(fq_ref))]
    for b in range(3):
        rows=pl.ds(pl.multiple_of(wr+b*qb,16),qb)
        qf.append((q_ref[rows,:],fq_ref[rows,:]))
    units=[(b,h) for b in range(4) for h in (0,1)]
    def score(b,h):
        return nt(jnp.where(lo if h==0 else ~lo,*qf[b]),kv[min(b,1)][h][0])
    pend=[score(*u) for u in units[:3]]
    accs=[]
    ls=[]
    for i,(b,h) in enumerate(units):
        s=pend.pop(0)
        if i+3<len(units):
            pend.append(score(*units[i+3]))
        m=jnp.max(s,axis=1,keepdims=True)
        p=jnp.exp2(s-m).astype(BF)
        acc=nn(p,kv[min(b,1)][h][1])
        l=acc[:,64:65] if h==0 else acc[:,0:1]
        accs.append(acc*(1.0/l))
        ls.append(-(m+jnp.log2(l)))
        if h==1:
            o=jnp.where(lo,accs[0],accs[1]).astype(BF)
            nl=jnp.where(lo,ls[1],ls[0])
            hi=nl.astype(BF).astype(F32)
            r1=nl-hi
            mid=r1.astype(BF).astype(F32)
            r2=r1-mid
            fx=jnp.where(l6==4,hi,jnp.where(l6==5,mid,jnp.where(l6==6,r2,qf[b][1].astype(F32)))).astype(BF)
            if b==0:
                o_ref[0:256,:]=o
                fx_ref[0:256,:]=fx
                o_ref[REST:L,:]=o
                fx_ref[REST:L,:]=fx
            else:
                at=wr+(b-1)*qb
                rows=pl.ds(pl.multiple_of(at,16),qb)
                pos=lax.broadcasted_iota(jnp.int32,(qb,1),0)+(at-s0)
                inside=(pos>=0)&(pos<MAIN)
                o_ref[rows,:]=jnp.where(inside,o,o_ref[rows,:])
                fx_ref[rows,:]=jnp.where(inside,fx,fx_ref[rows,:])
            accs=[]
            ls=[]


def attn_fwd(starts,q,k,v,fq,fk,prev,f0,n):
    T=q.shape[0]
    ns=T//L
    nu=ns*(D//128)
    blk=pl.BlockSpec((L,128),lambda i,s:(s[ns+f0+i],s[ns+nu+f0+i]))
    fb=pl.BlockSpec((L,128),lambda i,s:(s[ns+f0+i],0))
    prev=list(prev)
    return pl.pallas_call(
        functools.partial(fwd_kernel,f0=f0,ns=ns),
        grid_spec=pltpu.PrefetchScalarGridSpec(
            num_scalar_prefetch=1,grid=(n,),
            in_specs=[blk,blk,blk,fb,fb]+[ANY]*len(prev),out_specs=[blk,blk]),
        out_shape=[S_((T,D),BF)]*2,
        input_output_aliases={6+i:i for i in range(len(prev))},
        compiler_params=pltpu.CompilerParams(dimension_semantics=("arbitrary",)),
        cost_estimate=cost(n*2*4*L*L*256,n*L*128*14,n*2*L*L),
        name="attn_fwd")(starts,q,k,v,fq,fk,*prev)


def bwd_kernel(s_ref,q_ref,k_ref,v_ref,fx_ref,fk_ref,o_ref,do_ref,*refs,f0,ns):
    out_ref=refs[-1]
    s0=s_ref[s_ref[ns+f0+pl.program_id(0)]]
    wr,wl=windows(s0)
    lane=lax.broadcasted_iota(jnp.int32,(1,128),1)
    lo=lane<64
    l6=lane&63
    zero=jnp.zeros((),BF)
    ones2=jnp.where(l6<2,1.0,0.0).astype(BF)
    rest_row=lax.broadcasted_iota(jnp.int32,(256,1),0)
    ahead=rest_row<s0
    rest=lambda ref: jnp.where(ahead,ref[0:256,:],ref[REST:L,:])
    def block(take_k,nk,takes):
        k=take_k(k_ref)
        v=take_k(v_ref)
        fk=take_k(fk_ref)
        kx=[]
        vx=[]
        km=[]
        for own in (lo,~lo):
            kx.append(jnp.where(own,k,fk))
            vx.append(jnp.where(own,v,ones2))
            km.append(jnp.where(own,k,zero))
        dv=jnp.zeros((nk,128),F32)
        dk=jnp.zeros((nk,128),F32)
        dqs=[]
        for take in takes:
            q=take(q_ref)
            fx=take(fx_ref)
            do=take(do_ref)
            prod=do.astype(F32)*take(o_ref).astype(F32)
            d0=-jnp.sum(jnp.where(lo,prod,0.0),axis=1,keepdims=True)
            d1=-jnp.sum(jnp.where(lo,0.0,prod),axis=1,keepdims=True)
            nd=jnp.where(lo,d1,d0)
            hi=nd.astype(BF).astype(F32)
            fd=jnp.where(l6==0,hi,jnp.where(l6==1,nd-hi,0.0)).astype(BF)
            dq=jnp.zeros(q.shape,F32)
            for h,own in enumerate((lo,~lo)):
                p=jnp.exp2(nt(kx[h],jnp.where(own,q,fx)))
                dpt=nt(vx[h],jnp.where(own,do,fd))
                pb=p.astype(BF)
                ds=(p*dpt).astype(BF)
                dv=dv+nn(pb,jnp.where(own,do,zero))
                dk=dk+nn(ds,jnp.where(own,q,zero))
                dq=dq+tn(ds,km[h])
            dqs.append((dq*0.125).astype(BF))
        return dqs,(dk*LN2).astype(BF),dv.astype(BF)
    dqs,dk,dv=block(rest,256,[rest])
    for w,x in enumerate((dqs[0],dk,dv)):
        out_ref[w,0:256,:]=x
        out_ref[w,REST:L,:]=x
    at=lambda start,n: pl.ds(pl.multiple_of(start,16),n)
    cuts=[(0,256),(256,256),(512,256),(768,128)]
    dqs,dk,dv=block(lambda ref: ref[at(wr,ROWS),:],ROWS,[lambda ref,c=c: ref[at(wl+c[0],c[1]),:] for c in cuts])
    def put(w,start,x):
        n=x.shape[0]
        pos=lax.broadcasted_iota(jnp.int32,(n,1),0)+(start-s0)
        out_ref[w,at(start,n),:]=jnp.where((pos>=0)&(pos<MAIN),x,out_ref[w,at(start,n),:])
    for c,x in zip(cuts,dqs):
        put(0,wl+c[0],x)
    put(1,wr,dk)
    put(2,wr,dv)


def attn_bwd(starts,q,k,v,fx,fk,o,do,prev,f0,n):
    T=q.shape[0]
    ns=T//L
    nu=ns*(D//128)
    blk=pl.BlockSpec((L,128),lambda i,s:(s[ns+f0+i],s[ns+nu+f0+i]))
    fb=pl.BlockSpec((L,128),lambda i,s:(s[ns+f0+i],0))
    prev=list(prev)
    return pl.pallas_call(
        functools.partial(bwd_kernel,f0=f0,ns=ns),
        grid_spec=pltpu.PrefetchScalarGridSpec(
            num_scalar_prefetch=1,grid=(n,),
            in_specs=[blk,blk,blk,blk,fb,blk,blk]+[ANY]*len(prev),
            out_specs=pl.BlockSpec((3,L,128),lambda i,s:(0,s[ns+f0+i],s[ns+nu+f0+i]))),
        out_shape=S_((3,T,D),BF),
        input_output_aliases={8+i:i for i in range(len(prev))},
        compiler_params=pltpu.CompilerParams(dimension_semantics=("arbitrary",)),
        cost_estimate=cost(n*2*10*L*L*256,n*L*128*20,n*2*L*L),
        name="attn_bwd")(starts,q,k,v,fx,fk,o,do,*prev)


def mid_kernel(idx_ref,*refs,tb,fc,ns,wr,fr):
    tok_ref,row_ref,att_ref,cot_ref,vec_ref=refs[:5]
    own=refs[5:8]
    mine=refs[8:8+ns-1]
    other=refs[8+ns-1:8+2*(ns-1)]
    b0=8+2*(ns-1)
    res_ref,gm_ref,ga_ref,keep_ref,send_ref,sv_ref,sub_ref,ow,up,dn,aup,adn,aow,sem=refs[b0:]
    i=pl.program_id(0)
    n=pl.num_programs(0)
    c=idx_ref[0]
    def copies():
        cps=[]
        def put(src,dst):
            cps.append(pltpu.make_async_copy(src,dst,sem.at[len(cps)]))
        r16=lambda sh,m: pl.ds(pl.multiple_of(sh*m,16),m)
        sh=idx_ref[1+ns]
        put(own[0],ow.at[r16(sh,wr)])
        put(own[1],up.at[r16(sh,wr)])
        put(own[2],dn.at[r16(sh,fr)])
        for j in range(1,ns):
            for src,sh,cc in ((mine[j-1],idx_ref[1+ns+j],c),(other[j-1],idx_ref[1+2*ns+j],1-c)):
                cd=pl.ds(pl.multiple_of(cc*HC,128),HC)
                put(src.at[pl.ds(0,wr)],ow.at[r16(sh,wr),cd])
                for b in range(4):
                    put(src.at[pl.ds(wr+b*wr,wr)],up.at[r16(sh,wr),pl.ds(pl.multiple_of(cc*4*HC+b*HC,128),HC)])
                put(src.at[pl.ds(5*wr,fr)],dn.at[r16(sh,fr),cd])
        return cps
    @pl.when(i==0)
    def _():
        cps=copies()
        for cp in cps:
            cp.start()
        aup[...]=jnp.zeros_like(aup)
        adn[...]=jnp.zeros_like(adn)
        aow[...]=jnp.zeros_like(aow)
        sv_ref[...]=jnp.zeros_like(sv_ref)
        sub_ref[...]=jnp.zeros_like(sub_ref)
        for cp in cps:
            cp.wait()
    ob=vec_ref[4:5,:]
    g2=vec_ref[5:6,:]
    b2=vec_ref[6:7,:]
    db=vec_ref[7:8,:]
    att=att_ref[...]
    mixed=tok_ref[...]+row_ref[0]+nn(att,ow[...])+ob
    xhat,r=norm(mixed)
    n2=(xhat*g2+b2).astype(BF)
    n2t=n2.T
    cot=cot_ref[...]
    g=cot.astype(BF)
    res=mixed+db
    gn2=jnp.zeros((tb,D),F32)
    for j in range(FF//fc):
        cs=slice(j*fc,(j+1)*fc)
        pre=nn(n2,up[:,cs])+vec_ref[8+j:9+j,:]
        gact=nt(g,dn[cs,:])
        phi=0.5+0.5*lax.erf(pre*(2**-0.5))
        pdf=jnp.exp2(pre*pre*(-0.5*LOG2E))*(1.0/math.sqrt(2*math.pi))
        act=(pre*phi).astype(BF)
        gp=gact*(phi+pre*pdf)
        gpre=gp.astype(BF)
        sub_ref[:,cs]+=sum8(gp)
        res=res+nn(act,dn[cs,:])
        gn2=gn2+nt(gpre,up[:,cs])
        adn[cs,:]+=tn(act,g)
        aup[:,cs]+=nn(n2t,gpre)
    res_ref[...]=res
    e=gn2*g2
    c1=jnp.mean(e,axis=1,keepdims=True)
    c2=jnp.mean(e*xhat,axis=1,keepdims=True)
    gm=cot+r*(e-c1-xhat*c2)
    gml=gm.astype(BF)
    gm_ref[...]=gml
    ga_ref[...]=nt(gml,ow[...]).astype(BF)
    aow[...]+=tn(att,gml)
    sv_ref[0:8,:]+=sum8(gm)
    sv_ref[8:16,:]+=sum8(gn2*xhat)
    sv_ref[16:24,:]+=sum8(gn2)
    sv_ref[24:32,:]+=sum8(cot)
    @pl.when(i==n-1)
    def _():
        for ref,base,odd in ((keep_ref,1+ns,0),(send_ref,1+2*ns,1)):
            for ch in (0,1):
                @pl.when(c==(ch+odd)%2)
                def _():
                    def body(j,carry):
                        sh=idx_ref[base+j]
                        rw=pl.ds(pl.multiple_of(sh*wr,8),wr)
                        ref[j,0:wr,:]=aow[rw,ch*HC:(ch+1)*HC].astype(BF)
                        for b in range(4):
                            lo=(ch*4+b)*HC
                            ref[j,wr+b*wr:2*wr+b*wr,:]=aup[rw,lo:lo+HC].astype(BF)
                        ref[j,5*wr:5*wr+fr,:]=adn[pl.ds(pl.multiple_of(sh*fr,8),fr),ch*HC:(ch+1)*HC].astype(BF)
                        return carry
                    lax.fori_loop(0,ns,body,0)


def mid(idx,tok,row,att,cot,vec,own,mine,other,tb=256,fc=D):
    T=tok.shape[0]
    per=L//tb
    ns=len(mine)+1
    wr=own[0].shape[0]
    fr=own[2].shape[0]
    rb=5*wr+fr
    blk=pl.BlockSpec((tb,D),lambda i,*_:(i,0))
    return pl.pallas_call(
        functools.partial(mid_kernel,tb=tb,fc=fc,ns=ns,wr=wr,fr=fr),
        grid_spec=pltpu.PrefetchScalarGridSpec(
            num_scalar_prefetch=1,grid=(T//tb,),
            in_specs=[blk,pl.BlockSpec((1,1,D),lambda i,*_:(i//per,0,0)),blk,blk,full(VR,D)]+[ANY]*(3+2*(ns-1)),
            out_specs=[blk,blk,blk,full(ns,rb,HC),full(ns,rb,HC),full(32,D),full(8,FF)],
            scratch_shapes=[pltpu.VMEM((D,D),BF),pltpu.VMEM((D,FF),BF),pltpu.VMEM((FF,D),BF),
                pltpu.VMEM((D,FF),F32),pltpu.VMEM((FF,D),F32),pltpu.VMEM((D,D),F32),
                pltpu.SemaphoreType.DMA((3+12*(ns-1),))]),
        out_shape=[S_((T,D),F32),S_((T,D),BF),S_((T,D),BF),S_((ns,rb,HC),BF),S_((ns,rb,HC),BF),S_((32,D),F32),S_((8,FF),F32)],
        compiler_params=pltpu.CompilerParams(dimension_semantics=("arbitrary",),vmem_limit_bytes=67043328),
        cost_estimate=cost(6*T*D*(D+2*FF),T*D*20+30*D*FF,2*T*FF),
        name="mid")(idx,tok,row,att,cot,vec,*own,*mine,*other)


def dw_kernel(idx_ref,nt_ref,d_ref,keep_ref,send_ref,sv_ref,acc,*,ns,wr):
    i=pl.program_id(0)
    c=idx_ref[0]
    @pl.when(i==0)
    def _():
        acc[...]=jnp.zeros_like(acc)
        sv_ref[...]=jnp.zeros_like(sv_ref)
    for w in range(3):
        acc[w]+=nn(nt_ref[...],d_ref[w])
    sv_ref[0:8,:]+=sum8(d_ref[0].astype(F32))
    sv_ref[8:16,:]+=sum8(d_ref[2].astype(F32))
    @pl.when(i==pl.num_programs(0)-1)
    def _():
        for ref,base,odd in ((keep_ref,1+ns,0),(send_ref,1+2*ns,1)):
            for ch in (0,1):
                @pl.when(c==(ch+odd)%2)
                def _():
                    def body(j,carry):
                        rw=pl.ds(pl.multiple_of(idx_ref[base+j]*wr,8),wr)
                        for w in range(3):
                            ref[j,w*wr:(w+1)*wr,:]=acc[w,rw,ch*HC:(ch+1)*HC].astype(BF)
                        return carry
                    lax.fori_loop(0,ns,body,0)


def dw(idx,n1t,d,ns,tb=512):
    T=n1t.shape[1]
    wr=D//ns
    return pl.pallas_call(
        functools.partial(dw_kernel,ns=ns,wr=wr),
        grid_spec=pltpu.PrefetchScalarGridSpec(
            num_scalar_prefetch=1,grid=(T//tb,),
            in_specs=[pl.BlockSpec((D,tb),lambda i,*_:(0,i)),pl.BlockSpec((3,tb,D),lambda i,*_:(0,i,0))],
            out_specs=[full(ns,3*wr,HC),full(ns,3*wr,HC),full(16,D)],
            scratch_shapes=[pltpu.VMEM((3,D,D),F32)]),
        out_shape=[S_((ns,3*wr,HC),BF)]*2+[S_((16,D),F32)],
        compiler_params=pltpu.CompilerParams(dimension_semantics=("arbitrary",)),
        cost_estimate=cost(6*T*D*D,T*D*8+12*D*D),
        name="dw")(idx,n1t,d)


def dx_kernel(tok_ref,row_ref,d_ref,gm_ref,w_ref,vec_ref,gt_ref,sv_ref,ts_ref,*,per):
    i=pl.program_id(0)
    @pl.when(i==0)
    def _():
        sv_ref[...]=jnp.zeros_like(sv_ref)
    @pl.when(i%per==0)
    def _():
        ts_ref[...]=jnp.zeros_like(ts_ref)
    gn=nt(d_ref[0],w_ref[0])+nt(d_ref[1],w_ref[1])+nt(d_ref[2],w_ref[2])
    xhat,r=norm(tok_ref[...]+row_ref[0])
    e=gn*vec_ref[0:1,:]
    c1=jnp.mean(e,axis=1,keepdims=True)
    c2=jnp.mean(e*xhat,axis=1,keepdims=True)
    gt=gm_ref[...].astype(F32)+r*(e-c1-xhat*c2)
    gt_ref[...]=gt
    sv_ref[0:8,:]+=sum8(gn*xhat)
    sv_ref[8:16,:]+=sum8(gn)
    ts_ref[0]+=sum8(gt)


def dx(tok,row,d,gm,w,vec,tb=512):
    T=tok.shape[0]
    per=L//tb
    blk=pl.BlockSpec((tb,D),lambda i:(i,0))
    return pl.pallas_call(
        functools.partial(dx_kernel,per=per),grid=(T//tb,),
        in_specs=[blk,pl.BlockSpec((1,1,D),lambda i:(i//per,0,0)),pl.BlockSpec((3,tb,D),lambda i:(0,i,0)),blk,full(3,D,D),full(VR,D)],
        out_specs=[blk,full(16,D),pl.BlockSpec((1,8,D),lambda i:(i//per,0,0))],
        out_shape=[S_((T,D),F32),S_((16,D),F32),S_((T//L,8,D),F32)],
        compiler_params=pltpu.CompilerParams(dimension_semantics=("arbitrary",)),
        cost_estimate=cost(6*T*D*D,T*D*16+6*D*D),
        name="dx")(tok,row,d,gm,w,vec)


def rows8(x):
    return jnp.sum(x,axis=0,keepdims=True)


def sums_kernel(me_ref,id_ref,sv1_ref,svq_ref,sv2_ref,sub_ref,ts_ref,out_ref,acc,*,nseq):
    src=[sv1_ref[0:8],sv1_ref[8:16],svq_ref[0:8],svq_ref[8:16]]+[sv2_ref[8*i:8*i+8] for i in range(4)]
    src+=[sub_ref[:,i*D:(i+1)*D] for i in range(FF//D)]
    rows=[rows8(x) for x in src]+[id_ref[0:1],id_ref[1:2]]
    acc[...]=jnp.zeros_like(acc)
    for i in range(nseq):
        acc[me_ref[2]*nseq+i]=jnp.broadcast_to(rows8(ts_ref[i]),(1,D))
    out_ref[0:VP]=jnp.concatenate(rows+[jnp.zeros((VP-VR,D),F32)],axis=0).astype(BF)
    out_ref[VP:]=acc[...].reshape(acc.shape[0],D).astype(BF)


def sums(me,ids,sv1,svq,sv2,sub,ts,n):
    vm=pl.BlockSpec(memory_space=pltpu.VMEM)
    return pl.pallas_call(functools.partial(sums_kernel,nseq=ts.shape[0]),
        in_specs=[pl.BlockSpec(memory_space=pltpu.SMEM)]+[vm]*6,out_specs=vm,
        out_shape=S_((VP+n,D),BF),scratch_shapes=[pltpu.VMEM((n,1,D),F32)],
        cost_estimate=cost(0,10**6),name="sums")(me,ids,sv1,svq,sv2,sub,ts)


def table_kernel(me_ref,*refs,own):
    sum_ref,tab_ref=refs[-2:]
    tot=refs[0][...].astype(F32)
    for ref in refs[1:-2]:
        tot=tot+ref[...].astype(F32)
    n=tot.shape[0]-VP
    sum_ref[...]=tot[0:VP]
    ids=tot[NV:NV+1,0:n]*32.0+tot[NV+1:NV+2,0:n]
    line=lax.broadcasted_iota(jnp.int32,(own,n),0)+me_ref[1]*own
    hit=jnp.where(line==ids.astype(jnp.int32),1.0,0.0).astype(BF)
    tab_ref[...]=nn(hit,tot[VP:].astype(BF))


def table(me,pays,own):
    vm=pl.BlockSpec(memory_space=pltpu.VMEM)
    return pl.pallas_call(functools.partial(table_kernel,own=own),
        in_specs=[pl.BlockSpec(memory_space=pltpu.SMEM)]+[vm]*len(pays),out_specs=[vm,vm],
        out_shape=[S_((VP,D),F32),S_((own,D),F32)],
        cost_estimate=cost(0,4*10**6),name="table")(me,*pays)


def unpack_kernel(idx_ref,a_ref,b_ref,*outs,parts):
    for ch in (0,1):
        @pl.when(idx_ref[0]==ch)
        def _():
            for h,ref in enumerate((a_ref,b_ref) if ch==0 else (b_ref,a_ref)):
                r0=0
                for out,(nr,nb) in zip(outs,parts):
                    for b in range(nb):
                        out[:,(h*nb+b)*HC:(h*nb+b+1)*HC]=ref[r0:r0+nr,:].astype(F32)
                        r0+=nr


def unpack(idx,a,b,parts):
    vm=pl.BlockSpec(memory_space=pltpu.VMEM)
    return pl.pallas_call(functools.partial(unpack_kernel,parts=parts),
        in_specs=[pl.BlockSpec(memory_space=pltpu.SMEM),vm,vm],out_specs=[vm]*len(parts),
        out_shape=[S_((nr,2*nb*HC),F32) for nr,nb in parts],
        cost_estimate=cost(0,12*a.shape[0]*HC),name="unpack")(idx,a,b)


def small_kernel(me_ref,ts_ref,*refs,w,fr,nseq):
    vecs=refs[:9]
    out_ref,id_ref=refs[9:]
    def spread(rows,width,at):
        n=rows[0].shape[1]
        y=jnp.concatenate(rows+[jnp.zeros((8-len(rows),n),F32)]*(len(rows)<8),axis=0)
        y=jnp.concatenate([y,jnp.zeros((8,width-n),F32)],axis=1)
        return pltpu.roll(y,at,1)
    row=lambda ref: ref[...].astype(F32).reshape(1,ref.shape[0])
    v=spread([row(r) for r in vecs[:8]],D,me_ref[1]*w)
    u=spread([row(vecs[8])],FF,me_ref[1]*fr)
    lane=lax.broadcasted_iota(jnp.int32,(1,D),1)
    def steps(at,high):
        y=jnp.zeros((1,D),jnp.int32)
        for i in range(nseq):
            t=ts_ref[i]
            y=jnp.where(lane==at*nseq+i,t//32 if high else t%32,y)
        return y.astype(F32)
    id_ref[...]=jnp.concatenate([steps(me_ref[2],True),steps(me_ref[2],False)],axis=0)
    out_ref[...]=jnp.concatenate([v]+[u[0:1,i*D:(i+1)*D] for i in range(FF//D)]+[steps(me_ref[1],True),steps(me_ref[1],False)],axis=0).astype(BF)


def small_rows(me,time_steps,vecs):
    vm=pl.BlockSpec(memory_space=pltpu.VMEM)
    sm=pl.BlockSpec(memory_space=pltpu.SMEM)
    return pl.pallas_call(functools.partial(small_kernel,w=vecs[0].shape[0],fr=vecs[8].shape[0],nseq=time_steps.shape[0]),
        in_specs=[sm,sm]+[vm]*9,out_specs=[vm,vm],
        out_shape=[S_((VR,D),BF),S_((2,D),F32)],cost_estimate=cost(0,10**6),name="small")(me,time_steps,*vecs)


class Ring:
    def __init__(self,rep,shard):
        self.R,self.S=rep,shard
        self.nb=shard.bit_length()-1
        self.Z=rep//2
        r=lax.axis_index("rep")
        self.s=lax.axis_index("shard")
        self.c=r%2
        self.z=r//2

    def move(self,x,to):
        pairs=[]
        for r in range(self.R):
            for s in range(self.S):
                r2,s2=to(r,s)
                pairs.append((r*self.S+s,r2*self.S+s2))
        return lax.ppermute(x,("rep","shard"),pairs)

    def order(self,c,t):
        return (t+c*(self.nb//2))%self.nb

    def mask(self,c,j):
        m=0
        for t in range(self.nb):
            if j>>t&1:
                m|=1<<self.order(c,t)
        return m

    def step(self,x,t):
        return self.move(x,lambda r,s:(r,s^(1<<self.order(r%2,t))))

    def direct(self,x,j):
        return self.move(x,lambda r,s:(r,s^j))

    def core(self,x):
        return self.move(x,lambda r,s:(r^1,s))

    def plane(self,x,j):
        return self.move(x,lambda r,s:(r^(2*j),s))

    def direct2(self,x,j):
        return self.move(x,lambda r,s:(r,s^self.mask(r%2,j)))

    def index(self):
        m=[[self.mask(c,j) for j in range(self.S)] for c in (0,1)]
        base=list(range(self.S))
        t=jnp.where(self.c==0,jnp.array([0]+base+m[0]+m[1],jnp.int32),jnp.array([0]+base+m[1]+m[0],jnp.int32))
        head=jnp.arange(1+3*self.S)==0
        return jnp.where(head,self.c,t^self.s).astype(jnp.int32)


def tie(*xs):
    return lax.optimization_barrier(xs)


def add(*terms):
    y=terms[0].astype(F32)
    for x in terms[1:]:
        y=y+x.astype(F32)
    return y.astype(BF)


def upper(terms,n):
    return add(*[x[n:2*n] for x in terms])


def plane_rows(g,x):
    x=x.reshape(g.Z,-1,HC)
    return [lax.dynamic_index_in_dim(x,g.z^j,0,keepdims=False) for j in range(1,g.Z)]


def plane_send(g,rows):
    return [g.plane(x,j) for j,x in enumerate(rows,1)]


def plane_sum(g,x,parts):
    mine=lax.dynamic_index_in_dim(x.reshape(g.Z,-1,HC),g.z,0,keepdims=False).astype(F32)
    for p in parts:
        mine=mine+p.astype(F32)
    return mine.astype(BF)


def plane_join(g,mine,parts):
    out=jnp.zeros((g.Z,)+mine.shape,BF)
    for j,p in enumerate([mine]+parts):
        out=lax.dynamic_update_index_in_dim(out,p,g.z^j,0)
    return out.reshape(-1,HC)


def local(tokens,segments,time_steps,time_table,ln1_gain,ln1_bias,q_weight,q_bias,k_weight,v_weight,v_bias,o_weight,o_bias,ln2_gain,ln2_bias,up_weight,up_bias,down_weight,down_bias,cotangent):
    nseq=tokens.shape[0]
    T=nseq*L
    g=Ring(lax.axis_size("rep"),lax.axis_size("shard"))
    S=g.S
    w=ln1_gain.shape[0]
    fr=down_weight.shape[0]
    own=time_table.shape[0]
    idx=g.index()
    r=g.z*2+g.c
    me=jnp.stack([r,g.s,r*S+g.s]).astype(jnp.int32)
    small,ids=small_rows(me,time_steps,(ln1_gain,ln1_bias,q_bias,v_bias,o_bias,ln2_gain,ln2_bias,down_bias,up_bias))
    small,segments,o_weight_,q_weight_=tie(small,segments,o_weight,q_weight)
    pack_a=pack(pack_a_kernel,idx,(q_weight_,k_weight,v_weight),"pack_a")
    mine_a=[g.direct(pack_a,j) for j in range(1,S)]
    segments,pack_a=tie(segments,pack_a)
    vec=small.astype(F32)
    for j in reversed(range(1,S)):
        vec=vec+g.direct(small,j).astype(F32)
    steps=vec[NV,:S*nseq]*32.0+vec[NV+1,:S*nseq]
    hit=steps.astype(jnp.int32)[:,None]==jnp.arange(own)[None,:]+g.s*own
    rows=jnp.dot(hit.astype(BF),time_table,preferred_element_type=F32).astype(BF).reshape(S,nseq,D)
    pick=lambda j: lax.dynamic_index_in_dim(rows,g.s^j,0,keepdims=False)
    picks=[pick(j) for j in range(S)]
    picks[0],*mine_a=tie(picks[0],*mine_a)
    row=picks[0].astype(F32)
    for j in range(1,S):
        row=row+g.direct(picks[j],j).astype(F32)
    row=row.reshape(nseq,1,D)
    pack_b=pack(pack_b_kernel,idx,(o_weight_,up_weight,down_weight),"pack_b")
    tok=tokens.reshape(T,D)
    cot=cotangent.reshape(T,D)
    fq,fk=seg_features(segments.reshape(T))
    counts=jnp.sum(segments[:,:,None]==jnp.arange(4),axis=1)
    before=jnp.cumsum(counts==MAIN,axis=1)==0
    np_=D//128
    starts=jnp.concatenate([jnp.sum(jnp.where(before,counts,0),axis=1).astype(jnp.int32),
        jnp.array([i//np_ for i in range(nseq*np_)]+[i%np_ for i in range(nseq*np_)],jnp.int32)])
    other_a=[g.core(x) for x in mine_a]
    fq,fk,pack_b,row,*mine_a=tie(fq,fk,pack_b,row,*mine_a)
    mine_b=[pack_b]
    first=[g.step(pack_b,t) for t in range(g.nb)]
    q,k,v,n1t,wqkv=qkv(idx,tok,row,vec,(q_weight,k_weight,v_weight),mine_a,other_a)
    fwd=attn_fwd(starts,q,k,v,fq,fk,(),0,3*nseq//2)
    o1,fx1,*first=tie(*fwd,*first)
    for t in range(g.nb):
        mine_b=mine_b+[first[t]]+[g.step(x,t) for x in mine_b[1:]]
    direct=[1<<t for t in range(g.nb)]
    other_b=[None]+[g.core(x) if j in direct else None for j,x in enumerate(mine_b[1:],1)]
    fwd=attn_fwd(starts,q,k,v,fq,fk,(o1,fx1),3*nseq//2,3*nseq)
    late=[j for j in range(1,S) if j not in direct]
    o1,fx1,*got=tie(*fwd,*[mine_b[j] for j in late])
    for j,x in zip(late,got):
        mine_b[j]=x
        other_b[j]=g.core(x)
    att,fx=attn_fwd(starts,q,k,v,fq,fk,(o1,fx1),9*nseq//2,6*nseq-9*nseq//2)
    res,gm,ga,keep_b,send_b,sv2,sub=mid(idx,tok,row,att,cot,vec,(o_weight,up_weight,down_weight),mine_b[1:],other_b[1:])
    cuts=[0,nseq,nseq+5*nseq//2,5*nseq,6*nseq]
    call=lambda prev,i: attn_bwd(starts,q,k,v,fx,fk,att,ga,prev,cuts[i],cuts[i+1]-cuts[i])
    got=g.core(send_b)
    d=call((),0)
    d,got=tie(d,got)
    n=S
    x=[keep_b]
    for t in reversed(range(g.nb)):
        n//=2
        x=x+[got]
        up=upper(x,n)
        d,up=tie(d,up)
        got=g.step(up,t)
        i=g.nb-t
        if i<=2:
            d=call((d,),i)
            d,got=tie(d,got)
    xb=add(*[y[0] for y in x],got[0])
    d,xb,*rows_b=tie(d,xb,*plane_rows(g,xb))
    parts=plane_send(g,rows_b)
    d=call((d,),3)
    keep_a,send_a,svq=dw(idx,n1t,d,S)
    keep_a,send_a,*parts=tie(keep_a,send_a,*parts)
    got=g.core(send_a)
    mine_=plane_sum(g,xb,parts)
    back=[g.plane(mine_,j) for j in range(1,g.Z)]
    gm,mine_,got=tie(gm,mine_,got)
    outs=[add(keep_a[j],got[j]) for j in range(1,S)]
    gm,*outs=tie(gm,*outs)
    gots=[g.direct2(x,j) for j,x in enumerate(outs,1)]
    gt,sv1,ts=dx(tok,row,d,gm,wqkv,vec)
    sv1,back[0],*gots=tie(sv1,back[0],*gots)
    xa=add(keep_a[0],got[0],*gots)
    sv1,*rows_a=tie(sv1,*plane_rows(g,xa))
    parts_a=plane_send(g,rows_a)
    pay=sums(me,ids,sv1,svq,sv2,sub,ts,g.R*S*nseq)
    got_p=g.plane(pay,1)
    out_b=plane_join(g,mine_,back)
    hop=1
    while 2*hop<g.Z:
        pay=add(pay,got_p)
        hop*=2
        got_p=g.plane(pay,hop)
    pay,out_b,*parts_a=tie(pay,out_b,*parts_a)
    other_b=g.core(out_b)
    mine=plane_sum(g,xa,parts_a)
    back_a=[g.plane(mine,j) for j in range(1,g.Z)]
    pay=add(pay,got_p)
    got_p=g.core(pay)
    out_b,mine,pay=tie(out_b,mine,pay)
    go,gup,gdn=unpack(idx,out_b,other_b,((w,1),(w,4),(fr,1)))
    gup,got_p=tie(gup,got_p)
    pay=add(pay,got_p)
    pays=[g.direct(pay,j) for j in range(1,S)]
    pays[0],*back_a=tie(pays[0],*back_a)
    out_a=plane_join(g,mine,back_a)
    other_a=g.core(out_a)
    out_a,*pays=tie(out_a,*pays)
    vsum,gtab=table(me,[pay]+pays,own)
    gq,gk,gv=unpack(idx,out_a,other_a,((w,1),)*3)
    sums8=lax.dynamic_slice_in_dim(vsum[:8],g.s*w,w,1)
    subs=lax.dynamic_slice_in_dim(vsum[8:NV].reshape(FF),g.s*up_bias.shape[0],up_bias.shape[0],0)
    return (res.reshape(tokens.shape),gt.reshape(tokens.shape),gtab,sums8[0],sums8[1],gq,sums8[2],gk,gv,sums8[3],go,sums8[4],sums8[5],sums8[6],gup,subs,gdn,sums8[7])


def solution(mesh):
    b=("rep","shard")
    s=P("shard")
    m=P("shard",None)
    t=P(b,None,None)
    return jax.shard_map(local,mesh=mesh,
        in_specs=(t,P(b,None),P(b),m,s,s,m,s,m,m,s,m,s,s,s,m,s,m,s,t),
        out_specs=(t,t,m,s,s,m,s,m,m,s,m,s,s,s,m,s,m,s),check_vma=False)
```

```python
import functools
import math

import jax
import jax.numpy as jnp
from jax import lax
from jax.experimental import pallas as pl
from jax.experimental.pallas import tpu as pltpu
from jax.sharding import PartitionSpec as P

NEG=-1e30
EPS=1e-5
L=1024
D=768
FF=3072
HC=D//2
BF=jnp.bfloat16
F32=jnp.float32
LOG2E=math.log2(math.e)
LN2=math.log(2.0)
QS=0.125*LOG2E
VR=14
VP=16
NV=12
ANY=pl.BlockSpec(memory_space=pl.ANY)
S_=jax.ShapeDtypeStruct


def nt(a,b):
    return lax.dot_general(a,b,(((1,),(1,)),((),())),preferred_element_type=F32)


def nn(a,b):
    return lax.dot_general(a,b,(((1,),(0,)),((),())),preferred_element_type=F32)


def tn(a,b):
    return lax.dot_general(a,b,(((0,),(0,)),((),())),preferred_element_type=F32)


def full(*s):
    return pl.BlockSpec(s,lambda i,*_:(0,)*len(s),pipeline_mode=pl.Buffered(1))


def norm(x):
    mean=jnp.mean(x,axis=1,keepdims=True)
    off=x-mean
    var=jnp.mean(off*off,axis=1,keepdims=True)
    r=lax.rsqrt(var+EPS)
    return off*r,r


def sum8(x):
    return jnp.sum(x.reshape(x.shape[0]//8,8,x.shape[1]),axis=0)


def cost(flops,nbytes,trans=0):
    return pl.CostEstimate(flops=int(flops)//10,bytes_accessed=int(nbytes)//10,transcendentals=int(trans)//10)


def seg_features(seg):
    lane=jnp.arange(128)%64
    hit=seg[:,None]==lane[None,:]
    first=(lane<4)[None]
    fq=jnp.where(first&hit,1.0,0.0).astype(BF)
    fk=jnp.where(first,jnp.where(hit,0.0,NEG),jnp.where((lane<7)[None],1.0,0.0)).astype(BF)
    return fq,fk


def qkv_kernel(idx_ref,*refs,ns,wr):
    tok_ref,row_ref,vec_ref=refs[:3]
    own=refs[3:6]
    mine=refs[6:6+ns-1]
    other=refs[6+ns-1:6+2*(ns-1)]
    hi=6+2*(ns-1)
    q_ref,k_ref,v_ref,nt_ref,w_ref,sem=refs[hi:hi+6]
    def copies(w):
        c=idx_ref[0]
        cps=[]
        def put(src,sh,cols):
            rows=pl.ds(pl.multiple_of(sh*wr,16),wr)
            dst=w_ref.at[w,rows] if cols is None else w_ref.at[w,rows,pl.ds(pl.multiple_of(cols*HC,128),HC)]
            cps.append(pltpu.make_async_copy(src,dst,sem.at[w,len(cps)]))
        put(own[w],idx_ref[1],None)
        for j in range(1,ns):
            put(mine[j-1].at[pl.ds(w*wr,wr)],idx_ref[1+j],c)
            put(other[j-1].at[pl.ds(w*wr,wr)],idx_ref[1+j],1-c)
        return cps
    first=pl.program_id(0)==0
    @pl.when(first)
    def _():
        for w in range(3):
            for cp in copies(w):
                cp.start()
    def arrived(w):
        @pl.when(first)
        def _():
            for cp in copies(w):
                cp.wait()
    xhat,_=norm(tok_ref[...]+row_ref[0])
    n1=(xhat*vec_ref[0:1,:]+vec_ref[1:2,:]).astype(BF)
    arrived(0)
    q_ref[...]=((nn(n1,w_ref[0])+vec_ref[2:3,:])*QS).astype(BF)
    arrived(1)
    k_ref[...]=nn(n1,w_ref[1]).astype(BF)
    arrived(2)
    v_ref[...]=(nn(n1,w_ref[2])+vec_ref[3:4,:]).astype(BF)
    nt_ref[...]=n1.T


def qkv(idx,tok,row,vec,own,mine,other,tb=512):
    T=tok.shape[0]
    per=L//tb
    ns=len(mine)+1
    wr=own[0].shape[0]
    blk=pl.BlockSpec((tb,D),lambda i,*_:(i,0))
    return pl.pallas_call(
        functools.partial(qkv_kernel,ns=ns,wr=wr),
        grid_spec=pltpu.PrefetchScalarGridSpec(
            num_scalar_prefetch=1,grid=(T//tb,),
            in_specs=[blk,pl.BlockSpec((1,1,D),lambda i,*_:(i//per,0,0)),full(VR,D)]+[ANY]*(3+2*(ns-1)),
            out_specs=[blk]*3+[pl.BlockSpec((D,tb),lambda i,*_:(0,i)),full(3,D,D)],
            scratch_shapes=[pltpu.SemaphoreType.DMA((3,1+2*(ns-1)))]),
        out_shape=[S_((T,D),BF)]*3+[S_((D,T),BF),S_((3,D,D),BF)],
        compiler_params=pltpu.CompilerParams(dimension_semantics=("arbitrary",)),
        cost_estimate=cost(6*T*D*D,T*D*10+9*D*D),
        name="qkv")(idx,tok,row,vec,*own,*mine,*other)


def pack_a_kernel(idx_ref,q_ref,k_ref,v_ref,out_ref):
    wr=q_ref.shape[0]
    for ch in (0,1):
        @pl.when(idx_ref[0]==ch)
        def _():
            for w,ref in enumerate((q_ref,k_ref,v_ref)):
                out_ref[w*wr:(w+1)*wr,:]=ref[:,ch*HC:(ch+1)*HC]


def pack_b_kernel(idx_ref,o_ref,u_ref,d_ref,out_ref):
    wr=o_ref.shape[0]
    for ch in (0,1):
        @pl.when(idx_ref[0]==ch)
        def _():
            out_ref[0:wr,:]=o_ref[:,ch*HC:(ch+1)*HC]
            for b in range(4):
                out_ref[wr+b*wr:2*wr+b*wr,:]=u_ref[:,(ch*4+b)*HC:(ch*4+b+1)*HC]
            out_ref[5*wr:,:]=d_ref[:,ch*HC:(ch+1)*HC]


def pack(kernel,idx,ws,name):
    rows=sum(x.shape[0]*x.shape[1]//D for x in ws)
    vm=pl.BlockSpec(memory_space=pltpu.VMEM)
    return pl.pallas_call(kernel,in_specs=[pl.BlockSpec(memory_space=pltpu.SMEM)]+[vm]*3,out_specs=vm,
        out_shape=S_((rows,HC),BF),cost_estimate=cost(0,4*rows*D),name=name)(idx,*ws)


MAIN=800
ROWS=816
LANES=896
REST=768


def windows(s):
    s16=(s//16)*16
    return pl.multiple_of(jnp.minimum(s16,L-ROWS),16),pl.multiple_of(jnp.minimum(s16,L-LANES),16)


def fwd_kernel(s_ref,q_ref,k_ref,v_ref,fq_ref,fk_ref,*refs,f0,ns):
    o_ref,fx_ref=refs[-2:]
    s0=s_ref[s_ref[ns+f0+pl.program_id(0)]]
    wr,wl=windows(s0)
    lane=lax.broadcasted_iota(jnp.int32,(1,128),1)
    lo=lane<64
    l6=lane&63
    rest_row=lax.broadcasted_iota(jnp.int32,(256,1),0)
    ahead=rest_row<s0
    qb=ROWS//3
    rest=lambda ref: jnp.where(ahead,ref[0:256,:],ref[REST:L,:])
    main=lambda ref: ref[pl.ds(wl,LANES),:]
    one=jnp.where(l6==0,1.0,0.0).astype(BF)
    kv=[]
    for take in (rest,main):
        k=take(k_ref)
        v=take(v_ref)
        fk=take(fk_ref)
        kv.append([(jnp.where(own,k,fk),jnp.where(own,v,one)) for own in (lo,~lo)])
    qf=[(rest(q_ref),rest(fq_ref))]
    for b in range(3):
        rows=pl.ds(pl.multiple_of(wr+b*qb,16),qb)
        qf.append((q_ref[rows,:],fq_ref[rows,:]))
    units=[(b,h) for b in range(4) for h in (0,1)]
    def score(b,h):
        return nt(jnp.where(lo if h==0 else ~lo,*qf[b]),kv[min(b,1)][h][0])
    pend=[score(*u) for u in units[:3]]
    accs=[]
    ls=[]
    for i,(b,h) in enumerate(units):
        s=pend.pop(0)
        if i+3<len(units):
            pend.append(score(*units[i+3]))
        m=jnp.max(s,axis=1,keepdims=True)
        p=jnp.exp2(s-m).astype(BF)
        acc=nn(p,kv[min(b,1)][h][1])
        l=acc[:,64:65] if h==0 else acc[:,0:1]
        accs.append(acc*(1.0/l))
        ls.append(-(m+jnp.log2(l)))
        if h==1:
            o=jnp.where(lo,accs[0],accs[1]).astype(BF)
            nl=jnp.where(lo,ls[1],ls[0])
            hi=nl.astype(BF).astype(F32)
            r1=nl-hi
            mid=r1.astype(BF).astype(F32)
            r2=r1-mid
            fx=jnp.where(l6==4,hi,jnp.where(l6==5,mid,jnp.where(l6==6,r2,qf[b][1].astype(F32)))).astype(BF)
            if b==0:
                o_ref[0:256,:]=o
                fx_ref[0:256,:]=fx
                o_ref[REST:L,:]=o
                fx_ref[REST:L,:]=fx
            else:
                at=wr+(b-1)*qb
                rows=pl.ds(pl.multiple_of(at,16),qb)
                pos=lax.broadcasted_iota(jnp.int32,(qb,1),0)+(at-s0)
                inside=(pos>=0)&(pos<MAIN)
                o_ref[rows,:]=jnp.where(inside,o,o_ref[rows,:])
                fx_ref[rows,:]=jnp.where(inside,fx,fx_ref[rows,:])
            accs=[]
            ls=[]


def attn_fwd(starts,q,k,v,fq,fk,prev,f0,n):
    T=q.shape[0]
    ns=T//L
    nu=ns*(D//128)
    blk=pl.BlockSpec((L,128),lambda i,s:(s[ns+f0+i],s[ns+nu+f0+i]))
    fb=pl.BlockSpec((L,128),lambda i,s:(s[ns+f0+i],0))
    prev=list(prev)
    return pl.pallas_call(
        functools.partial(fwd_kernel,f0=f0,ns=ns),
        grid_spec=pltpu.PrefetchScalarGridSpec(
            num_scalar_prefetch=1,grid=(n,),
            in_specs=[blk,blk,blk,fb,fb]+[ANY]*len(prev),out_specs=[blk,blk]),
        out_shape=[S_((T,D),BF)]*2,
        input_output_aliases={6+i:i for i in range(len(prev))},
        compiler_params=pltpu.CompilerParams(dimension_semantics=("arbitrary",)),
        cost_estimate=cost(n*2*4*L*L*256,n*L*128*14,n*2*L*L),
        name="attn_fwd")(starts,q,k,v,fq,fk,*prev)


def bwd_kernel(s_ref,q_ref,k_ref,v_ref,fx_ref,fk_ref,o_ref,do_ref,*refs,f0,ns):
    out_ref=refs[-1]
    s0=s_ref[s_ref[ns+f0+pl.program_id(0)]]
    wr,wl=windows(s0)
    lane=lax.broadcasted_iota(jnp.int32,(1,128),1)
    lo=lane<64
    l6=lane&63
    zero=jnp.zeros((),BF)
    ones2=jnp.where(l6<2,1.0,0.0).astype(BF)
    rest_row=lax.broadcasted_iota(jnp.int32,(256,1),0)
    ahead=rest_row<s0
    rest=lambda ref: jnp.where(ahead,ref[0:256,:],ref[REST:L,:])
    def block(take_k,nk,takes):
        k=take_k(k_ref)
        v=take_k(v_ref)
        fk=take_k(fk_ref)
        kx=[]
        vx=[]
        km=[]
        for own in (lo,~lo):
            kx.append(jnp.where(own,k,fk))
            vx.append(jnp.where(own,v,ones2))
            km.append(jnp.where(own,k,zero))
        dv=jnp.zeros((nk,128),F32)
        dk=jnp.zeros((nk,128),F32)
        dqs=[]
        for take in takes:
            q=take(q_ref)
            fx=take(fx_ref)
            do=take(do_ref)
            prod=do.astype(F32)*take(o_ref).astype(F32)
            d0=-jnp.sum(jnp.where(lo,prod,0.0),axis=1,keepdims=True)
            d1=-jnp.sum(jnp.where(lo,0.0,prod),axis=1,keepdims=True)
            nd=jnp.where(lo,d1,d0)
            hi=nd.astype(BF).astype(F32)
            fd=jnp.where(l6==0,hi,jnp.where(l6==1,nd-hi,0.0)).astype(BF)
            dq=jnp.zeros(q.shape,F32)
            for h,own in enumerate((lo,~lo)):
                p=jnp.exp2(nt(kx[h],jnp.where(own,q,fx)))
                dpt=nt(vx[h],jnp.where(own,do,fd))
                pb=p.astype(BF)
                ds=(p*dpt).astype(BF)
                dv=dv+nn(pb,jnp.where(own,do,zero))
                dk=dk+nn(ds,jnp.where(own,q,zero))
                dq=dq+tn(ds,km[h])
            dqs.append((dq*0.125).astype(BF))
        return dqs,(dk*LN2).astype(BF),dv.astype(BF)
    dqs,dk,dv=block(rest,256,[rest])
    for w,x in enumerate((dqs[0],dk,dv)):
        out_ref[w,0:256,:]=x
        out_ref[w,REST:L,:]=x
    at=lambda start,n: pl.ds(pl.multiple_of(start,16),n)
    cuts=[(0,256),(256,256),(512,256),(768,128)]
    dqs,dk,dv=block(lambda ref: ref[at(wr,ROWS),:],ROWS,[lambda ref,c=c: ref[at(wl+c[0],c[1]),:] for c in cuts])
    def put(w,start,x):
        n=x.shape[0]
        pos=lax.broadcasted_iota(jnp.int32,(n,1),0)+(start-s0)
        out_ref[w,at(start,n),:]=jnp.where((pos>=0)&(pos<MAIN),x,out_ref[w,at(start,n),:])
    for c,x in zip(cuts,dqs):
        put(0,wl+c[0],x)
    put(1,wr,dk)
    put(2,wr,dv)


def attn_bwd(starts,q,k,v,fx,fk,o,do,prev,f0,n):
    T=q.shape[0]
    ns=T//L
    nu=ns*(D//128)
    blk=pl.BlockSpec((L,128),lambda i,s:(s[ns+f0+i],s[ns+nu+f0+i]))
    fb=pl.BlockSpec((L,128),lambda i,s:(s[ns+f0+i],0))
    prev=list(prev)
    return pl.pallas_call(
        functools.partial(bwd_kernel,f0=f0,ns=ns),
        grid_spec=pltpu.PrefetchScalarGridSpec(
            num_scalar_prefetch=1,grid=(n,),
            in_specs=[blk,blk,blk,blk,fb,blk,blk]+[ANY]*len(prev),
            out_specs=pl.BlockSpec((3,L,128),lambda i,s:(0,s[ns+f0+i],s[ns+nu+f0+i]))),
        out_shape=S_((3,T,D),BF),
        input_output_aliases={8+i:i for i in range(len(prev))},
        compiler_params=pltpu.CompilerParams(dimension_semantics=("arbitrary",)),
        cost_estimate=cost(n*2*10*L*L*256,n*L*128*20,n*2*L*L),
        name="attn_bwd")(starts,q,k,v,fx,fk,o,do,*prev)


def mid_kernel(idx_ref,*refs,tb,fc,ns,wr,fr):
    tok_ref,row_ref,att_ref,cot_ref,vec_ref=refs[:5]
    own=refs[5:8]
    mine=refs[8:8+ns-1]
    other=refs[8+ns-1:8+2*(ns-1)]
    b0=8+2*(ns-1)
    res_ref,gm_ref,ga_ref,keep_ref,send_ref,sv_ref,sub_ref,ow,up,dn,aup,adn,aow,sem=refs[b0:]
    i=pl.program_id(0)
    n=pl.num_programs(0)
    c=idx_ref[0]
    def copies():
        cps=[]
        def put(src,dst):
            cps.append(pltpu.make_async_copy(src,dst,sem.at[len(cps)]))
        r16=lambda sh,m: pl.ds(pl.multiple_of(sh*m,16),m)
        sh=idx_ref[1+ns]
        put(own[0],ow.at[r16(sh,wr)])
        put(own[1],up.at[r16(sh,wr)])
        put(own[2],dn.at[r16(sh,fr)])
        for j in range(1,ns):
            for src,sh,cc in ((mine[j-1],idx_ref[1+ns+j],c),(other[j-1],idx_ref[1+2*ns+j],1-c)):
                cd=pl.ds(pl.multiple_of(cc*HC,128),HC)
                put(src.at[pl.ds(0,wr)],ow.at[r16(sh,wr),cd])
                for b in range(4):
                    put(src.at[pl.ds(wr+b*wr,wr)],up.at[r16(sh,wr),pl.ds(pl.multiple_of(cc*4*HC+b*HC,128),HC)])
                put(src.at[pl.ds(5*wr,fr)],dn.at[r16(sh,fr),cd])
        return cps
    @pl.when(i==0)
    def _():
        cps=copies()
        for cp in cps:
            cp.start()
        aup[...]=jnp.zeros_like(aup)
        adn[...]=jnp.zeros_like(adn)
        aow[...]=jnp.zeros_like(aow)
        sv_ref[...]=jnp.zeros_like(sv_ref)
        sub_ref[...]=jnp.zeros_like(sub_ref)
        for cp in cps:
            cp.wait()
    ob=vec_ref[4:5,:]
    g2=vec_ref[5:6,:]
    b2=vec_ref[6:7,:]
    db=vec_ref[7:8,:]
    att=att_ref[...]
    mixed=tok_ref[...]+row_ref[0]+nn(att,ow[...])+ob
    xhat,r=norm(mixed)
    n2=(xhat*g2+b2).astype(BF)
    n2t=n2.T
    cot=cot_ref[...]
    g=cot.astype(BF)
    res=mixed+db
    gn2=jnp.zeros((tb,D),F32)
    for j in range(FF//fc):
        cs=slice(j*fc,(j+1)*fc)
        pre=nn(n2,up[:,cs])+vec_ref[8+j:9+j,:]
        gact=nt(g,dn[cs,:])
        phi=0.5+0.5*lax.erf(pre*(2**-0.5))
        pdf=jnp.exp2(pre*pre*(-0.5*LOG2E))*(1.0/math.sqrt(2*math.pi))
        act=(pre*phi).astype(BF)
        gp=gact*(phi+pre*pdf)
        gpre=gp.astype(BF)
        sub_ref[:,cs]+=sum8(gp)
        res=res+nn(act,dn[cs,:])
        gn2=gn2+nt(gpre,up[:,cs])
        adn[cs,:]+=tn(act,g)
        aup[:,cs]+=nn(n2t,gpre)
    res_ref[...]=res
    e=gn2*g2
    c1=jnp.mean(e,axis=1,keepdims=True)
    c2=jnp.mean(e*xhat,axis=1,keepdims=True)
    gm=cot+r*(e-c1-xhat*c2)
    gml=gm.astype(BF)
    gm_ref[...]=gml
    ga_ref[...]=nt(gml,ow[...]).astype(BF)
    aow[...]+=tn(att,gml)
    sv_ref[0:8,:]+=sum8(gm)
    sv_ref[8:16,:]+=sum8(gn2*xhat)
    sv_ref[16:24,:]+=sum8(gn2)
    sv_ref[24:32,:]+=sum8(cot)
    @pl.when(i==n-1)
    def _():
        for ref,base,odd in ((keep_ref,1+ns,0),(send_ref,1+2*ns,1)):
            for ch in (0,1):
                @pl.when(c==(ch+odd)%2)
                def _():
                    def body(j,carry):
                        sh=idx_ref[base+j]
                        rw=pl.ds(pl.multiple_of(sh*wr,8),wr)
                        ref[j,0:wr,:]=aow[rw,ch*HC:(ch+1)*HC].astype(BF)
                        for b in range(4):
                            lo=(ch*4+b)*HC
                            ref[j,wr+b*wr:2*wr+b*wr,:]=aup[rw,lo:lo+HC].astype(BF)
                        ref[j,5*wr:5*wr+fr,:]=adn[pl.ds(pl.multiple_of(sh*fr,8),fr),ch*HC:(ch+1)*HC].astype(BF)
                        return carry
                    lax.fori_loop(0,ns,body,0)


def mid(idx,tok,row,att,cot,vec,own,mine,other,tb=256,fc=D):
    T=tok.shape[0]
    per=L//tb
    ns=len(mine)+1
    wr=own[0].shape[0]
    fr=own[2].shape[0]
    rb=5*wr+fr
    blk=pl.BlockSpec((tb,D),lambda i,*_:(i,0))
    return pl.pallas_call(
        functools.partial(mid_kernel,tb=tb,fc=fc,ns=ns,wr=wr,fr=fr),
        grid_spec=pltpu.PrefetchScalarGridSpec(
            num_scalar_prefetch=1,grid=(T//tb,),
            in_specs=[blk,pl.BlockSpec((1,1,D),lambda i,*_:(i//per,0,0)),blk,blk,full(VR,D)]+[ANY]*(3+2*(ns-1)),
            out_specs=[blk,blk,blk,full(ns,rb,HC),full(ns,rb,HC),full(32,D),full(8,FF)],
            scratch_shapes=[pltpu.VMEM((D,D),BF),pltpu.VMEM((D,FF),BF),pltpu.VMEM((FF,D),BF),
                pltpu.VMEM((D,FF),F32),pltpu.VMEM((FF,D),F32),pltpu.VMEM((D,D),F32),
                pltpu.SemaphoreType.DMA((3+12*(ns-1),))]),
        out_shape=[S_((T,D),F32),S_((T,D),BF),S_((T,D),BF),S_((ns,rb,HC),BF),S_((ns,rb,HC),BF),S_((32,D),F32),S_((8,FF),F32)],
        compiler_params=pltpu.CompilerParams(dimension_semantics=("arbitrary",),vmem_limit_bytes=67043328),
        cost_estimate=cost(6*T*D*(D+2*FF),T*D*20+30*D*FF,2*T*FF),
        name="mid")(idx,tok,row,att,cot,vec,*own,*mine,*other)


def dw_kernel(idx_ref,nt_ref,d_ref,keep_ref,send_ref,sv_ref,acc,*,ns,wr):
    i=pl.program_id(0)
    c=idx_ref[0]
    @pl.when(i==0)
    def _():
        acc[...]=jnp.zeros_like(acc)
        sv_ref[...]=jnp.zeros_like(sv_ref)
    for w in range(3):
        acc[w]+=nn(nt_ref[...],d_ref[w])
    sv_ref[0:8,:]+=sum8(d_ref[0].astype(F32))
    sv_ref[8:16,:]+=sum8(d_ref[2].astype(F32))
    @pl.when(i==pl.num_programs(0)-1)
    def _():
        for ref,base,odd in ((keep_ref,1+ns,0),(send_ref,1+2*ns,1)):
            for ch in (0,1):
                @pl.when(c==(ch+odd)%2)
                def _():
                    def body(j,carry):
                        rw=pl.ds(pl.multiple_of(idx_ref[base+j]*wr,8),wr)
                        for w in range(3):
                            ref[j,w*wr:(w+1)*wr,:]=acc[w,rw,ch*HC:(ch+1)*HC].astype(BF)
                        return carry
                    lax.fori_loop(0,ns,body,0)


def dw(idx,n1t,d,ns,tb=512):
    T=n1t.shape[1]
    wr=D//ns
    return pl.pallas_call(
        functools.partial(dw_kernel,ns=ns,wr=wr),
        grid_spec=pltpu.PrefetchScalarGridSpec(
            num_scalar_prefetch=1,grid=(T//tb,),
            in_specs=[pl.BlockSpec((D,tb),lambda i,*_:(0,i)),pl.BlockSpec((3,tb,D),lambda i,*_:(0,i,0))],
            out_specs=[full(ns,3*wr,HC),full(ns,3*wr,HC),full(16,D)],
            scratch_shapes=[pltpu.VMEM((3,D,D),F32)]),
        out_shape=[S_((ns,3*wr,HC),BF)]*2+[S_((16,D),F32)],
        compiler_params=pltpu.CompilerParams(dimension_semantics=("arbitrary",)),
        cost_estimate=cost(6*T*D*D,T*D*8+12*D*D),
        name="dw")(idx,n1t,d)


def dx_kernel(tok_ref,row_ref,d_ref,gm_ref,w_ref,vec_ref,gt_ref,sv_ref,ts_ref,*,per):
    i=pl.program_id(0)
    @pl.when(i==0)
    def _():
        sv_ref[...]=jnp.zeros_like(sv_ref)
    @pl.when(i%per==0)
    def _():
        ts_ref[...]=jnp.zeros_like(ts_ref)
    gn=nt(d_ref[0],w_ref[0])+nt(d_ref[1],w_ref[1])+nt(d_ref[2],w_ref[2])
    xhat,r=norm(tok_ref[...]+row_ref[0])
    e=gn*vec_ref[0:1,:]
    c1=jnp.mean(e,axis=1,keepdims=True)
    c2=jnp.mean(e*xhat,axis=1,keepdims=True)
    gt=gm_ref[...].astype(F32)+r*(e-c1-xhat*c2)
    gt_ref[...]=gt
    sv_ref[0:8,:]+=sum8(gn*xhat)
    sv_ref[8:16,:]+=sum8(gn)
    ts_ref[0]+=sum8(gt)


def dx(tok,row,d,gm,w,vec,tb=512):
    T=tok.shape[0]
    per=L//tb
    blk=pl.BlockSpec((tb,D),lambda i:(i,0))
    return pl.pallas_call(
        functools.partial(dx_kernel,per=per),grid=(T//tb,),
        in_specs=[blk,pl.BlockSpec((1,1,D),lambda i:(i//per,0,0)),pl.BlockSpec((3,tb,D),lambda i:(0,i,0)),blk,full(3,D,D),full(VR,D)],
        out_specs=[blk,full(16,D),pl.BlockSpec((1,8,D),lambda i:(i//per,0,0))],
        out_shape=[S_((T,D),F32),S_((16,D),F32),S_((T//L,8,D),F32)],
        compiler_params=pltpu.CompilerParams(dimension_semantics=("arbitrary",)),
        cost_estimate=cost(6*T*D*D,T*D*16+6*D*D),
        name="dx")(tok,row,d,gm,w,vec)


def rows8(x):
    return jnp.sum(x,axis=0,keepdims=True)


def sums_kernel(id_ref,sv1_ref,svq_ref,sv2_ref,sub_ref,ts_ref,out_ref):
    src=[sv1_ref[0:8],sv1_ref[8:16],svq_ref[0:8],svq_ref[8:16]]+[sv2_ref[8*i:8*i+8] for i in range(4)]
    src+=[sub_ref[:,i*D:(i+1)*D] for i in range(FF//D)]
    rows=[rows8(x) for x in src]+[id_ref[0:1],id_ref[1:2]]+[rows8(ts_ref[i]) for i in range(ts_ref.shape[0])]
    out_ref[...]=jnp.concatenate(rows,axis=0).astype(BF)


def sums(ids,sv1,svq,sv2,sub,ts):
    vm=pl.BlockSpec(memory_space=pltpu.VMEM)
    return pl.pallas_call(sums_kernel,in_specs=[vm]*6,out_specs=vm,
        out_shape=S_((VR+ts.shape[0],D),BF),cost_estimate=cost(0,10**6),name="sums")(ids,sv1,svq,sv2,sub,ts)


def group_kernel(idx_ref,*refs,ns,nseq):
    out_ref,acc=refs[ns:]
    tot=refs[0][0:VR].astype(F32)
    for j in range(1,ns):
        tot=tot+refs[j][0:VR].astype(F32)
    for j in range(ns):
        acc[idx_ref[1+j]]=refs[j][VR:VR+nseq].astype(F32)
    out_ref[...]=jnp.concatenate([tot]+[acc[j] for j in range(ns)],axis=0).astype(BF)


def group(idx,pays,nseq):
    ns=len(pays)
    vm=pl.BlockSpec(memory_space=pltpu.VMEM)
    return pl.pallas_call(functools.partial(group_kernel,ns=ns,nseq=nseq),
        in_specs=[pl.BlockSpec(memory_space=pltpu.SMEM)]+[vm]*ns,out_specs=vm,
        out_shape=S_((VR+ns*nseq,D),BF),scratch_shapes=[pltpu.VMEM((ns,nseq,D),F32)],
        cost_estimate=cost(0,10**6),name="group")(idx,*pays)


def table_kernel(me_ref,*refs,nr,rows,own):
    sum_ref,tab_ref,acc,allr=refs[nr:]
    r0=me_ref[0]
    for j in range(nr):
        acc[r0^j]=refs[j][...].astype(F32)
    tot=acc[0,0:VR]
    for r in range(1,nr):
        tot=tot+acc[r,0:VR]
    sum_ref[...]=tot
    for r in range(nr):
        allr[r*rows:(r+1)*rows,:]=acc[r,VR:VR+rows]
    n=nr*rows
    ids=tot[NV:NV+1,0:n]*32.0+tot[NV+1:NV+2,0:n]
    line=lax.broadcasted_iota(jnp.int32,(own,n),0)+me_ref[1]*own
    hit=jnp.where(line==ids.astype(jnp.int32),1.0,0.0).astype(BF)
    tab_ref[...]=nn(hit,allr[...].astype(BF))


def table(me,pays,own):
    nr=len(pays)
    rows=pays[0].shape[0]-VR
    vm=pl.BlockSpec(memory_space=pltpu.VMEM)
    return pl.pallas_call(functools.partial(table_kernel,nr=nr,rows=rows,own=own),
        in_specs=[pl.BlockSpec(memory_space=pltpu.SMEM)]+[vm]*nr,out_specs=[vm,vm],
        out_shape=[S_((VR,D),F32),S_((own,D),F32)],
        scratch_shapes=[pltpu.VMEM((nr,VR+rows,D),F32),pltpu.VMEM((nr*rows,D),F32)],
        cost_estimate=cost(0,4*10**6),name="table")(me,*pays)


def unpack_kernel(idx_ref,a_ref,b_ref,*outs,parts):
    for ch in (0,1):
        @pl.when(idx_ref[0]==ch)
        def _():
            for h,ref in enumerate((a_ref,b_ref) if ch==0 else (b_ref,a_ref)):
                r0=0
                for out,(nr,nb) in zip(outs,parts):
                    for b in range(nb):
                        out[:,(h*nb+b)*HC:(h*nb+b+1)*HC]=ref[r0:r0+nr,:].astype(F32)
                        r0+=nr


def unpack(idx,a,b,parts):
    vm=pl.BlockSpec(memory_space=pltpu.VMEM)
    return pl.pallas_call(functools.partial(unpack_kernel,parts=parts),
        in_specs=[pl.BlockSpec(memory_space=pltpu.SMEM),vm,vm],out_specs=[vm]*len(parts),
        out_shape=[S_((nr,2*nb*HC),F32) for nr,nb in parts],
        cost_estimate=cost(0,12*a.shape[0]*HC),name="unpack")(idx,a,b)


def small_kernel(me_ref,ts_ref,*refs,w,fr,nseq):
    vecs=refs[:9]
    out_ref,id_ref=refs[9:]
    def spread(rows,width,at):
        n=rows[0].shape[1]
        y=jnp.concatenate(rows+[jnp.zeros((8-len(rows),n),F32)]*(len(rows)<8),axis=0)
        y=jnp.concatenate([y,jnp.zeros((8,width-n),F32)],axis=1)
        return pltpu.roll(y,at,1)
    row=lambda ref: ref[...].astype(F32).reshape(1,ref.shape[0])
    v=spread([row(r) for r in vecs[:8]],D,me_ref[1]*w)
    u=spread([row(vecs[8])],FF,me_ref[1]*fr)
    lane=lax.broadcasted_iota(jnp.int32,(1,D),1)
    def steps(at,high):
        y=jnp.zeros((1,D),jnp.int32)
        for i in range(nseq):
            t=ts_ref[i]
            y=jnp.where(lane==at*nseq+i,t//32 if high else t%32,y)
        return y.astype(F32)
    id_ref[...]=jnp.concatenate([steps(me_ref[2],True),steps(me_ref[2],False)],axis=0)
    out_ref[...]=jnp.concatenate([v]+[u[0:1,i*D:(i+1)*D] for i in range(FF//D)]+[steps(me_ref[1],True),steps(me_ref[1],False)],axis=0).astype(BF)


def small_rows(me,time_steps,vecs):
    vm=pl.BlockSpec(memory_space=pltpu.VMEM)
    sm=pl.BlockSpec(memory_space=pltpu.SMEM)
    return pl.pallas_call(functools.partial(small_kernel,w=vecs[0].shape[0],fr=vecs[8].shape[0],nseq=time_steps.shape[0]),
        in_specs=[sm,sm]+[vm]*9,out_specs=[vm,vm],
        out_shape=[S_((VR,D),BF),S_((2,D),F32)],cost_estimate=cost(0,10**6),name="small")(me,time_steps,*vecs)


class Ring:
    def __init__(self,rep,shard):
        self.R,self.S=rep,shard
        self.nb=shard.bit_length()-1
        self.Z=rep//2
        r=lax.axis_index("rep")
        self.s=lax.axis_index("shard")
        self.c=r%2
        self.z=r//2

    def move(self,x,to):
        pairs=[]
        for r in range(self.R):
            for s in range(self.S):
                r2,s2=to(r,s)
                pairs.append((r*self.S+s,r2*self.S+s2))
        return lax.ppermute(x,("rep","shard"),pairs)

    def order(self,c,t):
        return (t+c*(self.nb//2))%self.nb

    def mask(self,c,j):
        m=0
        for t in range(self.nb):
            if j>>t&1:
                m|=1<<self.order(c,t)
        return m

    def step(self,x,t):
        return self.move(x,lambda r,s:(r,s^(1<<self.order(r%2,t))))

    def direct(self,x,j):
        return self.move(x,lambda r,s:(r,s^j))

    def core(self,x):
        return self.move(x,lambda r,s:(r^1,s))

    def plane(self,x,j):
        return self.move(x,lambda r,s:(r^(2*j),s))

    def index(self):
        m=[[self.mask(c,j) for j in range(self.S)] for c in (0,1)]
        base=list(range(self.S))
        t=jnp.where(self.c==0,jnp.array([0]+base+m[0]+m[1],jnp.int32),jnp.array([0]+base+m[1]+m[0],jnp.int32))
        head=jnp.arange(1+3*self.S)==0
        return jnp.where(head,self.c,t^self.s).astype(jnp.int32)


def tie(*xs):
    return lax.optimization_barrier(xs)


def add(*terms):
    y=terms[0].astype(F32)
    for x in terms[1:]:
        y=y+x.astype(F32)
    return y.astype(BF)


def upper(terms,n):
    return add(*[x[n:] for x in terms]),[x[:n] for x in terms]


def plane_rows(g,x):
    x=x.reshape(g.Z,-1,HC)
    return [lax.dynamic_index_in_dim(x,g.z^j,0,keepdims=False) for j in range(1,g.Z)]


def plane_send(g,rows):
    return [g.plane(x,j) for j,x in enumerate(rows,1)]


def plane_sum(g,x,parts):
    mine=lax.dynamic_index_in_dim(x.reshape(g.Z,-1,HC),g.z,0,keepdims=False).astype(F32)
    for p in parts:
        mine=mine+p.astype(F32)
    return mine.astype(BF)


def plane_join(g,mine,parts):
    out=jnp.zeros((g.Z,)+mine.shape,BF)
    for j,p in enumerate([mine]+parts):
        out=lax.dynamic_update_index_in_dim(out,p,g.z^j,0)
    return out.reshape(-1,HC)


def local(tokens,segments,time_steps,time_table,ln1_gain,ln1_bias,q_weight,q_bias,k_weight,v_weight,v_bias,o_weight,o_bias,ln2_gain,ln2_bias,up_weight,up_bias,down_weight,down_bias,cotangent):
    nseq=tokens.shape[0]
    T=nseq*L
    g=Ring(lax.axis_size("rep"),lax.axis_size("shard"))
    S=g.S
    w=ln1_gain.shape[0]
    fr=down_weight.shape[0]
    own=time_table.shape[0]
    idx=g.index()
    r=g.z*2+g.c
    me=jnp.stack([r,g.s,r*S+g.s]).astype(jnp.int32)
    small,ids=small_rows(me,time_steps,(ln1_gain,ln1_bias,q_bias,v_bias,o_bias,ln2_gain,ln2_bias,down_bias,up_bias))
    small,segments,o_weight_,q_weight_=tie(small,segments,o_weight,q_weight)
    pack_a=pack(pack_a_kernel,idx,(q_weight_,k_weight,v_weight),"pack_a")
    mine_a=[g.direct(pack_a,j) for j in range(1,S)]
    segments,pack_a=tie(segments,pack_a)
    vec=small.astype(F32)
    for j in reversed(range(1,S)):
        vec=vec+g.direct(small,j).astype(F32)
    steps=vec[NV,:S*nseq]*32.0+vec[NV+1,:S*nseq]
    hit=steps.astype(jnp.int32)[:,None]==jnp.arange(own)[None,:]+g.s*own
    rows=jnp.dot(hit.astype(BF),time_table,preferred_element_type=F32).astype(BF).reshape(S,nseq,D)
    pick=lambda j: lax.dynamic_index_in_dim(rows,g.s^j,0,keepdims=False)
    picks=[pick(j) for j in range(S)]
    picks[0],*mine_a=tie(picks[0],*mine_a)
    row=picks[0].astype(F32)
    for j in range(1,S):
        row=row+g.direct(picks[j],j).astype(F32)
    row=row.reshape(nseq,1,D)
    pack_b=pack(pack_b_kernel,idx,(o_weight_,up_weight,down_weight),"pack_b")
    tok=tokens.reshape(T,D)
    cot=cotangent.reshape(T,D)
    fq,fk=seg_features(segments.reshape(T))
    counts=jnp.sum(segments[:,:,None]==jnp.arange(4),axis=1)
    before=jnp.cumsum(counts==MAIN,axis=1)==0
    np_=D//128
    starts=jnp.concatenate([jnp.sum(jnp.where(before,counts,0),axis=1).astype(jnp.int32),
        jnp.array([i//np_ for i in range(nseq*np_)]+[i%np_ for i in range(nseq*np_)],jnp.int32)])
    fq,fk,pack_b,row,*mine_a=tie(fq,fk,pack_b,row,*mine_a)
    other_a=[g.core(x) for x in mine_a]
    mine_b=[pack_b]
    first=[g.step(pack_b,t) for t in range(g.nb)]
    q,k,v,n1t,wqkv=qkv(idx,tok,row,vec,(q_weight,k_weight,v_weight),mine_a,other_a)
    fwd=attn_fwd(starts,q,k,v,fq,fk,(),0,3*nseq//2)
    o1,fx1,*first=tie(*fwd,*first)
    for t in range(g.nb):
        mine_b=mine_b+[first[t]]+[g.step(x,t) for x in mine_b[1:]]
    direct=[1<<t for t in range(g.nb)]
    other_b=[None]+[g.core(x) if j in direct else None for j,x in enumerate(mine_b[1:],1)]
    fwd=attn_fwd(starts,q,k,v,fq,fk,(o1,fx1),3*nseq//2,3*nseq)
    late=[j for j in range(1,S) if j not in direct]
    o1,fx1,*got=tie(*fwd,*[mine_b[j] for j in late])
    for j,x in zip(late,got):
        mine_b[j]=x
        other_b[j]=g.core(x)
    att,fx=attn_fwd(starts,q,k,v,fq,fk,(o1,fx1),9*nseq//2,6*nseq-9*nseq//2)
    res,gm,ga,keep_b,send_b,sv2,sub=mid(idx,tok,row,att,cot,vec,(o_weight,up_weight,down_weight),mine_b[1:],other_b[1:])
    cuts=[0,nseq,nseq+5*nseq//2,5*nseq,6*nseq]
    call=lambda prev,i: attn_bwd(starts,q,k,v,fx,fk,att,ga,prev,cuts[i],cuts[i+1]-cuts[i])
    got=g.core(send_b)
    d=call((),0)
    d,got=tie(d,got)
    n=S
    x=[keep_b]
    for t in reversed(range(g.nb)):
        n//=2
        up,x=upper(x+[got],n)
        d,up=tie(d,up)
        got=g.step(up,t)
        i=g.nb-t
        if i<=2:
            d=call((d,),i)
            d,got=tie(d,got)
    xb=add(*[y[0] for y in x],got[0])
    d,xb,*rows_b=tie(d,xb,*plane_rows(g,xb))
    parts=plane_send(g,rows_b)
    d=call((d,),3)
    keep_a,send_a,svq=dw(idx,n1t,d,S)
    keep_a,send_a,*parts=tie(keep_a,send_a,*parts)
    got=g.core(send_a)
    mine=plane_sum(g,xb,parts)
    back=[g.plane(mine,j) for j in range(1,g.Z)]
    gm,mine_,got=tie(gm,mine,got)
    up,x=upper([keep_a,got],S//2)
    gm,up=tie(gm,up)
    got=g.step(up,g.nb-1)
    gt,sv1,ts=dx(tok,row,d,gm,wqkv,vec)
    ts,got=tie(ts,got)
    n=S//2
    for t in reversed(range(g.nb-1)):
        n//=2
        up,x=upper(x+[got],n)
        ts,up=tie(ts,up)
        got=g.step(up,t)
    pay=sums(ids,sv1,svq,sv2,sub,ts)
    pays=[pay]+[g.direct(pay,j) for j in range(1,S)]
    pays[-1],got=tie(pays[-1],got)
    xa=add(*[y[0] for y in x],got[0])
    rows_a=plane_rows(g,xa)
    *pays,rows_a[0]=tie(*pays,rows_a[0])
    parts_a=plane_send(g,rows_a)
    pay=group(idx,pays,nseq)
    out_b=plane_join(g,mine_,back)
    out_b,pay,*parts_a=tie(out_b,pay,*parts_a)
    other_b=g.core(out_b)
    mine=plane_sum(g,xa,parts_a)
    pay,mine=tie(pay,mine)
    back_a=[g.plane(mine,j) for j in range(1,g.Z)]
    pays=[pay]+[g.move(pay,lambda r,s,j=j:(r^j,s)) for j in range(1,g.R)]
    go,gup,gdn=unpack(idx,out_b,other_b,((w,1),(w,4),(fr,1)))
    gup,*both=tie(gup,*back_a,*pays)
    back_a,pays=both[:g.Z-1],both[g.Z-1:]
    out_a=plane_join(g,mine,back_a)
    other_a=g.core(out_a)
    vsum,gtab=table(me,pays,own)
    vsum,other_a=tie(vsum,other_a)
    gq,gk,gv=unpack(idx,out_a,other_a,((w,1),)*3)
    sums8=lax.dynamic_slice_in_dim(vsum[:8],g.s*w,w,1)
    subs=lax.dynamic_slice_in_dim(vsum[8:NV].reshape(FF),g.s*up_bias.shape[0],up_bias.shape[0],0)
    return (res.reshape(tokens.shape),gt.reshape(tokens.shape),gtab,sums8[0],sums8[1],gq,sums8[2],gk,gv,sums8[3],go,sums8[4],sums8[5],sums8[6],gup,subs,gdn,sums8[7])


def solution(mesh):
    b=("rep","shard")
    s=P("shard")
    m=P("shard",None)
    t=P(b,None,None)
    return jax.shard_map(local,mesh=mesh,
        in_specs=(t,P(b,None),P(b),m,s,s,m,s,m,m,s,m,s,s,s,m,s,m,s,t),
        out_specs=(t,t,m,s,s,m,s,m,m,s,m,s,s,s,m,s,m,s),check_vma=False)
```

```python
import functools
import math

import jax
import jax.numpy as jnp
from jax import lax
from jax.experimental import pallas as pl
from jax.experimental.pallas import tpu as pltpu
from jax.sharding import PartitionSpec as P

NEG=-1e30
EPS=1e-5
L=1024
D=768
FF=3072
HC=D//2
BF=jnp.bfloat16
F32=jnp.float32
LOG2E=math.log2(math.e)
LN2=math.log(2.0)
QS=0.125*LOG2E
VR=14
VP=16
NV=12
ANY=pl.BlockSpec(memory_space=pl.ANY)
S_=jax.ShapeDtypeStruct


def nt(a,b):
    return lax.dot_general(a,b,(((1,),(1,)),((),())),preferred_element_type=F32)


def nn(a,b):
    return lax.dot_general(a,b,(((1,),(0,)),((),())),preferred_element_type=F32)


def tn(a,b):
    return lax.dot_general(a,b,(((0,),(0,)),((),())),preferred_element_type=F32)


def full(*s):
    return pl.BlockSpec(s,lambda i,*_:(0,)*len(s),pipeline_mode=pl.Buffered(1))


def norm(x):
    mean=jnp.mean(x,axis=1,keepdims=True)
    off=x-mean
    var=jnp.mean(off*off,axis=1,keepdims=True)
    r=lax.rsqrt(var+EPS)
    return off*r,r


def sum8(x):
    return jnp.sum(x.reshape(x.shape[0]//8,8,x.shape[1]),axis=0)


def cost(flops,nbytes,trans=0):
    return pl.CostEstimate(flops=int(flops)//10,bytes_accessed=int(nbytes)//10,transcendentals=int(trans)//10)


def seg_features(seg):
    lane=jnp.arange(128)%64
    hit=seg[:,None]==lane[None,:]
    first=(lane<4)[None]
    fq=jnp.where(first&hit,1.0,0.0).astype(BF)
    fk=jnp.where(first,jnp.where(hit,0.0,NEG),jnp.where((lane<7)[None],1.0,0.0)).astype(BF)
    return fq,fk


def qkv_kernel(idx_ref,*refs,ns,wr):
    tok_ref,row_ref,vec_ref=refs[:3]
    own=refs[3:6]
    mine=refs[6:6+ns-1]
    other=refs[6+ns-1:6+2*(ns-1)]
    hi=6+2*(ns-1)
    q_ref,k_ref,v_ref,nt_ref,w_ref,sem=refs[hi:hi+6]
    @pl.when(pl.program_id(0)==0)
    def _():
        c=idx_ref[0]
        def put(src,w,sh,cols):
            rows=pl.ds(pl.multiple_of(sh*wr,16),wr)
            dst=w_ref.at[w,rows] if cols is None else w_ref.at[w,rows,pl.ds(pl.multiple_of(cols*HC,128),HC)]
            pltpu.make_async_copy(src,dst,sem.at[0]).start()
        for w in range(3):
            put(own[w],w,idx_ref[1],None)
            for j in range(1,ns):
                put(mine[j-1].at[pl.ds(w*wr,wr)],w,idx_ref[1+j],c)
                put(other[j-1].at[pl.ds(w*wr,wr)],w,idx_ref[1+j],1-c)
        pltpu.make_async_copy(w_ref,w_ref,sem.at[0]).wait()
    xhat,_=norm(tok_ref[...]+row_ref[0])
    n1=(xhat*vec_ref[0:1,:]+vec_ref[1:2,:]).astype(BF)
    q_ref[...]=((nn(n1,w_ref[0])+vec_ref[2:3,:])*QS).astype(BF)
    k_ref[...]=nn(n1,w_ref[1]).astype(BF)
    v_ref[...]=(nn(n1,w_ref[2])+vec_ref[3:4,:]).astype(BF)
    nt_ref[...]=n1.T


def qkv(idx,tok,row,vec,own,mine,other,tb=512):
    T=tok.shape[0]
    per=L//tb
    ns=len(mine)+1
    wr=own[0].shape[0]
    blk=pl.BlockSpec((tb,D),lambda i,*_:(i,0))
    return pl.pallas_call(
        functools.partial(qkv_kernel,ns=ns,wr=wr),
        grid_spec=pltpu.PrefetchScalarGridSpec(
            num_scalar_prefetch=1,grid=(T//tb,),
            in_specs=[blk,pl.BlockSpec((1,1,D),lambda i,*_:(i//per,0,0)),full(VR,D)]+[ANY]*(3+2*(ns-1)),
            out_specs=[blk]*3+[pl.BlockSpec((D,tb),lambda i,*_:(0,i)),full(3,D,D)],
            scratch_shapes=[pltpu.SemaphoreType.DMA((1,))]),
        out_shape=[S_((T,D),BF)]*3+[S_((D,T),BF),S_((3,D,D),BF)],
        compiler_params=pltpu.CompilerParams(dimension_semantics=("arbitrary",)),
        cost_estimate=cost(6*T*D*D,T*D*10+9*D*D),
        name="qkv")(idx,tok,row,vec,*own,*mine,*other)


def pack_a_kernel(idx_ref,q_ref,k_ref,v_ref,out_ref):
    wr=q_ref.shape[0]
    for ch in (0,1):
        @pl.when(idx_ref[0]==ch)
        def _():
            for w,ref in enumerate((q_ref,k_ref,v_ref)):
                out_ref[w*wr:(w+1)*wr,:]=ref[:,ch*HC:(ch+1)*HC]


def pack_b_kernel(idx_ref,o_ref,u_ref,d_ref,out_ref):
    wr=o_ref.shape[0]
    for ch in (0,1):
        @pl.when(idx_ref[0]==ch)
        def _():
            out_ref[0:wr,:]=o_ref[:,ch*HC:(ch+1)*HC]
            for b in range(4):
                out_ref[wr+b*wr:2*wr+b*wr,:]=u_ref[:,(ch*4+b)*HC:(ch*4+b+1)*HC]
            out_ref[5*wr:,:]=d_ref[:,ch*HC:(ch+1)*HC]


def pack(kernel,idx,ws,name):
    rows=sum(x.shape[0]*x.shape[1]//D for x in ws)
    vm=pl.BlockSpec(memory_space=pltpu.VMEM)
    return pl.pallas_call(kernel,in_specs=[pl.BlockSpec(memory_space=pltpu.SMEM)]+[vm]*3,out_specs=vm,
        out_shape=S_((rows,HC),BF),cost_estimate=cost(0,4*rows*D),name=name)(idx,*ws)


MAIN=800
ROWS=816
LANES=896
REST=768


def windows(s):
    s16=(s//16)*16
    return pl.multiple_of(jnp.minimum(s16,L-ROWS),16),pl.multiple_of(jnp.minimum(s16,L-LANES),16)


def fwd_kernel(s_ref,q_ref,k_ref,v_ref,fq_ref,fk_ref,*refs,f0,ns):
    o_ref,fx_ref=refs[-2:]
    s0=s_ref[s_ref[ns+f0+pl.program_id(0)]]
    wr,wl=windows(s0)
    lane=lax.broadcasted_iota(jnp.int32,(1,128),1)
    lo=lane<64
    l6=lane&63
    rest_row=lax.broadcasted_iota(jnp.int32,(256,1),0)
    ahead=rest_row<s0
    qb=ROWS//3
    rest=lambda ref: jnp.where(ahead,ref[0:256,:],ref[REST:L,:])
    main=lambda ref: ref[pl.ds(wl,LANES),:]
    one=jnp.where(l6==0,1.0,0.0).astype(BF)
    kv=[]
    for take in (rest,main):
        k=take(k_ref)
        v=take(v_ref)
        fk=take(fk_ref)
        kv.append([(jnp.where(own,k,fk),jnp.where(own,v,one)) for own in (lo,~lo)])
    qf=[(rest(q_ref),rest(fq_ref))]
    for b in range(3):
        rows=pl.ds(pl.multiple_of(wr+b*qb,16),qb)
        qf.append((q_ref[rows,:],fq_ref[rows,:]))
    units=[(b,h) for b in range(4) for h in (0,1)]
    def score(b,h):
        return nt(jnp.where(lo if h==0 else ~lo,*qf[b]),kv[min(b,1)][h][0])
    pend=[score(*u) for u in units[:3]]
    accs=[]
    ls=[]
    for i,(b,h) in enumerate(units):
        s=pend.pop(0)
        if i+3<len(units):
            pend.append(score(*units[i+3]))
        m=jnp.max(s,axis=1,keepdims=True)
        p=jnp.exp2(s-m).astype(BF)
        acc=nn(p,kv[min(b,1)][h][1])
        l=acc[:,64:65] if h==0 else acc[:,0:1]
        accs.append(acc*(1.0/l))
        ls.append(-(m+jnp.log2(l)))
        if h==1:
            o=jnp.where(lo,accs[0],accs[1]).astype(BF)
            nl=jnp.where(lo,ls[1],ls[0])
            hi=nl.astype(BF).astype(F32)
            r1=nl-hi
            mid=r1.astype(BF).astype(F32)
            r2=r1-mid
            fx=jnp.where(l6==4,hi,jnp.where(l6==5,mid,jnp.where(l6==6,r2,qf[b][1].astype(F32)))).astype(BF)
            if b==0:
                o_ref[0:256,:]=o
                fx_ref[0:256,:]=fx
                o_ref[REST:L,:]=o
                fx_ref[REST:L,:]=fx
            else:
                at=wr+(b-1)*qb
                rows=pl.ds(pl.multiple_of(at,16),qb)
                pos=lax.broadcasted_iota(jnp.int32,(qb,1),0)+(at-s0)
                inside=(pos>=0)&(pos<MAIN)
                o_ref[rows,:]=jnp.where(inside,o,o_ref[rows,:])
                fx_ref[rows,:]=jnp.where(inside,fx,fx_ref[rows,:])
            accs=[]
            ls=[]


def attn_fwd(starts,q,k,v,fq,fk,prev,f0,n):
    T=q.shape[0]
    ns=T//L
    nu=ns*(D//128)
    blk=pl.BlockSpec((L,128),lambda i,s:(s[ns+f0+i],s[ns+nu+f0+i]))
    fb=pl.BlockSpec((L,128),lambda i,s:(s[ns+f0+i],0))
    prev=list(prev)
    return pl.pallas_call(
        functools.partial(fwd_kernel,f0=f0,ns=ns),
        grid_spec=pltpu.PrefetchScalarGridSpec(
            num_scalar_prefetch=1,grid=(n,),
            in_specs=[blk,blk,blk,fb,fb]+[ANY]*len(prev),out_specs=[blk,blk]),
        out_shape=[S_((T,D),BF)]*2,
        input_output_aliases={6+i:i for i in range(len(prev))},
        compiler_params=pltpu.CompilerParams(dimension_semantics=("arbitrary",)),
        cost_estimate=cost(n*2*4*L*L*256,n*L*128*14,n*2*L*L),
        name="attn_fwd")(starts,q,k,v,fq,fk,*prev)


def bwd_kernel(s_ref,q_ref,k_ref,v_ref,fx_ref,fk_ref,o_ref,do_ref,*refs,f0,ns):
    out_ref=refs[-1]
    s0=s_ref[s_ref[ns+f0+pl.program_id(0)]]
    wr,wl=windows(s0)
    lane=lax.broadcasted_iota(jnp.int32,(1,128),1)
    lo=lane<64
    l6=lane&63
    zero=jnp.zeros((),BF)
    ones2=jnp.where(l6<2,1.0,0.0).astype(BF)
    rest_row=lax.broadcasted_iota(jnp.int32,(256,1),0)
    ahead=rest_row<s0
    rest=lambda ref: jnp.where(ahead,ref[0:256,:],ref[REST:L,:])
    def block(take_k,nk,takes):
        k=take_k(k_ref)
        v=take_k(v_ref)
        fk=take_k(fk_ref)
        kx=[]
        vx=[]
        km=[]
        for own in (lo,~lo):
            kx.append(jnp.where(own,k,fk))
            vx.append(jnp.where(own,v,ones2))
            km.append(jnp.where(own,k,zero))
        dv=jnp.zeros((nk,128),F32)
        dk=jnp.zeros((nk,128),F32)
        dqs=[]
        for take in takes:
            q=take(q_ref)
            fx=take(fx_ref)
            do=take(do_ref)
            prod=do.astype(F32)*take(o_ref).astype(F32)
            d0=-jnp.sum(jnp.where(lo,prod,0.0),axis=1,keepdims=True)
            d1=-jnp.sum(jnp.where(lo,0.0,prod),axis=1,keepdims=True)
            nd=jnp.where(lo,d1,d0)
            hi=nd.astype(BF).astype(F32)
            fd=jnp.where(l6==0,hi,jnp.where(l6==1,nd-hi,0.0)).astype(BF)
            dq=jnp.zeros(q.shape,F32)
            for h,own in enumerate((lo,~lo)):
                p=jnp.exp2(nt(kx[h],jnp.where(own,q,fx)))
                dpt=nt(vx[h],jnp.where(own,do,fd))
                pb=p.astype(BF)
                ds=(p*dpt).astype(BF)
                dv=dv+nn(pb,jnp.where(own,do,zero))
                dk=dk+nn(ds,jnp.where(own,q,zero))
                dq=dq+tn(ds,km[h])
            dqs.append((dq*0.125).astype(BF))
        return dqs,(dk*LN2).astype(BF),dv.astype(BF)
    dqs,dk,dv=block(rest,256,[rest])
    for w,x in enumerate((dqs[0],dk,dv)):
        out_ref[w,0:256,:]=x
        out_ref[w,REST:L,:]=x
    at=lambda start,n: pl.ds(pl.multiple_of(start,16),n)
    cuts=[(0,256),(256,256),(512,256),(768,128)]
    dqs,dk,dv=block(lambda ref: ref[at(wr,ROWS),:],ROWS,[lambda ref,c=c: ref[at(wl+c[0],c[1]),:] for c in cuts])
    def put(w,start,x):
        n=x.shape[0]
        pos=lax.broadcasted_iota(jnp.int32,(n,1),0)+(start-s0)
        out_ref[w,at(start,n),:]=jnp.where((pos>=0)&(pos<MAIN),x,out_ref[w,at(start,n),:])
    for c,x in zip(cuts,dqs):
        put(0,wl+c[0],x)
    put(1,wr,dk)
    put(2,wr,dv)


def attn_bwd(starts,q,k,v,fx,fk,o,do,prev,f0,n):
    T=q.shape[0]
    ns=T//L
    nu=ns*(D//128)
    blk=pl.BlockSpec((L,128),lambda i,s:(s[ns+f0+i],s[ns+nu+f0+i]))
    fb=pl.BlockSpec((L,128),lambda i,s:(s[ns+f0+i],0))
    prev=list(prev)
    return pl.pallas_call(
        functools.partial(bwd_kernel,f0=f0,ns=ns),
        grid_spec=pltpu.PrefetchScalarGridSpec(
            num_scalar_prefetch=1,grid=(n,),
            in_specs=[blk,blk,blk,blk,fb,blk,blk]+[ANY]*len(prev),
            out_specs=pl.BlockSpec((3,L,128),lambda i,s:(0,s[ns+f0+i],s[ns+nu+f0+i]))),
        out_shape=S_((3,T,D),BF),
        input_output_aliases={8+i:i for i in range(len(prev))},
        compiler_params=pltpu.CompilerParams(dimension_semantics=("arbitrary",)),
        cost_estimate=cost(n*2*10*L*L*256,n*L*128*20,n*2*L*L),
        name="attn_bwd")(starts,q,k,v,fx,fk,o,do,*prev)


def mid_kernel(idx_ref,*refs,tb,fc,ns,wr,fr):
    tok_ref,row_ref,att_ref,cot_ref,vec_ref=refs[:5]
    own=refs[5:8]
    mine=refs[8:8+ns-1]
    other=refs[8+ns-1:8+2*(ns-1)]
    b0=8+2*(ns-1)
    res_ref,gm_ref,ga_ref,keep_ref,send_ref,sv_ref,sub_ref,ow,up,dn,aup,adn,aow,sem=refs[b0:]
    i=pl.program_id(0)
    n=pl.num_programs(0)
    c=idx_ref[0]
    @pl.when(i==0)
    def _():
        def put(src,dst,k):
            pltpu.make_async_copy(src,dst,sem.at[k]).start()
        r16=lambda sh,m: pl.ds(pl.multiple_of(sh*m,16),m)
        for k in range(3):
            sh=idx_ref[1+ns]
            dst=(ow,up,dn)[k]
            m=(wr,wr,fr)[k]
            put(own[k],dst.at[r16(sh,m)],k)
            for j in range(1,ns):
                for src,sh,cc in ((mine[j-1],idx_ref[1+ns+j],c),(other[j-1],idx_ref[1+2*ns+j],1-c)):
                    if k==1:
                        for b in range(4):
                            put(src.at[pl.ds(wr+b*wr,wr)],up.at[r16(sh,wr),pl.ds(pl.multiple_of(cc*4*HC+b*HC,128),HC)],k)
                    else:
                        put(src.at[pl.ds(0 if k==0 else 5*wr,m)],dst.at[r16(sh,m),pl.ds(pl.multiple_of(cc*HC,128),HC)],k)
        aup[...]=jnp.zeros_like(aup)
        adn[...]=jnp.zeros_like(adn)
        aow[...]=jnp.zeros_like(aow)
        sv_ref[...]=jnp.zeros_like(sv_ref)
        sub_ref[...]=jnp.zeros_like(sub_ref)
        for k,dst in enumerate((ow,up,dn)):
            pltpu.make_async_copy(dst,dst,sem.at[k]).wait()
    ob=vec_ref[4:5,:]
    g2=vec_ref[5:6,:]
    b2=vec_ref[6:7,:]
    db=vec_ref[7:8,:]
    att=att_ref[...]
    mixed=tok_ref[...]+row_ref[0]+nn(att,ow[...])+ob
    xhat,r=norm(mixed)
    n2=(xhat*g2+b2).astype(BF)
    n2t=n2.T
    cot=cot_ref[...]
    g=cot.astype(BF)
    res=mixed+db
    gn2=jnp.zeros((tb,D),F32)
    for j in range(FF//fc):
        cs=slice(j*fc,(j+1)*fc)
        pre=nn(n2,up[:,cs])+vec_ref[8+j:9+j,:]
        gact=nt(g,dn[cs,:])
        phi=0.5+0.5*lax.erf(pre*(2**-0.5))
        pdf=jnp.exp2(pre*pre*(-0.5*LOG2E))*(1.0/math.sqrt(2*math.pi))
        act=(pre*phi).astype(BF)
        gp=gact*(phi+pre*pdf)
        gpre=gp.astype(BF)
        sub_ref[:,cs]+=sum8(gp)
        res=res+nn(act,dn[cs,:])
        gn2=gn2+nt(gpre,up[:,cs])
        adn[cs,:]+=tn(act,g)
        aup[:,cs]+=nn(n2t,gpre)
    res_ref[...]=res
    e=gn2*g2
    c1=jnp.mean(e,axis=1,keepdims=True)
    c2=jnp.mean(e*xhat,axis=1,keepdims=True)
    gm=cot+r*(e-c1-xhat*c2)
    gml=gm.astype(BF)
    gm_ref[...]=gml
    ga_ref[...]=nt(gml,ow[...]).astype(BF)
    aow[...]+=tn(att,gml)
    sv_ref[0:8,:]+=sum8(gm)
    sv_ref[8:16,:]+=sum8(gn2*xhat)
    sv_ref[16:24,:]+=sum8(gn2)
    sv_ref[24:32,:]+=sum8(cot)
    @pl.when(i==n-1)
    def _():
        for ref,base,odd in ((keep_ref,1+ns,0),(send_ref,1+2*ns,1)):
            for ch in (0,1):
                @pl.when(c==(ch+odd)%2)
                def _():
                    def body(j,carry):
                        sh=idx_ref[base+j]
                        rw=pl.ds(pl.multiple_of(sh*wr,8),wr)
                        ref[j,0:wr,:]=aow[rw,ch*HC:(ch+1)*HC].astype(BF)
                        for b in range(4):
                            lo=(ch*4+b)*HC
                            ref[j,wr+b*wr:2*wr+b*wr,:]=aup[rw,lo:lo+HC].astype(BF)
                        ref[j,5*wr:5*wr+fr,:]=adn[pl.ds(pl.multiple_of(sh*fr,8),fr),ch*HC:(ch+1)*HC].astype(BF)
                        return carry
                    lax.fori_loop(0,ns,body,0)


def mid(idx,tok,row,att,cot,vec,own,mine,other,tb=256,fc=D):
    T=tok.shape[0]
    per=L//tb
    ns=len(mine)+1
    wr=own[0].shape[0]
    fr=own[2].shape[0]
    rb=5*wr+fr
    blk=pl.BlockSpec((tb,D),lambda i,*_:(i,0))
    return pl.pallas_call(
        functools.partial(mid_kernel,tb=tb,fc=fc,ns=ns,wr=wr,fr=fr),
        grid_spec=pltpu.PrefetchScalarGridSpec(
            num_scalar_prefetch=1,grid=(T//tb,),
            in_specs=[blk,pl.BlockSpec((1,1,D),lambda i,*_:(i//per,0,0)),blk,blk,full(VR,D)]+[ANY]*(3+2*(ns-1)),
            out_specs=[blk,blk,blk,full(ns,rb,HC),full(ns,rb,HC),full(32,D),full(8,FF)],
            scratch_shapes=[pltpu.VMEM((D,D),BF),pltpu.VMEM((D,FF),BF),pltpu.VMEM((FF,D),BF),
                pltpu.VMEM((D,FF),F32),pltpu.VMEM((FF,D),F32),pltpu.VMEM((D,D),F32),
                pltpu.SemaphoreType.DMA((3,))]),
        out_shape=[S_((T,D),F32),S_((T,D),BF),S_((T,D),BF),S_((ns,rb,HC),BF),S_((ns,rb,HC),BF),S_((32,D),F32),S_((8,FF),F32)],
        compiler_params=pltpu.CompilerParams(dimension_semantics=("arbitrary",),vmem_limit_bytes=67043328),
        cost_estimate=cost(6*T*D*(D+2*FF),T*D*20+30*D*FF,2*T*FF),
        name="mid")(idx,tok,row,att,cot,vec,*own,*mine,*other)


def dw_kernel(idx_ref,nt_ref,d_ref,keep_ref,send_ref,sv_ref,acc,*,ns,wr):
    i=pl.program_id(0)
    c=idx_ref[0]
    @pl.when(i==0)
    def _():
        acc[...]=jnp.zeros_like(acc)
        sv_ref[...]=jnp.zeros_like(sv_ref)
    for w in range(3):
        acc[w]+=nn(nt_ref[...],d_ref[w])
    sv_ref[0:8,:]+=sum8(d_ref[0].astype(F32))
    sv_ref[8:16,:]+=sum8(d_ref[2].astype(F32))
    @pl.when(i==pl.num_programs(0)-1)
    def _():
        for ref,base,odd in ((keep_ref,1+ns,0),(send_ref,1+2*ns,1)):
            for ch in (0,1):
                @pl.when(c==(ch+odd)%2)
                def _():
                    def body(j,carry):
                        rw=pl.ds(pl.multiple_of(idx_ref[base+j]*wr,8),wr)
                        for w in range(3):
                            ref[j,w*wr:(w+1)*wr,:]=acc[w,rw,ch*HC:(ch+1)*HC].astype(BF)
                        return carry
                    lax.fori_loop(0,ns,body,0)


def dw(idx,n1t,d,ns,tb=512):
    T=n1t.shape[1]
    wr=D//ns
    return pl.pallas_call(
        functools.partial(dw_kernel,ns=ns,wr=wr),
        grid_spec=pltpu.PrefetchScalarGridSpec(
            num_scalar_prefetch=1,grid=(T//tb,),
            in_specs=[pl.BlockSpec((D,tb),lambda i,*_:(0,i)),pl.BlockSpec((3,tb,D),lambda i,*_:(0,i,0))],
            out_specs=[full(ns,3*wr,HC),full(ns,3*wr,HC),full(16,D)],
            scratch_shapes=[pltpu.VMEM((3,D,D),F32)]),
        out_shape=[S_((ns,3*wr,HC),BF)]*2+[S_((16,D),F32)],
        compiler_params=pltpu.CompilerParams(dimension_semantics=("arbitrary",)),
        cost_estimate=cost(6*T*D*D,T*D*8+12*D*D),
        name="dw")(idx,n1t,d)


def dx_kernel(tok_ref,row_ref,d_ref,gm_ref,w_ref,vec_ref,gt_ref,sv_ref,ts_ref,*,per):
    i=pl.program_id(0)
    @pl.when(i==0)
    def _():
        sv_ref[...]=jnp.zeros_like(sv_ref)
    @pl.when(i%per==0)
    def _():
        ts_ref[...]=jnp.zeros_like(ts_ref)
    gn=nt(d_ref[0],w_ref[0])+nt(d_ref[1],w_ref[1])+nt(d_ref[2],w_ref[2])
    xhat,r=norm(tok_ref[...]+row_ref[0])
    e=gn*vec_ref[0:1,:]
    c1=jnp.mean(e,axis=1,keepdims=True)
    c2=jnp.mean(e*xhat,axis=1,keepdims=True)
    gt=gm_ref[...].astype(F32)+r*(e-c1-xhat*c2)
    gt_ref[...]=gt
    sv_ref[0:8,:]+=sum8(gn*xhat)
    sv_ref[8:16,:]+=sum8(gn)
    ts_ref[0]+=sum8(gt)


def dx(tok,row,d,gm,w,vec,tb=512):
    T=tok.shape[0]
    per=L//tb
    blk=pl.BlockSpec((tb,D),lambda i:(i,0))
    return pl.pallas_call(
        functools.partial(dx_kernel,per=per),grid=(T//tb,),
        in_specs=[blk,pl.BlockSpec((1,1,D),lambda i:(i//per,0,0)),pl.BlockSpec((3,tb,D),lambda i:(0,i,0)),blk,full(3,D,D),full(VR,D)],
        out_specs=[blk,full(16,D),pl.BlockSpec((1,8,D),lambda i:(i//per,0,0))],
        out_shape=[S_((T,D),F32),S_((16,D),F32),S_((T//L,8,D),F32)],
        compiler_params=pltpu.CompilerParams(dimension_semantics=("arbitrary",)),
        cost_estimate=cost(6*T*D*D,T*D*16+6*D*D),
        name="dx")(tok,row,d,gm,w,vec)


def rows8(x):
    return jnp.sum(x,axis=0,keepdims=True)


def sums_kernel(id_ref,sv1_ref,svq_ref,sv2_ref,sub_ref,ts_ref,out_ref):
    src=[sv1_ref[0:8],sv1_ref[8:16],svq_ref[0:8],svq_ref[8:16]]+[sv2_ref[8*i:8*i+8] for i in range(4)]
    src+=[sub_ref[:,i*D:(i+1)*D] for i in range(FF//D)]
    rows=[rows8(x) for x in src]+[id_ref[0:1],id_ref[1:2]]+[rows8(ts_ref[i]) for i in range(ts_ref.shape[0])]
    out_ref[...]=jnp.concatenate(rows,axis=0).astype(BF)


def sums(ids,sv1,svq,sv2,sub,ts):
    vm=pl.BlockSpec(memory_space=pltpu.VMEM)
    return pl.pallas_call(sums_kernel,in_specs=[vm]*6,out_specs=vm,
        out_shape=S_((VR+ts.shape[0],D),BF),cost_estimate=cost(0,10**6),name="sums")(ids,sv1,svq,sv2,sub,ts)


def group_kernel(idx_ref,*refs,ns,nseq):
    out_ref,acc=refs[ns:]
    tot=refs[0][0:VR].astype(F32)
    for j in range(1,ns):
        tot=tot+refs[j][0:VR].astype(F32)
    for j in range(ns):
        acc[idx_ref[1+j]]=refs[j][VR:VR+nseq].astype(F32)
    out_ref[...]=jnp.concatenate([tot]+[acc[j] for j in range(ns)],axis=0).astype(BF)


def group(idx,pays,nseq):
    ns=len(pays)
    vm=pl.BlockSpec(memory_space=pltpu.VMEM)
    return pl.pallas_call(functools.partial(group_kernel,ns=ns,nseq=nseq),
        in_specs=[pl.BlockSpec(memory_space=pltpu.SMEM)]+[vm]*ns,out_specs=vm,
        out_shape=S_((VR+ns*nseq,D),BF),scratch_shapes=[pltpu.VMEM((ns,nseq,D),F32)],
        cost_estimate=cost(0,10**6),name="group")(idx,*pays)


def table_kernel(idx_ref,*refs,nr,rows,own,me,w,fr):
    sum_ref,sub_ref,tab_ref,acc,allr=refs[nr:]
    r0=idx_ref[me]
    s0=idx_ref[me+1]
    for j in range(nr):
        acc[r0^j]=refs[j][...].astype(F32)
    tot=acc[0,0:VR]
    for r in range(1,nr):
        tot=tot+acc[r,0:VR]
    sum_ref[...]=pltpu.roll(tot[0:8],D-s0*w,1)[:,0:w]
    wide=jnp.concatenate([tot[8+i:9+i] for i in range(FF//D)],axis=1)
    sub_ref[...]=pltpu.roll(jnp.broadcast_to(wide,(8,FF)),FF-s0*fr,1)[0:1,0:fr]
    for r in range(nr):
        allr[r*rows:(r+1)*rows,:]=acc[r,VR:VR+rows]
    n=nr*rows
    ids=tot[NV:NV+1,0:n]*32.0+tot[NV+1:NV+2,0:n]
    line=lax.broadcasted_iota(jnp.int32,(own,n),0)+s0*own
    hit=jnp.where(line==ids.astype(jnp.int32),1.0,0.0).astype(BF)
    tab_ref[...]=nn(hit,allr[...].astype(BF))


def table(idx,pays,own,w,fr):
    nr=len(pays)
    rows=pays[0].shape[0]-VR
    vm=pl.BlockSpec(memory_space=pltpu.VMEM)
    return pl.pallas_call(functools.partial(table_kernel,nr=nr,rows=rows,own=own,me=idx.shape[0]-3,w=w,fr=fr),
        in_specs=[pl.BlockSpec(memory_space=pltpu.SMEM)]+[vm]*nr,out_specs=[vm]*3,
        out_shape=[S_((8,w),F32),S_((1,fr),F32),S_((own,D),F32)],
        scratch_shapes=[pltpu.VMEM((nr,VR+rows,D),F32),pltpu.VMEM((nr*rows,D),F32)],
        cost_estimate=cost(0,4*10**6),name="table")(idx,*pays)


def unpack_kernel(idx_ref,a_ref,b_ref,*outs,parts):
    for ch in (0,1):
        @pl.when(idx_ref[0]==ch)
        def _():
            for h,ref in enumerate((a_ref,b_ref) if ch==0 else (b_ref,a_ref)):
                r0=0
                for out,(nr,nb) in zip(outs,parts):
                    for b in range(nb):
                        out[:,(h*nb+b)*HC:(h*nb+b+1)*HC]=ref[r0:r0+nr,:].astype(F32)
                        r0+=nr


def unpack(idx,a,b,parts):
    vm=pl.BlockSpec(memory_space=pltpu.VMEM)
    return pl.pallas_call(functools.partial(unpack_kernel,parts=parts),
        in_specs=[pl.BlockSpec(memory_space=pltpu.SMEM),vm,vm],out_specs=[vm]*len(parts),
        out_shape=[S_((nr,2*nb*HC),F32) for nr,nb in parts],
        cost_estimate=cost(0,12*a.shape[0]*HC),name="unpack")(idx,a,b)


def small_kernel(idx_ref,ts_ref,*refs,w,fr,nseq,me):
    me_ref=[idx_ref[me+i] for i in range(3)]
    vecs=refs[:9]
    out_ref,id_ref=refs[9:]
    def spread(rows,width,at):
        n=rows[0].shape[1]
        y=jnp.concatenate(rows+[jnp.zeros((8-len(rows),n),F32)]*(len(rows)<8),axis=0)
        y=jnp.concatenate([y,jnp.zeros((8,width-n),F32)],axis=1)
        return pltpu.roll(y,at,1)
    row=lambda ref: ref[...].astype(F32).reshape(1,ref.shape[0])
    v=spread([row(r) for r in vecs[:8]],D,me_ref[1]*w)
    u=spread([row(vecs[8])],FF,me_ref[1]*fr)
    lane=lax.broadcasted_iota(jnp.int32,(1,D),1)
    def steps(at,high):
        y=jnp.zeros((1,D),jnp.int32)
        for i in range(nseq):
            t=ts_ref[i]
            y=jnp.where(lane==at*nseq+i,t//32 if high else t%32,y)
        return y.astype(F32)
    id_ref[...]=jnp.concatenate([steps(me_ref[2],True),steps(me_ref[2],False)],axis=0)
    out_ref[...]=jnp.concatenate([v]+[u[0:1,i*D:(i+1)*D] for i in range(FF//D)]+[steps(me_ref[1],True),steps(me_ref[1],False)],axis=0).astype(BF)


def small_rows(idx,time_steps,vecs):
    vm=pl.BlockSpec(memory_space=pltpu.VMEM)
    sm=pl.BlockSpec(memory_space=pltpu.SMEM)
    return pl.pallas_call(functools.partial(small_kernel,w=vecs[0].shape[0],fr=vecs[8].shape[0],nseq=time_steps.shape[0],me=idx.shape[0]-3),
        in_specs=[sm,sm]+[vm]*9,out_specs=[vm,vm],
        out_shape=[S_((VR,D),BF),S_((2,D),F32)],cost_estimate=cost(0,10**6),name="small")(idx,time_steps,*vecs)


class Ring:
    def __init__(self,rep,shard):
        self.R,self.S=rep,shard
        self.nb=shard.bit_length()-1
        self.Z=rep//2
        r=lax.axis_index("rep")
        self.s=lax.axis_index("shard")
        self.c=r%2
        self.z=r//2

    def move(self,x,to):
        pairs=[]
        for r in range(self.R):
            for s in range(self.S):
                r2,s2=to(r,s)
                pairs.append((r*self.S+s,r2*self.S+s2))
        return lax.ppermute(x,("rep","shard"),pairs)

    def order(self,c,t):
        return (t+c*(self.nb//2))%self.nb

    def mask(self,c,j):
        m=0
        for t in range(self.nb):
            if j>>t&1:
                m|=1<<self.order(c,t)
        return m

    def step(self,x,t):
        return self.move(x,lambda r,s:(r,s^(1<<self.order(r%2,t))))

    def direct(self,x,j):
        return self.move(x,lambda r,s:(r,s^j))

    def core(self,x):
        return self.move(x,lambda r,s:(r^1,s))

    def plane(self,x,j):
        return self.move(x,lambda r,s:(r^(2*j),s))

    def index(self):
        m=[[self.mask(c,j) for j in range(self.S)] for c in (0,1)]
        base=list(range(self.S))
        n=1+3*self.S
        t=jnp.where(self.c==0,jnp.array([0]+base+m[0]+m[1]+[0]*3,jnp.int32),jnp.array([0]+base+m[1]+m[0]+[0]*3,jnp.int32))
        at=jnp.arange(n+3)
        r=self.z*2+self.c
        t=jnp.where(at==0,self.c,t^self.s)
        t=jnp.where(at==n,r,jnp.where(at==n+1,self.s,jnp.where(at==n+2,r*self.S+self.s,t)))
        return t.astype(jnp.int32)


def tie(*xs):
    return lax.optimization_barrier(xs)


def add(*terms):
    y=terms[0].astype(F32)
    for x in terms[1:]:
        y=y+x.astype(F32)
    return y.astype(BF)


def upper(terms,n):
    return add(*[x[n:] for x in terms]),[x[:n] for x in terms]


def plane_rows(g,x):
    x=x.reshape(g.Z,-1,HC)
    return [lax.dynamic_index_in_dim(x,g.z^j,0,keepdims=False) for j in range(1,g.Z)]


def plane_send(g,rows):
    return [g.plane(x,j) for j,x in enumerate(rows,1)]


def plane_sum(g,x,parts):
    mine=lax.dynamic_index_in_dim(x.reshape(g.Z,-1,HC),g.z,0,keepdims=False).astype(F32)
    for p in parts:
        mine=mine+p.astype(F32)
    return mine.astype(BF)


def plane_join(g,mine,parts):
    out=jnp.zeros((g.Z,)+mine.shape,BF)
    for j,p in enumerate([mine]+parts):
        out=lax.dynamic_update_index_in_dim(out,p,g.z^j,0)
    return out.reshape(-1,HC)


def local(tokens,segments,time_steps,time_table,ln1_gain,ln1_bias,q_weight,q_bias,k_weight,v_weight,v_bias,o_weight,o_bias,ln2_gain,ln2_bias,up_weight,up_bias,down_weight,down_bias,cotangent):
    nseq=tokens.shape[0]
    T=nseq*L
    g=Ring(lax.axis_size("rep"),lax.axis_size("shard"))
    S=g.S
    w=ln1_gain.shape[0]
    fr=down_weight.shape[0]
    own=time_table.shape[0]
    idx=g.index()
    small,ids=small_rows(idx,time_steps,(ln1_gain,ln1_bias,q_bias,v_bias,o_bias,ln2_gain,ln2_bias,down_bias,up_bias))
    small,segments,o_weight_,q_weight_=tie(small,segments,o_weight,q_weight)
    pack_a=pack(pack_a_kernel,idx,(q_weight_,k_weight,v_weight),"pack_a")
    mine_a=[g.direct(pack_a,j) for j in range(1,S)]
    segments,pack_a=tie(segments,pack_a)
    vec=small.astype(F32)
    for j in reversed(range(1,S)):
        vec=vec+g.direct(small,j).astype(F32)
    steps=vec[NV,:S*nseq]*32.0+vec[NV+1,:S*nseq]
    hit=steps.astype(jnp.int32)[:,None]==jnp.arange(own)[None,:]+g.s*own
    rows=jnp.dot(hit.astype(BF),time_table,preferred_element_type=F32).astype(BF).reshape(S,nseq,D)
    pick=lambda j: lax.dynamic_index_in_dim(rows,g.s^j,0,keepdims=False)
    picks=[pick(j) for j in range(S)]
    picks[0],*mine_a=tie(picks[0],*mine_a)
    row=picks[0].astype(F32)
    for j in range(1,S):
        row=row+g.direct(picks[j],j).astype(F32)
    row=row.reshape(nseq,1,D)
    pack_b=pack(pack_b_kernel,idx,(o_weight_,up_weight,down_weight),"pack_b")
    tok=tokens.reshape(T,D)
    cot=cotangent.reshape(T,D)
    fq,fk=seg_features(segments.reshape(T))
    counts=jnp.sum(segments[:,:,None]==jnp.arange(4),axis=1)
    before=jnp.cumsum(counts==MAIN,axis=1)==0
    np_=D//128
    starts=jnp.concatenate([jnp.sum(jnp.where(before,counts,0),axis=1).astype(jnp.int32),
        jnp.array([i//np_ for i in range(nseq*np_)]+[i%np_ for i in range(nseq*np_)],jnp.int32)])
    fq,fk,pack_b,row,*mine_a=tie(fq,fk,pack_b,row,*mine_a)
    other_a=[g.core(x) for x in mine_a]
    mine_b=[pack_b]
    first=[g.step(pack_b,t) for t in range(g.nb)]
    q,k,v,n1t,wqkv=qkv(idx,tok,row,vec,(q_weight,k_weight,v_weight),mine_a,other_a)
    fwd=attn_fwd(starts,q,k,v,fq,fk,(),0,3*nseq//2)
    o1,fx1,*first=tie(*fwd,*first)
    for t in range(g.nb):
        mine_b=mine_b+[first[t]]+[g.step(x,t) for x in mine_b[1:]]
    direct=[1<<t for t in range(g.nb)]
    other_b=[None]+[g.core(x) if j in direct else None for j,x in enumerate(mine_b[1:],1)]
    fwd=attn_fwd(starts,q,k,v,fq,fk,(o1,fx1),3*nseq//2,3*nseq)
    late=[j for j in range(1,S) if j not in direct]
    o1,fx1,*got=tie(*fwd,*[mine_b[j] for j in late])
    for j,x in zip(late,got):
        mine_b[j]=x
        other_b[j]=g.core(x)
    att,fx=attn_fwd(starts,q,k,v,fq,fk,(o1,fx1),9*nseq//2,6*nseq-9*nseq//2)
    res,gm,ga,keep_b,send_b,sv2,sub=mid(idx,tok,row,att,cot,vec,(o_weight,up_weight,down_weight),mine_b[1:],other_b[1:])
    cuts=[0,nseq,nseq+5*nseq//2,5*nseq,6*nseq]
    call=lambda prev,i: attn_bwd(starts,q,k,v,fx,fk,att,ga,prev,cuts[i],cuts[i+1]-cuts[i])
    got=g.core(send_b)
    d=call((),0)
    d,got=tie(d,got)
    n=S
    x=[keep_b]
    for t in reversed(range(g.nb)):
        n//=2
        up,x=upper(x+[got],n)
        d,up=tie(d,up)
        got=g.step(up,t)
        i=g.nb-t
        if i<=2:
            d=call((d,),i)
            d,got=tie(d,got)
    xb=add(*[y[0] for y in x],got[0])
    d,xb,*rows_b=tie(d,xb,*plane_rows(g,xb))
    parts=plane_send(g,rows_b)
    d=call((d,),3)
    keep_a,send_a,svq=dw(idx,n1t,d,S)
    keep_a,send_a,*parts=tie(keep_a,send_a,*parts)
    got=g.core(send_a)
    mine=plane_sum(g,xb,parts)
    back=[g.plane(mine,j) for j in range(1,g.Z)]
    gm,mine_,got=tie(gm,mine,got)
    up,x=upper([keep_a,got],S//2)
    gm,up=tie(gm,up)
    got=g.step(up,g.nb-1)
    gt,sv1,ts=dx(tok,row,d,gm,wqkv,vec)
    ts,got=tie(ts,got)
    n=S//2
    for t in reversed(range(g.nb-1)):
        n//=2
        up,x=upper(x+[got],n)
        ts,up=tie(ts,up)
        got=g.step(up,t)
    pay=sums(ids,sv1,svq,sv2,sub,ts)
    pays=[pay]+[g.direct(pay,j) for j in range(1,S)]
    pays[-1],got=tie(pays[-1],got)
    xa=add(*[y[0] for y in x],got[0])
    rows_a=plane_rows(g,xa)
    *pays,rows_a[0]=tie(*pays,rows_a[0])
    parts_a=plane_send(g,rows_a)
    pay=group(idx,pays,nseq)
    out_b=plane_join(g,mine_,back)
    out_b,pay,*parts_a=tie(out_b,pay,*parts_a)
    other_b=g.core(out_b)
    mine=plane_sum(g,xa,parts_a)
    pay,mine=tie(pay,mine)
    back_a=[g.plane(mine,j) for j in range(1,g.Z)]
    pays=[pay]+[g.move(pay,lambda r,s,j=j:(r^j,s)) for j in range(1,g.R)]
    go,gup,gdn=unpack(idx,out_b,other_b,((w,1),(w,4),(fr,1)))
    gup,*both=tie(gup,*back_a,*pays)
    back_a,pays=both[:g.Z-1],both[g.Z-1:]
    out_a=plane_join(g,mine,back_a)
    other_a=g.core(out_a)
    sums8,subs,gtab=table(idx,pays,own,w,up_bias.shape[0])
    sums8,other_a=tie(sums8,other_a)
    gq,gk,gv=unpack(idx,out_a,other_a,((w,1),)*3)
    return (res.reshape(tokens.shape),gt.reshape(tokens.shape),gtab,sums8[0],sums8[1],gq,sums8[2],gk,gv,sums8[3],go,sums8[4],sums8[5],sums8[6],gup,subs[0],gdn,sums8[7])


def solution(mesh):
    b=("rep","shard")
    s=P("shard")
    m=P("shard",None)
    t=P(b,None,None)
    return jax.shard_map(local,mesh=mesh,
        in_specs=(t,P(b,None),P(b),m,s,s,m,s,m,m,s,m,s,s,s,m,s,m,s,t),
        out_specs=(t,t,m,s,s,m,s,m,m,s,m,s,s,s,m,s,m,s),check_vma=False)
```

```python
import functools
import math

import jax
import jax.numpy as jnp
from jax import lax
from jax.experimental import pallas as pl
from jax.experimental.pallas import tpu as pltpu
from jax.sharding import PartitionSpec as P

NEG=-1e30
EPS=1e-5
L=1024
D=768
FF=3072
HC=D//2
BF=jnp.bfloat16
F32=jnp.float32
LOG2E=math.log2(math.e)
LN2=math.log(2.0)
QS=0.125*LOG2E
VR=14
VP=16
NV=12
ANY=pl.BlockSpec(memory_space=pl.ANY)
S_=jax.ShapeDtypeStruct


def nt(a,b):
    return lax.dot_general(a,b,(((1,),(1,)),((),())),preferred_element_type=F32)


def nn(a,b):
    return lax.dot_general(a,b,(((1,),(0,)),((),())),preferred_element_type=F32)


def tn(a,b):
    return lax.dot_general(a,b,(((0,),(0,)),((),())),preferred_element_type=F32)


def full(*s):
    return pl.BlockSpec(s,lambda i,*_:(0,)*len(s),pipeline_mode=pl.Buffered(1))


def norm(x):
    mean=jnp.mean(x,axis=1,keepdims=True)
    off=x-mean
    var=jnp.mean(off*off,axis=1,keepdims=True)
    r=lax.rsqrt(var+EPS)
    return off*r,r


def sum8(x):
    return jnp.sum(x.reshape(x.shape[0]//8,8,x.shape[1]),axis=0)


def cost(flops,nbytes,trans=0):
    return pl.CostEstimate(flops=int(flops)//10,bytes_accessed=int(nbytes)//10,transcendentals=int(trans)//10)


def seg_features(seg):
    lane=jnp.arange(128)%64
    hit=seg[:,None]==lane[None,:]
    first=(lane<4)[None]
    fq=jnp.where(first&hit,1.0,0.0).astype(BF)
    fk=jnp.where(first,jnp.where(hit,0.0,NEG),jnp.where((lane<7)[None],1.0,0.0)).astype(BF)
    return fq,fk


def qkv_kernel(idx_ref,*refs,ns,wr):
    tok_ref,row_ref,vec_ref=refs[:3]
    own=refs[3:6]
    mine=refs[6:6+ns-1]
    other=refs[6+ns-1:6+2*(ns-1)]
    hi=6+2*(ns-1)
    q_ref,k_ref,v_ref,nt_ref,w_ref,sem=refs[hi:hi+6]
    @pl.when(pl.program_id(0)==0)
    def _():
        c=idx_ref[0]
        def put(src,w,sh,cols):
            rows=pl.ds(pl.multiple_of(sh*wr,16),wr)
            dst=w_ref.at[w,rows] if cols is None else w_ref.at[w,rows,pl.ds(pl.multiple_of(cols*HC,128),HC)]
            pltpu.make_async_copy(src,dst,sem.at[0]).start()
        for w in range(3):
            put(own[w],w,idx_ref[1],None)
            for j in range(1,ns):
                put(mine[j-1].at[pl.ds(w*wr,wr)],w,idx_ref[1+j],c)
                put(other[j-1].at[pl.ds(w*wr,wr)],w,idx_ref[1+j],1-c)
    xhat,_=norm(tok_ref[...]+row_ref[0])
    n1=(xhat*vec_ref[0:1,:]+vec_ref[1:2,:]).astype(BF)
    nt_ref[...]=n1.T
    @pl.when(pl.program_id(0)==0)
    def _():
        pltpu.make_async_copy(w_ref,w_ref,sem.at[0]).wait()
    q_ref[...]=((nn(n1,w_ref[0])+vec_ref[2:3,:])*QS).astype(BF)
    k_ref[...]=nn(n1,w_ref[1]).astype(BF)
    v_ref[...]=(nn(n1,w_ref[2])+vec_ref[3:4,:]).astype(BF)


def qkv(idx,tok,row,vec,own,mine,other,tb=512):
    T=tok.shape[0]
    per=L//tb
    ns=len(mine)+1
    wr=own[0].shape[0]
    blk=pl.BlockSpec((tb,D),lambda i,*_:(i,0))
    return pl.pallas_call(
        functools.partial(qkv_kernel,ns=ns,wr=wr),
        grid_spec=pltpu.PrefetchScalarGridSpec(
            num_scalar_prefetch=1,grid=(T//tb,),
            in_specs=[blk,pl.BlockSpec((1,1,D),lambda i,*_:(i//per,0,0)),full(VR,D)]+[ANY]*(3+2*(ns-1)),
            out_specs=[blk]*3+[pl.BlockSpec((D,tb),lambda i,*_:(0,i)),full(3,D,D)],
            scratch_shapes=[pltpu.SemaphoreType.DMA((1,))]),
        out_shape=[S_((T,D),BF)]*3+[S_((D,T),BF),S_((3,D,D),BF)],
        compiler_params=pltpu.CompilerParams(dimension_semantics=("arbitrary",)),
        cost_estimate=cost(6*T*D*D,T*D*10+9*D*D),
        name="qkv")(idx,tok,row,vec,*own,*mine,*other)


def pack_a_kernel(idx_ref,q_ref,k_ref,v_ref,out_ref):
    wr=q_ref.shape[0]
    for ch in (0,1):
        @pl.when(idx_ref[0]==ch)
        def _():
            for w,ref in enumerate((q_ref,k_ref,v_ref)):
                out_ref[w*wr:(w+1)*wr,:]=ref[:,ch*HC:(ch+1)*HC]


def pack_b_kernel(idx_ref,o_ref,u_ref,d_ref,out_ref):
    wr=o_ref.shape[0]
    for ch in (0,1):
        @pl.when(idx_ref[0]==ch)
        def _():
            out_ref[0:wr,:]=o_ref[:,ch*HC:(ch+1)*HC]
            for b in range(4):
                out_ref[wr+b*wr:2*wr+b*wr,:]=u_ref[:,(ch*4+b)*HC:(ch*4+b+1)*HC]
            out_ref[5*wr:,:]=d_ref[:,ch*HC:(ch+1)*HC]


def pack(kernel,idx,ws,name):
    rows=sum(x.shape[0]*x.shape[1]//D for x in ws)
    vm=pl.BlockSpec(memory_space=pltpu.VMEM)
    return pl.pallas_call(kernel,in_specs=[pl.BlockSpec(memory_space=pltpu.SMEM)]+[vm]*3,out_specs=vm,
        out_shape=S_((rows,HC),BF),cost_estimate=cost(0,4*rows*D),name=name)(idx,*ws)


MAIN=800
ROWS=816
LANES=896
REST=768


def windows(s):
    s16=(s//16)*16
    return pl.multiple_of(jnp.minimum(s16,L-ROWS),16),pl.multiple_of(jnp.minimum(s16,L-LANES),16)


def fwd_kernel(s_ref,q_ref,k_ref,v_ref,fq_ref,fk_ref,*refs,f0,ns):
    o_ref,fx_ref=refs[-2:]
    s0=s_ref[s_ref[ns+f0+pl.program_id(0)]]
    wr,wl=windows(s0)
    lane=lax.broadcasted_iota(jnp.int32,(1,128),1)
    lo=lane<64
    l6=lane&63
    rest_row=lax.broadcasted_iota(jnp.int32,(256,1),0)
    ahead=rest_row<s0
    qb=ROWS//3
    rest=lambda ref: jnp.where(ahead,ref[0:256,:],ref[REST:L,:])
    main=lambda ref: ref[pl.ds(wl,LANES),:]
    one=jnp.where(l6==0,1.0,0.0).astype(BF)
    kv=[]
    for take in (rest,main):
        k=take(k_ref)
        v=take(v_ref)
        fk=take(fk_ref)
        kv.append([(jnp.where(own,k,fk),jnp.where(own,v,one)) for own in (lo,~lo)])
    qf=[(rest(q_ref),rest(fq_ref))]
    for b in range(3):
        rows=pl.ds(pl.multiple_of(wr+b*qb,16),qb)
        qf.append((q_ref[rows,:],fq_ref[rows,:]))
    units=[(b,h) for b in range(4) for h in (0,1)]
    def score(b,h):
        return nt(jnp.where(lo if h==0 else ~lo,*qf[b]),kv[min(b,1)][h][0])
    pend=[score(*u) for u in units[:3]]
    accs=[]
    ls=[]
    for i,(b,h) in enumerate(units):
        s=pend.pop(0)
        if i+3<len(units):
            pend.append(score(*units[i+3]))
        m=jnp.max(s,axis=1,keepdims=True)
        p=jnp.exp2(s-m).astype(BF)
        acc=nn(p,kv[min(b,1)][h][1])
        l=acc[:,64:65] if h==0 else acc[:,0:1]
        accs.append(acc*(1.0/l))
        ls.append(-(m+jnp.log2(l)))
        if h==1:
            o=jnp.where(lo,accs[0],accs[1]).astype(BF)
            nl=jnp.where(lo,ls[1],ls[0])
            hi=nl.astype(BF).astype(F32)
            r1=nl-hi
            mid=r1.astype(BF).astype(F32)
            r2=r1-mid
            fx=jnp.where(l6==4,hi,jnp.where(l6==5,mid,jnp.where(l6==6,r2,qf[b][1].astype(F32)))).astype(BF)
            if b==0:
                o_ref[0:256,:]=o
                fx_ref[0:256,:]=fx
                o_ref[REST:L,:]=o
                fx_ref[REST:L,:]=fx
            else:
                at=wr+(b-1)*qb
                rows=pl.ds(pl.multiple_of(at,16),qb)
                pos=lax.broadcasted_iota(jnp.int32,(qb,1),0)+(at-s0)
                inside=(pos>=0)&(pos<MAIN)
                o_ref[rows,:]=jnp.where(inside,o,o_ref[rows,:])
                fx_ref[rows,:]=jnp.where(inside,fx,fx_ref[rows,:])
            accs=[]
            ls=[]


def attn_fwd(starts,q,k,v,fq,fk,prev,f0,n):
    T=q.shape[0]
    ns=T//L
    nu=ns*(D//128)
    blk=pl.BlockSpec((L,128),lambda i,s:(s[ns+f0+i],s[ns+nu+f0+i]))
    fb=pl.BlockSpec((L,128),lambda i,s:(s[ns+f0+i],0))
    prev=list(prev)
    return pl.pallas_call(
        functools.partial(fwd_kernel,f0=f0,ns=ns),
        grid_spec=pltpu.PrefetchScalarGridSpec(
            num_scalar_prefetch=1,grid=(n,),
            in_specs=[blk,blk,blk,fb,fb]+[ANY]*len(prev),out_specs=[blk,blk]),
        out_shape=[S_((T,D),BF)]*2,
        input_output_aliases={6+i:i for i in range(len(prev))},
        compiler_params=pltpu.CompilerParams(dimension_semantics=("arbitrary",)),
        cost_estimate=cost(n*2*4*L*L*256,n*L*128*14,n*2*L*L),
        name="attn_fwd")(starts,q,k,v,fq,fk,*prev)


def bwd_kernel(s_ref,q_ref,k_ref,v_ref,fx_ref,fk_ref,o_ref,do_ref,*refs,f0,ns):
    out_ref=refs[-1]
    s0=s_ref[s_ref[ns+f0+pl.program_id(0)]]
    wr,wl=windows(s0)
    lane=lax.broadcasted_iota(jnp.int32,(1,128),1)
    lo=lane<64
    l6=lane&63
    zero=jnp.zeros((),BF)
    ones2=jnp.where(l6<2,1.0,0.0).astype(BF)
    rest_row=lax.broadcasted_iota(jnp.int32,(256,1),0)
    ahead=rest_row<s0
    rest=lambda ref: jnp.where(ahead,ref[0:256,:],ref[REST:L,:])
    def block(take_k,nk,takes):
        k=take_k(k_ref)
        v=take_k(v_ref)
        fk=take_k(fk_ref)
        kx=[]
        vx=[]
        km=[]
        for own in (lo,~lo):
            kx.append(jnp.where(own,k,fk))
            vx.append(jnp.where(own,v,ones2))
            km.append(jnp.where(own,k,zero))
        dv=jnp.zeros((nk,128),F32)
        dk=jnp.zeros((nk,128),F32)
        dqs=[]
        for take in takes:
            q=take(q_ref)
            fx=take(fx_ref)
            do=take(do_ref)
            prod=do.astype(F32)*take(o_ref).astype(F32)
            d0=-jnp.sum(jnp.where(lo,prod,0.0),axis=1,keepdims=True)
            d1=-jnp.sum(jnp.where(lo,0.0,prod),axis=1,keepdims=True)
            nd=jnp.where(lo,d1,d0)
            hi=nd.astype(BF).astype(F32)
            fd=jnp.where(l6==0,hi,jnp.where(l6==1,nd-hi,0.0)).astype(BF)
            dq=jnp.zeros(q.shape,F32)
            for h,own in enumerate((lo,~lo)):
                p=jnp.exp2(nt(kx[h],jnp.where(own,q,fx)))
                dpt=nt(vx[h],jnp.where(own,do,fd))
                pb=p.astype(BF)
                ds=(p*dpt).astype(BF)
                dv=dv+nn(pb,jnp.where(own,do,zero))
                dk=dk+nn(ds,jnp.where(own,q,zero))
                dq=dq+tn(ds,km[h])
            dqs.append((dq*0.125).astype(BF))
        return dqs,(dk*LN2).astype(BF),dv.astype(BF)
    dqs,dk,dv=block(rest,256,[rest])
    for w,x in enumerate((dqs[0],dk,dv)):
        out_ref[w,0:256,:]=x
        out_ref[w,REST:L,:]=x
    at=lambda start,n: pl.ds(pl.multiple_of(start,16),n)
    cuts=[(0,256),(256,256),(512,256),(768,128)]
    dqs,dk,dv=block(lambda ref: ref[at(wr,ROWS),:],ROWS,[lambda ref,c=c: ref[at(wl+c[0],c[1]),:] for c in cuts])
    def put(w,start,x):
        n=x.shape[0]
        pos=lax.broadcasted_iota(jnp.int32,(n,1),0)+(start-s0)
        out_ref[w,at(start,n),:]=jnp.where((pos>=0)&(pos<MAIN),x,out_ref[w,at(start,n),:])
    for c,x in zip(cuts,dqs):
        put(0,wl+c[0],x)
    put(1,wr,dk)
    put(2,wr,dv)


def attn_bwd(starts,q,k,v,fx,fk,o,do,prev,f0,n):
    T=q.shape[0]
    ns=T//L
    nu=ns*(D//128)
    blk=pl.BlockSpec((L,128),lambda i,s:(s[ns+f0+i],s[ns+nu+f0+i]))
    fb=pl.BlockSpec((L,128),lambda i,s:(s[ns+f0+i],0))
    prev=list(prev)
    return pl.pallas_call(
        functools.partial(bwd_kernel,f0=f0,ns=ns),
        grid_spec=pltpu.PrefetchScalarGridSpec(
            num_scalar_prefetch=1,grid=(n,),
            in_specs=[blk,blk,blk,blk,fb,blk,blk]+[ANY]*len(prev),
            out_specs=pl.BlockSpec((3,L,128),lambda i,s:(0,s[ns+f0+i],s[ns+nu+f0+i]))),
        out_shape=S_((3,T,D),BF),
        input_output_aliases={8+i:i for i in range(len(prev))},
        compiler_params=pltpu.CompilerParams(dimension_semantics=("arbitrary",)),
        cost_estimate=cost(n*2*10*L*L*256,n*L*128*20,n*2*L*L),
        name="attn_bwd")(starts,q,k,v,fx,fk,o,do,*prev)


def mid_kernel(idx_ref,*refs,tb,fc,ns,wr,fr):
    tok_ref,row_ref,att_ref,cot_ref,vec_ref=refs[:5]
    own=refs[5:8]
    mine=refs[8:8+ns-1]
    other=refs[8+ns-1:8+2*(ns-1)]
    b0=8+2*(ns-1)
    res_ref,gm_ref,ga_ref,keep_ref,send_ref,sv_ref,sub_ref,ow,up,dn,aup,adn,aow,sem=refs[b0:]
    i=pl.program_id(0)
    n=pl.num_programs(0)
    c=idx_ref[0]
    @pl.when(i==0)
    def _():
        def put(src,dst,k):
            pltpu.make_async_copy(src,dst,sem.at[k]).start()
        r16=lambda sh,m: pl.ds(pl.multiple_of(sh*m,16),m)
        for k in range(3):
            sh=idx_ref[1+ns]
            dst=(ow,up,dn)[k]
            m=(wr,wr,fr)[k]
            put(own[k],dst.at[r16(sh,m)],k)
            for j in range(1,ns):
                for src,sh,cc in ((mine[j-1],idx_ref[1+ns+j],c),(other[j-1],idx_ref[1+2*ns+j],1-c)):
                    if k==1:
                        for b in range(4):
                            put(src.at[pl.ds(wr+b*wr,wr)],up.at[r16(sh,wr),pl.ds(pl.multiple_of(cc*4*HC+b*HC,128),HC)],k)
                    else:
                        put(src.at[pl.ds(0 if k==0 else 5*wr,m)],dst.at[r16(sh,m),pl.ds(pl.multiple_of(cc*HC,128),HC)],k)
        aup[...]=jnp.zeros_like(aup)
        adn[...]=jnp.zeros_like(adn)
        aow[...]=jnp.zeros_like(aow)
        sv_ref[...]=jnp.zeros_like(sv_ref)
        sub_ref[...]=jnp.zeros_like(sub_ref)
        for k,dst in enumerate((ow,up,dn)):
            pltpu.make_async_copy(dst,dst,sem.at[k]).wait()
    ob=vec_ref[4:5,:]
    g2=vec_ref[5:6,:]
    b2=vec_ref[6:7,:]
    db=vec_ref[7:8,:]
    att=att_ref[...]
    mixed=tok_ref[...]+row_ref[0]+nn(att,ow[...])+ob
    xhat,r=norm(mixed)
    n2=(xhat*g2+b2).astype(BF)
    n2t=n2.T
    cot=cot_ref[...]
    g=cot.astype(BF)
    res=mixed+db
    gn2=jnp.zeros((tb,D),F32)
    for j in range(FF//fc):
        cs=slice(j*fc,(j+1)*fc)
        pre=nn(n2,up[:,cs])+vec_ref[8+j:9+j,:]
        gact=nt(g,dn[cs,:])
        phi=0.5+0.5*lax.erf(pre*(2**-0.5))
        pdf=jnp.exp2(pre*pre*(-0.5*LOG2E))*(1.0/math.sqrt(2*math.pi))
        act=(pre*phi).astype(BF)
        gp=gact*(phi+pre*pdf)
        gpre=gp.astype(BF)
        sub_ref[:,cs]+=sum8(gp)
        res=res+nn(act,dn[cs,:])
        gn2=gn2+nt(gpre,up[:,cs])
        adn[cs,:]+=tn(act,g)
        aup[:,cs]+=nn(n2t,gpre)
    res_ref[...]=res
    e=gn2*g2
    c1=jnp.mean(e,axis=1,keepdims=True)
    c2=jnp.mean(e*xhat,axis=1,keepdims=True)
    gm=cot+r*(e-c1-xhat*c2)
    gml=gm.astype(BF)
    gm_ref[...]=gml
    ga_ref[...]=nt(gml,ow[...]).astype(BF)
    aow[...]+=tn(att,gml)
    sv_ref[0:8,:]+=sum8(gm)
    sv_ref[8:16,:]+=sum8(gn2*xhat)
    sv_ref[16:24,:]+=sum8(gn2)
    sv_ref[24:32,:]+=sum8(cot)
    @pl.when(i==n-1)
    def _():
        for ref,base,odd in ((keep_ref,1+ns,0),(send_ref,1+2*ns,1)):
            for ch in (0,1):
                @pl.when(c==(ch+odd)%2)
                def _():
                    def body(j,carry):
                        sh=idx_ref[base+j]
                        rw=pl.ds(pl.multiple_of(sh*wr,8),wr)
                        ref[j,0:wr,:]=aow[rw,ch*HC:(ch+1)*HC].astype(BF)
                        for b in range(4):
                            lo=(ch*4+b)*HC
                            ref[j,wr+b*wr:2*wr+b*wr,:]=aup[rw,lo:lo+HC].astype(BF)
                        ref[j,5*wr:5*wr+fr,:]=adn[pl.ds(pl.multiple_of(sh*fr,8),fr),ch*HC:(ch+1)*HC].astype(BF)
                        return carry
                    lax.fori_loop(0,ns,body,0)


def mid(idx,tok,row,att,cot,vec,own,mine,other,tb=256,fc=D):
    T=tok.shape[0]
    per=L//tb
    ns=len(mine)+1
    wr=own[0].shape[0]
    fr=own[2].shape[0]
    rb=5*wr+fr
    blk=pl.BlockSpec((tb,D),lambda i,*_:(i,0))
    return pl.pallas_call(
        functools.partial(mid_kernel,tb=tb,fc=fc,ns=ns,wr=wr,fr=fr),
        grid_spec=pltpu.PrefetchScalarGridSpec(
            num_scalar_prefetch=1,grid=(T//tb,),
            in_specs=[blk,pl.BlockSpec((1,1,D),lambda i,*_:(i//per,0,0)),blk,blk,full(VR,D)]+[ANY]*(3+2*(ns-1)),
            out_specs=[blk,blk,blk,full(ns,rb,HC),full(ns,rb,HC),full(32,D),full(8,FF)],
            scratch_shapes=[pltpu.VMEM((D,D),BF),pltpu.VMEM((D,FF),BF),pltpu.VMEM((FF,D),BF),
                pltpu.VMEM((D,FF),F32),pltpu.VMEM((FF,D),F32),pltpu.VMEM((D,D),F32),
                pltpu.SemaphoreType.DMA((3,))]),
        out_shape=[S_((T,D),F32),S_((T,D),BF),S_((T,D),BF),S_((ns,rb,HC),BF),S_((ns,rb,HC),BF),S_((32,D),F32),S_((8,FF),F32)],
        compiler_params=pltpu.CompilerParams(dimension_semantics=("arbitrary",),vmem_limit_bytes=67043328),
        cost_estimate=cost(6*T*D*(D+2*FF),T*D*20+30*D*FF,2*T*FF),
        name="mid")(idx,tok,row,att,cot,vec,*own,*mine,*other)


def dw_kernel(idx_ref,nt_ref,d_ref,keep_ref,send_ref,sv_ref,acc,*,ns,wr):
    i=pl.program_id(0)
    c=idx_ref[0]
    @pl.when(i==0)
    def _():
        acc[...]=jnp.zeros_like(acc)
        sv_ref[...]=jnp.zeros_like(sv_ref)
    for w in range(3):
        acc[w]+=nn(nt_ref[...],d_ref[w])
    sv_ref[0:8,:]+=sum8(d_ref[0].astype(F32))
    sv_ref[8:16,:]+=sum8(d_ref[2].astype(F32))
    @pl.when(i==pl.num_programs(0)-1)
    def _():
        for ref,base,odd in ((keep_ref,1+ns,0),(send_ref,1+2*ns,1)):
            for ch in (0,1):
                @pl.when(c==(ch+odd)%2)
                def _():
                    def body(j,carry):
                        rw=pl.ds(pl.multiple_of(idx_ref[base+j]*wr,8),wr)
                        for w in range(3):
                            ref[j,w*wr:(w+1)*wr,:]=acc[w,rw,ch*HC:(ch+1)*HC].astype(BF)
                        return carry
                    lax.fori_loop(0,ns,body,0)


def dw(idx,n1t,d,ns,tb=512):
    T=n1t.shape[1]
    wr=D//ns
    return pl.pallas_call(
        functools.partial(dw_kernel,ns=ns,wr=wr),
        grid_spec=pltpu.PrefetchScalarGridSpec(
            num_scalar_prefetch=1,grid=(T//tb,),
            in_specs=[pl.BlockSpec((D,tb),lambda i,*_:(0,i)),pl.BlockSpec((3,tb,D),lambda i,*_:(0,i,0))],
            out_specs=[full(ns,3*wr,HC),full(ns,3*wr,HC),full(16,D)],
            scratch_shapes=[pltpu.VMEM((3,D,D),F32)]),
        out_shape=[S_((ns,3*wr,HC),BF)]*2+[S_((16,D),F32)],
        compiler_params=pltpu.CompilerParams(dimension_semantics=("arbitrary",)),
        cost_estimate=cost(6*T*D*D,T*D*8+12*D*D),
        name="dw")(idx,n1t,d)


def dx_kernel(tok_ref,row_ref,d_ref,gm_ref,w_ref,vec_ref,gt_ref,sv_ref,ts_ref,*,per):
    i=pl.program_id(0)
    @pl.when(i==0)
    def _():
        sv_ref[...]=jnp.zeros_like(sv_ref)
    @pl.when(i%per==0)
    def _():
        ts_ref[...]=jnp.zeros_like(ts_ref)
    gn=nt(d_ref[0],w_ref[0])+nt(d_ref[1],w_ref[1])+nt(d_ref[2],w_ref[2])
    xhat,r=norm(tok_ref[...]+row_ref[0])
    e=gn*vec_ref[0:1,:]
    c1=jnp.mean(e,axis=1,keepdims=True)
    c2=jnp.mean(e*xhat,axis=1,keepdims=True)
    gt=gm_ref[...].astype(F32)+r*(e-c1-xhat*c2)
    gt_ref[...]=gt
    sv_ref[0:8,:]+=sum8(gn*xhat)
    sv_ref[8:16,:]+=sum8(gn)
    ts_ref[0]+=sum8(gt)


def dx(tok,row,d,gm,w,vec,tb=512):
    T=tok.shape[0]
    per=L//tb
    blk=pl.BlockSpec((tb,D),lambda i:(i,0))
    return pl.pallas_call(
        functools.partial(dx_kernel,per=per),grid=(T//tb,),
        in_specs=[blk,pl.BlockSpec((1,1,D),lambda i:(i//per,0,0)),pl.BlockSpec((3,tb,D),lambda i:(0,i,0)),blk,full(3,D,D),full(VR,D)],
        out_specs=[blk,full(16,D),pl.BlockSpec((1,8,D),lambda i:(i//per,0,0))],
        out_shape=[S_((T,D),F32),S_((16,D),F32),S_((T//L,8,D),F32)],
        compiler_params=pltpu.CompilerParams(dimension_semantics=("arbitrary",)),
        cost_estimate=cost(6*T*D*D,T*D*16+6*D*D),
        name="dx")(tok,row,d,gm,w,vec)


def rows8(x):
    return jnp.sum(x,axis=0,keepdims=True)


def sums_kernel(id_ref,sv1_ref,svq_ref,sv2_ref,sub_ref,ts_ref,out_ref):
    src=[sv1_ref[0:8],sv1_ref[8:16],svq_ref[0:8],svq_ref[8:16]]+[sv2_ref[8*i:8*i+8] for i in range(4)]
    src+=[sub_ref[:,i*D:(i+1)*D] for i in range(FF//D)]
    rows=[rows8(x) for x in src]+[id_ref[0:1],id_ref[1:2]]+[rows8(ts_ref[i]) for i in range(ts_ref.shape[0])]
    out_ref[...]=jnp.concatenate(rows,axis=0).astype(BF)


def sums(ids,sv1,svq,sv2,sub,ts):
    vm=pl.BlockSpec(memory_space=pltpu.VMEM)
    return pl.pallas_call(sums_kernel,in_specs=[vm]*6,out_specs=vm,
        out_shape=S_((VR+ts.shape[0],D),BF),cost_estimate=cost(0,10**6),name="sums")(ids,sv1,svq,sv2,sub,ts)


def group_kernel(idx_ref,*refs,ns,nseq):
    out_ref,acc=refs[ns:]
    tot=refs[0][0:VR].astype(F32)
    for j in range(1,ns):
        tot=tot+refs[j][0:VR].astype(F32)
    for j in range(ns):
        acc[idx_ref[1+j]]=refs[j][VR:VR+nseq].astype(F32)
    out_ref[...]=jnp.concatenate([tot]+[acc[j] for j in range(ns)],axis=0).astype(BF)


def group(idx,pays,nseq):
    ns=len(pays)
    vm=pl.BlockSpec(memory_space=pltpu.VMEM)
    return pl.pallas_call(functools.partial(group_kernel,ns=ns,nseq=nseq),
        in_specs=[pl.BlockSpec(memory_space=pltpu.SMEM)]+[vm]*ns,out_specs=vm,
        out_shape=S_((VR+ns*nseq,D),BF),scratch_shapes=[pltpu.VMEM((ns,nseq,D),F32)],
        cost_estimate=cost(0,10**6),name="group")(idx,*pays)


def table_kernel(idx_ref,*refs,nr,rows,own,me,w,fr):
    sum_refs=refs[nr:nr+8]
    sub_ref,tab_ref,acc,allr=refs[nr+8:]
    r0=idx_ref[me]
    s0=idx_ref[me+1]
    for j in range(nr):
        acc[r0^j]=refs[j][...].astype(F32)
    tot=acc[0,0:VR]
    for r in range(1,nr):
        tot=tot+acc[r,0:VR]
    mine=pltpu.roll(tot[0:8],D-s0*w,1)
    for i,ref in enumerate(sum_refs):
        ref[...]=mine[i:i+1,0:w].reshape(w)
    wide=jnp.concatenate([tot[8+i:9+i] for i in range(FF//D)],axis=1)
    sub_ref[...]=pltpu.roll(jnp.broadcast_to(wide,(8,FF)),FF-s0*fr,1)[0:1,0:fr].reshape(fr)
    for r in range(nr):
        allr[r*rows:(r+1)*rows,:]=acc[r,VR:VR+rows]
    n=nr*rows
    ids=tot[NV:NV+1,0:n]*32.0+tot[NV+1:NV+2,0:n]
    line=lax.broadcasted_iota(jnp.int32,(own,n),0)+s0*own
    hit=jnp.where(line==ids.astype(jnp.int32),1.0,0.0).astype(BF)
    tab_ref[...]=nn(hit,allr[...].astype(BF))


def table(idx,pays,own,w,fr):
    nr=len(pays)
    rows=pays[0].shape[0]-VR
    vm=pl.BlockSpec(memory_space=pltpu.VMEM)
    return pl.pallas_call(functools.partial(table_kernel,nr=nr,rows=rows,own=own,me=idx.shape[0]-3,w=w,fr=fr),
        in_specs=[pl.BlockSpec(memory_space=pltpu.SMEM)]+[vm]*nr,out_specs=[vm]*10,
        out_shape=[S_((w,),F32)]*8+[S_((fr,),F32),S_((own,D),F32)],
        scratch_shapes=[pltpu.VMEM((nr,VR+rows,D),F32),pltpu.VMEM((nr*rows,D),F32)],
        cost_estimate=cost(0,4*10**6),name="table")(idx,*pays)


def unpack_kernel(idx_ref,a_ref,b_ref,*outs,parts):
    for ch in (0,1):
        @pl.when(idx_ref[0]==ch)
        def _():
            for h,ref in enumerate((a_ref,b_ref) if ch==0 else (b_ref,a_ref)):
                r0=0
                for out,(nr,nb) in zip(outs,parts):
                    for b in range(nb):
                        out[:,(h*nb+b)*HC:(h*nb+b+1)*HC]=ref[r0:r0+nr,:].astype(F32)
                        r0+=nr


def unpack(idx,a,b,parts):
    vm=pl.BlockSpec(memory_space=pltpu.VMEM)
    return pl.pallas_call(functools.partial(unpack_kernel,parts=parts),
        in_specs=[pl.BlockSpec(memory_space=pltpu.SMEM),vm,vm],out_specs=[vm]*len(parts),
        out_shape=[S_((nr,2*nb*HC),F32) for nr,nb in parts],
        cost_estimate=cost(0,12*a.shape[0]*HC),name="unpack")(idx,a,b)


def small_kernel(idx_ref,ts_ref,*refs,w,fr,nseq,me):
    me_ref=[idx_ref[me+i] for i in range(3)]
    vecs=refs[:9]
    out_ref,id_ref=refs[9:]
    def spread(rows,width,at):
        n=rows[0].shape[1]
        y=jnp.concatenate(rows+[jnp.zeros((8-len(rows),n),F32)]*(len(rows)<8),axis=0)
        y=jnp.concatenate([y,jnp.zeros((8,width-n),F32)],axis=1)
        return pltpu.roll(y,at,1)
    row=lambda ref: ref[...].astype(F32).reshape(1,ref.shape[0])
    v=spread([row(r) for r in vecs[:8]],D,me_ref[1]*w)
    u=spread([row(vecs[8])],FF,me_ref[1]*fr)
    lane=lax.broadcasted_iota(jnp.int32,(1,D),1)
    def steps(at,high):
        y=jnp.zeros((1,D),jnp.int32)
        for i in range(nseq):
            t=ts_ref[i]
            y=jnp.where(lane==at*nseq+i,t//32 if high else t%32,y)
        return y.astype(F32)
    id_ref[...]=jnp.concatenate([steps(me_ref[2],True),steps(me_ref[2],False)],axis=0)
    out_ref[...]=jnp.concatenate([v]+[u[0:1,i*D:(i+1)*D] for i in range(FF//D)]+[steps(me_ref[1],True),steps(me_ref[1],False)],axis=0).astype(BF)


def small_rows(idx,time_steps,vecs):
    vm=pl.BlockSpec(memory_space=pltpu.VMEM)
    sm=pl.BlockSpec(memory_space=pltpu.SMEM)
    return pl.pallas_call(functools.partial(small_kernel,w=vecs[0].shape[0],fr=vecs[8].shape[0],nseq=time_steps.shape[0],me=idx.shape[0]-3),
        in_specs=[sm,sm]+[vm]*9,out_specs=[vm,vm],
        out_shape=[S_((VR,D),BF),S_((2,D),F32)],cost_estimate=cost(0,10**6),name="small")(idx,time_steps,*vecs)


class Ring:
    def __init__(self,rep,shard):
        self.R,self.S=rep,shard
        self.nb=shard.bit_length()-1
        self.Z=rep//2
        r=lax.axis_index("rep")
        self.s=lax.axis_index("shard")
        self.c=r%2
        self.z=r//2

    def move(self,x,to):
        pairs=[]
        for r in range(self.R):
            for s in range(self.S):
                r2,s2=to(r,s)
                pairs.append((r*self.S+s,r2*self.S+s2))
        return lax.ppermute(x,("rep","shard"),pairs)

    def order(self,c,t):
        return (t+c*(self.nb//2))%self.nb

    def mask(self,c,j):
        m=0
        for t in range(self.nb):
            if j>>t&1:
                m|=1<<self.order(c,t)
        return m

    def step(self,x,t):
        return self.move(x,lambda r,s:(r,s^(1<<self.order(r%2,t))))

    def direct(self,x,j):
        return self.move(x,lambda r,s:(r,s^j))

    def core(self,x):
        return self.move(x,lambda r,s:(r^1,s))

    def plane(self,x,j):
        return self.move(x,lambda r,s:(r^(2*j),s))

    def index(self):
        m=[[self.mask(c,j) for j in range(self.S)] for c in (0,1)]
        base=list(range(self.S))
        n=1+3*self.S
        t=jnp.where(self.c==0,jnp.array([0]+base+m[0]+m[1]+[0]*3,jnp.int32),jnp.array([0]+base+m[1]+m[0]+[0]*3,jnp.int32))
        at=jnp.arange(n+3)
        r=self.z*2+self.c
        t=jnp.where(at==0,self.c,t^self.s)
        t=jnp.where(at==n,r,jnp.where(at==n+1,self.s,jnp.where(at==n+2,r*self.S+self.s,t)))
        return t.astype(jnp.int32)


def tie(*xs):
    return lax.optimization_barrier(xs)


def add(*terms):
    y=terms[0].astype(F32)
    for x in terms[1:]:
        y=y+x.astype(F32)
    return y.astype(BF)


def upper(terms,n):
    return add(*[x[n:] for x in terms]),[x[:n] for x in terms]


def plane_rows(g,x):
    x=x.reshape(g.Z,-1,HC)
    return [lax.dynamic_index_in_dim(x,g.z^j,0,keepdims=False) for j in range(1,g.Z)]


def plane_send(g,rows):
    return [g.plane(x,j) for j,x in enumerate(rows,1)]


def plane_sum(g,x,parts):
    mine=lax.dynamic_index_in_dim(x.reshape(g.Z,-1,HC),g.z,0,keepdims=False).astype(F32)
    for p in parts:
        mine=mine+p.astype(F32)
    return mine.astype(BF)


def plane_join(g,mine,parts):
    out=jnp.zeros((g.Z,)+mine.shape,BF)
    for j,p in enumerate([mine]+parts):
        out=lax.dynamic_update_index_in_dim(out,p,g.z^j,0)
    return out.reshape(-1,HC)


def local(tokens,segments,time_steps,time_table,ln1_gain,ln1_bias,q_weight,q_bias,k_weight,v_weight,v_bias,o_weight,o_bias,ln2_gain,ln2_bias,up_weight,up_bias,down_weight,down_bias,cotangent):
    nseq=tokens.shape[0]
    T=nseq*L
    g=Ring(lax.axis_size("rep"),lax.axis_size("shard"))
    S=g.S
    w=ln1_gain.shape[0]
    fr=down_weight.shape[0]
    own=time_table.shape[0]
    idx=g.index()
    small,ids=small_rows(idx,time_steps,(ln1_gain,ln1_bias,q_bias,v_bias,o_bias,ln2_gain,ln2_bias,down_bias,up_bias))
    small,segments,o_weight_,q_weight_=tie(small,segments,o_weight,q_weight)
    pack_a=pack(pack_a_kernel,idx,(q_weight_,k_weight,v_weight),"pack_a")
    mine_a=[g.direct(pack_a,j) for j in range(1,S)]
    segments,pack_a=tie(segments,pack_a)
    vec=small.astype(F32)
    for j in reversed(range(1,S)):
        vec=vec+g.direct(small,j).astype(F32)
    steps=vec[NV,:S*nseq]*32.0+vec[NV+1,:S*nseq]
    hit=steps.astype(jnp.int32)[:,None]==jnp.arange(own)[None,:]+g.s*own
    rows=jnp.dot(hit.astype(BF),time_table,preferred_element_type=F32).astype(BF).reshape(S,nseq,D)
    pick=lambda j: lax.dynamic_index_in_dim(rows,g.s^j,0,keepdims=False)
    picks=[pick(j) for j in range(S)]
    picks[0],*mine_a=tie(picks[0],*mine_a)
    row=picks[0].astype(F32)
    for j in range(1,S):
        row=row+g.direct(picks[j],j).astype(F32)
    row=row.reshape(nseq,1,D)
    pack_b=pack(pack_b_kernel,idx,(o_weight_,up_weight,down_weight),"pack_b")
    tok=tokens.reshape(T,D)
    cot=cotangent.reshape(T,D)
    fq,fk=seg_features(segments.reshape(T))
    counts=jnp.sum(segments[:,:,None]==jnp.arange(4),axis=1)
    before=jnp.cumsum(counts==MAIN,axis=1)==0
    np_=D//128
    starts=jnp.concatenate([jnp.sum(jnp.where(before,counts,0),axis=1).astype(jnp.int32),
        jnp.array([i//np_ for i in range(nseq*np_)]+[i%np_ for i in range(nseq*np_)],jnp.int32)])
    fq,fk,pack_b,row,*mine_a=tie(fq,fk,pack_b,row,*mine_a)
    other_a=[g.core(x) for x in mine_a]
    mine_b=[pack_b]
    first=[g.step(pack_b,t) for t in range(g.nb)]
    q,k,v,n1t,wqkv=qkv(idx,tok,row,vec,(q_weight,k_weight,v_weight),mine_a,other_a)
    fwd=attn_fwd(starts,q,k,v,fq,fk,(),0,3*nseq//2)
    o1,fx1,*first=tie(*fwd,*first)
    for t in range(g.nb):
        mine_b=mine_b+[first[t]]+[g.step(x,t) for x in mine_b[1:]]
    direct=[1<<t for t in range(g.nb)]
    other_b=[None]+[g.core(x) if j in direct else None for j,x in enumerate(mine_b[1:],1)]
    fwd=attn_fwd(starts,q,k,v,fq,fk,(o1,fx1),3*nseq//2,3*nseq)
    late=[j for j in range(1,S) if j not in direct]
    o1,fx1,*got=tie(*fwd,*[mine_b[j] for j in late])
    for j,x in zip(late,got):
        mine_b[j]=x
        other_b[j]=g.core(x)
    att,fx=attn_fwd(starts,q,k,v,fq,fk,(o1,fx1),9*nseq//2,6*nseq-9*nseq//2)
    res,gm,ga,keep_b,send_b,sv2,sub=mid(idx,tok,row,att,cot,vec,(o_weight,up_weight,down_weight),mine_b[1:],other_b[1:])
    cuts=[0,nseq,nseq+5*nseq//2,5*nseq,6*nseq]
    call=lambda prev,i: attn_bwd(starts,q,k,v,fx,fk,att,ga,prev,cuts[i],cuts[i+1]-cuts[i])
    got=g.core(send_b)
    d=call((),0)
    d,got=tie(d,got)
    n=S
    x=[keep_b]
    for t in reversed(range(g.nb)):
        n//=2
        up,x=upper(x+[got],n)
        d,up=tie(d,up)
        got=g.step(up,t)
        i=g.nb-t
        if i<=2:
            d=call((d,),i)
            d,got=tie(d,got)
    xb=add(*[y[0] for y in x],got[0])
    d,xb,*rows_b=tie(d,xb,*plane_rows(g,xb))
    parts=plane_send(g,rows_b)
    d=call((d,),3)
    keep_a,send_a,svq=dw(idx,n1t,d,S)
    keep_a,send_a,*parts=tie(keep_a,send_a,*parts)
    got=g.core(send_a)
    mine=plane_sum(g,xb,parts)
    back=[g.plane(mine,j) for j in range(1,g.Z)]
    gm,mine_,got=tie(gm,mine,got)
    up,x=upper([keep_a,got],S//2)
    gm,up=tie(gm,up)
    got=g.step(up,g.nb-1)
    gt,sv1,ts=dx(tok,row,d,gm,wqkv,vec)
    ts,got=tie(ts,got)
    n=S//2
    for t in reversed(range(g.nb-1)):
        n//=2
        up,x=upper(x+[got],n)
        ts,up=tie(ts,up)
        got=g.step(up,t)
    pay=sums(ids,sv1,svq,sv2,sub,ts)
    pays=[pay]+[g.direct(pay,j) for j in range(1,S)]
    pays[-1],got=tie(pays[-1],got)
    xa=add(*[y[0] for y in x],got[0])
    rows_a=plane_rows(g,xa)
    *pays,rows_a[0]=tie(*pays,rows_a[0])
    parts_a=plane_send(g,rows_a)
    pay=group(idx,pays,nseq)
    out_b=plane_join(g,mine_,back)
    out_b,pay,*parts_a=tie(out_b,pay,*parts_a)
    other_b=g.core(out_b)
    mine=plane_sum(g,xa,parts_a)
    pay,mine=tie(pay,mine)
    back_a=[g.plane(mine,j) for j in range(1,g.Z)]
    pays=[pay]+[g.move(pay,lambda r,s,j=j:(r^j,s)) for j in range(1,g.R)]
    go,gup,gdn=unpack(idx,out_b,other_b,((w,1),(w,4),(fr,1)))
    gup,*both=tie(gup,*back_a,*pays)
    back_a,pays=both[:g.Z-1],both[g.Z-1:]
    out_a=plane_join(g,mine,back_a)
    other_a=g.core(out_a)
    *sums8,subs,gtab=table(idx,pays,own,w,up_bias.shape[0])
    gtab,other_a=tie(gtab,other_a)
    gq,gk,gv=unpack(idx,out_a,other_a,((w,1),)*3)
    return (res.reshape(tokens.shape),gt.reshape(tokens.shape),gtab,sums8[0],sums8[1],gq,sums8[2],gk,gv,sums8[3],go,sums8[4],sums8[5],sums8[6],gup,subs,gdn,sums8[7])


def solution(mesh):
    b=("rep","shard")
    s=P("shard")
    m=P("shard",None)
    t=P(b,None,None)
    return jax.shard_map(local,mesh=mesh,
        in_specs=(t,P(b,None),P(b),m,s,s,m,s,m,m,s,m,s,s,s,m,s,m,s,t),
        out_specs=(t,t,m,s,s,m,s,m,m,s,m,s,s,s,m,s,m,s),check_vma=False)
```

```python
import functools
import math

import jax
import jax.numpy as jnp
from jax import lax
from jax.experimental import pallas as pl
from jax.experimental.pallas import tpu as pltpu
from jax.sharding import PartitionSpec as P

NEG=-1e30
EPS=1e-5
L=1024
D=768
FF=3072
HC=D//2
BF=jnp.bfloat16
F32=jnp.float32
LOG2E=math.log2(math.e)
LN2=math.log(2.0)
QS=0.125*LOG2E
VR=14
VP=16
NV=12
ANY=pl.BlockSpec(memory_space=pl.ANY)
S_=jax.ShapeDtypeStruct


def nt(a,b):
    return lax.dot_general(a,b,(((1,),(1,)),((),())),preferred_element_type=F32)


def nn(a,b):
    return lax.dot_general(a,b,(((1,),(0,)),((),())),preferred_element_type=F32)


def tn(a,b):
    return lax.dot_general(a,b,(((0,),(0,)),((),())),preferred_element_type=F32)


def full(*s):
    return pl.BlockSpec(s,lambda i,*_:(0,)*len(s),pipeline_mode=pl.Buffered(1))


def norm(x):
    mean=jnp.mean(x,axis=1,keepdims=True)
    off=x-mean
    var=jnp.mean(off*off,axis=1,keepdims=True)
    r=lax.rsqrt(var+EPS)
    return off*r,r


def sum8(x):
    return jnp.sum(x.reshape(x.shape[0]//8,8,x.shape[1]),axis=0)


def cost(flops,nbytes,trans=0):
    return pl.CostEstimate(flops=int(flops)//10,bytes_accessed=int(nbytes)//10,transcendentals=int(trans)//10)


def seg_features(seg):
    lane=jnp.arange(128)%64
    hit=seg[:,None]==lane[None,:]
    first=(lane<4)[None]
    fq=jnp.where(first&hit,1.0,0.0).astype(BF)
    fk=jnp.where(first,jnp.where(hit,0.0,NEG),jnp.where((lane<7)[None],1.0,0.0)).astype(BF)
    return fq,fk


def qkv_kernel(idx_ref,*refs,ns,wr):
    tok_ref,row_ref,vec_ref=refs[:3]
    own=refs[3:6]
    mine=refs[6:6+ns-1]
    other=refs[6+ns-1:6+2*(ns-1)]
    hi=6+2*(ns-1)
    q_ref,k_ref,v_ref,nt_ref,w_ref,sem=refs[hi:hi+6]
    @pl.when(pl.program_id(0)==0)
    def _():
        c=idx_ref[0]
        def put(src,w,sh,cols):
            rows=pl.ds(pl.multiple_of(sh*wr,16),wr)
            dst=w_ref.at[w,rows] if cols is None else w_ref.at[w,rows,pl.ds(pl.multiple_of(cols*HC,128),HC)]
            pltpu.make_async_copy(src,dst,sem.at[w]).start()
        for w in range(3):
            put(own[w],w,idx_ref[1],None)
            for j in range(1,ns):
                put(mine[j-1].at[pl.ds(w*wr,wr)],w,idx_ref[1+j],c)
                put(other[j-1].at[pl.ds(w*wr,wr)],w,idx_ref[1+j],1-c)
    xhat,_=norm(tok_ref[...]+row_ref[0])
    n1=(xhat*vec_ref[0:1,:]+vec_ref[1:2,:]).astype(BF)
    nt_ref[...]=n1.T
    def arrived(w):
        @pl.when(pl.program_id(0)==0)
        def _():
            pltpu.make_async_copy(w_ref.at[w],w_ref.at[w],sem.at[w]).wait()
    arrived(0)
    q_ref[...]=((nn(n1,w_ref[0])+vec_ref[2:3,:])*QS).astype(BF)
    arrived(1)
    k_ref[...]=nn(n1,w_ref[1]).astype(BF)
    arrived(2)
    v_ref[...]=(nn(n1,w_ref[2])+vec_ref[3:4,:]).astype(BF)


def qkv(idx,tok,row,vec,own,mine,other,tb=512):
    T=tok.shape[0]
    per=L//tb
    ns=len(mine)+1
    wr=own[0].shape[0]
    blk=pl.BlockSpec((tb,D),lambda i,*_:(i,0))
    return pl.pallas_call(
        functools.partial(qkv_kernel,ns=ns,wr=wr),
        grid_spec=pltpu.PrefetchScalarGridSpec(
            num_scalar_prefetch=1,grid=(T//tb,),
            in_specs=[blk,pl.BlockSpec((1,1,D),lambda i,*_:(i//per,0,0)),full(VR,D)]+[ANY]*(3+2*(ns-1)),
            out_specs=[blk]*3+[pl.BlockSpec((D,tb),lambda i,*_:(0,i)),full(3,D,D)],
            scratch_shapes=[pltpu.SemaphoreType.DMA((3,))]),
        out_shape=[S_((T,D),BF)]*3+[S_((D,T),BF),S_((3,D,D),BF)],
        compiler_params=pltpu.CompilerParams(dimension_semantics=("arbitrary",)),
        cost_estimate=cost(6*T*D*D,T*D*10+9*D*D),
        name="qkv")(idx,tok,row,vec,*own,*mine,*other)


def pack_a_kernel(idx_ref,q_ref,k_ref,v_ref,out_ref):
    wr=q_ref.shape[0]
    for ch in (0,1):
        @pl.when(idx_ref[0]==ch)
        def _():
            for w,ref in enumerate((q_ref,k_ref,v_ref)):
                out_ref[w*wr:(w+1)*wr,:]=ref[:,ch*HC:(ch+1)*HC]


def pack_b_kernel(idx_ref,o_ref,u_ref,d_ref,out_ref):
    wr=o_ref.shape[0]
    for ch in (0,1):
        @pl.when(idx_ref[0]==ch)
        def _():
            out_ref[0:wr,:]=o_ref[:,ch*HC:(ch+1)*HC]
            for b in range(4):
                out_ref[wr+b*wr:2*wr+b*wr,:]=u_ref[:,(ch*4+b)*HC:(ch*4+b+1)*HC]
            out_ref[5*wr:,:]=d_ref[:,ch*HC:(ch+1)*HC]


def pack(kernel,idx,ws,name):
    rows=sum(x.shape[0]*x.shape[1]//D for x in ws)
    vm=pl.BlockSpec(memory_space=pltpu.VMEM)
    return pl.pallas_call(kernel,in_specs=[pl.BlockSpec(memory_space=pltpu.SMEM)]+[vm]*3,out_specs=vm,
        out_shape=S_((rows,HC),BF),cost_estimate=cost(0,4*rows*D),name=name)(idx,*ws)


MAIN=800
ROWS=816
LANES=896
REST=768


def windows(s):
    s16=(s//16)*16
    return pl.multiple_of(jnp.minimum(s16,L-ROWS),16),pl.multiple_of(jnp.minimum(s16,L-LANES),16)


def fwd_kernel(s_ref,q_ref,k_ref,v_ref,fq_ref,fk_ref,*refs,f0,ns):
    o_ref,fx_ref=refs[-2:]
    s0=s_ref[s_ref[ns+f0+pl.program_id(0)]]
    wr,wl=windows(s0)
    lane=lax.broadcasted_iota(jnp.int32,(1,128),1)
    lo=lane<64
    l6=lane&63
    rest_row=lax.broadcasted_iota(jnp.int32,(256,1),0)
    ahead=rest_row<s0
    qb=ROWS//3
    rest=lambda ref: jnp.where(ahead,ref[0:256,:],ref[REST:L,:])
    main=lambda ref: ref[pl.ds(wl,LANES),:]
    one=jnp.where(l6==0,1.0,0.0).astype(BF)
    kv=[]
    for take in (rest,main):
        k=take(k_ref)
        v=take(v_ref)
        fk=take(fk_ref)
        kv.append([(jnp.where(own,k,fk),jnp.where(own,v,one)) for own in (lo,~lo)])
    qf=[(rest(q_ref),rest(fq_ref))]
    for b in range(3):
        rows=pl.ds(pl.multiple_of(wr+b*qb,16),qb)
        qf.append((q_ref[rows,:],fq_ref[rows,:]))
    units=[(b,h) for b in range(4) for h in (0,1)]
    def score(b,h):
        return nt(jnp.where(lo if h==0 else ~lo,*qf[b]),kv[min(b,1)][h][0])
    pend=[score(*u) for u in units[:3]]
    accs=[]
    ls=[]
    for i,(b,h) in enumerate(units):
        s=pend.pop(0)
        if i+3<len(units):
            pend.append(score(*units[i+3]))
        m=jnp.max(s,axis=1,keepdims=True)
        p=jnp.exp2(s-m).astype(BF)
        acc=nn(p,kv[min(b,1)][h][1])
        l=acc[:,64:65] if h==0 else acc[:,0:1]
        accs.append(acc*(1.0/l))
        ls.append(-(m+jnp.log2(l)))
        if h==1:
            o=jnp.where(lo,accs[0],accs[1]).astype(BF)
            nl=jnp.where(lo,ls[1],ls[0])
            hi=nl.astype(BF).astype(F32)
            r1=nl-hi
            mid=r1.astype(BF).astype(F32)
            r2=r1-mid
            fx=jnp.where(l6==4,hi,jnp.where(l6==5,mid,jnp.where(l6==6,r2,qf[b][1].astype(F32)))).astype(BF)
            if b==0:
                o_ref[0:256,:]=o
                fx_ref[0:256,:]=fx
                o_ref[REST:L,:]=o
                fx_ref[REST:L,:]=fx
            else:
                at=wr+(b-1)*qb
                rows=pl.ds(pl.multiple_of(at,16),qb)
                pos=lax.broadcasted_iota(jnp.int32,(qb,1),0)+(at-s0)
                inside=(pos>=0)&(pos<MAIN)
                o_ref[rows,:]=jnp.where(inside,o,o_ref[rows,:])
                fx_ref[rows,:]=jnp.where(inside,fx,fx_ref[rows,:])
            accs=[]
            ls=[]


def attn_fwd(starts,q,k,v,fq,fk,prev,f0,n):
    T=q.shape[0]
    ns=T//L
    nu=ns*(D//128)
    blk=pl.BlockSpec((L,128),lambda i,s:(s[ns+f0+i],s[ns+nu+f0+i]))
    fb=pl.BlockSpec((L,128),lambda i,s:(s[ns+f0+i],0))
    prev=list(prev)
    return pl.pallas_call(
        functools.partial(fwd_kernel,f0=f0,ns=ns),
        grid_spec=pltpu.PrefetchScalarGridSpec(
            num_scalar_prefetch=1,grid=(n,),
            in_specs=[blk,blk,blk,fb,fb]+[ANY]*len(prev),out_specs=[blk,blk]),
        out_shape=[S_((T,D),BF)]*2,
        input_output_aliases={6+i:i for i in range(len(prev))},
        compiler_params=pltpu.CompilerParams(dimension_semantics=("arbitrary",)),
        cost_estimate=cost(n*2*4*L*L*256,n*L*128*14,n*2*L*L),
        name="attn_fwd")(starts,q,k,v,fq,fk,*prev)


def bwd_kernel(s_ref,q_ref,k_ref,v_ref,fx_ref,fk_ref,o_ref,do_ref,*refs,f0,ns):
    out_ref=refs[-1]
    s0=s_ref[s_ref[ns+f0+pl.program_id(0)]]
    wr,wl=windows(s0)
    lane=lax.broadcasted_iota(jnp.int32,(1,128),1)
    lo=lane<64
    l6=lane&63
    zero=jnp.zeros((),BF)
    ones2=jnp.where(l6<2,1.0,0.0).astype(BF)
    rest_row=lax.broadcasted_iota(jnp.int32,(256,1),0)
    ahead=rest_row<s0
    rest=lambda ref: jnp.where(ahead,ref[0:256,:],ref[REST:L,:])
    def block(take_k,nk,takes):
        k=take_k(k_ref)
        v=take_k(v_ref)
        fk=take_k(fk_ref)
        kx=[]
        vx=[]
        km=[]
        for own in (lo,~lo):
            kx.append(jnp.where(own,k,fk))
            vx.append(jnp.where(own,v,ones2))
            km.append(jnp.where(own,k,zero))
        dv=jnp.zeros((nk,128),F32)
        dk=jnp.zeros((nk,128),F32)
        dqs=[]
        for take in takes:
            q=take(q_ref)
            fx=take(fx_ref)
            do=take(do_ref)
            prod=do.astype(F32)*take(o_ref).astype(F32)
            d0=-jnp.sum(jnp.where(lo,prod,0.0),axis=1,keepdims=True)
            d1=-jnp.sum(jnp.where(lo,0.0,prod),axis=1,keepdims=True)
            nd=jnp.where(lo,d1,d0)
            hi=nd.astype(BF).astype(F32)
            fd=jnp.where(l6==0,hi,jnp.where(l6==1,nd-hi,0.0)).astype(BF)
            dq=jnp.zeros(q.shape,F32)
            for h,own in enumerate((lo,~lo)):
                p=jnp.exp2(nt(kx[h],jnp.where(own,q,fx)))
                dpt=nt(vx[h],jnp.where(own,do,fd))
                pb=p.astype(BF)
                ds=(p*dpt).astype(BF)
                dv=dv+nn(pb,jnp.where(own,do,zero))
                dk=dk+nn(ds,jnp.where(own,q,zero))
                dq=dq+tn(ds,km[h])
            dqs.append((dq*0.125).astype(BF))
        return dqs,(dk*LN2).astype(BF),dv.astype(BF)
    dqs,dk,dv=block(rest,256,[rest])
    for w,x in enumerate((dqs[0],dk,dv)):
        out_ref[w,0:256,:]=x
        out_ref[w,REST:L,:]=x
    at=lambda start,n: pl.ds(pl.multiple_of(start,16),n)
    cuts=[(0,256),(256,256),(512,256),(768,128)]
    dqs,dk,dv=block(lambda ref: ref[at(wr,ROWS),:],ROWS,[lambda ref,c=c: ref[at(wl+c[0],c[1]),:] for c in cuts])
    def put(w,start,x):
        n=x.shape[0]
        pos=lax.broadcasted_iota(jnp.int32,(n,1),0)+(start-s0)
        out_ref[w,at(start,n),:]=jnp.where((pos>=0)&(pos<MAIN),x,out_ref[w,at(start,n),:])
    for c,x in zip(cuts,dqs):
        put(0,wl+c[0],x)
    put(1,wr,dk)
    put(2,wr,dv)


def attn_bwd(starts,q,k,v,fx,fk,o,do,prev,f0,n):
    T=q.shape[0]
    ns=T//L
    nu=ns*(D//128)
    blk=pl.BlockSpec((L,128),lambda i,s:(s[ns+f0+i],s[ns+nu+f0+i]))
    fb=pl.BlockSpec((L,128),lambda i,s:(s[ns+f0+i],0))
    prev=list(prev)
    return pl.pallas_call(
        functools.partial(bwd_kernel,f0=f0,ns=ns),
        grid_spec=pltpu.PrefetchScalarGridSpec(
            num_scalar_prefetch=1,grid=(n,),
            in_specs=[blk,blk,blk,blk,fb,blk,blk]+[ANY]*len(prev),
            out_specs=pl.BlockSpec((3,L,128),lambda i,s:(0,s[ns+f0+i],s[ns+nu+f0+i]))),
        out_shape=S_((3,T,D),BF),
        input_output_aliases={8+i:i for i in range(len(prev))},
        compiler_params=pltpu.CompilerParams(dimension_semantics=("arbitrary",)),
        cost_estimate=cost(n*2*10*L*L*256,n*L*128*20,n*2*L*L),
        name="attn_bwd")(starts,q,k,v,fx,fk,o,do,*prev)


def mid_kernel(idx_ref,*refs,tb,fc,ns,wr,fr):
    tok_ref,row_ref,att_ref,cot_ref,vec_ref=refs[:5]
    own=refs[5:8]
    mine=refs[8:8+ns-1]
    other=refs[8+ns-1:8+2*(ns-1)]
    b0=8+2*(ns-1)
    res_ref,gm_ref,ga_ref,keep_ref,send_ref,sv_ref,sub_ref,ow,up,dn,aup,adn,aow,sem=refs[b0:]
    i=pl.program_id(0)
    n=pl.num_programs(0)
    c=idx_ref[0]
    @pl.when(i==0)
    def _():
        def put(src,dst,k):
            pltpu.make_async_copy(src,dst,sem.at[k]).start()
        r16=lambda sh,m: pl.ds(pl.multiple_of(sh*m,16),m)
        for k in range(3):
            sh=idx_ref[1+ns]
            dst=(ow,up,dn)[k]
            m=(wr,wr,fr)[k]
            put(own[k],dst.at[r16(sh,m)],k)
            for j in range(1,ns):
                for src,sh,cc in ((mine[j-1],idx_ref[1+ns+j],c),(other[j-1],idx_ref[1+2*ns+j],1-c)):
                    if k==1:
                        for b in range(4):
                            put(src.at[pl.ds(wr+b*wr,wr)],up.at[r16(sh,wr),pl.ds(pl.multiple_of(cc*4*HC+b*HC,128),HC)],k)
                    else:
                        put(src.at[pl.ds(0 if k==0 else 5*wr,m)],dst.at[r16(sh,m),pl.ds(pl.multiple_of(cc*HC,128),HC)],k)
        aup[...]=jnp.zeros_like(aup)
        adn[...]=jnp.zeros_like(adn)
        aow[...]=jnp.zeros_like(aow)
        sv_ref[...]=jnp.zeros_like(sv_ref)
        sub_ref[...]=jnp.zeros_like(sub_ref)
        pltpu.make_async_copy(ow,ow,sem.at[0]).wait()
    ob=vec_ref[4:5,:]
    g2=vec_ref[5:6,:]
    b2=vec_ref[6:7,:]
    db=vec_ref[7:8,:]
    att=att_ref[...]
    mixed=tok_ref[...]+row_ref[0]+nn(att,ow[...])+ob
    xhat,r=norm(mixed)
    n2=(xhat*g2+b2).astype(BF)
    n2t=n2.T
    cot=cot_ref[...]
    g=cot.astype(BF)
    res=mixed+db
    @pl.when(i==0)
    def _():
        pltpu.make_async_copy(up,up,sem.at[1]).wait()
        pltpu.make_async_copy(dn,dn,sem.at[2]).wait()
    gn2=jnp.zeros((tb,D),F32)
    for j in range(FF//fc):
        cs=slice(j*fc,(j+1)*fc)
        pre=nn(n2,up[:,cs])+vec_ref[8+j:9+j,:]
        gact=nt(g,dn[cs,:])
        phi=0.5+0.5*lax.erf(pre*(2**-0.5))
        pdf=jnp.exp2(pre*pre*(-0.5*LOG2E))*(1.0/math.sqrt(2*math.pi))
        act=(pre*phi).astype(BF)
        gp=gact*(phi+pre*pdf)
        gpre=gp.astype(BF)
        sub_ref[:,cs]+=sum8(gp)
        res=res+nn(act,dn[cs,:])
        gn2=gn2+nt(gpre,up[:,cs])
        adn[cs,:]+=tn(act,g)
        aup[:,cs]+=nn(n2t,gpre)
    res_ref[...]=res
    e=gn2*g2
    c1=jnp.mean(e,axis=1,keepdims=True)
    c2=jnp.mean(e*xhat,axis=1,keepdims=True)
    gm=cot+r*(e-c1-xhat*c2)
    gml=gm.astype(BF)
    gm_ref[...]=gml
    ga_ref[...]=nt(gml,ow[...]).astype(BF)
    aow[...]+=tn(att,gml)
    sv_ref[0:8,:]+=sum8(gm)
    sv_ref[8:16,:]+=sum8(gn2*xhat)
    sv_ref[16:24,:]+=sum8(gn2)
    sv_ref[24:32,:]+=sum8(cot)
    @pl.when(i==n-1)
    def _():
        for ref,base,odd in ((keep_ref,1+ns,0),(send_ref,1+2*ns,1)):
            for ch in (0,1):
                @pl.when(c==(ch+odd)%2)
                def _():
                    def body(j,carry):
                        sh=idx_ref[base+j]
                        rw=pl.ds(pl.multiple_of(sh*wr,8),wr)
                        ref[j,0:wr,:]=aow[rw,ch*HC:(ch+1)*HC].astype(BF)
                        for b in range(4):
                            lo=(ch*4+b)*HC
                            ref[j,wr+b*wr:2*wr+b*wr,:]=aup[rw,lo:lo+HC].astype(BF)
                        ref[j,5*wr:5*wr+fr,:]=adn[pl.ds(pl.multiple_of(sh*fr,8),fr),ch*HC:(ch+1)*HC].astype(BF)
                        return carry
                    lax.fori_loop(0,ns,body,0)


def mid(idx,tok,row,att,cot,vec,own,mine,other,tb=256,fc=D):
    T=tok.shape[0]
    per=L//tb
    ns=len(mine)+1
    wr=own[0].shape[0]
    fr=own[2].shape[0]
    rb=5*wr+fr
    blk=pl.BlockSpec((tb,D),lambda i,*_:(i,0))
    return pl.pallas_call(
        functools.partial(mid_kernel,tb=tb,fc=fc,ns=ns,wr=wr,fr=fr),
        grid_spec=pltpu.PrefetchScalarGridSpec(
            num_scalar_prefetch=1,grid=(T//tb,),
            in_specs=[blk,pl.BlockSpec((1,1,D),lambda i,*_:(i//per,0,0)),blk,blk,full(VR,D)]+[ANY]*(3+2*(ns-1)),
            out_specs=[blk,blk,blk,full(ns,rb,HC),full(ns,rb,HC),full(32,D),full(8,FF)],
            scratch_shapes=[pltpu.VMEM((D,D),BF),pltpu.VMEM((D,FF),BF),pltpu.VMEM((FF,D),BF),
                pltpu.VMEM((D,FF),F32),pltpu.VMEM((FF,D),F32),pltpu.VMEM((D,D),F32),
                pltpu.SemaphoreType.DMA((3,))]),
        out_shape=[S_((T,D),F32),S_((T,D),BF),S_((T,D),BF),S_((ns,rb,HC),BF),S_((ns,rb,HC),BF),S_((32,D),F32),S_((8,FF),F32)],
        compiler_params=pltpu.CompilerParams(dimension_semantics=("arbitrary",),vmem_limit_bytes=67043328),
        cost_estimate=cost(6*T*D*(D+2*FF),T*D*20+30*D*FF,2*T*FF),
        name="mid")(idx,tok,row,att,cot,vec,*own,*mine,*other)


def dw_kernel(idx_ref,nt_ref,d_ref,keep_ref,send_ref,sv_ref,acc,*,ns,wr):
    i=pl.program_id(0)
    c=idx_ref[0]
    @pl.when(i==0)
    def _():
        acc[...]=jnp.zeros_like(acc)
        sv_ref[...]=jnp.zeros_like(sv_ref)
    for w in range(3):
        acc[w]+=nn(nt_ref[...],d_ref[w])
    sv_ref[0:8,:]+=sum8(d_ref[0].astype(F32))
    sv_ref[8:16,:]+=sum8(d_ref[2].astype(F32))
    @pl.when(i==pl.num_programs(0)-1)
    def _():
        for ref,base,odd in ((keep_ref,1+ns,0),(send_ref,1+2*ns,1)):
            for ch in (0,1):
                @pl.when(c==(ch+odd)%2)
                def _():
                    def body(j,carry):
                        rw=pl.ds(pl.multiple_of(idx_ref[base+j]*wr,8),wr)
                        for w in range(3):
                            ref[j,w*wr:(w+1)*wr,:]=acc[w,rw,ch*HC:(ch+1)*HC].astype(BF)
                        return carry
                    lax.fori_loop(0,ns,body,0)


def dw(idx,n1t,d,ns,tb=512):
    T=n1t.shape[1]
    wr=D//ns
    return pl.pallas_call(
        functools.partial(dw_kernel,ns=ns,wr=wr),
        grid_spec=pltpu.PrefetchScalarGridSpec(
            num_scalar_prefetch=1,grid=(T//tb,),
            in_specs=[pl.BlockSpec((D,tb),lambda i,*_:(0,i)),pl.BlockSpec((3,tb,D),lambda i,*_:(0,i,0))],
            out_specs=[full(ns,3*wr,HC),full(ns,3*wr,HC),full(16,D)],
            scratch_shapes=[pltpu.VMEM((3,D,D),F32)]),
        out_shape=[S_((ns,3*wr,HC),BF)]*2+[S_((16,D),F32)],
        compiler_params=pltpu.CompilerParams(dimension_semantics=("arbitrary",)),
        cost_estimate=cost(6*T*D*D,T*D*8+12*D*D),
        name="dw")(idx,n1t,d)


def dx_kernel(tok_ref,row_ref,d_ref,gm_ref,w_ref,vec_ref,gt_ref,sv_ref,ts_ref,*,per):
    i=pl.program_id(0)
    @pl.when(i==0)
    def _():
        sv_ref[...]=jnp.zeros_like(sv_ref)
    @pl.when(i%per==0)
    def _():
        ts_ref[...]=jnp.zeros_like(ts_ref)
    gn=nt(d_ref[0],w_ref[0])+nt(d_ref[1],w_ref[1])+nt(d_ref[2],w_ref[2])
    xhat,r=norm(tok_ref[...]+row_ref[0])
    e=gn*vec_ref[0:1,:]
    c1=jnp.mean(e,axis=1,keepdims=True)
    c2=jnp.mean(e*xhat,axis=1,keepdims=True)
    gt=gm_ref[...].astype(F32)+r*(e-c1-xhat*c2)
    gt_ref[...]=gt
    sv_ref[0:8,:]+=sum8(gn*xhat)
    sv_ref[8:16,:]+=sum8(gn)
    ts_ref[0]+=sum8(gt)


def dx(tok,row,d,gm,w,vec,tb=512):
    T=tok.shape[0]
    per=L//tb
    blk=pl.BlockSpec((tb,D),lambda i:(i,0))
    return pl.pallas_call(
        functools.partial(dx_kernel,per=per),grid=(T//tb,),
        in_specs=[blk,pl.BlockSpec((1,1,D),lambda i:(i//per,0,0)),pl.BlockSpec((3,tb,D),lambda i:(0,i,0)),blk,full(3,D,D),full(VR,D)],
        out_specs=[blk,full(16,D),pl.BlockSpec((1,8,D),lambda i:(i//per,0,0))],
        out_shape=[S_((T,D),F32),S_((16,D),F32),S_((T//L,8,D),F32)],
        compiler_params=pltpu.CompilerParams(dimension_semantics=("arbitrary",)),
        cost_estimate=cost(6*T*D*D,T*D*16+6*D*D),
        name="dx")(tok,row,d,gm,w,vec)


def rows8(x):
    return jnp.sum(x,axis=0,keepdims=True)


def sums_kernel(id_ref,sv1_ref,svq_ref,sv2_ref,sub_ref,ts_ref,out_ref):
    src=[sv1_ref[0:8],sv1_ref[8:16],svq_ref[0:8],svq_ref[8:16]]+[sv2_ref[8*i:8*i+8] for i in range(4)]
    src+=[sub_ref[:,i*D:(i+1)*D] for i in range(FF//D)]
    rows=[rows8(x) for x in src]+[id_ref[0:1],id_ref[1:2]]+[rows8(ts_ref[i]) for i in range(ts_ref.shape[0])]
    out_ref[...]=jnp.concatenate(rows,axis=0).astype(BF)


def sums(ids,sv1,svq,sv2,sub,ts):
    vm=pl.BlockSpec(memory_space=pltpu.VMEM)
    return pl.pallas_call(sums_kernel,in_specs=[vm]*6,out_specs=vm,
        out_shape=S_((VR+ts.shape[0],D),BF),cost_estimate=cost(0,10**6),name="sums")(ids,sv1,svq,sv2,sub,ts)


def group_kernel(idx_ref,*refs,ns,nseq):
    out_ref,acc=refs[ns:]
    tot=refs[0][0:VR].astype(F32)
    for j in range(1,ns):
        tot=tot+refs[j][0:VR].astype(F32)
    for j in range(ns):
        acc[idx_ref[1+j]]=refs[j][VR:VR+nseq].astype(F32)
    out_ref[...]=jnp.concatenate([tot]+[acc[j] for j in range(ns)],axis=0).astype(BF)


def group(idx,pays,nseq):
    ns=len(pays)
    vm=pl.BlockSpec(memory_space=pltpu.VMEM)
    return pl.pallas_call(functools.partial(group_kernel,ns=ns,nseq=nseq),
        in_specs=[pl.BlockSpec(memory_space=pltpu.SMEM)]+[vm]*ns,out_specs=vm,
        out_shape=S_((VR+ns*nseq,D),BF),scratch_shapes=[pltpu.VMEM((ns,nseq,D),F32)],
        cost_estimate=cost(0,10**6),name="group")(idx,*pays)


def table_kernel(idx_ref,*refs,nr,rows,own,me,w,fr):
    sum_refs=refs[nr:nr+8]
    sub_ref,tab_ref,acc,allr=refs[nr+8:]
    r0=idx_ref[me]
    s0=idx_ref[me+1]
    for j in range(nr):
        acc[r0^j]=refs[j][...].astype(F32)
    tot=acc[0,0:VR]
    for r in range(1,nr):
        tot=tot+acc[r,0:VR]
    mine=pltpu.roll(tot[0:8],D-s0*w,1)
    for i,ref in enumerate(sum_refs):
        ref[...]=mine[i:i+1,0:w].reshape(w)
    wide=jnp.concatenate([tot[8+i:9+i] for i in range(FF//D)],axis=1)
    sub_ref[...]=pltpu.roll(jnp.broadcast_to(wide,(8,FF)),FF-s0*fr,1)[0:1,0:fr].reshape(fr)
    for r in range(nr):
        allr[r*rows:(r+1)*rows,:]=acc[r,VR:VR+rows]
    n=nr*rows
    ids=tot[NV:NV+1,0:n]*32.0+tot[NV+1:NV+2,0:n]
    line=lax.broadcasted_iota(jnp.int32,(own,n),0)+s0*own
    hit=jnp.where(line==ids.astype(jnp.int32),1.0,0.0).astype(BF)
    tab_ref[...]=nn(hit,allr[...].astype(BF))


def table(idx,pays,own,w,fr):
    nr=len(pays)
    rows=pays[0].shape[0]-VR
    vm=pl.BlockSpec(memory_space=pltpu.VMEM)
    return pl.pallas_call(functools.partial(table_kernel,nr=nr,rows=rows,own=own,me=idx.shape[0]-3,w=w,fr=fr),
        in_specs=[pl.BlockSpec(memory_space=pltpu.SMEM)]+[vm]*nr,out_specs=[vm]*10,
        out_shape=[S_((w,),F32)]*8+[S_((fr,),F32),S_((own,D),F32)],
        scratch_shapes=[pltpu.VMEM((nr,VR+rows,D),F32),pltpu.VMEM((nr*rows,D),F32)],
        cost_estimate=cost(0,4*10**6),name="table")(idx,*pays)


def unpack_kernel(idx_ref,a_ref,b_ref,*outs,parts):
    for ch in (0,1):
        @pl.when(idx_ref[0]==ch)
        def _():
            for h,ref in enumerate((a_ref,b_ref) if ch==0 else (b_ref,a_ref)):
                r0=0
                for out,(nr,nb) in zip(outs,parts):
                    for b in range(nb):
                        out[:,(h*nb+b)*HC:(h*nb+b+1)*HC]=ref[r0:r0+nr,:].astype(F32)
                        r0+=nr


def unpack(idx,a,b,parts):
    vm=pl.BlockSpec(memory_space=pltpu.VMEM)
    return pl.pallas_call(functools.partial(unpack_kernel,parts=parts),
        in_specs=[pl.BlockSpec(memory_space=pltpu.SMEM),vm,vm],out_specs=[vm]*len(parts),
        out_shape=[S_((nr,2*nb*HC),F32) for nr,nb in parts],
        cost_estimate=cost(0,12*a.shape[0]*HC),name="unpack")(idx,a,b)


def small_kernel(idx_ref,ts_ref,*refs,w,fr,nseq,me):
    me_ref=[idx_ref[me+i] for i in range(3)]
    vecs=refs[:9]
    out_ref,id_ref=refs[9:]
    def spread(rows,width,at):
        n=rows[0].shape[1]
        y=jnp.concatenate(rows+[jnp.zeros((8-len(rows),n),F32)]*(len(rows)<8),axis=0)
        y=jnp.concatenate([y,jnp.zeros((8,width-n),F32)],axis=1)
        return pltpu.roll(y,at,1)
    row=lambda ref: ref[...].astype(F32).reshape(1,ref.shape[0])
    v=spread([row(r) for r in vecs[:8]],D,me_ref[1]*w)
    u=spread([row(vecs[8])],FF,me_ref[1]*fr)
    lane=lax.broadcasted_iota(jnp.int32,(1,D),1)
    def steps(at,high):
        y=jnp.zeros((1,D),jnp.int32)
        for i in range(nseq):
            t=ts_ref[i]
            y=jnp.where(lane==at*nseq+i,t//32 if high else t%32,y)
        return y.astype(F32)
    id_ref[...]=jnp.concatenate([steps(me_ref[2],True),steps(me_ref[2],False)],axis=0)
    out_ref[...]=jnp.concatenate([v]+[u[0:1,i*D:(i+1)*D] for i in range(FF//D)]+[steps(me_ref[1],True),steps(me_ref[1],False)],axis=0).astype(BF)


def small_rows(idx,time_steps,vecs):
    vm=pl.BlockSpec(memory_space=pltpu.VMEM)
    sm=pl.BlockSpec(memory_space=pltpu.SMEM)
    return pl.pallas_call(functools.partial(small_kernel,w=vecs[0].shape[0],fr=vecs[8].shape[0],nseq=time_steps.shape[0],me=idx.shape[0]-3),
        in_specs=[sm,sm]+[vm]*9,out_specs=[vm,vm],
        out_shape=[S_((VR,D),BF),S_((2,D),F32)],cost_estimate=cost(0,10**6),name="small")(idx,time_steps,*vecs)


class Ring:
    def __init__(self,rep,shard):
        self.R,self.S=rep,shard
        self.nb=shard.bit_length()-1
        self.Z=rep//2
        r=lax.axis_index("rep")
        self.s=lax.axis_index("shard")
        self.c=r%2
        self.z=r//2

    def move(self,x,to):
        pairs=[]
        for r in range(self.R):
            for s in range(self.S):
                r2,s2=to(r,s)
                pairs.append((r*self.S+s,r2*self.S+s2))
        return lax.ppermute(x,("rep","shard"),pairs)

    def order(self,c,t):
        return (t+c*(self.nb//2))%self.nb

    def mask(self,c,j):
        m=0
        for t in range(self.nb):
            if j>>t&1:
                m|=1<<self.order(c,t)
        return m

    def step(self,x,t):
        return self.move(x,lambda r,s:(r,s^(1<<self.order(r%2,t))))

    def direct(self,x,j):
        return self.move(x,lambda r,s:(r,s^j))

    def core(self,x):
        return self.move(x,lambda r,s:(r^1,s))

    def plane(self,x,j):
        return self.move(x,lambda r,s:(r^(2*j),s))

    def index(self):
        m=[[self.mask(c,j) for j in range(self.S)] for c in (0,1)]
        base=list(range(self.S))
        n=1+3*self.S
        t=jnp.where(self.c==0,jnp.array([0]+base+m[0]+m[1]+[0]*3,jnp.int32),jnp.array([0]+base+m[1]+m[0]+[0]*3,jnp.int32))
        at=jnp.arange(n+3)
        r=self.z*2+self.c
        t=jnp.where(at==0,self.c,t^self.s)
        t=jnp.where(at==n,r,jnp.where(at==n+1,self.s,jnp.where(at==n+2,r*self.S+self.s,t)))
        return t.astype(jnp.int32)


def tie(*xs):
    return lax.optimization_barrier(xs)


def add(*terms):
    y=terms[0].astype(F32)
    for x in terms[1:]:
        y=y+x.astype(F32)
    return y.astype(BF)


def upper(terms,n):
    return add(*[x[n:] for x in terms]),[x[:n] for x in terms]


def plane_rows(g,x):
    x=x.reshape(g.Z,-1,HC)
    return [lax.dynamic_index_in_dim(x,g.z^j,0,keepdims=False) for j in range(1,g.Z)]


def plane_send(g,rows):
    return [g.plane(x,j) for j,x in enumerate(rows,1)]


def plane_sum(g,x,parts):
    mine=lax.dynamic_index_in_dim(x.reshape(g.Z,-1,HC),g.z,0,keepdims=False).astype(F32)
    for p in parts:
        mine=mine+p.astype(F32)
    return mine.astype(BF)


def plane_join(g,mine,parts):
    out=jnp.zeros((g.Z,)+mine.shape,BF)
    for j,p in enumerate([mine]+parts):
        out=lax.dynamic_update_index_in_dim(out,p,g.z^j,0)
    return out.reshape(-1,HC)


def local(tokens,segments,time_steps,time_table,ln1_gain,ln1_bias,q_weight,q_bias,k_weight,v_weight,v_bias,o_weight,o_bias,ln2_gain,ln2_bias,up_weight,up_bias,down_weight,down_bias,cotangent):
    nseq=tokens.shape[0]
    T=nseq*L
    g=Ring(lax.axis_size("rep"),lax.axis_size("shard"))
    S=g.S
    w=ln1_gain.shape[0]
    fr=down_weight.shape[0]
    own=time_table.shape[0]
    idx=g.index()
    small,ids=small_rows(idx,time_steps,(ln1_gain,ln1_bias,q_bias,v_bias,o_bias,ln2_gain,ln2_bias,down_bias,up_bias))
    small,segments,o_weight_,q_weight_=tie(small,segments,o_weight,q_weight)
    pack_a=pack(pack_a_kernel,idx,(q_weight_,k_weight,v_weight),"pack_a")
    mine_a=[g.direct(pack_a,j) for j in range(1,S)]
    segments,pack_a=tie(segments,pack_a)
    vec=small.astype(F32)
    for j in reversed(range(1,S)):
        vec=vec+g.direct(small,j).astype(F32)
    steps=vec[NV,:S*nseq]*32.0+vec[NV+1,:S*nseq]
    hit=steps.astype(jnp.int32)[:,None]==jnp.arange(own)[None,:]+g.s*own
    rows=jnp.dot(hit.astype(BF),time_table,preferred_element_type=F32).astype(BF).reshape(S,nseq,D)
    pick=lambda j: lax.dynamic_index_in_dim(rows,g.s^j,0,keepdims=False)
    picks=[pick(j) for j in range(S)]
    picks[0],*mine_a=tie(picks[0],*mine_a)
    row=picks[0].astype(F32)
    for j in range(1,S):
        row=row+g.direct(picks[j],j).astype(F32)
    row=row.reshape(nseq,1,D)
    pack_b=pack(pack_b_kernel,idx,(o_weight_,up_weight,down_weight),"pack_b")
    tok=tokens.reshape(T,D)
    cot=cotangent.reshape(T,D)
    fq,fk=seg_features(segments.reshape(T))
    counts=jnp.sum(segments[:,:,None]==jnp.arange(4),axis=1)
    before=jnp.cumsum(counts==MAIN,axis=1)==0
    np_=D//128
    starts=jnp.concatenate([jnp.sum(jnp.where(before,counts,0),axis=1).astype(jnp.int32),
        jnp.array([i//np_ for i in range(nseq*np_)]+[i%np_ for i in range(nseq*np_)],jnp.int32)])
    fq,fk,pack_b,row,*mine_a=tie(fq,fk,pack_b,row,*mine_a)
    other_a=[g.core(x) for x in mine_a]
    mine_b=[pack_b]
    first=[g.step(pack_b,t) for t in range(g.nb)]
    q,k,v,n1t,wqkv=qkv(idx,tok,row,vec,(q_weight,k_weight,v_weight),mine_a,other_a)
    fwd=attn_fwd(starts,q,k,v,fq,fk,(),0,3*nseq//2)
    o1,fx1,*first=tie(*fwd,*first)
    for t in range(g.nb):
        mine_b=mine_b+[first[t]]+[g.step(x,t) for x in mine_b[1:]]
    direct=[1<<t for t in range(g.nb)]
    other_b=[None]+[g.core(x) if j in direct else None for j,x in enumerate(mine_b[1:],1)]
    fwd=attn_fwd(starts,q,k,v,fq,fk,(o1,fx1),3*nseq//2,3*nseq)
    late=[j for j in range(1,S) if j not in direct]
    o1,fx1,*got=tie(*fwd,*[mine_b[j] for j in late])
    for j,x in zip(late,got):
        mine_b[j]=x
        other_b[j]=g.core(x)
    att,fx=attn_fwd(starts,q,k,v,fq,fk,(o1,fx1),9*nseq//2,6*nseq-9*nseq//2)
    res,gm,ga,keep_b,send_b,sv2,sub=mid(idx,tok,row,att,cot,vec,(o_weight,up_weight,down_weight),mine_b[1:],other_b[1:])
    cuts=[0,nseq,nseq+5*nseq//2,5*nseq,6*nseq]
    call=lambda prev,i: attn_bwd(starts,q,k,v,fx,fk,att,ga,prev,cuts[i],cuts[i+1]-cuts[i])
    got=g.core(send_b)
    d=call((),0)
    d,got=tie(d,got)
    n=S
    x=[keep_b]
    for t in reversed(range(g.nb)):
        n//=2
        up,x=upper(x+[got],n)
        d,up=tie(d,up)
        got=g.step(up,t)
        i=g.nb-t
        if i<=2:
            d=call((d,),i)
            d,got=tie(d,got)
    xb=add(*[y[0] for y in x],got[0])
    d,xb,*rows_b=tie(d,xb,*plane_rows(g,xb))
    parts=plane_send(g,rows_b)
    d=call((d,),3)
    keep_a,send_a,svq=dw(idx,n1t,d,S)
    keep_a,send_a,*parts=tie(keep_a,send_a,*parts)
    got=g.core(send_a)
    mine=plane_sum(g,xb,parts)
    back=[g.plane(mine,j) for j in range(1,g.Z)]
    gm,mine_,got=tie(gm,mine,got)
    up,x=upper([keep_a,got],S//2)
    gm,up=tie(gm,up)
    got=g.step(up,g.nb-1)
    gt,sv1,ts=dx(tok,row,d,gm,wqkv,vec)
    ts,got=tie(ts,got)
    n=S//2
    for t in reversed(range(g.nb-1)):
        n//=2
        up,x=upper(x+[got],n)
        ts,up=tie(ts,up)
        got=g.step(up,t)
    pay=sums(ids,sv1,svq,sv2,sub,ts)
    pays=[pay]+[g.direct(pay,j) for j in range(1,S)]
    pays[-1],got=tie(pays[-1],got)
    xa=add(*[y[0] for y in x],got[0])
    rows_a=plane_rows(g,xa)
    *pays,rows_a[0]=tie(*pays,rows_a[0])
    parts_a=plane_send(g,rows_a)
    pay=group(idx,pays,nseq)
    out_b=plane_join(g,mine_,back)
    out_b,pay,*parts_a=tie(out_b,pay,*parts_a)
    other_b=g.core(out_b)
    mine=plane_sum(g,xa,parts_a)
    pay,mine=tie(pay,mine)
    back_a=[g.plane(mine,j) for j in range(1,g.Z)]
    pays=[pay]+[g.move(pay,lambda r,s,j=j:(r^j,s)) for j in range(1,g.R)]
    go,gup,gdn=unpack(idx,out_b,other_b,((w,1),(w,4),(fr,1)))
    gup,*both=tie(gup,*back_a,*pays)
    back_a,pays=both[:g.Z-1],both[g.Z-1:]
    out_a=plane_join(g,mine,back_a)
    other_a=g.core(out_a)
    *sums8,subs,gtab=table(idx,pays,own,w,up_bias.shape[0])
    gtab,other_a=tie(gtab,other_a)
    gq,gk,gv=unpack(idx,out_a,other_a,((w,1),)*3)
    return (res.reshape(tokens.shape),gt.reshape(tokens.shape),gtab,sums8[0],sums8[1],gq,sums8[2],gk,gv,sums8[3],go,sums8[4],sums8[5],sums8[6],gup,subs,gdn,sums8[7])


def solution(mesh):
    b=("rep","shard")
    s=P("shard")
    m=P("shard",None)
    t=P(b,None,None)
    return jax.shard_map(local,mesh=mesh,
        in_specs=(t,P(b,None),P(b),m,s,s,m,s,m,m,s,m,s,s,s,m,s,m,s,t),
        out_specs=(t,t,m,s,s,m,s,m,m,s,m,s,s,s,m,s,m,s),check_vma=False)
```

```python
import functools
import math

import jax
import jax.numpy as jnp
from jax import lax
from jax.experimental import pallas as pl
from jax.experimental.pallas import tpu as pltpu
from jax.sharding import PartitionSpec as P

NEG=-1e30
EPS=1e-5
L=1024
D=768
FF=3072
HC=D//2
BF=jnp.bfloat16
F32=jnp.float32
LOG2E=math.log2(math.e)
LN2=math.log(2.0)
QS=0.125*LOG2E
VR=14
VP=16
NV=12
ANY=pl.BlockSpec(memory_space=pl.ANY)
S_=jax.ShapeDtypeStruct


def nt(a,b):
    return lax.dot_general(a,b,(((1,),(1,)),((),())),preferred_element_type=F32)


def nn(a,b):
    return lax.dot_general(a,b,(((1,),(0,)),((),())),preferred_element_type=F32)


def tn(a,b):
    return lax.dot_general(a,b,(((0,),(0,)),((),())),preferred_element_type=F32)


def full(*s):
    return pl.BlockSpec(s,lambda i,*_:(0,)*len(s),pipeline_mode=pl.Buffered(1))


def norm(x):
    mean=jnp.mean(x,axis=1,keepdims=True)
    off=x-mean
    var=jnp.mean(off*off,axis=1,keepdims=True)
    r=lax.rsqrt(var+EPS)
    return off*r,r


def sum8(x):
    return jnp.sum(x.reshape(x.shape[0]//8,8,x.shape[1]),axis=0)


def cost(flops,nbytes,trans=0):
    return pl.CostEstimate(flops=int(flops)//10,bytes_accessed=int(nbytes)//10,transcendentals=int(trans)//10)


def seg_features(seg):
    lane=jnp.arange(128)%64
    hit=seg[:,None]==lane[None,:]
    first=(lane<4)[None]
    fq=jnp.where(first&hit,1.0,0.0).astype(BF)
    fk=jnp.where(first,jnp.where(hit,0.0,NEG),jnp.where((lane<7)[None],1.0,0.0)).astype(BF)
    return fq,fk


def qkv_kernel(idx_ref,*refs,ns,wr):
    tok_ref,row_ref,vec_ref=refs[:3]
    own=refs[3:6]
    mine=refs[6:6+ns-1]
    other=refs[6+ns-1:6+2*(ns-1)]
    hi=6+2*(ns-1)
    q_ref,k_ref,v_ref,nt_ref,w_ref,sem=refs[hi:hi+6]
    def copies(w):
        c=idx_ref[0]
        cps=[]
        def put(src,sh,cols):
            rows=pl.ds(pl.multiple_of(sh*wr,16),wr)
            dst=w_ref.at[w,rows] if cols is None else w_ref.at[w,rows,pl.ds(pl.multiple_of(cols*HC,128),HC)]
            cps.append(pltpu.make_async_copy(src,dst,sem.at[w,len(cps)]))
        put(own[w],idx_ref[1],None)
        for j in range(1,ns):
            put(mine[j-1].at[pl.ds(w*wr,wr)],idx_ref[1+j],c)
            put(other[j-1].at[pl.ds(w*wr,wr)],idx_ref[1+j],1-c)
        return cps
    first=pl.program_id(0)==0
    @pl.when(first)
    def _():
        for w in range(3):
            for cp in copies(w):
                cp.start()
    def arrived(w):
        @pl.when(first)
        def _():
            for cp in copies(w):
                cp.wait()
    xhat,_=norm(tok_ref[...]+row_ref[0])
    n1=(xhat*vec_ref[0:1,:]+vec_ref[1:2,:]).astype(BF)
    arrived(0)
    q_ref[...]=((nn(n1,w_ref[0])+vec_ref[2:3,:])*QS).astype(BF)
    arrived(1)
    k_ref[...]=nn(n1,w_ref[1]).astype(BF)
    arrived(2)
    v_ref[...]=(nn(n1,w_ref[2])+vec_ref[3:4,:]).astype(BF)
    nt_ref[...]=n1.T


def qkv(idx,tok,row,vec,own,mine,other,tb=512):
    T=tok.shape[0]
    per=L//tb
    ns=len(mine)+1
    wr=own[0].shape[0]
    blk=pl.BlockSpec((tb,D),lambda i,*_:(i,0))
    return pl.pallas_call(
        functools.partial(qkv_kernel,ns=ns,wr=wr),
        grid_spec=pltpu.PrefetchScalarGridSpec(
            num_scalar_prefetch=1,grid=(T//tb,),
            in_specs=[blk,pl.BlockSpec((1,1,D),lambda i,*_:(i//per,0,0)),full(VR,D)]+[ANY]*(3+2*(ns-1)),
            out_specs=[blk]*3+[pl.BlockSpec((D,tb),lambda i,*_:(0,i)),full(3,D,D)],
            scratch_shapes=[pltpu.SemaphoreType.DMA((3,1+2*(ns-1)))]),
        out_shape=[S_((T,D),BF)]*3+[S_((D,T),BF),S_((3,D,D),BF)],
        compiler_params=pltpu.CompilerParams(dimension_semantics=("arbitrary",)),
        cost_estimate=cost(6*T*D*D,T*D*10+9*D*D),
        name="qkv")(idx,tok,row,vec,*own,*mine,*other)


def pack_a_kernel(idx_ref,q_ref,k_ref,v_ref,out_ref):
    wr=q_ref.shape[0]
    for ch in (0,1):
        @pl.when(idx_ref[0]==ch)
        def _():
            for w,ref in enumerate((q_ref,k_ref,v_ref)):
                out_ref[w*wr:(w+1)*wr,:]=ref[:,ch*HC:(ch+1)*HC]


def pack_b_kernel(idx_ref,o_ref,u_ref,d_ref,out_ref):
    wr=o_ref.shape[0]
    for ch in (0,1):
        @pl.when(idx_ref[0]==ch)
        def _():
            out_ref[0:wr,:]=o_ref[:,ch*HC:(ch+1)*HC]
            for b in range(4):
                out_ref[wr+b*wr:2*wr+b*wr,:]=u_ref[:,(ch*4+b)*HC:(ch*4+b+1)*HC]
            out_ref[5*wr:,:]=d_ref[:,ch*HC:(ch+1)*HC]


def pack(kernel,idx,ws,name):
    rows=sum(x.shape[0]*x.shape[1]//D for x in ws)
    vm=pl.BlockSpec(memory_space=pltpu.VMEM)
    return pl.pallas_call(kernel,in_specs=[pl.BlockSpec(memory_space=pltpu.SMEM)]+[vm]*3,out_specs=vm,
        out_shape=S_((rows,HC),BF),cost_estimate=cost(0,4*rows*D),name=name)(idx,*ws)


MAIN=800
ROWS=816
LANES=896
REST=768


def windows(s):
    s16=(s//16)*16
    return pl.multiple_of(jnp.minimum(s16,L-ROWS),16),pl.multiple_of(jnp.minimum(s16,L-LANES),16)


def fwd_kernel(s_ref,q_ref,k_ref,v_ref,fq_ref,fk_ref,*refs,f0,ns):
    o_ref,fx_ref=refs[-2:]
    s0=s_ref[s_ref[ns+f0+pl.program_id(0)]]
    wr,wl=windows(s0)
    lane=lax.broadcasted_iota(jnp.int32,(1,128),1)
    lo=lane<64
    l6=lane&63
    rest_row=lax.broadcasted_iota(jnp.int32,(256,1),0)
    ahead=rest_row<s0
    qb=ROWS//3
    rest=lambda ref: jnp.where(ahead,ref[0:256,:],ref[REST:L,:])
    main=lambda ref: ref[pl.ds(wl,LANES),:]
    one=jnp.where(l6==0,1.0,0.0).astype(BF)
    kv=[]
    for take in (rest,main):
        k=take(k_ref)
        v=take(v_ref)
        fk=take(fk_ref)
        kv.append([(jnp.where(own,k,fk),jnp.where(own,v,one)) for own in (lo,~lo)])
    qf=[(rest(q_ref),rest(fq_ref))]
    for b in range(3):
        rows=pl.ds(pl.multiple_of(wr+b*qb,16),qb)
        qf.append((q_ref[rows,:],fq_ref[rows,:]))
    units=[(b,h) for b in range(4) for h in (0,1)]
    def score(b,h):
        return nt(jnp.where(lo if h==0 else ~lo,*qf[b]),kv[min(b,1)][h][0])
    pend=[score(*u) for u in units[:3]]
    accs=[]
    ls=[]
    for i,(b,h) in enumerate(units):
        s=pend.pop(0)
        if i+3<len(units):
            pend.append(score(*units[i+3]))
        m=jnp.max(s,axis=1,keepdims=True)
        p=jnp.exp2(s-m).astype(BF)
        acc=nn(p,kv[min(b,1)][h][1])
        l=acc[:,64:65] if h==0 else acc[:,0:1]
        accs.append(acc*(1.0/l))
        ls.append(-(m+jnp.log2(l)))
        if h==1:
            o=jnp.where(lo,accs[0],accs[1]).astype(BF)
            nl=jnp.where(lo,ls[1],ls[0])
            hi=nl.astype(BF).astype(F32)
            r1=nl-hi
            mid=r1.astype(BF).astype(F32)
            r2=r1-mid
            fx=jnp.where(l6==4,hi,jnp.where(l6==5,mid,jnp.where(l6==6,r2,qf[b][1].astype(F32)))).astype(BF)
            if b==0:
                o_ref[0:256,:]=o
                fx_ref[0:256,:]=fx
                o_ref[REST:L,:]=o
                fx_ref[REST:L,:]=fx
            else:
                at=wr+(b-1)*qb
                rows=pl.ds(pl.multiple_of(at,16),qb)
                pos=lax.broadcasted_iota(jnp.int32,(qb,1),0)+(at-s0)
                inside=(pos>=0)&(pos<MAIN)
                o_ref[rows,:]=jnp.where(inside,o,o_ref[rows,:])
                fx_ref[rows,:]=jnp.where(inside,fx,fx_ref[rows,:])
            accs=[]
            ls=[]


def attn_fwd(starts,q,k,v,fq,fk,prev,f0,n):
    T=q.shape[0]
    ns=T//L
    nu=ns*(D//128)
    blk=pl.BlockSpec((L,128),lambda i,s:(s[ns+f0+i],s[ns+nu+f0+i]))
    fb=pl.BlockSpec((L,128),lambda i,s:(s[ns+f0+i],0))
    prev=list(prev)
    return pl.pallas_call(
        functools.partial(fwd_kernel,f0=f0,ns=ns),
        grid_spec=pltpu.PrefetchScalarGridSpec(
            num_scalar_prefetch=1,grid=(n,),
            in_specs=[blk,blk,blk,fb,fb]+[ANY]*len(prev),out_specs=[blk,blk]),
        out_shape=[S_((T,D),BF)]*2,
        input_output_aliases={6+i:i for i in range(len(prev))},
        compiler_params=pltpu.CompilerParams(dimension_semantics=("arbitrary",)),
        cost_estimate=cost(n*2*4*L*L*256,n*L*128*14,n*2*L*L),
        name="attn_fwd")(starts,q,k,v,fq,fk,*prev)


def bwd_kernel(s_ref,q_ref,k_ref,v_ref,fx_ref,fk_ref,o_ref,do_ref,*refs,f0,ns):
    out_ref=refs[-1]
    s0=s_ref[s_ref[ns+f0+pl.program_id(0)]]
    wr,wl=windows(s0)
    lane=lax.broadcasted_iota(jnp.int32,(1,128),1)
    lo=lane<64
    l6=lane&63
    zero=jnp.zeros((),BF)
    ones2=jnp.where(l6<2,1.0,0.0).astype(BF)
    rest_row=lax.broadcasted_iota(jnp.int32,(256,1),0)
    ahead=rest_row<s0
    rest=lambda ref: jnp.where(ahead,ref[0:256,:],ref[REST:L,:])
    def block(take_k,nk,takes):
        k=take_k(k_ref)
        v=take_k(v_ref)
        fk=take_k(fk_ref)
        kx=[]
        vx=[]
        km=[]
        for own in (lo,~lo):
            kx.append(jnp.where(own,k,fk))
            vx.append(jnp.where(own,v,ones2))
            km.append(jnp.where(own,k,zero))
        dv=jnp.zeros((nk,128),F32)
        dk=jnp.zeros((nk,128),F32)
        dqs=[]
        for take in takes:
            q=take(q_ref)
            fx=take(fx_ref)
            do=take(do_ref)
            prod=do.astype(F32)*take(o_ref).astype(F32)
            d0=-jnp.sum(jnp.where(lo,prod,0.0),axis=1,keepdims=True)
            d1=-jnp.sum(jnp.where(lo,0.0,prod),axis=1,keepdims=True)
            nd=jnp.where(lo,d1,d0)
            hi=nd.astype(BF).astype(F32)
            fd=jnp.where(l6==0,hi,jnp.where(l6==1,nd-hi,0.0)).astype(BF)
            dq=jnp.zeros(q.shape,F32)
            for h,own in enumerate((lo,~lo)):
                p=jnp.exp2(nt(kx[h],jnp.where(own,q,fx)))
                dpt=nt(vx[h],jnp.where(own,do,fd))
                pb=p.astype(BF)
                ds=(p*dpt).astype(BF)
                dv=dv+nn(pb,jnp.where(own,do,zero))
                dk=dk+nn(ds,jnp.where(own,q,zero))
                dq=dq+tn(ds,km[h])
            dqs.append((dq*0.125).astype(BF))
        return dqs,(dk*LN2).astype(BF),dv.astype(BF)
    dqs,dk,dv=block(rest,256,[rest])
    for w,x in enumerate((dqs[0],dk,dv)):
        out_ref[w,0:256,:]=x
        out_ref[w,REST:L,:]=x
    at=lambda start,n: pl.ds(pl.multiple_of(start,16),n)
    cuts=[(0,256),(256,256),(512,256),(768,128)]
    dqs,dk,dv=block(lambda ref: ref[at(wr,ROWS),:],ROWS,[lambda ref,c=c: ref[at(wl+c[0],c[1]),:] for c in cuts])
    def put(w,start,x):
        n=x.shape[0]
        pos=lax.broadcasted_iota(jnp.int32,(n,1),0)+(start-s0)
        out_ref[w,at(start,n),:]=jnp.where((pos>=0)&(pos<MAIN),x,out_ref[w,at(start,n),:])
    for c,x in zip(cuts,dqs):
        put(0,wl+c[0],x)
    put(1,wr,dk)
    put(2,wr,dv)


def attn_bwd(starts,q,k,v,fx,fk,o,do,prev,f0,n):
    T=q.shape[0]
    ns=T//L
    nu=ns*(D//128)
    blk=pl.BlockSpec((L,128),lambda i,s:(s[ns+f0+i],s[ns+nu+f0+i]))
    fb=pl.BlockSpec((L,128),lambda i,s:(s[ns+f0+i],0))
    prev=list(prev)
    return pl.pallas_call(
        functools.partial(bwd_kernel,f0=f0,ns=ns),
        grid_spec=pltpu.PrefetchScalarGridSpec(
            num_scalar_prefetch=1,grid=(n,),
            in_specs=[blk,blk,blk,blk,fb,blk,blk]+[ANY]*len(prev),
            out_specs=pl.BlockSpec((3,L,128),lambda i,s:(0,s[ns+f0+i],s[ns+nu+f0+i]))),
        out_shape=S_((3,T,D),BF),
        input_output_aliases={8+i:i for i in range(len(prev))},
        compiler_params=pltpu.CompilerParams(dimension_semantics=("arbitrary",)),
        cost_estimate=cost(n*2*10*L*L*256,n*L*128*20,n*2*L*L),
        name="attn_bwd")(starts,q,k,v,fx,fk,o,do,*prev)


def mid_kernel(idx_ref,*refs,tb,fc,ns,wr,fr):
    tok_ref,row_ref,att_ref,cot_ref,vec_ref=refs[:5]
    own=refs[5:8]
    mine=refs[8:8+ns-1]
    other=refs[8+ns-1:8+2*(ns-1)]
    b0=8+2*(ns-1)
    res_ref,gm_ref,ga_ref,keep_ref,send_ref,sv_ref,sub_ref,ow,up,dn,aup,adn,aow,sem=refs[b0:]
    i=pl.program_id(0)
    n=pl.num_programs(0)
    c=idx_ref[0]
    def copies():
        cps=[]
        def put(src,dst):
            cps.append(pltpu.make_async_copy(src,dst,sem.at[len(cps)]))
        r16=lambda sh,m: pl.ds(pl.multiple_of(sh*m,16),m)
        sh=idx_ref[1+ns]
        put(own[0],ow.at[r16(sh,wr)])
        put(own[1],up.at[r16(sh,wr)])
        put(own[2],dn.at[r16(sh,fr)])
        for j in range(1,ns):
            for src,sh,cc in ((mine[j-1],idx_ref[1+ns+j],c),(other[j-1],idx_ref[1+2*ns+j],1-c)):
                cd=pl.ds(pl.multiple_of(cc*HC,128),HC)
                put(src.at[pl.ds(0,wr)],ow.at[r16(sh,wr),cd])
                for b in range(4):
                    put(src.at[pl.ds(wr+b*wr,wr)],up.at[r16(sh,wr),pl.ds(pl.multiple_of(cc*4*HC+b*HC,128),HC)])
                put(src.at[pl.ds(5*wr,fr)],dn.at[r16(sh,fr),cd])
        return cps
    @pl.when(i==0)
    def _():
        cps=copies()
        for cp in cps:
            cp.start()
        aup[...]=jnp.zeros_like(aup)
        adn[...]=jnp.zeros_like(adn)
        aow[...]=jnp.zeros_like(aow)
        sv_ref[...]=jnp.zeros_like(sv_ref)
        sub_ref[...]=jnp.zeros_like(sub_ref)
        for cp in cps:
            cp.wait()
    ob=vec_ref[4:5,:]
    g2=vec_ref[5:6,:]
    b2=vec_ref[6:7,:]
    db=vec_ref[7:8,:]
    att=att_ref[...]
    mixed=tok_ref[...]+row_ref[0]+nn(att,ow[...])+ob
    xhat,r=norm(mixed)
    n2=(xhat*g2+b2).astype(BF)
    n2t=n2.T
    cot=cot_ref[...]
    g=cot.astype(BF)
    res=mixed+db
    gn2=jnp.zeros((tb,D),F32)
    for j in range(FF//fc):
        cs=slice(j*fc,(j+1)*fc)
        pre=nn(n2,up[:,cs])+vec_ref[8+j:9+j,:]
        gact=nt(g,dn[cs,:])
        phi=0.5+0.5*lax.erf(pre*(2**-0.5))
        pdf=jnp.exp2(pre*pre*(-0.5*LOG2E))*(1.0/math.sqrt(2*math.pi))
        act=(pre*phi).astype(BF)
        gp=gact*(phi+pre*pdf)
        gpre=gp.astype(BF)
        sub_ref[:,cs]+=sum8(gp)
        res=res+nn(act,dn[cs,:])
        gn2=gn2+nt(gpre,up[:,cs])
        adn[cs,:]+=tn(act,g)
        aup[:,cs]+=nn(n2t,gpre)
    res_ref[...]=res
    e=gn2*g2
    c1=jnp.mean(e,axis=1,keepdims=True)
    c2=jnp.mean(e*xhat,axis=1,keepdims=True)
    gm=cot+r*(e-c1-xhat*c2)
    gml=gm.astype(BF)
    gm_ref[...]=gml
    ga_ref[...]=nt(gml,ow[...]).astype(BF)
    aow[...]+=tn(att,gml)
    sv_ref[0:8,:]+=sum8(gm)
    sv_ref[8:16,:]+=sum8(gn2*xhat)
    sv_ref[16:24,:]+=sum8(gn2)
    sv_ref[24:32,:]+=sum8(cot)
    @pl.when(i==n-1)
    def _():
        for ref,base,odd in ((keep_ref,1+ns,0),(send_ref,1+2*ns,1)):
            for ch in (0,1):
                @pl.when(c==(ch+odd)%2)
                def _():
                    def body(j,carry):
                        sh=idx_ref[base+j]
                        rw=pl.ds(pl.multiple_of(sh*wr,8),wr)
                        ref[j,0:wr,:]=aow[rw,ch*HC:(ch+1)*HC].astype(BF)
                        for b in range(4):
                            lo=(ch*4+b)*HC
                            ref[j,wr+b*wr:2*wr+b*wr,:]=aup[rw,lo:lo+HC].astype(BF)
                        ref[j,5*wr:5*wr+fr,:]=adn[pl.ds(pl.multiple_of(sh*fr,8),fr),ch*HC:(ch+1)*HC].astype(BF)
                        return carry
                    lax.fori_loop(0,ns,body,0)


def mid(idx,tok,row,att,cot,vec,own,mine,other,tb=256,fc=D):
    T=tok.shape[0]
    per=L//tb
    ns=len(mine)+1
    wr=own[0].shape[0]
    fr=own[2].shape[0]
    rb=5*wr+fr
    blk=pl.BlockSpec((tb,D),lambda i,*_:(i,0))
    return pl.pallas_call(
        functools.partial(mid_kernel,tb=tb,fc=fc,ns=ns,wr=wr,fr=fr),
        grid_spec=pltpu.PrefetchScalarGridSpec(
            num_scalar_prefetch=1,grid=(T//tb,),
            in_specs=[blk,pl.BlockSpec((1,1,D),lambda i,*_:(i//per,0,0)),blk,blk,full(VR,D)]+[ANY]*(3+2*(ns-1)),
            out_specs=[blk,blk,blk,full(ns,rb,HC),full(ns,rb,HC),full(32,D),full(8,FF)],
            scratch_shapes=[pltpu.VMEM((D,D),BF),pltpu.VMEM((D,FF),BF),pltpu.VMEM((FF,D),BF),
                pltpu.VMEM((D,FF),F32),pltpu.VMEM((FF,D),F32),pltpu.VMEM((D,D),F32),
                pltpu.SemaphoreType.DMA((3+12*(ns-1),))]),
        out_shape=[S_((T,D),F32),S_((T,D),BF),S_((T,D),BF),S_((ns,rb,HC),BF),S_((ns,rb,HC),BF),S_((32,D),F32),S_((8,FF),F32)],
        compiler_params=pltpu.CompilerParams(dimension_semantics=("arbitrary",),vmem_limit_bytes=67043328),
        cost_estimate=cost(6*T*D*(D+2*FF),T*D*20+30*D*FF,2*T*FF),
        name="mid")(idx,tok,row,att,cot,vec,*own,*mine,*other)


def dw_kernel(idx_ref,nt_ref,d_ref,keep_ref,send_ref,sv_ref,acc,*,ns,wr):
    i=pl.program_id(0)
    c=idx_ref[0]
    @pl.when(i==0)
    def _():
        acc[...]=jnp.zeros_like(acc)
        sv_ref[...]=jnp.zeros_like(sv_ref)
    for w in range(3):
        acc[w]+=nn(nt_ref[...],d_ref[w])
    sv_ref[0:8,:]+=sum8(d_ref[0].astype(F32))
    sv_ref[8:16,:]+=sum8(d_ref[2].astype(F32))
    @pl.when(i==pl.num_programs(0)-1)
    def _():
        for ref,base,odd in ((keep_ref,1+ns,0),(send_ref,1+2*ns,1)):
            for ch in (0,1):
                @pl.when(c==(ch+odd)%2)
                def _():
                    def body(j,carry):
                        rw=pl.ds(pl.multiple_of(idx_ref[base+j]*wr,8),wr)
                        for w in range(3):
                            ref[j,w*wr:(w+1)*wr,:]=acc[w,rw,ch*HC:(ch+1)*HC].astype(BF)
                        return carry
                    lax.fori_loop(0,ns,body,0)


def dw(idx,n1t,d,ns,tb=512):
    T=n1t.shape[1]
    wr=D//ns
    return pl.pallas_call(
        functools.partial(dw_kernel,ns=ns,wr=wr),
        grid_spec=pltpu.PrefetchScalarGridSpec(
            num_scalar_prefetch=1,grid=(T//tb,),
            in_specs=[pl.BlockSpec((D,tb),lambda i,*_:(0,i)),pl.BlockSpec((3,tb,D),lambda i,*_:(0,i,0))],
            out_specs=[full(ns,3*wr,HC),full(ns,3*wr,HC),full(16,D)],
            scratch_shapes=[pltpu.VMEM((3,D,D),F32)]),
        out_shape=[S_((ns,3*wr,HC),BF)]*2+[S_((16,D),F32)],
        compiler_params=pltpu.CompilerParams(dimension_semantics=("arbitrary",)),
        cost_estimate=cost(6*T*D*D,T*D*8+12*D*D),
        name="dw")(idx,n1t,d)


def dx_kernel(tok_ref,row_ref,d_ref,gm_ref,w_ref,vec_ref,gt_ref,sv_ref,ts_ref,*,per):
    i=pl.program_id(0)
    @pl.when(i==0)
    def _():
        sv_ref[...]=jnp.zeros_like(sv_ref)
    @pl.when(i%per==0)
    def _():
        ts_ref[...]=jnp.zeros_like(ts_ref)
    gn=nt(d_ref[0],w_ref[0])+nt(d_ref[1],w_ref[1])+nt(d_ref[2],w_ref[2])
    xhat,r=norm(tok_ref[...]+row_ref[0])
    e=gn*vec_ref[0:1,:]
    c1=jnp.mean(e,axis=1,keepdims=True)
    c2=jnp.mean(e*xhat,axis=1,keepdims=True)
    gt=gm_ref[...].astype(F32)+r*(e-c1-xhat*c2)
    gt_ref[...]=gt
    sv_ref[0:8,:]+=sum8(gn*xhat)
    sv_ref[8:16,:]+=sum8(gn)
    ts_ref[0]+=sum8(gt)


def dx(tok,row,d,gm,w,vec,tb=512):
    T=tok.shape[0]
    per=L//tb
    blk=pl.BlockSpec((tb,D),lambda i:(i,0))
    return pl.pallas_call(
        functools.partial(dx_kernel,per=per),grid=(T//tb,),
        in_specs=[blk,pl.BlockSpec((1,1,D),lambda i:(i//per,0,0)),pl.BlockSpec((3,tb,D),lambda i:(0,i,0)),blk,full(3,D,D),full(VR,D)],
        out_specs=[blk,full(16,D),pl.BlockSpec((1,8,D),lambda i:(i//per,0,0))],
        out_shape=[S_((T,D),F32),S_((16,D),F32),S_((T//L,8,D),F32)],
        compiler_params=pltpu.CompilerParams(dimension_semantics=("arbitrary",)),
        cost_estimate=cost(6*T*D*D,T*D*16+6*D*D),
        name="dx")(tok,row,d,gm,w,vec)


def rows8(x):
    return jnp.sum(x,axis=0,keepdims=True)


def sums_kernel(id_ref,sv1_ref,svq_ref,sv2_ref,sub_ref,ts_ref,out_ref):
    src=[sv1_ref[0:8],sv1_ref[8:16],svq_ref[0:8],svq_ref[8:16]]+[sv2_ref[8*i:8*i+8] for i in range(4)]
    src+=[sub_ref[:,i*D:(i+1)*D] for i in range(FF//D)]
    rows=[rows8(x) for x in src]+[id_ref[0:1],id_ref[1:2]]+[rows8(ts_ref[i]) for i in range(ts_ref.shape[0])]
    out_ref[...]=jnp.concatenate(rows,axis=0).astype(BF)


def sums(ids,sv1,svq,sv2,sub,ts):
    vm=pl.BlockSpec(memory_space=pltpu.VMEM)
    return pl.pallas_call(sums_kernel,in_specs=[vm]*6,out_specs=vm,
        out_shape=S_((VR+ts.shape[0],D),BF),cost_estimate=cost(0,10**6),name="sums")(ids,sv1,svq,sv2,sub,ts)


def group_kernel(idx_ref,*refs,ns,nseq):
    out_ref,acc=refs[ns:]
    tot=refs[0][0:VR].astype(F32)
    for j in range(1,ns):
        tot=tot+refs[j][0:VR].astype(F32)
    for j in range(ns):
        acc[idx_ref[1+j]]=refs[j][VR:VR+nseq].astype(F32)
    out_ref[...]=jnp.concatenate([tot]+[acc[j] for j in range(ns)],axis=0).astype(BF)


def group(idx,pays,nseq):
    ns=len(pays)
    vm=pl.BlockSpec(memory_space=pltpu.VMEM)
    return pl.pallas_call(functools.partial(group_kernel,ns=ns,nseq=nseq),
        in_specs=[pl.BlockSpec(memory_space=pltpu.SMEM)]+[vm]*ns,out_specs=vm,
        out_shape=S_((VR+ns*nseq,D),BF),scratch_shapes=[pltpu.VMEM((ns,nseq,D),F32)],
        cost_estimate=cost(0,10**6),name="group")(idx,*pays)


def table_kernel(idx_ref,*refs,nr,rows,own,me,w,fr):
    sum_refs=refs[nr:nr+8]
    sub_ref,tab_ref,acc,allr=refs[nr+8:]
    r0=idx_ref[me]
    s0=idx_ref[me+1]
    for j in range(nr):
        acc[r0^j]=refs[j][...].astype(F32)
    tot=acc[0,0:VR]
    for r in range(1,nr):
        tot=tot+acc[r,0:VR]
    mine=pltpu.roll(tot[0:8],D-s0*w,1)
    for i,ref in enumerate(sum_refs):
        ref[...]=mine[i:i+1,0:w].reshape(w)
    wide=jnp.concatenate([tot[8+i:9+i] for i in range(FF//D)],axis=1)
    sub_ref[...]=pltpu.roll(jnp.broadcast_to(wide,(8,FF)),FF-s0*fr,1)[0:1,0:fr].reshape(fr)
    for r in range(nr):
        allr[r*rows:(r+1)*rows,:]=acc[r,VR:VR+rows]
    n=nr*rows
    ids=tot[NV:NV+1,0:n]*32.0+tot[NV+1:NV+2,0:n]
    line=lax.broadcasted_iota(jnp.int32,(own,n),0)+s0*own
    hit=jnp.where(line==ids.astype(jnp.int32),1.0,0.0).astype(BF)
    tab_ref[...]=nn(hit,allr[...].astype(BF))


def table(idx,pays,own,w,fr):
    nr=len(pays)
    rows=pays[0].shape[0]-VR
    vm=pl.BlockSpec(memory_space=pltpu.VMEM)
    return pl.pallas_call(functools.partial(table_kernel,nr=nr,rows=rows,own=own,me=idx.shape[0]-3,w=w,fr=fr),
        in_specs=[pl.BlockSpec(memory_space=pltpu.SMEM)]+[vm]*nr,out_specs=[vm]*10,
        out_shape=[S_((w,),F32)]*8+[S_((fr,),F32),S_((own,D),F32)],
        scratch_shapes=[pltpu.VMEM((nr,VR+rows,D),F32),pltpu.VMEM((nr*rows,D),F32)],
        cost_estimate=cost(0,4*10**6),name="table")(idx,*pays)


def unpack_kernel(idx_ref,a_ref,b_ref,*outs,parts):
    for ch in (0,1):
        @pl.when(idx_ref[0]==ch)
        def _():
            for h,ref in enumerate((a_ref,b_ref) if ch==0 else (b_ref,a_ref)):
                r0=0
                for out,(nr,nb) in zip(outs,parts):
                    for b in range(nb):
                        out[:,(h*nb+b)*HC:(h*nb+b+1)*HC]=ref[r0:r0+nr,:].astype(F32)
                        r0+=nr


def unpack(idx,a,b,parts):
    vm=pl.BlockSpec(memory_space=pltpu.VMEM)
    return pl.pallas_call(functools.partial(unpack_kernel,parts=parts),
        in_specs=[pl.BlockSpec(memory_space=pltpu.SMEM),vm,vm],out_specs=[vm]*len(parts),
        out_shape=[S_((nr,2*nb*HC),F32) for nr,nb in parts],
        cost_estimate=cost(0,12*a.shape[0]*HC),name="unpack")(idx,a,b)


def small_kernel(idx_ref,ts_ref,*refs,w,fr,nseq,me):
    me_ref=[idx_ref[me+i] for i in range(3)]
    vecs=refs[:9]
    out_ref,id_ref=refs[9:]
    def spread(rows,width,at):
        n=rows[0].shape[1]
        y=jnp.concatenate(rows+[jnp.zeros((8-len(rows),n),F32)]*(len(rows)<8),axis=0)
        y=jnp.concatenate([y,jnp.zeros((8,width-n),F32)],axis=1)
        return pltpu.roll(y,at,1)
    row=lambda ref: ref[...].astype(F32).reshape(1,ref.shape[0])
    v=spread([row(r) for r in vecs[:8]],D,me_ref[1]*w)
    u=spread([row(vecs[8])],FF,me_ref[1]*fr)
    lane=lax.broadcasted_iota(jnp.int32,(1,D),1)
    def steps(at,high):
        y=jnp.zeros((1,D),jnp.int32)
        for i in range(nseq):
            t=ts_ref[i]
            y=jnp.where(lane==at*nseq+i,t//32 if high else t%32,y)
        return y.astype(F32)
    id_ref[...]=jnp.concatenate([steps(me_ref[2],True),steps(me_ref[2],False)],axis=0)
    out_ref[...]=jnp.concatenate([v]+[u[0:1,i*D:(i+1)*D] for i in range(FF//D)]+[steps(me_ref[1],True),steps(me_ref[1],False)],axis=0).astype(BF)


def small_rows(idx,time_steps,vecs):
    vm=pl.BlockSpec(memory_space=pltpu.VMEM)
    sm=pl.BlockSpec(memory_space=pltpu.SMEM)
    return pl.pallas_call(functools.partial(small_kernel,w=vecs[0].shape[0],fr=vecs[8].shape[0],nseq=time_steps.shape[0],me=idx.shape[0]-3),
        in_specs=[sm,sm]+[vm]*9,out_specs=[vm,vm],
        out_shape=[S_((VR,D),BF),S_((2,D),F32)],cost_estimate=cost(0,10**6),name="small")(idx,time_steps,*vecs)


class Ring:
    def __init__(self,rep,shard):
        self.R,self.S=rep,shard
        self.nb=shard.bit_length()-1
        self.Z=rep//2
        r=lax.axis_index("rep")
        self.s=lax.axis_index("shard")
        self.c=r%2
        self.z=r//2

    def move(self,x,to):
        pairs=[]
        for r in range(self.R):
            for s in range(self.S):
                r2,s2=to(r,s)
                pairs.append((r*self.S+s,r2*self.S+s2))
        return lax.ppermute(x,("rep","shard"),pairs)

    def order(self,c,t):
        return (t+c*(self.nb//2))%self.nb

    def mask(self,c,j):
        m=0
        for t in range(self.nb):
            if j>>t&1:
                m|=1<<self.order(c,t)
        return m

    def step(self,x,t):
        return self.move(x,lambda r,s:(r,s^(1<<self.order(r%2,t))))

    def direct(self,x,j):
        return self.move(x,lambda r,s:(r,s^j))

    def core(self,x):
        return self.move(x,lambda r,s:(r^1,s))

    def plane(self,x,j):
        return self.move(x,lambda r,s:(r^(2*j),s))

    def index(self):
        m=[[self.mask(c,j) for j in range(self.S)] for c in (0,1)]
        base=list(range(self.S))
        n=1+3*self.S
        t=jnp.where(self.c==0,jnp.array([0]+base+m[0]+m[1]+[0]*3,jnp.int32),jnp.array([0]+base+m[1]+m[0]+[0]*3,jnp.int32))
        at=jnp.arange(n+3)
        r=self.z*2+self.c
        t=jnp.where(at==0,self.c,t^self.s)
        t=jnp.where(at==n,r,jnp.where(at==n+1,self.s,jnp.where(at==n+2,r*self.S+self.s,t)))
        return t.astype(jnp.int32)


def tie(*xs):
    return lax.optimization_barrier(xs)


def add(*terms):
    y=terms[0].astype(F32)
    for x in terms[1:]:
        y=y+x.astype(F32)
    return y.astype(BF)


def upper(terms,n):
    return add(*[x[n:] for x in terms]),[x[:n] for x in terms]


def plane_rows(g,x):
    x=x.reshape(g.Z,-1,HC)
    return [lax.dynamic_index_in_dim(x,g.z^j,0,keepdims=False) for j in range(1,g.Z)]


def plane_send(g,rows):
    return [g.plane(x,j) for j,x in enumerate(rows,1)]


def plane_sum(g,x,parts):
    mine=lax.dynamic_index_in_dim(x.reshape(g.Z,-1,HC),g.z,0,keepdims=False).astype(F32)
    for p in parts:
        mine=mine+p.astype(F32)
    return mine.astype(BF)


def plane_join(g,mine,parts):
    out=jnp.zeros((g.Z,)+mine.shape,BF)
    for j,p in enumerate([mine]+parts):
        out=lax.dynamic_update_index_in_dim(out,p,g.z^j,0)
    return out.reshape(-1,HC)


def local(tokens,segments,time_steps,time_table,ln1_gain,ln1_bias,q_weight,q_bias,k_weight,v_weight,v_bias,o_weight,o_bias,ln2_gain,ln2_bias,up_weight,up_bias,down_weight,down_bias,cotangent):
    nseq=tokens.shape[0]
    T=nseq*L
    g=Ring(lax.axis_size("rep"),lax.axis_size("shard"))
    S=g.S
    w=ln1_gain.shape[0]
    fr=down_weight.shape[0]
    own=time_table.shape[0]
    idx=g.index()
    small,ids=small_rows(idx,time_steps,(ln1_gain,ln1_bias,q_bias,v_bias,o_bias,ln2_gain,ln2_bias,down_bias,up_bias))
    small,segments,o_weight_,q_weight_=tie(small,segments,o_weight,q_weight)
    pack_a=pack(pack_a_kernel,idx,(q_weight_,k_weight,v_weight),"pack_a")
    mine_a=[g.direct(pack_a,j) for j in range(1,S)]
    segments,pack_a=tie(segments,pack_a)
    vec=small.astype(F32)
    for j in reversed(range(1,S)):
        vec=vec+g.direct(small,j).astype(F32)
    steps=vec[NV,:S*nseq]*32.0+vec[NV+1,:S*nseq]
    hit=steps.astype(jnp.int32)[:,None]==jnp.arange(own)[None,:]+g.s*own
    rows=jnp.dot(hit.astype(BF),time_table,preferred_element_type=F32).astype(BF).reshape(S,nseq,D)
    pick=lambda j: lax.dynamic_index_in_dim(rows,g.s^j,0,keepdims=False)
    picks=[pick(j) for j in range(S)]
    picks[0],*mine_a=tie(picks[0],*mine_a)
    row=picks[0].astype(F32)
    for j in range(1,S):
        row=row+g.direct(picks[j],j).astype(F32)
    row=row.reshape(nseq,1,D)
    pack_b=pack(pack_b_kernel,idx,(o_weight_,up_weight,down_weight),"pack_b")
    tok=tokens.reshape(T,D)
    cot=cotangent.reshape(T,D)
    fq,fk=seg_features(segments.reshape(T))
    counts=jnp.sum(segments[:,:,None]==jnp.arange(4),axis=1)
    before=jnp.cumsum(counts==MAIN,axis=1)==0
    np_=D//128
    starts=jnp.concatenate([jnp.sum(jnp.where(before,counts,0),axis=1).astype(jnp.int32),
        jnp.array([i//np_ for i in range(nseq*np_)]+[i%np_ for i in range(nseq*np_)],jnp.int32)])
    fq,fk,pack_b,row,*mine_a=tie(fq,fk,pack_b,row,*mine_a)
    other_a=[g.core(x) for x in mine_a]
    mine_b=[pack_b]
    first=[g.step(pack_b,t) for t in range(g.nb)]
    q,k,v,n1t,wqkv=qkv(idx,tok,row,vec,(q_weight,k_weight,v_weight),mine_a,other_a)
    fwd=attn_fwd(starts,q,k,v,fq,fk,(),0,3*nseq//2)
    o1,fx1,*first=tie(*fwd,*first)
    for t in range(g.nb):
        mine_b=mine_b+[first[t]]+[g.step(x,t) for x in mine_b[1:]]
    direct=[1<<t for t in range(g.nb)]
    other_b=[None]+[g.core(x) if j in direct else None for j,x in enumerate(mine_b[1:],1)]
    fwd=attn_fwd(starts,q,k,v,fq,fk,(o1,fx1),3*nseq//2,3*nseq)
    late=[j for j in range(1,S) if j not in direct]
    o1,fx1,*got=tie(*fwd,*[mine_b[j] for j in late])
    for j,x in zip(late,got):
        mine_b[j]=x
        other_b[j]=g.core(x)
    att,fx=attn_fwd(starts,q,k,v,fq,fk,(o1,fx1),9*nseq//2,6*nseq-9*nseq//2)
    res,gm,ga,keep_b,send_b,sv2,sub=mid(idx,tok,row,att,cot,vec,(o_weight,up_weight,down_weight),mine_b[1:],other_b[1:])
    cuts=[0,nseq,nseq+5*nseq//2,5*nseq,6*nseq]
    call=lambda prev,i: attn_bwd(starts,q,k,v,fx,fk,att,ga,prev,cuts[i],cuts[i+1]-cuts[i])
    got=g.core(send_b)
    d=call((),0)
    d,got=tie(d,got)
    n=S
    x=[keep_b]
    for t in reversed(range(g.nb)):
        n//=2
        up,x=upper(x+[got],n)
        d,up=tie(d,up)
        got=g.step(up,t)
        i=g.nb-t
        if i<=2:
            d=call((d,),i)
            d,got=tie(d,got)
    xb=add(*[y[0] for y in x],got[0])
    d,xb,*rows_b=tie(d,xb,*plane_rows(g,xb))
    parts=plane_send(g,rows_b)
    d=call((d,),3)
    keep_a,send_a,svq=dw(idx,n1t,d,S)
    keep_a,send_a,*parts=tie(keep_a,send_a,*parts)
    got=g.core(send_a)
    mine=plane_sum(g,xb,parts)
    back=[g.plane(mine,j) for j in range(1,g.Z)]
    gm,mine_,got=tie(gm,mine,got)
    up,x=upper([keep_a,got],S//2)
    gm,up=tie(gm,up)
    got=g.step(up,g.nb-1)
    gt,sv1,ts=dx(tok,row,d,gm,wqkv,vec)
    ts,got=tie(ts,got)
    n=S//2
    for t in reversed(range(g.nb-1)):
        n//=2
        up,x=upper(x+[got],n)
        ts,up=tie(ts,up)
        got=g.step(up,t)
    pay=sums(ids,sv1,svq,sv2,sub,ts)
    pays=[pay]+[g.direct(pay,j) for j in range(1,S)]
    pays[-1],got=tie(pays[-1],got)
    xa=add(*[y[0] for y in x],got[0])
    rows_a=plane_rows(g,xa)
    *pays,rows_a[0]=tie(*pays,rows_a[0])
    parts_a=plane_send(g,rows_a)
    pay=group(idx,pays,nseq)
    out_b=plane_join(g,mine_,back)
    out_b,pay,*parts_a=tie(out_b,pay,*parts_a)
    other_b=g.core(out_b)
    mine=plane_sum(g,xa,parts_a)
    pay,mine=tie(pay,mine)
    back_a=[g.plane(mine,j) for j in range(1,g.Z)]
    pays=[pay]+[g.move(pay,lambda r,s,j=j:(r^j,s)) for j in range(1,g.R)]
    go,gup,gdn=unpack(idx,out_b,other_b,((w,1),(w,4),(fr,1)))
    gup,*both=tie(gup,*back_a,*pays)
    back_a,pays=both[:g.Z-1],both[g.Z-1:]
    out_a=plane_join(g,mine,back_a)
    other_a=g.core(out_a)
    *sums8,subs,gtab=table(idx,pays,own,w,up_bias.shape[0])
    gtab,other_a=tie(gtab,other_a)
    gq,gk,gv=unpack(idx,out_a,other_a,((w,1),)*3)
    return (res.reshape(tokens.shape),gt.reshape(tokens.shape),gtab,sums8[0],sums8[1],gq,sums8[2],gk,gv,sums8[3],go,sums8[4],sums8[5],sums8[6],gup,subs,gdn,sums8[7])


def solution(mesh):
    b=("rep","shard")
    s=P("shard")
    m=P("shard",None)
    t=P(b,None,None)
    return jax.shard_map(local,mesh=mesh,
        in_specs=(t,P(b,None),P(b),m,s,s,m,s,m,m,s,m,s,s,s,m,s,m,s,t),
        out_specs=(t,t,m,s,s,m,s,m,m,s,m,s,s,s,m,s,m,s),check_vma=False)
```

```python
import functools
import math

import jax
import jax.numpy as jnp
from jax import lax
from jax.experimental import pallas as pl
from jax.experimental.pallas import tpu as pltpu
from jax.sharding import PartitionSpec as P

NEG=-1e30
EPS=1e-5
L=1024
D=768
FF=3072
HC=D//2
BF=jnp.bfloat16
F32=jnp.float32
LOG2E=math.log2(math.e)
LN2=math.log(2.0)
QS=0.125*LOG2E
VR=14
VP=16
NV=12
ANY=pl.BlockSpec(memory_space=pl.ANY)
S_=jax.ShapeDtypeStruct


def nt(a,b):
    return lax.dot_general(a,b,(((1,),(1,)),((),())),preferred_element_type=F32)


def nn(a,b):
    return lax.dot_general(a,b,(((1,),(0,)),((),())),preferred_element_type=F32)


def tn(a,b):
    return lax.dot_general(a,b,(((0,),(0,)),((),())),preferred_element_type=F32)


def full(*s):
    return pl.BlockSpec(s,lambda i,*_:(0,)*len(s),pipeline_mode=pl.Buffered(1))


def norm(x):
    mean=jnp.mean(x,axis=1,keepdims=True)
    off=x-mean
    var=jnp.mean(off*off,axis=1,keepdims=True)
    r=lax.rsqrt(var+EPS)
    return off*r,r


def sum8(x):
    return jnp.sum(x.reshape(x.shape[0]//8,8,x.shape[1]),axis=0)


def cost(flops,nbytes,trans=0):
    return pl.CostEstimate(flops=int(flops)//10,bytes_accessed=int(nbytes)//10,transcendentals=int(trans)//10)


def seg_features(seg):
    lane=jnp.arange(128)%64
    hit=seg[:,None]==lane[None,:]
    first=(lane<4)[None]
    fq=jnp.where(first&hit,1.0,0.0).astype(BF)
    fk=jnp.where(first,jnp.where(hit,0.0,NEG),jnp.where((lane<7)[None],1.0,0.0)).astype(BF)
    return fq,fk


def qkv_kernel(idx_ref,*refs,ns,wr):
    tok_ref,row_ref,vec_ref=refs[:3]
    own=refs[3:6]
    mine=refs[6:6+ns-1]
    other=refs[6+ns-1:6+2*(ns-1)]
    hi=6+2*(ns-1)
    q_ref,k_ref,v_ref,nt_ref,w_ref,sem=refs[hi:hi+6]
    def copies(w):
        c=idx_ref[0]
        cps=[]
        def put(src,sh,cols):
            rows=pl.ds(pl.multiple_of(sh*wr,16),wr)
            dst=w_ref.at[w,rows] if cols is None else w_ref.at[w,rows,pl.ds(pl.multiple_of(cols*HC,128),HC)]
            cps.append(pltpu.make_async_copy(src,dst,sem.at[w,len(cps)]))
        put(own[w],idx_ref[1],None)
        for j in range(1,ns):
            put(mine[j-1].at[pl.ds(w*wr,wr)],idx_ref[1+j],c)
            put(other[j-1].at[pl.ds(w*wr,wr)],idx_ref[1+j],1-c)
        return cps
    first=pl.program_id(0)==0
    @pl.when(first)
    def _():
        for w in range(3):
            for cp in copies(w):
                cp.start()
    def arrived(w):
        @pl.when(first)
        def _():
            for cp in copies(w):
                cp.wait()
    xhat,_=norm(tok_ref[...]+row_ref[0])
    n1=(xhat*vec_ref[0:1,:]+vec_ref[1:2,:]).astype(BF)
    arrived(0)
    q_ref[...]=((nn(n1,w_ref[0])+vec_ref[2:3,:])*QS).astype(BF)
    arrived(1)
    k_ref[...]=nn(n1,w_ref[1]).astype(BF)
    arrived(2)
    v_ref[...]=(nn(n1,w_ref[2])+vec_ref[3:4,:]).astype(BF)
    nt_ref[...]=n1.T


def qkv(idx,tok,row,vec,own,mine,other,tb=512):
    T=tok.shape[0]
    per=L//tb
    ns=len(mine)+1
    wr=own[0].shape[0]
    blk=pl.BlockSpec((tb,D),lambda i,*_:(i,0))
    return pl.pallas_call(
        functools.partial(qkv_kernel,ns=ns,wr=wr),
        grid_spec=pltpu.PrefetchScalarGridSpec(
            num_scalar_prefetch=1,grid=(T//tb,),
            in_specs=[blk,pl.BlockSpec((1,1,D),lambda i,*_:(i//per,0,0)),full(VR,D)]+[ANY]*(3+2*(ns-1)),
            out_specs=[blk]*3+[pl.BlockSpec((D,tb),lambda i,*_:(0,i)),full(3,D,D)],
            scratch_shapes=[pltpu.SemaphoreType.DMA((3,1+2*(ns-1)))]),
        out_shape=[S_((T,D),BF)]*3+[S_((D,T),BF),S_((3,D,D),BF)],
        compiler_params=pltpu.CompilerParams(dimension_semantics=("arbitrary",)),
        cost_estimate=cost(6*T*D*D,T*D*10+9*D*D),
        name="qkv")(idx,tok,row,vec,*own,*mine,*other)


def pack_a_kernel(idx_ref,q_ref,k_ref,v_ref,out_ref):
    wr=q_ref.shape[0]
    for ch in (0,1):
        @pl.when(idx_ref[0]==ch)
        def _():
            for w,ref in enumerate((q_ref,k_ref,v_ref)):
                out_ref[w*wr:(w+1)*wr,:]=ref[:,ch*HC:(ch+1)*HC]


def pack_b_kernel(idx_ref,o_ref,u_ref,d_ref,out_ref):
    wr=o_ref.shape[0]
    for ch in (0,1):
        @pl.when(idx_ref[0]==ch)
        def _():
            out_ref[0:wr,:]=o_ref[:,ch*HC:(ch+1)*HC]
            for b in range(4):
                out_ref[wr+b*wr:2*wr+b*wr,:]=u_ref[:,(ch*4+b)*HC:(ch*4+b+1)*HC]
            out_ref[5*wr:,:]=d_ref[:,ch*HC:(ch+1)*HC]


def pack(kernel,idx,ws,name):
    rows=sum(x.shape[0]*x.shape[1]//D for x in ws)
    vm=pl.BlockSpec(memory_space=pltpu.VMEM)
    return pl.pallas_call(kernel,in_specs=[pl.BlockSpec(memory_space=pltpu.SMEM)]+[vm]*3,out_specs=vm,
        out_shape=S_((rows,HC),BF),cost_estimate=cost(0,4*rows*D),name=name)(idx,*ws)


MAIN=800
ROWS=816
LANES=896
REST=768


def windows(s):
    s16=(s//16)*16
    return pl.multiple_of(jnp.minimum(s16,L-ROWS),16),pl.multiple_of(jnp.minimum(s16,L-LANES),16)


def fwd_kernel(s_ref,q_ref,k_ref,v_ref,fq_ref,fk_ref,*refs,f0,ns):
    o_ref,fx_ref=refs[-2:]
    s0=s_ref[s_ref[ns+f0+pl.program_id(0)]]
    wr,wl=windows(s0)
    lane=lax.broadcasted_iota(jnp.int32,(1,128),1)
    lo=lane<64
    l6=lane&63
    rest_row=lax.broadcasted_iota(jnp.int32,(256,1),0)
    ahead=rest_row<s0
    qb=ROWS//3
    rest=lambda ref: jnp.where(ahead,ref[0:256,:],ref[REST:L,:])
    main=lambda ref: ref[pl.ds(wl,LANES),:]
    one=jnp.where(l6==0,1.0,0.0).astype(BF)
    kv=[]
    for take in (rest,main):
        k=take(k_ref)
        v=take(v_ref)
        fk=take(fk_ref)
        kv.append([(jnp.where(own,k,fk),jnp.where(own,v,one)) for own in (lo,~lo)])
    qf=[(rest(q_ref),rest(fq_ref))]
    for b in range(3):
        rows=pl.ds(pl.multiple_of(wr+b*qb,16),qb)
        qf.append((q_ref[rows,:],fq_ref[rows,:]))
    units=[(b,h) for b in range(4) for h in (0,1)]
    def score(b,h):
        return nt(jnp.where(lo if h==0 else ~lo,*qf[b]),kv[min(b,1)][h][0])
    pend=[score(*u) for u in units[:3]]
    accs=[]
    ls=[]
    for i,(b,h) in enumerate(units):
        s=pend.pop(0)
        if i+3<len(units):
            pend.append(score(*units[i+3]))
        m=jnp.max(s,axis=1,keepdims=True)
        p=jnp.exp2(s-m).astype(BF)
        acc=nn(p,kv[min(b,1)][h][1])
        l=acc[:,64:65] if h==0 else acc[:,0:1]
        accs.append(acc*(1.0/l))
        ls.append(-(m+jnp.log2(l)))
        if h==1:
            o=jnp.where(lo,accs[0],accs[1]).astype(BF)
            nl=jnp.where(lo,ls[1],ls[0])
            hi=nl.astype(BF).astype(F32)
            r1=nl-hi
            mid=r1.astype(BF).astype(F32)
            r2=r1-mid
            fx=jnp.where(l6==4,hi,jnp.where(l6==5,mid,jnp.where(l6==6,r2,qf[b][1].astype(F32)))).astype(BF)
            if b==0:
                o_ref[0:256,:]=o
                fx_ref[0:256,:]=fx
                o_ref[REST:L,:]=o
                fx_ref[REST:L,:]=fx
            else:
                at=wr+(b-1)*qb
                rows=pl.ds(pl.multiple_of(at,16),qb)
                pos=lax.broadcasted_iota(jnp.int32,(qb,1),0)+(at-s0)
                inside=(pos>=0)&(pos<MAIN)
                o_ref[rows,:]=jnp.where(inside,o,o_ref[rows,:])
                fx_ref[rows,:]=jnp.where(inside,fx,fx_ref[rows,:])
            accs=[]
            ls=[]


def attn_fwd(starts,q,k,v,fq,fk,prev,f0,n):
    T=q.shape[0]
    ns=T//L
    nu=ns*(D//128)
    blk=pl.BlockSpec((L,128),lambda i,s:(s[ns+f0+i],s[ns+nu+f0+i]))
    fb=pl.BlockSpec((L,128),lambda i,s:(s[ns+f0+i],0))
    prev=list(prev)
    return pl.pallas_call(
        functools.partial(fwd_kernel,f0=f0,ns=ns),
        grid_spec=pltpu.PrefetchScalarGridSpec(
            num_scalar_prefetch=1,grid=(n,),
            in_specs=[blk,blk,blk,fb,fb]+[ANY]*len(prev),out_specs=[blk,blk]),
        out_shape=[S_((T,D),BF)]*2,
        input_output_aliases={6+i:i for i in range(len(prev))},
        compiler_params=pltpu.CompilerParams(dimension_semantics=("arbitrary",)),
        cost_estimate=cost(n*2*4*L*L*256,n*L*128*14,n*2*L*L),
        name="attn_fwd")(starts,q,k,v,fq,fk,*prev)


def bwd_kernel(s_ref,q_ref,k_ref,v_ref,fx_ref,fk_ref,o_ref,do_ref,*refs,f0,ns):
    out_ref=refs[-1]
    s0=s_ref[s_ref[ns+f0+pl.program_id(0)]]
    wr,wl=windows(s0)
    lane=lax.broadcasted_iota(jnp.int32,(1,128),1)
    lo=lane<64
    l6=lane&63
    zero=jnp.zeros((),BF)
    ones2=jnp.where(l6<2,1.0,0.0).astype(BF)
    rest_row=lax.broadcasted_iota(jnp.int32,(256,1),0)
    ahead=rest_row<s0
    rest=lambda ref: jnp.where(ahead,ref[0:256,:],ref[REST:L,:])
    def block(take_k,nk,takes):
        k=take_k(k_ref)
        v=take_k(v_ref)
        fk=take_k(fk_ref)
        kx=[]
        vx=[]
        km=[]
        for own in (lo,~lo):
            kx.append(jnp.where(own,k,fk))
            vx.append(jnp.where(own,v,ones2))
            km.append(jnp.where(own,k,zero))
        dv=jnp.zeros((nk,128),F32)
        dk=jnp.zeros((nk,128),F32)
        dqs=[]
        for take in takes:
            q=take(q_ref)
            fx=take(fx_ref)
            do=take(do_ref)
            prod=do.astype(F32)*take(o_ref).astype(F32)
            d0=-jnp.sum(jnp.where(lo,prod,0.0),axis=1,keepdims=True)
            d1=-jnp.sum(jnp.where(lo,0.0,prod),axis=1,keepdims=True)
            nd=jnp.where(lo,d1,d0)
            hi=nd.astype(BF).astype(F32)
            fd=jnp.where(l6==0,hi,jnp.where(l6==1,nd-hi,0.0)).astype(BF)
            dq=jnp.zeros(q.shape,F32)
            for h,own in enumerate((lo,~lo)):
                p=jnp.exp2(nt(kx[h],jnp.where(own,q,fx)))
                dpt=nt(vx[h],jnp.where(own,do,fd))
                pb=p.astype(BF)
                ds=(p*dpt).astype(BF)
                dv=dv+nn(pb,jnp.where(own,do,zero))
                dk=dk+nn(ds,jnp.where(own,q,zero))
                dq=dq+tn(ds,km[h])
            dqs.append((dq*0.125).astype(BF))
        return dqs,(dk*LN2).astype(BF),dv.astype(BF)
    dqs,dk,dv=block(rest,256,[rest])
    for w,x in enumerate((dqs[0],dk,dv)):
        out_ref[w,0:256,:]=x
        out_ref[w,REST:L,:]=x
    at=lambda start,n: pl.ds(pl.multiple_of(start,16),n)
    cuts=[(0,256),(256,256),(512,256),(768,128)]
    dqs,dk,dv=block(lambda ref: ref[at(wr,ROWS),:],ROWS,[lambda ref,c=c: ref[at(wl+c[0],c[1]),:] for c in cuts])
    def put(w,start,x):
        n=x.shape[0]
        pos=lax.broadcasted_iota(jnp.int32,(n,1),0)+(start-s0)
        out_ref[w,at(start,n),:]=jnp.where((pos>=0)&(pos<MAIN),x,out_ref[w,at(start,n),:])
    for c,x in zip(cuts,dqs):
        put(0,wl+c[0],x)
    put(1,wr,dk)
    put(2,wr,dv)


def attn_bwd(starts,q,k,v,fx,fk,o,do,prev,f0,n):
    T=q.shape[0]
    ns=T//L
    nu=ns*(D//128)
    blk=pl.BlockSpec((L,128),lambda i,s:(s[ns+f0+i],s[ns+nu+f0+i]))
    fb=pl.BlockSpec((L,128),lambda i,s:(s[ns+f0+i],0))
    prev=list(prev)
    return pl.pallas_call(
        functools.partial(bwd_kernel,f0=f0,ns=ns),
        grid_spec=pltpu.PrefetchScalarGridSpec(
            num_scalar_prefetch=1,grid=(n,),
            in_specs=[blk,blk,blk,blk,fb,blk,blk]+[ANY]*len(prev),
            out_specs=pl.BlockSpec((3,L,128),lambda i,s:(0,s[ns+f0+i],s[ns+nu+f0+i]))),
        out_shape=S_((3,T,D),BF),
        input_output_aliases={8+i:i for i in range(len(prev))},
        compiler_params=pltpu.CompilerParams(dimension_semantics=("arbitrary",)),
        cost_estimate=cost(n*2*10*L*L*256,n*L*128*20,n*2*L*L),
        name="attn_bwd")(starts,q,k,v,fx,fk,o,do,*prev)


def mid_kernel(idx_ref,*refs,tb,fc,ns,wr,fr):
    tok_ref,row_ref,att_ref,cot_ref,vec_ref=refs[:5]
    own=refs[5:8]
    mine=refs[8:8+ns-1]
    other=refs[8+ns-1:8+2*(ns-1)]
    b0=8+2*(ns-1)
    res_ref,gm_ref,ga_ref,keep_ref,send_ref,sv_ref,sub_ref,ow,up,dn,aup,adn,aow,sem=refs[b0:]
    i=pl.program_id(0)
    n=pl.num_programs(0)
    c=idx_ref[0]
    def copies():
        cps=[]
        def put(src,dst):
            cps.append(pltpu.make_async_copy(src,dst,sem.at[len(cps)]))
        r16=lambda sh,m: pl.ds(pl.multiple_of(sh*m,16),m)
        sh=idx_ref[1+ns]
        put(own[0],ow.at[r16(sh,wr)])
        put(own[1],up.at[r16(sh,wr)])
        put(own[2],dn.at[r16(sh,fr)])
        for j in range(1,ns):
            for src,sh,cc in ((mine[j-1],idx_ref[1+ns+j],c),(other[j-1],idx_ref[1+2*ns+j],1-c)):
                cd=pl.ds(pl.multiple_of(cc*HC,128),HC)
                put(src.at[pl.ds(0,wr)],ow.at[r16(sh,wr),cd])
                for b in range(4):
                    put(src.at[pl.ds(wr+b*wr,wr)],up.at[r16(sh,wr),pl.ds(pl.multiple_of(cc*4*HC+b*HC,128),HC)])
                put(src.at[pl.ds(5*wr,fr)],dn.at[r16(sh,fr),cd])
        return cps
    def early():
        return [0]+[3+6*k for k in range(2*(ns-1))]
    @pl.when(i==0)
    def _():
        cps=copies()
        for cp in cps:
            cp.start()
        aup[...]=jnp.zeros_like(aup)
        adn[...]=jnp.zeros_like(adn)
        aow[...]=jnp.zeros_like(aow)
        sv_ref[...]=jnp.zeros_like(sv_ref)
        sub_ref[...]=jnp.zeros_like(sub_ref)
        for k in early():
            cps[k].wait()
    ob=vec_ref[4:5,:]
    g2=vec_ref[5:6,:]
    b2=vec_ref[6:7,:]
    db=vec_ref[7:8,:]
    att=att_ref[...]
    mixed=tok_ref[...]+row_ref[0]+nn(att,ow[...])+ob
    xhat,r=norm(mixed)
    n2=(xhat*g2+b2).astype(BF)
    n2t=n2.T
    cot=cot_ref[...]
    g=cot.astype(BF)
    res=mixed+db
    @pl.when(i==0)
    def _():
        cps=copies()
        for k in range(len(cps)):
            if k not in early():
                cps[k].wait()
    gn2=jnp.zeros((tb,D),F32)
    for j in range(FF//fc):
        cs=slice(j*fc,(j+1)*fc)
        pre=nn(n2,up[:,cs])+vec_ref[8+j:9+j,:]
        gact=nt(g,dn[cs,:])
        phi=0.5+0.5*lax.erf(pre*(2**-0.5))
        pdf=jnp.exp2(pre*pre*(-0.5*LOG2E))*(1.0/math.sqrt(2*math.pi))
        act=(pre*phi).astype(BF)
        gp=gact*(phi+pre*pdf)
        gpre=gp.astype(BF)
        sub_ref[:,cs]+=sum8(gp)
        res=res+nn(act,dn[cs,:])
        gn2=gn2+nt(gpre,up[:,cs])
        adn[cs,:]+=tn(act,g)
        aup[:,cs]+=nn(n2t,gpre)
    res_ref[...]=res
    e=gn2*g2
    c1=jnp.mean(e,axis=1,keepdims=True)
    c2=jnp.mean(e*xhat,axis=1,keepdims=True)
    gm=cot+r*(e-c1-xhat*c2)
    gml=gm.astype(BF)
    gm_ref[...]=gml
    ga_ref[...]=nt(gml,ow[...]).astype(BF)
    aow[...]+=tn(att,gml)
    sv_ref[0:8,:]+=sum8(gm)
    sv_ref[8:16,:]+=sum8(gn2*xhat)
    sv_ref[16:24,:]+=sum8(gn2)
    sv_ref[24:32,:]+=sum8(cot)
    @pl.when(i==n-1)
    def _():
        for ref,base,odd in ((keep_ref,1+ns,0),(send_ref,1+2*ns,1)):
            for ch in (0,1):
                @pl.when(c==(ch+odd)%2)
                def _():
                    def body(j,carry):
                        sh=idx_ref[base+j]
                        rw=pl.ds(pl.multiple_of(sh*wr,8),wr)
                        ref[j,0:wr,:]=aow[rw,ch*HC:(ch+1)*HC].astype(BF)
                        for b in range(4):
                            lo=(ch*4+b)*HC
                            ref[j,wr+b*wr:2*wr+b*wr,:]=aup[rw,lo:lo+HC].astype(BF)
                        ref[j,5*wr:5*wr+fr,:]=adn[pl.ds(pl.multiple_of(sh*fr,8),fr),ch*HC:(ch+1)*HC].astype(BF)
                        return carry
                    lax.fori_loop(0,ns,body,0)


def mid(idx,tok,row,att,cot,vec,own,mine,other,tb=256,fc=D):
    T=tok.shape[0]
    per=L//tb
    ns=len(mine)+1
    wr=own[0].shape[0]
    fr=own[2].shape[0]
    rb=5*wr+fr
    blk=pl.BlockSpec((tb,D),lambda i,*_:(i,0))
    return pl.pallas_call(
        functools.partial(mid_kernel,tb=tb,fc=fc,ns=ns,wr=wr,fr=fr),
        grid_spec=pltpu.PrefetchScalarGridSpec(
            num_scalar_prefetch=1,grid=(T//tb,),
            in_specs=[blk,pl.BlockSpec((1,1,D),lambda i,*_:(i//per,0,0)),blk,blk,full(VR,D)]+[ANY]*(3+2*(ns-1)),
            out_specs=[blk,blk,blk,full(ns,rb,HC),full(ns,rb,HC),full(32,D),full(8,FF)],
            scratch_shapes=[pltpu.VMEM((D,D),BF),pltpu.VMEM((D,FF),BF),pltpu.VMEM((FF,D),BF),
                pltpu.VMEM((D,FF),F32),pltpu.VMEM((FF,D),F32),pltpu.VMEM((D,D),F32),
                pltpu.SemaphoreType.DMA((3+12*(ns-1),))]),
        out_shape=[S_((T,D),F32),S_((T,D),BF),S_((T,D),BF),S_((ns,rb,HC),BF),S_((ns,rb,HC),BF),S_((32,D),F32),S_((8,FF),F32)],
        compiler_params=pltpu.CompilerParams(dimension_semantics=("arbitrary",),vmem_limit_bytes=67043328),
        cost_estimate=cost(6*T*D*(D+2*FF),T*D*20+30*D*FF,2*T*FF),
        name="mid")(idx,tok,row,att,cot,vec,*own,*mine,*other)


def dw_kernel(idx_ref,nt_ref,d_ref,keep_ref,send_ref,acc,*,ns,wr):
    i=pl.program_id(0)
    c=idx_ref[0]
    @pl.when(i==0)
    def _():
        acc[...]=jnp.zeros_like(acc)
    for w in range(3):
        acc[w]+=nn(nt_ref[...],d_ref[w])
    @pl.when(i==pl.num_programs(0)-1)
    def _():
        for ref,base,odd in ((keep_ref,1+ns,0),(send_ref,1+2*ns,1)):
            for ch in (0,1):
                @pl.when(c==(ch+odd)%2)
                def _():
                    def body(j,carry):
                        rw=pl.ds(pl.multiple_of(idx_ref[base+j]*wr,8),wr)
                        for w in range(3):
                            ref[j,w*wr:(w+1)*wr,:]=acc[w,rw,ch*HC:(ch+1)*HC].astype(BF)
                        return carry
                    lax.fori_loop(0,ns,body,0)


def dw(idx,n1t,d,ns,tb=512):
    T=n1t.shape[1]
    wr=D//ns
    return pl.pallas_call(
        functools.partial(dw_kernel,ns=ns,wr=wr),
        grid_spec=pltpu.PrefetchScalarGridSpec(
            num_scalar_prefetch=1,grid=(T//tb,),
            in_specs=[pl.BlockSpec((D,tb),lambda i,*_:(0,i)),pl.BlockSpec((3,tb,D),lambda i,*_:(0,i,0))],
            out_specs=[full(ns,3*wr,HC),full(ns,3*wr,HC)],
            scratch_shapes=[pltpu.VMEM((3,D,D),F32)]),
        out_shape=[S_((ns,3*wr,HC),BF)]*2,
        compiler_params=pltpu.CompilerParams(dimension_semantics=("arbitrary",)),
        cost_estimate=cost(6*T*D*D,T*D*8+12*D*D),
        name="dw")(idx,n1t,d)


def dx_kernel(tok_ref,row_ref,d_ref,gm_ref,w_ref,vec_ref,gt_ref,sv_ref,ts_ref,*,per):
    i=pl.program_id(0)
    @pl.when(i==0)
    def _():
        sv_ref[...]=jnp.zeros_like(sv_ref)
    @pl.when(i%per==0)
    def _():
        ts_ref[...]=jnp.zeros_like(ts_ref)
    gn=nt(d_ref[0],w_ref[0])+nt(d_ref[1],w_ref[1])+nt(d_ref[2],w_ref[2])
    xhat,r=norm(tok_ref[...]+row_ref[0])
    e=gn*vec_ref[0:1,:]
    c1=jnp.mean(e,axis=1,keepdims=True)
    c2=jnp.mean(e*xhat,axis=1,keepdims=True)
    gt=gm_ref[...].astype(F32)+r*(e-c1-xhat*c2)
    gt_ref[...]=gt
    sv_ref[0:8,:]+=sum8(gn*xhat)
    sv_ref[8:16,:]+=sum8(gn)
    sv_ref[16:24,:]+=sum8(d_ref[0].astype(F32))
    sv_ref[24:32,:]+=sum8(d_ref[2].astype(F32))
    ts_ref[0]+=sum8(gt)


def dx(tok,row,d,gm,w,vec,tb=512):
    T=tok.shape[0]
    per=L//tb
    blk=pl.BlockSpec((tb,D),lambda i:(i,0))
    return pl.pallas_call(
        functools.partial(dx_kernel,per=per),grid=(T//tb,),
        in_specs=[blk,pl.BlockSpec((1,1,D),lambda i:(i//per,0,0)),pl.BlockSpec((3,tb,D),lambda i:(0,i,0)),blk,full(3,D,D),full(VR,D)],
        out_specs=[blk,full(32,D),pl.BlockSpec((1,8,D),lambda i:(i//per,0,0))],
        out_shape=[S_((T,D),F32),S_((32,D),F32),S_((T//L,8,D),F32)],
        compiler_params=pltpu.CompilerParams(dimension_semantics=("arbitrary",)),
        cost_estimate=cost(6*T*D*D,T*D*16+6*D*D),
        name="dx")(tok,row,d,gm,w,vec)


def rows8(x):
    return jnp.sum(x,axis=0,keepdims=True)


def sums_kernel(id_ref,sv1_ref,sv2_ref,sub_ref,ts_ref,out_ref):
    src=[sv1_ref[8*i:8*i+8] for i in range(4)]+[sv2_ref[8*i:8*i+8] for i in range(4)]
    src+=[sub_ref[:,i*D:(i+1)*D] for i in range(FF//D)]
    rows=[rows8(x) for x in src]+[id_ref[0:1],id_ref[1:2]]+[rows8(ts_ref[i]) for i in range(ts_ref.shape[0])]
    out_ref[...]=jnp.concatenate(rows,axis=0).astype(BF)


def sums(ids,sv1,sv2,sub,ts):
    vm=pl.BlockSpec(memory_space=pltpu.VMEM)
    return pl.pallas_call(sums_kernel,in_specs=[vm]*5,out_specs=vm,
        out_shape=S_((VR+ts.shape[0],D),BF),cost_estimate=cost(0,10**6),name="sums")(ids,sv1,sv2,sub,ts)


def group_kernel(idx_ref,*refs,ns,nseq):
    out_ref,acc=refs[ns:]
    tot=refs[0][0:VR].astype(F32)
    for j in range(1,ns):
        tot=tot+refs[j][0:VR].astype(F32)
    for j in range(ns):
        acc[idx_ref[1+j]]=refs[j][VR:VR+nseq].astype(F32)
    out_ref[...]=jnp.concatenate([tot]+[acc[j] for j in range(ns)],axis=0).astype(BF)


def group(idx,pays,nseq):
    ns=len(pays)
    vm=pl.BlockSpec(memory_space=pltpu.VMEM)
    return pl.pallas_call(functools.partial(group_kernel,ns=ns,nseq=nseq),
        in_specs=[pl.BlockSpec(memory_space=pltpu.SMEM)]+[vm]*ns,out_specs=vm,
        out_shape=S_((VR+ns*nseq,D),BF),scratch_shapes=[pltpu.VMEM((ns,nseq,D),F32)],
        cost_estimate=cost(0,10**6),name="group")(idx,*pays)


def table_kernel(idx_ref,*refs,nr,rows,own,me,w,fr):
    sum_refs=refs[nr:nr+8]
    sub_ref,tab_ref,acc,allr=refs[nr+8:]
    r0=idx_ref[me]
    s0=idx_ref[me+1]
    for j in range(nr):
        acc[r0^j]=refs[j][...].astype(F32)
    tot=acc[0,0:VR]
    for r in range(1,nr):
        tot=tot+acc[r,0:VR]
    mine=pltpu.roll(tot[0:8],D-s0*w,1)
    for i,ref in enumerate(sum_refs):
        ref[...]=mine[i:i+1,0:w].reshape(w)
    wide=jnp.concatenate([tot[8+i:9+i] for i in range(FF//D)],axis=1)
    sub_ref[...]=pltpu.roll(jnp.broadcast_to(wide,(8,FF)),FF-s0*fr,1)[0:1,0:fr].reshape(fr)
    for r in range(nr):
        allr[r*rows:(r+1)*rows,:]=acc[r,VR:VR+rows]
    n=nr*rows
    ids=tot[NV:NV+1,0:n]*32.0+tot[NV+1:NV+2,0:n]
    line=lax.broadcasted_iota(jnp.int32,(own,n),0)+s0*own
    hit=jnp.where(line==ids.astype(jnp.int32),1.0,0.0).astype(BF)
    tab_ref[...]=nn(hit,allr[...].astype(BF))


def table(idx,pays,own,w,fr):
    nr=len(pays)
    rows=pays[0].shape[0]-VR
    vm=pl.BlockSpec(memory_space=pltpu.VMEM)
    return pl.pallas_call(functools.partial(table_kernel,nr=nr,rows=rows,own=own,me=idx.shape[0]-3,w=w,fr=fr),
        in_specs=[pl.BlockSpec(memory_space=pltpu.SMEM)]+[vm]*nr,out_specs=[vm]*10,
        out_shape=[S_((w,),F32)]*8+[S_((fr,),F32),S_((own,D),F32)],
        scratch_shapes=[pltpu.VMEM((nr,VR+rows,D),F32),pltpu.VMEM((nr*rows,D),F32)],
        cost_estimate=cost(0,4*10**6),name="table")(idx,*pays)


def unpack_kernel(idx_ref,a_ref,b_ref,*outs,parts):
    for ch in (0,1):
        @pl.when(idx_ref[0]==ch)
        def _():
            for h,ref in enumerate((a_ref,b_ref) if ch==0 else (b_ref,a_ref)):
                r0=0
                for out,(nr,nb) in zip(outs,parts):
                    for b in range(nb):
                        out[:,(h*nb+b)*HC:(h*nb+b+1)*HC]=ref[r0:r0+nr,:].astype(F32)
                        r0+=nr


def unpack(idx,a,b,parts):
    vm=pl.BlockSpec(memory_space=pltpu.VMEM)
    return pl.pallas_call(functools.partial(unpack_kernel,parts=parts),
        in_specs=[pl.BlockSpec(memory_space=pltpu.SMEM),vm,vm],out_specs=[vm]*len(parts),
        out_shape=[S_((nr,2*nb*HC),F32) for nr,nb in parts],
        cost_estimate=cost(0,12*a.shape[0]*HC),name="unpack")(idx,a,b)


def small_kernel(idx_ref,ts_ref,*refs,w,fr,nseq,me):
    me_ref=[idx_ref[me+i] for i in range(3)]
    vecs=refs[:9]
    out_ref,id_ref=refs[9:]
    def spread(rows,width,at):
        n=rows[0].shape[1]
        y=jnp.concatenate(rows+[jnp.zeros((8-len(rows),n),F32)]*(len(rows)<8),axis=0)
        y=jnp.concatenate([y,jnp.zeros((8,width-n),F32)],axis=1)
        return pltpu.roll(y,at,1)
    row=lambda ref: ref[...].astype(F32).reshape(1,ref.shape[0])
    v=spread([row(r) for r in vecs[:8]],D,me_ref[1]*w)
    u=spread([row(vecs[8])],FF,me_ref[1]*fr)
    lane=lax.broadcasted_iota(jnp.int32,(1,D),1)
    def steps(at,high):
        y=jnp.zeros((1,D),jnp.int32)
        for i in range(nseq):
            t=ts_ref[i]
            y=jnp.where(lane==at*nseq+i,t//32 if high else t%32,y)
        return y.astype(F32)
    id_ref[...]=jnp.concatenate([steps(me_ref[2],True),steps(me_ref[2],False)],axis=0)
    out_ref[...]=jnp.concatenate([v]+[u[0:1,i*D:(i+1)*D] for i in range(FF//D)]+[steps(me_ref[1],True),steps(me_ref[1],False)],axis=0).astype(BF)


def small_rows(idx,time_steps,vecs):
    vm=pl.BlockSpec(memory_space=pltpu.VMEM)
    sm=pl.BlockSpec(memory_space=pltpu.SMEM)
    return pl.pallas_call(functools.partial(small_kernel,w=vecs[0].shape[0],fr=vecs[8].shape[0],nseq=time_steps.shape[0],me=idx.shape[0]-3),
        in_specs=[sm,sm]+[vm]*9,out_specs=[vm,vm],
        out_shape=[S_((VR,D),BF),S_((2,D),F32)],cost_estimate=cost(0,10**6),name="small")(idx,time_steps,*vecs)


def fold_kernel(*refs):
    y=refs[0][...].astype(F32)
    for ref in refs[1:-1]:
        y=y+ref[...].astype(F32)
    refs[-1][...]=y.astype(BF)


def fold(terms,n):
    rows=terms[0].shape[1]
    cut=2 if n==1 and rows%32==0 else 1
    return pl.pallas_call(fold_kernel,grid=(n,cut),
        in_specs=[pl.BlockSpec((1,rows//cut,HC),lambda i,j:(n+i,j,0))]*len(terms),
        out_specs=pl.BlockSpec((1,rows//cut,HC),lambda i,j:(i,j,0)),
        out_shape=S_((n,rows,HC),BF),cost_estimate=cost(0,4*n*rows*HC),name="fold")(*terms)


class Ring:
    def __init__(self,rep,shard):
        self.R,self.S=rep,shard
        self.nb=shard.bit_length()-1
        self.Z=rep//2
        r=lax.axis_index("rep")
        self.s=lax.axis_index("shard")
        self.c=r%2
        self.z=r//2

    def move(self,x,to):
        pairs=[]
        for r in range(self.R):
            for s in range(self.S):
                r2,s2=to(r,s)
                pairs.append((r*self.S+s,r2*self.S+s2))
        return lax.ppermute(x,("rep","shard"),pairs)

    def order(self,c,t):
        return (t+c*(self.nb//2))%self.nb

    def mask(self,c,j):
        m=0
        for t in range(self.nb):
            if j>>t&1:
                m|=1<<self.order(c,t)
        return m

    def step(self,x,t):
        return self.move(x,lambda r,s:(r,s^(1<<self.order(r%2,t))))

    def direct(self,x,j):
        return self.move(x,lambda r,s:(r,s^j))

    def core(self,x):
        return self.move(x,lambda r,s:(r^1,s))

    def plane(self,x,j):
        return self.move(x,lambda r,s:(r^(2*j),s))

    def index(self):
        m=[[self.mask(c,j) for j in range(self.S)] for c in (0,1)]
        base=list(range(self.S))
        n=1+3*self.S
        t=jnp.where(self.c==0,jnp.array([0]+base+m[0]+m[1]+[0]*3,jnp.int32),jnp.array([0]+base+m[1]+m[0]+[0]*3,jnp.int32))
        at=jnp.arange(n+3)
        r=self.z*2+self.c
        t=jnp.where(at==0,self.c,t^self.s)
        t=jnp.where(at==n,r,jnp.where(at==n+1,self.s,jnp.where(at==n+2,r*self.S+self.s,t)))
        return t.astype(jnp.int32)


def tie(*xs):
    return lax.optimization_barrier(xs)


def add(*terms):
    y=terms[0].astype(F32)
    for x in terms[1:]:
        y=y+x.astype(F32)
    return y.astype(BF)


def upper(terms,n):
    return add(*[x[n:] for x in terms]),[x[:n] for x in terms]


def plane_rows(g,x):
    x=x.reshape(g.Z,-1,HC)
    return [lax.dynamic_index_in_dim(x,g.z^j,0,keepdims=False) for j in range(1,g.Z)]


def plane_send(g,rows):
    return [g.plane(x,j) for j,x in enumerate(rows,1)]


def plane_sum(g,x,parts):
    mine=lax.dynamic_index_in_dim(x.reshape(g.Z,-1,HC),g.z,0,keepdims=False).astype(F32)
    for p in parts:
        mine=mine+p.astype(F32)
    return mine.astype(BF)


def plane_join(g,mine,parts):
    out=jnp.zeros((g.Z,)+mine.shape,BF)
    for j,p in enumerate([mine]+parts):
        out=lax.dynamic_update_index_in_dim(out,p,g.z^j,0)
    return out.reshape(-1,HC)


def local(tokens,segments,time_steps,time_table,ln1_gain,ln1_bias,q_weight,q_bias,k_weight,v_weight,v_bias,o_weight,o_bias,ln2_gain,ln2_bias,up_weight,up_bias,down_weight,down_bias,cotangent):
    nseq=tokens.shape[0]
    T=nseq*L
    g=Ring(lax.axis_size("rep"),lax.axis_size("shard"))
    S=g.S
    w=ln1_gain.shape[0]
    fr=down_weight.shape[0]
    own=time_table.shape[0]
    idx=g.index()
    small,ids=small_rows(idx,time_steps,(ln1_gain,ln1_bias,q_bias,v_bias,o_bias,ln2_gain,ln2_bias,down_bias,up_bias))
    small,segments,o_weight_,q_weight_=tie(small,segments,o_weight,q_weight)
    pack_a=pack(pack_a_kernel,idx,(q_weight_,k_weight,v_weight),"pack_a")
    mine_a=[g.direct(pack_a,j) for j in range(1,S)]
    segments,pack_a=tie(segments,pack_a)
    vec=small.astype(F32)
    for j in reversed(range(1,S)):
        vec=vec+g.direct(small,j).astype(F32)
    steps=vec[NV,:S*nseq]*32.0+vec[NV+1,:S*nseq]
    hit=steps.astype(jnp.int32)[:,None]==jnp.arange(own)[None,:]+g.s*own
    rows=jnp.dot(hit.astype(BF),time_table,preferred_element_type=F32).astype(BF).reshape(S,nseq,D)
    pick=lambda j: lax.dynamic_index_in_dim(rows,g.s^j,0,keepdims=False)
    picks=[pick(j) for j in range(S)]
    picks[0],*mine_a=tie(picks[0],*mine_a)
    row=picks[0].astype(F32)
    for j in range(1,S):
        row=row+g.direct(picks[j],j).astype(F32)
    row=row.reshape(nseq,1,D)
    pack_b=pack(pack_b_kernel,idx,(o_weight_,up_weight,down_weight),"pack_b")
    tok=tokens.reshape(T,D)
    cot=cotangent.reshape(T,D)
    fq,fk=seg_features(segments.reshape(T))
    counts=jnp.sum(segments[:,:,None]==jnp.arange(4),axis=1)
    before=jnp.cumsum(counts==MAIN,axis=1)==0
    np_=D//128
    starts=jnp.concatenate([jnp.sum(jnp.where(before,counts,0),axis=1).astype(jnp.int32),
        jnp.array([i//np_ for i in range(nseq*np_)]+[i%np_ for i in range(nseq*np_)],jnp.int32)])
    fq,fk,pack_b,row,*mine_a=tie(fq,fk,pack_b,row,*mine_a)
    other_a=[g.core(x) for x in mine_a]
    mine_b=[pack_b]
    first=[g.step(pack_b,t) for t in range(g.nb)]
    q,k,v,n1t,wqkv=qkv(idx,tok,row,vec,(q_weight,k_weight,v_weight),mine_a,other_a)
    fwd=attn_fwd(starts,q,k,v,fq,fk,(),0,3*nseq//2)
    o1,fx1,*first=tie(*fwd,*first)
    for t in range(g.nb):
        mine_b=mine_b+[first[t]]+[g.step(x,t) for x in mine_b[1:]]
    direct=[1<<t for t in range(g.nb)]
    other_b=[None]+[g.core(x) if j in direct else None for j,x in enumerate(mine_b[1:],1)]
    fwd=attn_fwd(starts,q,k,v,fq,fk,(o1,fx1),3*nseq//2,3*nseq)
    late=[j for j in range(1,S) if j not in direct]
    o1,fx1,*got=tie(*fwd,*[mine_b[j] for j in late])
    for j,x in zip(late,got):
        mine_b[j]=x
        other_b[j]=g.core(x)
    att,fx=attn_fwd(starts,q,k,v,fq,fk,(o1,fx1),9*nseq//2,6*nseq-9*nseq//2)
    res,gm,ga,keep_b,send_b,sv2,sub=mid(idx,tok,row,att,cot,vec,(o_weight,up_weight,down_weight),mine_b[1:],other_b[1:])
    cuts=[0,nseq,nseq+5*nseq//2,5*nseq,6*nseq]
    call=lambda prev,i: attn_bwd(starts,q,k,v,fx,fk,att,ga,prev,cuts[i],cuts[i+1]-cuts[i])
    got=g.core(send_b)
    d=call((),0)
    d,got=tie(d,got)
    n=S
    x=[keep_b]
    for t in reversed(range(g.nb)):
        n//=2
        x=x+[got]
        up=fold(x,n)
        d,up=tie(d,up)
        got=g.step(up,t)
        i=g.nb-t
        if i<=2:
            d=call((d,),i)
            d,got=tie(d,got)
    xb=add(*[y[0] for y in x],got[0])
    d,xb,*rows_b=tie(d,xb,*plane_rows(g,xb))
    parts=plane_send(g,rows_b)
    d=call((d,),3)
    keep_a,send_a=dw(idx,n1t,d,S)
    keep_a,send_a,*parts=tie(keep_a,send_a,*parts)
    got=g.core(send_a)
    mine=plane_sum(g,xb,parts)
    back=[g.plane(mine,j) for j in range(1,g.Z)]
    gm,mine_,got=tie(gm,mine,got)
    up,x=upper([keep_a,got],S//2)
    gm,up=tie(gm,up)
    got=g.step(up,g.nb-1)
    gt,sv1,ts=dx(tok,row,d,gm,wqkv,vec)
    ts,got=tie(ts,got)
    n=S//2
    for t in reversed(range(g.nb-1)):
        n//=2
        up,x=upper(x+[got],n)
        ts,up=tie(ts,up)
        got=g.step(up,t)
    pay=sums(ids,sv1,sv2,sub,ts)
    pays=[pay]+[g.direct(pay,j) for j in range(1,S)]
    pays[-1],got=tie(pays[-1],got)
    xa=add(*[y[0] for y in x],got[0])
    rows_a=plane_rows(g,xa)
    *pays,rows_a[0]=tie(*pays,rows_a[0])
    parts_a=plane_send(g,rows_a)
    pay=group(idx,pays,nseq)
    out_b=plane_join(g,mine_,back)
    out_b,pay,*parts_a=tie(out_b,pay,*parts_a)
    other_b=g.core(out_b)
    mine=plane_sum(g,xa,parts_a)
    pay,mine=tie(pay,mine)
    back_a=[g.plane(mine,j) for j in range(1,g.Z)]
    pays=[pay]+[g.move(pay,lambda r,s,j=j:(r^j,s)) for j in range(1,g.R)]
    go,gup,gdn=unpack(idx,out_b,other_b,((w,1),(w,4),(fr,1)))
    gup,*both=tie(gup,*back_a,*pays)
    back_a,pays=both[:g.Z-1],both[g.Z-1:]
    out_a=plane_join(g,mine,back_a)
    other_a=g.core(out_a)
    *sums8,subs,gtab=table(idx,pays,own,w,up_bias.shape[0])
    gtab,other_a=tie(gtab,other_a)
    gq,gk,gv=unpack(idx,out_a,other_a,((w,1),)*3)
    return (res.reshape(tokens.shape),gt.reshape(tokens.shape),gtab,sums8[0],sums8[1],gq,sums8[2],gk,gv,sums8[3],go,sums8[4],sums8[5],sums8[6],gup,subs,gdn,sums8[7])


def solution(mesh):
    b=("rep","shard")
    s=P("shard")
    m=P("shard",None)
    t=P(b,None,None)
    return jax.shard_map(local,mesh=mesh,
        in_specs=(t,P(b,None),P(b),m,s,s,m,s,m,m,s,m,s,s,s,m,s,m,s,t),
        out_specs=(t,t,m,s,s,m,s,m,m,s,m,s,s,s,m,s,m,s),check_vma=False)
```
